128 devices in a mesh: dp: 8 (over y_hi, z), seq: 16 (over x, y_lo, core).
Axes of the slice: x: 4, y: 4 (y_hi: 2, y_lo: 2; y = y_hi * 2 + y_lo), z: 4, core: 2. Of those that a mesh axis runs over, the one named last changes fastest.
Arguments:
- tokens: bfloat16 [8, 2048, 1024], P('dp', 'seq'), may hold values from -6 to 6
- positions: int32 [8, 2048], P('dp', 'seq'), may hold values from 0 to 2047, as said below
- in_gain: bfloat16 [1024], P(('dp', 'seq')), may hold values from 0.099609375 to 1.8984375
- q_gain: bfloat16 [128], P(('dp', 'seq')), may hold values from 0.099609375 to 1.8984375
- k_gain: bfloat16 [128], P(('dp', 'seq')), may hold values from 0.099609375 to 1.8984375
- w_query: bfloat16 [1024, 2048], P(('dp', 'seq')), may hold values from -0.1875 to 0.1875
- w_key: bfloat16 [1024, 1024], P(('dp', 'seq')), may hold values from -0.1875 to 0.1875
- w_value: bfloat16 [1024, 1024], P(('dp', 'seq')), may hold values from -0.1875 to 0.1875
- w_out: bfloat16 [2048, 1024], P(None, ('dp', 'seq')), may hold values from -4 to 4
- post_gain: bfloat16 [1024], P(('dp', 'seq')), may hold values from 0.099609375 to 1.8984375
- w_gate: bfloat16 [1024, 3072], P(('dp', 'seq')), may hold values from -0.1875 to 0.1875
- w_up: bfloat16 [1024, 3072], P(('dp', 'seq')), may hold values from -0.1875 to 0.1875
- w_down: bfloat16 [3072, 1024], P(None, ('dp', 'seq')), may hold values from -0.109375 to 0.109375
- cotangent: bfloat16 [8, 2048, 1024], P('dp', 'seq'), may hold values from -6 to 6
Outputs:
- output: bfloat16 [8, 2048, 1024], P('dp', 'seq')
- input_grad: bfloat16 [8, 2048, 1024], P('dp', 'seq')
- in_gain_grad: float32 [1024], P(('dp', 'seq'))
- q_gain_grad: float32 [128], P(('dp', 'seq'))
- k_gain_grad: float32 [128], P(('dp', 'seq'))
- query_grad: float32 [1024, 2048], P(('dp', 'seq'))
- key_grad: float32 [1024, 1024], P(('dp', 'seq'))
- value_grad: float32 [1024, 1024], P(('dp', 'seq'))
- out_grad: float32 [2048, 1024], P(None, ('dp', 'seq'))
- post_gain_grad: float32 [1024], P(('dp', 'seq'))
- gate_grad: float32 [1024, 3072], P(('dp', 'seq'))
- up_grad: float32 [1024, 3072], P(('dp', 'seq'))
- down_grad: float32 [3072, 1024], P(None, ('dp', 'seq'))
The draws below stay inside these ranges and needn't reach their ends.
Inputs may be any that keep to these rules, and one draw needn't show every extreme that they name: `positions`: each sequence is a pack of documents and a token's position is its distance from the first token of its document; the first sequence is a single document.
All inputs are finite; a program needn't handle non-finite values.
Results may differ from the reference program's by a relative error of at most 0.035.
Values may be sent and summed in bfloat16 or wider, within the bound.
A program may use at most 256 MiB of HBM per device.

```python
import math
import jax
import jax.numpy as jnp
from jax import lax

D = 1024
HEADS = 16
KV_HEADS = 8
HEAD_DIM = 128
FF = 3072
BLOCK = 256
SEQS = 8
LEN = 2048


def draw_positions(key, part):
    marks = jax.random.randint(key, (SEQS, LEN), 0, max(LEN // 6, 2))
    spots = jnp.arange(LEN, dtype=jnp.int32)
    seq_rows = jnp.arange(SEQS, dtype=jnp.int32)[:, None]
    begins = (marks == 0) & (seq_rows > 0) | (spots[None, :] == 0)
    latest = lax.cummax(jnp.where(begins, spots[None, :], 0), axis=1)
    return (spots[None, :] - latest).astype(jnp.int32)


def levels(rng, dims, shards, least, high):
    level = 1.0
    for dim, shards_of in shards:
        steps = jax.random.uniform(jax.random.fold_in(jax.random.fold_in(rng, 6), dim), (shards_of,), jnp.float32, least / len(shards), high / len(shards))
        level = level * jnp.repeat(jnp.exp(steps), dims[dim] // shards_of).reshape((-1,) + (1,) * (len(dims) - 1 - dim))
    return level


def centred(stream_key, extent, spread, most, cuts=(), held_as=jnp.bfloat16):
    entries = spread * jax.random.normal(stream_key, extent, jnp.float32)
    if cuts:
        entries = entries * levels(stream_key, extent, cuts, -0.22, 0.18)
    return jnp.clip(entries, -most, most).astype(held_as)


def setup_inputs(seed: int = 0) -> dict:
    seeds = jax.random.split(jax.random.key(seed), 15)
    return {
        "tokens": centred(seeds[0], (SEQS, LEN, D), 1.0, 6.0, ((0, 8), (1, 16))),
        "positions": draw_positions(jax.random.fold_in(seeds[14], 71), 0),
        "in_gain": jnp.clip(1.0 + 0.18 * jax.random.normal(seeds[2], (D,), jnp.float32), 0.099609375, 1.8984375).astype(jnp.bfloat16),
        "q_gain": jnp.clip(1.0 + 0.18 * jax.random.normal(seeds[3], (HEAD_DIM,), jnp.float32), 0.099609375, 1.8984375).astype(jnp.bfloat16),
        "k_gain": jnp.clip(1.0 + 0.18 * jax.random.normal(seeds[4], (HEAD_DIM,), jnp.float32), 0.099609375, 1.8984375).astype(jnp.bfloat16),
        "w_query": centred(seeds[5], (D, HEADS * HEAD_DIM), D ** -0.5, 0.1875, ((0, 128),)),
        "w_key": centred(seeds[6], (D, KV_HEADS * HEAD_DIM), D ** -0.5, 0.1875, ((0, 128),)),
        "w_value": centred(seeds[7], (D, KV_HEADS * HEAD_DIM), D ** -0.5, 0.1875, ((0, 128),)),
        "w_out": centred(seeds[8], (HEADS * HEAD_DIM, D), (max(2 * HEADS * HEAD_DIM // LEN, 1)) ** -0.5, 4.0, ((1, 128),)),
        "post_gain": jnp.clip(1.0 + 0.18 * jax.random.normal(seeds[9], (D,), jnp.float32), 0.099609375, 1.8984375).astype(jnp.bfloat16),
        "w_gate": centred(seeds[10], (D, FF), D ** -0.5, 0.1875, ((0, 128),)),
        "w_up": centred(seeds[11], (D, FF), D ** -0.5, 0.1875, ((0, 128),)),
        "w_down": centred(seeds[12], (FF, D), FF ** -0.5, 0.109375, ((1, 128),)),
        "cotangent": centred(seeds[13], (SEQS, LEN, D), 1.0, 6.0, ((0, 8), (1, 16))),
    }


eps_norm = 1e-06
rope_base = 1000000.0
neg_big = -1e+30
top_prec = lax.Precision.HIGHEST

@jax.custom_vjp
def low(v):
    return lax.optimization_barrier(v.astype(jnp.bfloat16)).astype(jnp.float32)

@jax.custom_vjp
def low_back(v):
    return v

def low_keep(v):
    return (low(v), None)

def low_pass(kept, grad):
    return (grad,)

def back_keep(v):
    return (v, None)

def back_low(kept, grad):
    return (low(grad),)
low.defvjp(low_keep, low_pass)
low_back.defvjp(back_keep, back_low)

def rms_norm(values, gain):
    scale_factor = lax.rsqrt(lax.optimization_barrier(jnp.mean(values * values, axis=-1, keepdims=True)) + eps_norm)
    return values * scale_factor * gain

def rope_tables(places):
    half_dim = HEAD_DIM // 2
    frequency = rope_base ** (-2.0 * jnp.arange(half_dim, dtype=jnp.float32) / HEAD_DIM)
    angles = places.astype(jnp.float32)[:, None] * frequency[None, :]
    cosine = jnp.cos(angles)
    sine_vals = jnp.sin(angles)
    return (jnp.concatenate([cosine, cosine], axis=-1), jnp.concatenate([sine_vals, sine_vals], axis=-1))

def rotate(values, cosine, sine_vals):
    half_dim = values.shape[-1] // 2
    turned = jnp.concatenate([-values[..., half_dim:], values[..., :half_dim]], axis=-1)
    return values * cosine[:, None, :] + turned * sine_vals[:, None, :]

def attend(query_low, key_low, value_low):
    length = key_low.shape[0]
    q_block = min(512, length)
    group_size = HEADS // KV_HEADS
    score_scale = 1.0 / math.sqrt(HEAD_DIM)
    grouped = query_low.reshape(length // q_block, q_block, KV_HEADS, group_size, HEAD_DIM)
    key_marks = jnp.arange(length, dtype=jnp.int32) // BLOCK

    def one_block(packed):
        query_piece, first_row = packed
        raw_scores = jnp.einsum('tkgd,skd->kgts', query_piece, key_low, precision=top_prec) * score_scale
        raw_scores = low_back(raw_scores)
        query_marks = (first_row + jnp.arange(q_block, dtype=jnp.int32)) // BLOCK
        allowed = key_marks[None, :] <= query_marks[:, None]
        probs = jax.nn.softmax(jnp.where(allowed, raw_scores, neg_big), axis=-1)
        return jnp.einsum('kgts,skd->tkgd', low(probs), value_low, precision=top_prec)
    first_rows = jnp.arange(length // q_block, dtype=jnp.int32) * q_block
    mixed = lax.map(jax.checkpoint(one_block), (grouped, first_rows))
    return mixed.reshape(length, HEADS * HEAD_DIM)

def layer(inputs, places, params):
    in_gain, q_gain, k_gain, w_query, w_key, w_value, w_out, post_gain, w_gate, w_up, w_down = params
    length = inputs.shape[0]
    normed = low(rms_norm(inputs, in_gain))
    query_pre = low_back(jnp.dot(normed, w_query, precision=top_prec)).reshape(length, HEADS, HEAD_DIM)
    key_pre = low_back(jnp.dot(normed, w_key, precision=top_prec)).reshape(length, KV_HEADS, HEAD_DIM)
    value_low = low(low_back(jnp.dot(normed, w_value, precision=top_prec))).reshape(length, KV_HEADS, HEAD_DIM)
    cosine, sine_vals = rope_tables(places)
    query_low = low(rotate(rms_norm(query_pre, q_gain), cosine, sine_vals))
    key_low = low(rotate(rms_norm(key_pre, k_gain), cosine, sine_vals))
    attended = low(low_back(attend(query_low, key_low, value_low)))
    middle = inputs + low_back(jnp.dot(attended, w_out, precision=top_prec))
    hidden_in = low(rms_norm(middle, post_gain))
    gate_vals = low_back(jnp.dot(hidden_in, w_gate, precision=top_prec))
    up_vals = low_back(jnp.dot(hidden_in, w_up, precision=top_prec))
    act_low = low(jax.nn.silu(gate_vals) * up_vals)
    return middle + low_back(jnp.dot(act_low, w_down, precision=top_prec))

def reference(tokens, positions, in_gain, q_gain, k_gain, w_query, w_key, w_value, w_out, post_gain, w_gate, w_up, w_down, cotangent):
    weights = (in_gain.astype(jnp.float32), q_gain.astype(jnp.float32), k_gain.astype(jnp.float32), w_query.astype(jnp.float32), w_key.astype(jnp.float32), w_value.astype(jnp.float32), w_out.astype(jnp.float32), post_gain.astype(jnp.float32), w_gate.astype(jnp.float32), w_up.astype(jnp.float32), w_down.astype(jnp.float32))

    def forward(inputs, params):

        def one_seq(packed):
            return jax.checkpoint(layer)(packed[0], packed[1], params)
        return lax.map(one_seq, (inputs, positions))
    result, pull_back = jax.vjp(forward, tokens.astype(jnp.float32), weights)
    grad_inputs, grad_weights = pull_back(cotangent.astype(jnp.float32))
    return (result.astype(jnp.bfloat16), grad_inputs.astype(jnp.bfloat16), grad_weights[0], grad_weights[1], grad_weights[2], grad_weights[3], grad_weights[4], grad_weights[5], grad_weights[6], grad_weights[7], grad_weights[8], grad_weights[9], grad_weights[10])
```

```python
import functools
import math

import jax
import jax.numpy as jnp
from jax import lax
from jax.experimental import pallas as pl
from jax.experimental.pallas import tpu as pltpu
from jax.sharding import PartitionSpec as P

HEADS = 16
KV_HEADS = 8
HEAD_DIM = 128
D = 1024
FF = 3072
BLOCK = 256
CORES = 2

WIDTHS = (1024, 512, 512, 1024, 1536, 1536, 1536)
TILE = 128

eps_norm = 1e-06
rope_base = 1000000.0
score_scale = 1.0 / math.sqrt(HEAD_DIM)
log2e = math.log2(math.e)


def place():
    dp = lax.axis_index("dp")
    seq = lax.axis_index("seq")
    return dp // 4, dp % 4, seq // 4, (seq // 2) % 2, seq % 2


def device(yh, z, x, yl, c):
    return {"dp": yh * 4 + z, "seq": x * 4 + yl * 2 + c}


def sibling():
    yh, z, x, yl, c = place()
    return device(yh, z, x, yl, 1 - c)


def neighbour(axis, step):
    yh, z, x, yl, c = place()
    if axis == "x":
        return device(yh, z, (x + step + 4) % 4, yl, c)
    if axis == "z":
        return device(yh, (z + step + 4) % 4, x, yl, c)
    y = (yh * 2 + yl + step + 4) % 4
    return device(y // 2, z, x, y % 2, c)


ORDERS = (("x", "y", "z"), ("y", "z", "x"), ("z", "x", "y"))


def chip_set(whole_axes, axis, step):
    yh, z, x, yl, _ = place()
    iz, ix, iyh, iyl = z, x, yh, yl
    if axis == "x":
        ix = (x + step + 4) % 4
    elif axis == "z":
        iz = (z + step + 4) % 4
    else:
        y = (yh * 2 + yl + step + 4) % 4
        iyh, iyl = y // 2, y % 2
    every = slice(None)
    if "x" in whole_axes:
        ix = every
    if "z" in whole_axes:
        iz = every
    if "y" in whole_axes:
        iyh, iyl = every, every
    return (iyh, iz, ix, iyl)


def set_dims(whole_axes):
    dims = ()
    if "y" in whole_axes:
        dims += (2,)
    if "z" in whole_axes:
        dims += (4,)
    if "x" in whole_axes:
        dims += (4,)
    if "y" in whole_axes:
        dims += (2,)
    return dims


FULL_PIECES = (
    (((4, 0, 10),), ((5, 0, 10),)),
    (((6, 0, 10),), ((0, 0, 8), (4, 10, 2))),
    (((3, 0, 8), (5, 10, 2)), ((1, 0, 4), (2, 0, 4), (6, 10, 2), (7, 0, 1))),
)


def flat_pieces(pieces):
    out = []
    for colour in range(3):
        for half in range(2):
            for array, first, tiles in pieces[colour][half]:
                out.append((colour, half, array, pl.ds(first * TILE, tiles * TILE), tiles * TILE))
    return out


def greet(others):
    barrier = pltpu.get_barrier_semaphore()
    for other in others:
        pl.semaphore_signal(barrier, inc=1, device_id=other)
    pl.semaphore_wait(barrier, len(others))


def torus_neighbours():
    return [neighbour(axis, step) for axis in ("x", "y", "z") for step in (1, -1)]


def gather_kernel(n_w, n_p, pieces, *refs):
    shards, pairs_in = refs[:n_w], refs[n_w : n_w + n_p]
    outs = refs[n_w + n_p : 2 * n_w + n_p]
    pairs = refs[2 * n_w + n_p : 2 * (n_w + n_p)]
    send, recv, pair_send, pair_recv, local = refs[2 * (n_w + n_p) :]
    yh, z, x, yl, c = place()
    sib = sibling()
    greet(torus_neighbours() + [sib])
    first, later = [], []
    for k in range(n_w):
        mine = outs[k].at[yh, z, x, yl, c]
        own = pltpu.make_async_copy(shards[k].at[c], mine, local.at[k])
        own.start()
        away = pltpu.make_async_remote_copy(
            shards[k].at[1 - c], mine, pair_send.at[k], pair_recv.at[k], device_id=sib
        )
        away.start()
        first += [own, away]
    for k in range(n_p):
        own = pltpu.make_async_copy(pairs_in[k], pairs[k].at[c], local.at[n_w + k])
        own.start()
        away = pltpu.make_async_remote_copy(
            pairs_in[k], pairs[k].at[c], pair_send.at[n_w + k], pair_recv.at[n_w + k], device_id=sib
        )
        away.start()
        later += [own, away]
    for copy in first:
        copy.wait()
    flat = flat_pieces(pieces)
    for phase in range(3):
        copies = {}

        def send_block(n, step, offset, which):
            colour, half, array, cols, _ = flat[n]
            axis, whole = ORDERS[colour][phase], ORDERS[colour][:phase]
            ref = outs[array].at[(*chip_set(whole, axis, offset), slice(None), slice(None), cols)]
            copy = pltpu.make_async_remote_copy(
                ref, ref, send.at[phase, n, which], recv.at[phase, n, which],
                device_id=neighbour(axis, step),
            )
            copy.start()
            copies[n, which] = copy

        for n, piece in enumerate(flat):
            send_block(n, 1 if piece[1] == 0 else -1, 0, 0)
        for n, piece in enumerate(flat):
            send_block(n, -1 if piece[1] == 0 else 1, 0, 1)
        for n, piece in enumerate(flat):
            copies[n, 0].wait_recv()
            step = 1 if piece[1] == 0 else -1
            send_block(n, step, -step, 2)
        for n in range(len(flat)):
            copies[n, 1].wait_recv()
            copies[n, 2].wait_recv()
        for n in range(len(flat)):
            for which in range(3):
                copies[n, which].wait_send()
    for copy in later:
        copy.wait()


def gather_weights(shards, pairs):
    n_w, n_p = len(shards), len(pairs)
    n_pieces = len(flat_pieces(FULL_PIECES))
    any_space = pl.BlockSpec(memory_space=pl.ANY)
    return pl.pallas_call(
        functools.partial(gather_kernel, n_w, n_p, FULL_PIECES),
        out_shape=[jax.ShapeDtypeStruct((2, 4, 4, 2, 2, 8, s.shape[-1]), s.dtype) for s in shards]
        + [jax.ShapeDtypeStruct((2, *p.shape), p.dtype) for p in pairs],
        in_specs=[any_space] * (n_w + n_p),
        out_specs=[any_space] * (n_w + n_p),
        scratch_shapes=[
            pltpu.SemaphoreType.DMA((3, n_pieces, 3)),
            pltpu.SemaphoreType.DMA((3, n_pieces, 3)),
            pltpu.SemaphoreType.DMA((n_w + n_p,)),
            pltpu.SemaphoreType.DMA((n_w + n_p,)),
            pltpu.SemaphoreType.DMA((n_w + n_p,)),
        ],
        compiler_params=pltpu.CompilerParams(collective_id=0, has_side_effects=True),
        name="gather_weights",
    )(*shards, *pairs)


def scatter_kernel(n_w, pieces, *refs):
    grads, outs = refs[:n_w], refs[n_w : 2 * n_w]
    flat = flat_pieces(pieces)
    n_pieces = len(flat)
    scratch = refs[2 * n_w :]
    held, scratch = scratch[:n_w], scratch[n_w:]
    fin, scratch = scratch[:n_w], scratch[n_w:]
    landing, scratch = scratch[: 9 * n_pieces], scratch[9 * n_pieces :]
    send, recv, pair_send, pair_recv, local = scratch
    yh, z, x, yl, c = place()
    sib = sibling()
    loads = [pltpu.make_async_copy(grads[k], held[k], local.at[k]) for k in range(n_w)]
    for load in loads:
        load.start()
    greet(torus_neighbours() + [sib])
    for load in loads:
        load.wait()
    for phase in range(3):
        copies = {}

        def spot(n, offset):
            colour, _, array, cols, _ = flat[n]
            order = ORDERS[colour]
            return held[array].at[
                (*chip_set(order[: 2 - phase], order[2 - phase], offset), slice(None), cols)
            ]

        def send_block(n, offset, step, which):
            axis = ORDERS[flat[n][0]][2 - phase]
            copy = pltpu.make_async_remote_copy(
                spot(n, offset), landing[(phase * n_pieces + n) * 3 + which],
                send.at[phase, n, which], recv.at[phase, n, which],
                device_id=neighbour(axis, step),
            )
            copy.start()
            copies[n, which] = copy

        def add_sets(n, offset, whichs):
            colour, _, _, _, width = flat[n]
            dims = set_dims(ORDERS[colour][: 2 - phase])
            target = spot(n, offset)
            terms = [landing[(phase * n_pieces + n) * 3 + w] for w in whichs]

            def one(flat_index, _):
                index, rest = [], flat_index
                for size in reversed(dims):
                    index.insert(0, rest % size)
                    rest = rest // size
                at = tuple(index)
                total = target[at].astype(jnp.float32)
                for term in terms:
                    total = total + term[at].astype(jnp.float32)
                target[at] = total.astype(jnp.bfloat16)
                return 0

            if dims:
                lax.fori_loop(0, math.prod(dims), one, 0)
            else:
                total = target[...].astype(jnp.float32)
                for term in terms:
                    total = total + term[...].astype(jnp.float32)
                target[...] = total.astype(jnp.bfloat16)

        ways = [1 if piece[1] == 0 else -1 for piece in flat]
        for n in range(n_pieces):
            send_block(n, 2, ways[n], 0)
        for n in range(n_pieces):
            send_block(n, -ways[n], -ways[n], 1)
        for n in range(n_pieces):
            copies[n, 0].wait_recv()
            add_sets(n, ways[n], (0,))
            send_block(n, ways[n], ways[n], 2)
        for n in range(n_pieces):
            copies[n, 1].wait_recv()
            copies[n, 2].wait_recv()
            add_sets(n, 0, (1, 2))
        for n in range(n_pieces):
            for which in range(3):
                copies[n, which].wait_send()
    copies = []
    for k in range(n_w):
        unit = held[k][yh, z, x, yl].astype(jnp.float32)
        fin[k][0] = unit[:8]
        fin[k][1] = unit[8:]
        away = pltpu.make_async_remote_copy(
            fin[k].at[1 - c], outs[k].at[c], pair_send.at[k], pair_recv.at[k], device_id=sib
        )
        away.start()
        outs_own = pltpu.make_async_copy(fin[k].at[c], outs[k].at[c], local.at[k])
        outs_own.start()
        copies += [away, outs_own]
    for copy in copies:
        copy.wait()


def scatter_grads(grads):
    n_w = len(grads)
    flat = flat_pieces(FULL_PIECES)
    n_pieces = len(flat)
    any_space = pl.BlockSpec(memory_space=pl.ANY)
    vmem = pl.BlockSpec(memory_space=pltpu.VMEM)
    landing = []
    for phase in range(3):
        for colour, _, _, _, width in flat:
            dims = set_dims(ORDERS[colour][: 2 - phase])
            landing += [pltpu.VMEM((*dims, 16, width), jnp.bfloat16)] * 3
    return pl.pallas_call(
        functools.partial(scatter_kernel, n_w, FULL_PIECES),
        out_shape=[jax.ShapeDtypeStruct((2, 8, g.shape[-1]), jnp.float32) for g in grads],
        in_specs=[any_space] * n_w,
        out_specs=[vmem] * n_w,
        scratch_shapes=[pltpu.VMEM(g.shape, g.dtype) for g in grads]
        + [pltpu.VMEM((2, 8, g.shape[-1]), jnp.float32) for g in grads]
        + landing
        + [
            pltpu.SemaphoreType.DMA((3, n_pieces, 3)),
            pltpu.SemaphoreType.DMA((3, n_pieces, 3)),
            pltpu.SemaphoreType.DMA((n_w,)),
            pltpu.SemaphoreType.DMA((n_w,)),
            pltpu.SemaphoreType.DMA((n_w,)),
        ],
        compiler_params=pltpu.CompilerParams(
            collective_id=1, has_side_effects=True, vmem_limit_bytes=56 << 20
        ),
        name="scatter_grads",
    )(*grads)


def exchange_kernel(n_in, n_out, items, *refs):
    ins, outs = refs[:n_in], refs[n_in : n_in + n_out]
    send, recv, local = refs[n_in + n_out :]
    yh, z, x, yl, c = place()
    me = x * 2 + yl

    def chip(number):
        return device(yh, z, number // 2, number % 2, c)

    greet([chip((me + step) % 8) for step in range(1, 8)])
    copies = []
    for step in range(1, 8):
        there = (me + step) % 8
        for n, (source, target) in enumerate(items):
            copy = pltpu.make_async_remote_copy(
                source(ins, there), target(outs, me), send.at[step, n], recv.at[step, n],
                device_id=chip(there),
            )
            copy.start()
            copies.append(copy)
    for n, (source, target) in enumerate(items):
        copy = pltpu.make_async_copy(source(ins, me), target(outs, me), local.at[n])
        copy.start()
        copies.append(copy)
    for copy in copies:
        copy.wait()


def exchange(arrays, out_shapes, items, number, name):
    any_space = pl.BlockSpec(memory_space=pl.ANY)
    return pl.pallas_call(
        functools.partial(exchange_kernel, len(arrays), len(out_shapes), items),
        out_shape=[jax.ShapeDtypeStruct(s, jnp.bfloat16) for s in out_shapes],
        in_specs=[any_space] * len(arrays),
        out_specs=[any_space] * len(out_shapes),
        scratch_shapes=[
            pltpu.SemaphoreType.DMA((8, len(items))),
            pltpu.SemaphoreType.DMA((8, len(items))),
            pltpu.SemaphoreType.DMA((len(items),)),
        ],
        compiler_params=pltpu.CompilerParams(collective_id=number, has_side_effects=True),
        name=name,
    )(*arrays)


def columns(head):
    return pl.ds(pl.multiple_of(head * HEAD_DIM, HEAD_DIM), HEAD_DIM)


def head_source(n, share=1):
    return lambda ins, there: ins[n].at[:, columns(there // share)]


def block_target(n):
    return lambda outs, me: outs[n].at[me]


def block_source(n):
    return lambda ins, there: ins[n].at[there]


def head_target(n):
    return lambda outs, me: outs[n].at[:, columns(me)]


def part_target(n):
    return lambda outs, me: outs[n].at[me % 2, :, columns(me // 2)]


def nt(left, right):
    return lax.dot_general(left, right, (((1,), (1,)), ((), ())), preferred_element_type=jnp.float32)


def attend_kernel(q_ref, k_ref, v_ref, o_ref, o32_ref, lse_ref, scores, vt):
    for j in range(8):
        vt[j] = v_ref[j].T

    def one_block(i, _):
        q = q_ref[i]

        def score(j, top):
            s = nt(k_ref[j], q) * (score_scale * log2e)
            scores[j] = s
            return jnp.maximum(top, jnp.max(s, axis=0, keepdims=True))

        top = lax.fori_loop(0, i + 1, score, jnp.full((1, BLOCK), -1e30, jnp.float32))

        def weigh(j, carry):
            total, mixed = carry
            p = jnp.exp2(scores[j] - top)
            total = total + jnp.sum(p, axis=0, keepdims=True)
            mixed = mixed + jnp.dot(vt[j], p.astype(jnp.bfloat16), preferred_element_type=jnp.float32)
            return total, mixed

        total, mixed = lax.fori_loop(
            0, i + 1, weigh,
            (jnp.zeros((1, BLOCK), jnp.float32), jnp.zeros((HEAD_DIM, BLOCK), jnp.float32)),
        )
        out = (mixed / total).T
        o32_ref[i] = out
        o_ref[i] = out.astype(jnp.bfloat16)
        lse_ref[i] = top + jnp.log2(total)
        return 0

    lax.fori_loop(0, 8, one_block, 0)


def attend(q, k, v):
    vmem = pl.BlockSpec(memory_space=pltpu.VMEM)
    return pl.pallas_call(
        attend_kernel,
        out_shape=[
            jax.ShapeDtypeStruct(q.shape, jnp.bfloat16),
            jax.ShapeDtypeStruct(q.shape, jnp.float32),
            jax.ShapeDtypeStruct((8, 1, BLOCK), jnp.float32),
        ],
        in_specs=[vmem] * 3,
        out_specs=[vmem] * 3,
        scratch_shapes=[
            pltpu.VMEM((8, BLOCK, BLOCK), jnp.float32),
            pltpu.VMEM((8, HEAD_DIM, BLOCK), jnp.bfloat16),
        ],
        compiler_params=pltpu.CompilerParams(vmem_limit_bytes=32 << 20),
        name="attend",
    )(q, k, v)


def attend_back_kernel(
    q_ref, k_ref, v_ref, do_ref, o32_ref, lse_ref, dq_ref, dk_ref, dv_ref, kt, dk_acc, dv_acc
):
    for j in range(8):
        kt[j] = k_ref[j].T
    dk_acc[...] = jnp.zeros_like(dk_acc)
    dv_acc[...] = jnp.zeros_like(dv_acc)

    def one_block(i, _):
        q, do, lse = q_ref[i], do_ref[i], lse_ref[i]
        delta = jnp.sum((do.astype(jnp.float32) * o32_ref[i]).T, axis=0, keepdims=True)

        def one_pair(j, dqt):
            p = jnp.exp2(nt(k_ref[j], q) * (score_scale * log2e) - lse)
            dp = nt(v_ref[j], do)
            ds = (p * (dp - delta)).astype(jnp.bfloat16)
            dv_acc[j] += jnp.dot(p.astype(jnp.bfloat16), do, preferred_element_type=jnp.float32)
            dk_acc[j] += jnp.dot(ds, q, preferred_element_type=jnp.float32)
            return dqt + jnp.dot(kt[j], ds, preferred_element_type=jnp.float32)

        dqt = lax.fori_loop(0, i + 1, one_pair, jnp.zeros((HEAD_DIM, BLOCK), jnp.float32))
        dq_ref[i] = (dqt * score_scale).T.astype(jnp.bfloat16)
        return 0

    lax.fori_loop(0, 8, one_block, 0)
    dk_ref[...] = (dk_acc[...] * score_scale).astype(jnp.bfloat16)
    dv_ref[...] = dv_acc[...].astype(jnp.bfloat16)


def attend_back(q, k, v, do, o32, lse):
    vmem = pl.BlockSpec(memory_space=pltpu.VMEM)
    return pl.pallas_call(
        attend_back_kernel,
        out_shape=[jax.ShapeDtypeStruct(q.shape, jnp.bfloat16)] * 3,
        in_specs=[vmem] * 6,
        out_specs=[vmem] * 3,
        scratch_shapes=[
            pltpu.VMEM((8, HEAD_DIM, BLOCK), jnp.bfloat16),
            pltpu.VMEM((8, BLOCK, HEAD_DIM), jnp.float32),
            pltpu.VMEM((8, BLOCK, HEAD_DIM), jnp.float32),
        ],
        compiler_params=pltpu.CompilerParams(vmem_limit_bytes=32 << 20),
        name="attend_back",
    )(q, k, v, do, o32, lse)


def contract(left_op, right_op, left_dim, right_dim):
    return lax.dot_general(
        left_op,
        right_op,
        (((left_dim,), (right_dim,)), ((), ())),
        preferred_element_type=jnp.float32,
    )


def rms_scale(values):
    return lax.rsqrt(jnp.mean(values * values, axis=-1, keepdims=True) + eps_norm)


def norm_back(grad_out, values, scale_factor, gain):
    weighted = grad_out * gain
    inner = jnp.mean(weighted * values, axis=-1, keepdims=True)
    grad_in = (
        scale_factor * weighted - values * (scale_factor * scale_factor * scale_factor) * inner
    )
    return (grad_in, grad_out * values * scale_factor)


def rope_tables(places):
    half_dim = HEAD_DIM // 2
    frequency = rope_base ** (-2.0 * jnp.arange(half_dim, dtype=jnp.float32) / HEAD_DIM)
    angles = places.astype(jnp.float32)[:, None] * frequency[None, :]
    cosine = jnp.cos(angles)
    sine_vals = jnp.sin(angles)
    return (
        jnp.concatenate([cosine, cosine], axis=-1),
        jnp.concatenate([sine_vals, sine_vals], axis=-1),
    )


def rotate(values, cosine, sine_vals):
    half_dim = values.shape[-1] // 2
    turned = jnp.concatenate([-values[..., half_dim:], values[..., :half_dim]], axis=-1)
    return values * cosine[:, None, :] + turned * sine_vals[:, None, :]


def rotate_back(grads, cosine, sine_vals):
    half_dim = grads.shape[-1] // 2
    moved = grads * sine_vals[:, None, :]
    return grads * cosine[:, None, :] + jnp.concatenate(
        [moved[..., half_dim:], -moved[..., :half_dim]], axis=-1
    )


def split_columns(shard):
    rows, width = shard.shape
    return jnp.transpose(shard.reshape(rows, CORES, width // CORES), (1, 0, 2))


def other_core(values):
    return lax.ppermute(values, "seq", [(s, s ^ 1) for s in range(16)])


def body(
    tokens,
    positions,
    in_gain,
    q_gain,
    k_gain,
    w_query,
    w_key,
    w_value,
    w_out,
    post_gain,
    w_gate,
    w_up,
    w_down,
    cotangent,
):
    core = lax.axis_index("seq") % 2
    rows = tokens.shape[1]
    both = 2 * rows

    gain_tile = jnp.zeros((8, TILE), jnp.bfloat16)
    gain_tile = gain_tile.at[:, 0].set(in_gain).at[:, 1].set(post_gain)
    gain_tile = gain_tile.at[0, 2].set(q_gain[0]).at[1, 2].set(k_gain[0])
    shards = [
        split_columns(w)
        for w in (w_query, w_key, w_value, w_out.T, w_gate, w_up, w_down.T)
    ] + [jnp.broadcast_to(gain_tile[None], (2, 8, TILE))]
    gathered = gather_weights(shards, [tokens[0], cotangent[0], positions])
    wq, wk, wv, wo, wg, wu, wd, gains = [w.reshape(D, w.shape[-1]) for w in gathered[:8]]
    inputs = gathered[8].reshape(both, D).astype(jnp.float32)
    grad_low = gathered[9].reshape(both, D)
    places = gathered[10].reshape(both)
    gains = gains[:, :4].astype(jnp.float32)
    gain_in = gains[:, 0]
    gain_post = gains[:, 1]
    gain_qk = gains[:, 2].reshape(HEAD_DIM, 8)
    gain_q, gain_k = gain_qk[:, 0], gain_qk[:, 1]

    def own_rows(values):
        return lax.dynamic_slice_in_dim(values, core * rows, rows, 0)

    def sum_cores_own(values):
        away = lax.dynamic_slice_in_dim(values, (1 - core) * rows, rows, 0)
        return own_rows(values) + other_core(away)

    scale_in = rms_scale(inputs)
    normed = (inputs * scale_in * gain_in).astype(jnp.bfloat16)
    query_pre = jnp.dot(normed, wq, preferred_element_type=jnp.float32).reshape(both, -1, HEAD_DIM)
    key_pre = jnp.dot(normed, wk, preferred_element_type=jnp.float32).reshape(both, -1, HEAD_DIM)
    value_low = jnp.dot(normed, wv, preferred_element_type=jnp.float32).astype(jnp.bfloat16)
    query_scale, key_scale = rms_scale(query_pre), rms_scale(key_pre)
    cosine, sine_vals = rope_tables(places)
    query_low = rotate(query_pre * query_scale * gain_q, cosine, sine_vals).astype(jnp.bfloat16)
    key_low = rotate(key_pre * key_scale * gain_k, cosine, sine_vals).astype(jnp.bfloat16)

    head_blocks = (8, BLOCK, HEAD_DIM)
    q_all, k_all, v_all = exchange(
        [query_low.reshape(both, -1), key_low.reshape(both, -1), value_low],
        [head_blocks] * 3,
        [
            (head_source(0), block_target(0)),
            (head_source(1, 2), block_target(1)),
            (head_source(2, 2), block_target(2)),
        ],
        2,
        "heads_out",
    )
    mixed_low, mixed, log_total = attend(q_all, k_all, v_all)
    (attended_low,) = exchange(
        [mixed_low], [(both, 1024)], [(block_source(0), head_target(0))], 3, "heads_back"
    )
    branch = contract(attended_low, wo, 1, 1)
    middle = inputs + (branch + other_core(branch))
    scale_post = rms_scale(middle)
    hidden_in = (middle * scale_post * gain_post).astype(jnp.bfloat16)
    gate_vals = jnp.dot(hidden_in, wg, preferred_element_type=jnp.float32)
    up_vals = jnp.dot(hidden_in, wu, preferred_element_type=jnp.float32)
    sigma = jax.nn.sigmoid(gate_vals)
    swish = gate_vals * sigma
    act_low = (swish * up_vals).astype(jnp.bfloat16)
    output = (own_rows(middle) + sum_cores_own(contract(act_low, wd, 1, 1))).astype(jnp.bfloat16)

    grad_act = jnp.dot(grad_low, wd, preferred_element_type=jnp.float32)
    slope = sigma * (1.0 + gate_vals * (1.0 - sigma))
    grad_gate = (grad_act * up_vals * slope).astype(jnp.bfloat16)
    grad_up = (grad_act * swish).astype(jnp.bfloat16)
    grad_hidden = contract(grad_gate, wg, 1, 1) + contract(grad_up, wu, 1, 1)
    grad_hidden = grad_hidden + other_core(grad_hidden)
    grad_mid_in, post_terms = norm_back(grad_hidden, middle, scale_post, gain_post)
    grad_middle = grad_low.astype(jnp.float32) + grad_mid_in
    branch_grad = grad_middle.astype(jnp.bfloat16)
    grad_att = jnp.dot(branch_grad, wo, preferred_element_type=jnp.float32).astype(jnp.bfloat16)
    (do_all,) = exchange(
        [grad_att], [head_blocks], [(head_source(0), block_target(0))], 4, "grads_out"
    )
    dq_all, dk_all, dv_all = attend_back(q_all, k_all, v_all, do_all, mixed, log_total)
    grad_query, key_parts, value_parts = exchange(
        [dq_all, dk_all, dv_all],
        [(both, 1024), (2, both, 512), (2, both, 512)],
        [
            (block_source(0), head_target(0)),
            (block_source(1), part_target(1)),
            (block_source(2), part_target(2)),
        ],
        5,
        "grads_back",
    )
    query_rot_grad = rotate_back(
        grad_query.reshape(query_pre.shape).astype(jnp.float32), cosine, sine_vals
    )
    query_pre_grad, q_terms = norm_back(query_rot_grad, query_pre, query_scale, gain_q)
    key_sum = key_parts[0].astype(jnp.float32) + key_parts[1].astype(jnp.float32)
    key_rot_grad = rotate_back(key_sum.reshape(key_pre.shape), cosine, sine_vals)
    key_pre_grad, k_terms = norm_back(key_rot_grad, key_pre, key_scale, gain_k)
    query_grad_low = query_pre_grad.reshape(both, -1).astype(jnp.bfloat16)
    key_grad_low = key_pre_grad.reshape(both, -1).astype(jnp.bfloat16)
    value_grad_low = (
        value_parts[0].astype(jnp.float32) + value_parts[1].astype(jnp.float32)
    ).astype(jnp.bfloat16)
    grad_normed = sum_cores_own(
        contract(query_grad_low, wq, 1, 1)
        + contract(key_grad_low, wk, 1, 1)
        + contract(value_grad_low, wv, 1, 1)
    )
    grad_in_part, in_terms = norm_back(
        grad_normed, own_rows(inputs), own_rows(scale_in), gain_in
    )
    input_grad = (own_rows(grad_middle) + grad_in_part).astype(jnp.bfloat16)

    qk_part = jnp.stack([jnp.sum(q_terms, axis=(0, 1)), jnp.sum(k_terms, axis=(0, 1))], axis=1)
    qk_part = jnp.pad(qk_part, ((0, 0), (0, 6))).reshape(D)
    gain_part = jnp.stack(
        [jnp.sum(in_terms, axis=0), jnp.sum(own_rows(post_terms), axis=0), qk_part], axis=1
    )
    gain_part = jnp.pad(gain_part, ((0, 0), (0, TILE - 3)))
    grads = [
        contract(normed, query_grad_low, 0, 0),
        contract(normed, key_grad_low, 0, 0),
        contract(normed, value_grad_low, 0, 0),
        contract(branch_grad, attended_low, 0, 0),
        contract(hidden_in, grad_gate, 0, 0),
        contract(hidden_in, grad_up, 0, 0),
        contract(grad_low, act_low, 0, 0),
        gain_part,
    ]
    sums = scatter_grads(
        [g.astype(jnp.bfloat16).reshape(2, 4, 4, 2, 16, g.shape[-1]) for g in grads]
    )
    wide = [jnp.concatenate([s[0], s[1]], axis=1) for s in sums[:7]]
    gain_sum = sums[7][0] + sums[7][1]
    return (
        output[None],
        input_grad[None],
        gain_sum[:, 0],
        gain_sum[0:1, 2],
        gain_sum[1:2, 2],
        wide[0],
        wide[1],
        wide[2],
        wide[3].T,
        gain_sum[:, 1],
        wide[4],
        wide[5],
        wide[6].T,
    )


def solution(mesh):
    placed = (
        P("dp", "seq", None),
        P("dp", "seq"),
        P(("dp", "seq")),
        P(("dp", "seq")),
        P(("dp", "seq")),
        P(("dp", "seq"), None),
        P(("dp", "seq"), None),
        P(("dp", "seq"), None),
        P(None, ("dp", "seq")),
        P(("dp", "seq")),
        P(("dp", "seq"), None),
        P(("dp", "seq"), None),
        P(None, ("dp", "seq")),
        P("dp", "seq", None),
    )
    return jax.shard_map(
        body,
        mesh=mesh,
        in_specs=placed,
        out_specs=(
            P("dp", "seq", None),
            P("dp", "seq", None),
            P(("dp", "seq")),
            P(("dp", "seq")),
            P(("dp", "seq")),
            P(("dp", "seq"), None),
            P(("dp", "seq"), None),
            P(("dp", "seq"), None),
            P(None, ("dp", "seq")),
            P(("dp", "seq")),
            P(("dp", "seq"), None),
            P(("dp", "seq"), None),
            P(None, ("dp", "seq")),
        ),
        check_vma=False,
    )
```

```python
import functools
import math

import jax
import jax.numpy as jnp
from jax import lax
from jax.experimental import pallas as pl
from jax.experimental.pallas import tpu as pltpu
from jax.sharding import PartitionSpec as P

HEADS = 16
KV_HEADS = 8
HEAD_DIM = 128
D = 1024
FF = 3072
BLOCK = 256
CORES = 2

TILE = 128

eps_norm = 1e-06
rope_base = 1000000.0
score_scale = 1.0 / math.sqrt(HEAD_DIM)
log2e = math.log2(math.e)


def place():
    dp = lax.axis_index("dp")
    seq = lax.axis_index("seq")
    return dp // 4, dp % 4, seq // 4, (seq // 2) % 2, seq % 2


def device(yh, z, x, yl, c):
    return {"dp": yh * 4 + z, "seq": x * 4 + yl * 2 + c}


def sibling():
    yh, z, x, yl, c = place()
    return device(yh, z, x, yl, 1 - c)


def neighbour(axis, step):
    yh, z, x, yl, c = place()
    if axis == "x":
        return device(yh, z, (x + step + 4) % 4, yl, c)
    if axis == "z":
        return device(yh, (z + step + 4) % 4, x, yl, c)
    y = (yh * 2 + yl + step + 4) % 4
    return device(y // 2, z, x, y % 2, c)


ORDERS = (("x", "y", "z"), ("y", "z", "x"), ("z", "x", "y"))


def chip_set(whole_axes, axis, step):
    yh, z, x, yl, _ = place()
    iz, ix, iyh, iyl = z, x, yh, yl
    if axis == "x":
        ix = (x + step + 4) % 4
    elif axis == "z":
        iz = (z + step + 4) % 4
    else:
        y = (yh * 2 + yl + step + 4) % 4
        iyh, iyl = y // 2, y % 2
    every = slice(None)
    if "x" in whole_axes:
        ix = every
    if "z" in whole_axes:
        iz = every
    if "y" in whole_axes:
        iyh, iyl = every, every
    return (iyh, iz, ix, iyl)


def set_dims(whole_axes):
    dims = ()
    if "y" in whole_axes:
        dims += (2,)
    if "z" in whole_axes:
        dims += (4,)
    if "x" in whole_axes:
        dims += (4,)
    if "y" in whole_axes:
        dims += (2,)
    return dims


NEAR_PIECES = (
    (((0, 0, 3),), ((0, 3, 3),)),
    (((1, 0, 3),), ((2, 0, 3),)),
    (((0, 6, 2), (1, 3, 1)), ((2, 3, 1), (3, 0, 1))),
)
FAR_PIECES = (
    (((4, 0, 8),), ((5, 0, 7),)),
    (((5, 7, 5), (6, 0, 2)), ((6, 2, 8),)),
    (((6, 10, 2), (7, 0, 5)), ((7, 5, 7),)),
)
NEAR = 4


class Piece:
    def __init__(self, colour, half, array, first, tiles):
        self.order = ORDERS[colour]
        self.way = 1 if half == 0 else -1
        self.array = array
        self.width = tiles * TILE
        self.cols = pl.ds(first * TILE, self.width)


def flat_pieces(pieces):
    return [
        Piece(colour, half, *piece)
        for colour in range(3)
        for half in range(2)
        for piece in pieces[colour][half]
    ]


def greet(others):
    barrier = pltpu.get_barrier_semaphore()
    for other in others:
        pl.semaphore_signal(barrier, inc=1, device_id=other)
    pl.semaphore_wait(barrier, len(others))


def torus_neighbours():
    return [neighbour(axis, step) for axis in ("x", "y", "z") for step in (1, -1)]


def sequence_chip(number):
    yh, z, x, yl, c = place()
    return device(yh, z, number // 2, number % 2, c)


def sequence_others():
    yh, z, x, yl, c = place()
    me = x * 2 + yl
    return [sequence_chip((me + step) % 8) for step in range(1, 8)]


ANY = pl.BlockSpec(memory_space=pl.ANY)
VMEM = pl.BlockSpec(memory_space=pltpu.VMEM)


class Gather:
    def __init__(self, outs, send, recv):
        self.outs, self.send, self.recv = outs, send, recv
        self.copies = {}

    def start(self, n, piece, phase, which):
        axis, whole = piece.order[phase], piece.order[:phase]
        step, offset = ((piece.way, 0), (-piece.way, 0), (piece.way, -piece.way))[which]
        ref = self.outs[piece.array].at[
            (*chip_set(whole, axis, offset), slice(None), slice(None), piece.cols)
        ]
        copy = pltpu.make_async_remote_copy(
            ref, ref, self.send.at[n, which], self.recv.at[n, which],
            device_id=neighbour(axis, step),
        )
        copy.start()
        self.copies[n, which] = copy

    def begin(self, active):
        for which in (0, 1):
            for n, piece, phase in active:
                self.start(n, piece, phase, which)

    def forward(self, active):
        for n, piece, phase in active:
            self.copies[n, 0].wait_recv()
            self.start(n, piece, phase, 2)

    def arrive(self, active):
        for n, _, _ in active:
            self.copies[n, 1].wait_recv()
            self.copies[n, 2].wait_recv()

    def drain(self):
        for copy in self.copies.values():
            copy.wait_send()


def gather_kernel(n_w, n_p, *refs):
    shards, pairs_in = refs[:n_w], refs[n_w : n_w + n_p]
    outs = refs[n_w + n_p : 2 * n_w + n_p]
    pairs = refs[2 * n_w + n_p : 2 * (n_w + n_p)]
    send, recv, pair_send, pair_recv, local = refs[2 * (n_w + n_p) :]
    yh, z, x, yl, c = place()
    sib = sibling()
    greet(torus_neighbours() + [sib])
    units, others = [], []
    for k in range(n_w):
        mine = outs[k].at[yh, z, x, yl, c]
        own = pltpu.make_async_copy(shards[k].at[c], mine, local.at[k])
        own.start()
        away = pltpu.make_async_remote_copy(
            shards[k].at[1 - c], mine, pair_send.at[k], pair_recv.at[k], device_id=sib
        )
        away.start()
        units.append((own, away))
    for k in range(n_p):
        own = pltpu.make_async_copy(pairs_in[k], pairs[k].at[c], local.at[n_w + k])
        own.start()
        away = pltpu.make_async_remote_copy(
            pairs_in[k], pairs[k].at[c], pair_send.at[n_w + k], pair_recv.at[n_w + k], device_id=sib
        )
        away.start()
        others.append((own, away))
    near, far = flat_pieces(NEAR_PIECES), flat_pieces(FAR_PIECES)
    gather = Gather(outs, send, recv)
    for own, away in units[:NEAR]:
        own.wait()
        away.wait_recv()
    base = 3 * len(near)
    for stage in range(3):
        active = [(stage * len(near) + n, piece, stage) for n, piece in enumerate(near)]
        if stage == 1:
            for own, away in units[NEAR:]:
                own.wait()
                away.wait_recv()
        if stage >= 1:
            active += [
                (base + (stage - 1) * len(far) + n, piece, stage - 1) for n, piece in enumerate(far)
            ]
        gather.begin(active)
        gather.forward(active)
        gather.arrive(active)
    gather.drain()
    for own, away in units:
        away.wait_send()
    for own, away in others:
        own.wait()
        away.wait()


def gather_weights(shards, pairs):
    n_w, n_p = len(shards), len(pairs)
    count = 3 * len(flat_pieces(NEAR_PIECES)) + 2 * len(flat_pieces(FAR_PIECES))
    return pl.pallas_call(
        functools.partial(gather_kernel, n_w, n_p),
        out_shape=[jax.ShapeDtypeStruct((2, 4, 4, 2, 2, 8, s.shape[-1]), s.dtype) for s in shards]
        + [jax.ShapeDtypeStruct((2, *p.shape), p.dtype) for p in pairs],
        in_specs=[ANY] * (n_w + n_p),
        out_specs=[ANY] * (n_w + n_p),
        scratch_shapes=[
            pltpu.SemaphoreType.DMA((count, 3)),
            pltpu.SemaphoreType.DMA((count, 3)),
            pltpu.SemaphoreType.DMA((n_w + n_p,)),
            pltpu.SemaphoreType.DMA((n_w + n_p,)),
            pltpu.SemaphoreType.DMA((n_w + n_p,)),
        ],
        compiler_params=pltpu.CompilerParams(collective_id=0, has_side_effects=True),
        name="gather_weights",
    )(*shards, *pairs)


def kept_index(kept, axis, step):
    iyh, iz, ix, iyl = chip_set(tuple(a for a in kept if a != axis), axis, step)
    index = ()
    if "y" in kept:
        index += (iyh,)
    if "z" in kept:
        index += (iz,)
    if "x" in kept:
        index += (ix,)
    if "y" in kept:
        index += (iyl,)
    return index


def add_sets(dims, target, terms):
    def one(flat_index, _):
        index, rest = [], flat_index
        for size in reversed(dims):
            index.insert(0, rest % size)
            rest = rest // size
        at = tuple(index)
        total = terms[0][at].astype(jnp.float32)
        for term in terms[1:]:
            total = total + term[at].astype(jnp.float32)
        target[at] = total.astype(jnp.bfloat16)
        return 0

    if dims:
        lax.fori_loop(0, math.prod(dims), one, 0)
    else:
        total = terms[0][...].astype(jnp.float32)
        for term in terms[1:]:
            total = total + term[...].astype(jnp.float32)
        target[...] = total.astype(jnp.bfloat16)


class Scatter:
    def __init__(self, landing, send, recv):
        self.landing, self.send, self.recv = landing, send, recv
        self.copies = {}

    def start(self, n, axis, step, source, which):
        copy = pltpu.make_async_remote_copy(
            source, self.landing[3 * n + which], self.send.at[n, which], self.recv.at[n, which],
            device_id=neighbour(axis, step),
        )
        copy.start()
        self.copies[n, which] = copy

    def drain(self):
        for copy in self.copies.values():
            copy.wait_send()


def scatter_dims(piece, phase):
    return set_dims(piece.order[: 2 - phase])


def landing_shapes(steps):
    return [
        pltpu.VMEM((*scatter_dims(piece, phase), 16, piece.width), jnp.bfloat16)
        for piece, phase in steps
        for _ in range(3)
    ]


def mid_shapes(steps):
    return [
        pltpu.VMEM((*scatter_dims(piece, phase), 16, piece.width), jnp.bfloat16)
        for piece, phase in steps
    ]


def grad_spot(grads, piece, offset):
    return grads[piece.array].at[
        (*chip_set(piece.order[:2], piece.order[2], offset), slice(None), piece.cols)
    ]


def scatter_kernel(n_near, n_planes, n_w, *refs):
    near, far = flat_pieces(NEAR_PIECES), flat_pieces(FAR_PIECES)
    grads, refs = refs[:n_near], refs[n_near:]
    far_planes, refs = refs[:n_planes], refs[n_planes:]
    outs, refs = refs[:n_w], refs[n_w:]
    steps = [(p, ph) for ph in range(3) for p in near] + [(p, ph) for ph in (1, 2) for p in far]
    fin, refs = refs[:n_w], refs[n_w:]
    landing, refs = refs[: 3 * len(steps)], refs[3 * len(steps) :]
    mids, refs = refs[: len(steps)], refs[len(steps) :]
    bases, refs = refs[: len(near)], refs[len(near) :]
    results, refs = refs[: len(steps)], refs[len(steps) :]
    send, recv, pair_send, pair_recv, local, load = refs
    yh, z, x, yl, c = place()
    sib = sibling()
    loads = {}
    for n, piece in enumerate(near):
        for m, (offset, target) in enumerate(((piece.way, mids[n]), (0, bases[n]))):
            loads[n, m] = pltpu.make_async_copy(grad_spot(grads, piece, offset), target, load.at[n, m])
            loads[n, m].start()
    greet(torus_neighbours() + [sib])
    scatter = Scatter(landing, send, recv)
    number = {}
    for n, (piece, phase) in enumerate(steps):
        number[id(piece), phase] = n

    def source(piece, phase, offset):
        if phase == 0:
            return grad_spot(grads, piece, offset)
        axis = piece.order[2 - phase]
        kept = piece.order[: 3 - phase]
        if phase == 1 and (id(piece), 0) not in number:
            held = far_planes[far.index(piece)]
        else:
            held = results[number[id(piece), phase - 1]]
        return held.at[(*kept_index(kept, axis, offset), slice(None), slice(None))]

    for stage in range(3):
        active = [(piece, stage) for piece in near]
        if stage < 2:
            active += [(piece, stage + 1) for piece in far]
        for which in (0, 1):
            for piece, phase in active:
                axis = piece.order[2 - phase]
                offset, step = ((2, piece.way), (-piece.way, -piece.way))[which]
                scatter.start(
                    number[id(piece), phase], axis, step, source(piece, phase, offset), which
                )
        for piece, phase in active:
            n = number[id(piece), phase]
            scatter.copies[n, 0].wait_recv()
            if phase == 0:
                loads[n, 0].wait()
                terms = [mids[n], landing[3 * n]]
            else:
                terms = [source(piece, phase, piece.way), landing[3 * n]]
            add_sets(scatter_dims(piece, phase), mids[n], terms)
            scatter.start(n, piece.order[2 - phase], piece.way, mids[n], 2)
        for piece, phase in active:
            n = number[id(piece), phase]
            scatter.copies[n, 1].wait_recv()
            scatter.copies[n, 2].wait_recv()
            if phase == 0:
                loads[n, 1].wait()
                base = bases[n]
            else:
                base = source(piece, phase, 0)
            if phase < 2:
                add_sets(
                    scatter_dims(piece, phase), results[n], [base, landing[3 * n + 1], landing[3 * n + 2]]
                )
            else:
                total = (
                    base[...].astype(jnp.float32)
                    + landing[3 * n + 1][...].astype(jnp.float32)
                    + landing[3 * n + 2][...].astype(jnp.float32)
                )
                fin[piece.array][0, :, piece.cols] = total[:8]
                fin[piece.array][1, :, piece.cols] = total[8:]
    copies = []
    for k in range(n_w):
        away = pltpu.make_async_remote_copy(
            fin[k].at[1 - c], outs[k].at[c], pair_send.at[k], pair_recv.at[k], device_id=sib
        )
        away.start()
        own = pltpu.make_async_copy(fin[k].at[c], outs[k].at[c], local.at[k])
        own.start()
        copies += [away, own]
    scatter.drain()
    for copy in copies:
        copy.wait()


def scatter_grads(grads, planes, widths):
    near, far = flat_pieces(NEAR_PIECES), flat_pieces(FAR_PIECES)
    steps = [(p, ph) for ph in range(3) for p in near] + [(p, ph) for ph in (1, 2) for p in far]
    n_w = len(widths)
    return pl.pallas_call(
        functools.partial(scatter_kernel, len(grads), len(planes), n_w),
        out_shape=[jax.ShapeDtypeStruct((2, 8, w), jnp.float32) for w in widths],
        in_specs=[ANY] * len(grads) + [VMEM] * len(planes),
        out_specs=[VMEM] * n_w,
        scratch_shapes=[pltpu.VMEM((2, 8, w), jnp.float32) for w in widths]
        + landing_shapes(steps)
        + mid_shapes(steps)
        + mid_shapes([(p, 0) for p in near])
        + mid_shapes(steps)
        + [
            pltpu.SemaphoreType.DMA((len(steps), 3)),
            pltpu.SemaphoreType.DMA((len(steps), 3)),
            pltpu.SemaphoreType.DMA((n_w,)),
            pltpu.SemaphoreType.DMA((n_w,)),
            pltpu.SemaphoreType.DMA((n_w,)),
            pltpu.SemaphoreType.DMA((len(near), 2)),
        ],
        compiler_params=pltpu.CompilerParams(
            collective_id=1, has_side_effects=True, vmem_limit_bytes=56 << 20
        ),
        name="scatter_grads",
    )(*grads, *planes)


def columns(head):
    return pl.ds(pl.multiple_of(head * HEAD_DIM, HEAD_DIM), HEAD_DIM)


def exchange_start(moves, me, send, recv, local, first):
    copies = []
    for step in range(1, 8):
        there = (me + step) % 8
        for n, (source, target) in enumerate(moves):
            copy = pltpu.make_async_remote_copy(
                source(there), target(me), send.at[first + n, step], recv.at[first + n, step],
                device_id=sequence_chip(there),
            )
            copy.start()
            copies.append(copy)
    for n, (source, target) in enumerate(moves):
        copy = pltpu.make_async_copy(source(me), target(me), local.at[first + n])
        copy.start()
        copies.append(copy)
    return copies


def nt(left, right):
    return lax.dot_general(left, right, (((1,), (1,)), ((), ())), preferred_element_type=jnp.float32)


def forward_kernel(*refs):
    q_in, k_in, v_in = refs[:3]
    weights = refs[7:11]
    q_ref, k_ref, v_ref, o32_ref, lse_ref, attended = refs[11:17]
    o_low, scores, vt, send, recv, head_send, head_recv, local = refs[17:]
    yh, z, x, yl, c = place()
    me = x * 2 + yl
    far = flat_pieces(FAR_PIECES)
    greet(torus_neighbours() + sequence_others())
    arriving = exchange_start(
        [
            (lambda j: q_in.at[:, columns(j)], lambda i: q_ref.at[i]),
            (lambda j: k_in.at[:, columns(j // 2)], lambda i: k_ref.at[i]),
            (lambda j: v_in.at[:, columns(j // 2)], lambda i: v_ref.at[i]),
        ],
        me, head_send, head_recv, local, 0,
    )
    gather = Gather([None] * NEAR + list(weights), send, recv)
    active = [(n, piece, 2) for n, piece in enumerate(far)]
    gather.begin(active)
    for copy in arriving:
        copy.wait()
    for j in range(8):
        vt[j] = v_ref[j].T

    def one_block(i, _):
        q = q_ref[i]

        def score(j, top):
            s = nt(k_ref[j], q) * (score_scale * log2e)
            scores[j] = s
            return jnp.maximum(top, jnp.max(s, axis=0, keepdims=True))

        top = lax.fori_loop(0, i + 1, score, jnp.full((1, BLOCK), -1e30, jnp.float32))

        def weigh(j, carry):
            total, mixed = carry
            p = jnp.exp2(scores[j] - top)
            total = total + jnp.sum(p, axis=0, keepdims=True)
            mixed = mixed + jnp.dot(vt[j], p.astype(jnp.bfloat16), preferred_element_type=jnp.float32)
            return total, mixed

        total, mixed = lax.fori_loop(
            0, i + 1, weigh,
            (jnp.zeros((1, BLOCK), jnp.float32), jnp.zeros((HEAD_DIM, BLOCK), jnp.float32)),
        )
        out = (mixed / total).T
        o32_ref[i] = out
        o_low[i] = out.astype(jnp.bfloat16)
        lse_ref[i] = top + jnp.log2(total)
        return 0

    lax.fori_loop(0, 6, one_block, 0)
    gather.forward(active)
    lax.fori_loop(6, 8, one_block, 0)
    leaving = exchange_start(
        [(lambda j: o_low.at[j], lambda i: attended.at[:, columns(i)])],
        me, head_send, head_recv, local, 3,
    )
    gather.arrive(active)
    gather.drain()
    for copy in leaving:
        copy.wait()


def attend(q, k, v, weights):
    blocks = (8, BLOCK, HEAD_DIM)
    n_far = len(flat_pieces(FAR_PIECES))
    return pl.pallas_call(
        forward_kernel,
        out_shape=[jax.ShapeDtypeStruct(w.shape, w.dtype) for w in weights]
        + [jax.ShapeDtypeStruct(blocks, jnp.bfloat16)] * 3
        + [
            jax.ShapeDtypeStruct(blocks, jnp.float32),
            jax.ShapeDtypeStruct((8, 1, BLOCK), jnp.float32),
            jax.ShapeDtypeStruct((BLOCK, 1024), jnp.bfloat16),
        ],
        in_specs=[ANY] * 7,
        out_specs=[ANY] * 4 + [VMEM] * 5 + [ANY],
        input_output_aliases={3: 0, 4: 1, 5: 2, 6: 3},
        scratch_shapes=[
            pltpu.VMEM(blocks, jnp.bfloat16),
            pltpu.VMEM((8, BLOCK, BLOCK), jnp.float32),
            pltpu.VMEM((8, HEAD_DIM, BLOCK), jnp.bfloat16),
            pltpu.SemaphoreType.DMA((n_far, 3)),
            pltpu.SemaphoreType.DMA((n_far, 3)),
            pltpu.SemaphoreType.DMA((4, 8)),
            pltpu.SemaphoreType.DMA((4, 8)),
            pltpu.SemaphoreType.DMA((4,)),
        ],
        compiler_params=pltpu.CompilerParams(
            collective_id=2, has_side_effects=True, vmem_limit_bytes=40 << 20
        ),
        name="attend",
    )(q, k, v, *weights)


def backward_kernel(*refs):
    far = flat_pieces(FAR_PIECES)
    n_far = len(far)
    q_ref, k_ref, v_ref, o32_ref, lse_ref, do_in = refs[:6]
    grads = [None] * NEAR + list(refs[6:10])
    dq_out, dk_out, dv_out = refs[10:13]
    planes, refs = refs[13 : 13 + n_far], refs[13 + n_far :]
    do_ref, dq_low, dk_low, dv_low, kt, dk_acc, dv_acc = refs[:7]
    refs = refs[7:]
    landing, refs = refs[: 3 * n_far], refs[3 * n_far :]
    mids, bases, refs = refs[:n_far], refs[n_far : 2 * n_far], refs[2 * n_far :]
    send, recv, load, head_send, head_recv, local = refs
    yh, z, x, yl, c = place()
    me = x * 2 + yl
    loads = {}
    for n, piece in enumerate(far):
        for m, (offset, target) in enumerate(((piece.way, mids[n]), (0, bases[n]))):
            loads[n, m] = pltpu.make_async_copy(grad_spot(grads, piece, offset), target, load.at[n, m])
            loads[n, m].start()
    greet(torus_neighbours() + sequence_others())
    arriving = exchange_start(
        [(lambda j: do_in.at[:, columns(j)], lambda i: do_ref.at[i])],
        me, head_send, head_recv, local, 0,
    )
    scatter = Scatter(landing, send, recv)
    for which in (0, 1):
        for n, piece in enumerate(far):
            offset, step = ((2, piece.way), (-piece.way, -piece.way))[which]
            scatter.start(n, piece.order[2], step, grad_spot(grads, piece, offset), which)
    for j in range(8):
        kt[j] = k_ref[j].T
    dk_acc[...] = jnp.zeros_like(dk_acc)
    dv_acc[...] = jnp.zeros_like(dv_acc)
    for copy in arriving:
        copy.wait()

    def one_block(i, _):
        q, do, lse = q_ref[i], do_ref[i], lse_ref[i]
        delta = jnp.sum((do.astype(jnp.float32) * o32_ref[i]).T, axis=0, keepdims=True)

        def one_pair(j, dqt):
            p = jnp.exp2(nt(k_ref[j], q) * (score_scale * log2e) - lse)
            dp = nt(v_ref[j], do)
            ds = (p * (dp - delta)).astype(jnp.bfloat16)
            dv_acc[j] += jnp.dot(p.astype(jnp.bfloat16), do, preferred_element_type=jnp.float32)
            dk_acc[j] += jnp.dot(ds, q, preferred_element_type=jnp.float32)
            return dqt + jnp.dot(kt[j], ds, preferred_element_type=jnp.float32)

        dqt = lax.fori_loop(0, i + 1, one_pair, jnp.zeros((HEAD_DIM, BLOCK), jnp.float32))
        dq_low[i] = (dqt * score_scale).T.astype(jnp.bfloat16)
        return 0

    lax.fori_loop(0, 6, one_block, 0)
    for n, piece in enumerate(far):
        scatter.copies[n, 0].wait_recv()
        loads[n, 0].wait()
        add_sets(scatter_dims(piece, 0), mids[n], [mids[n], landing[3 * n]])
        scatter.start(n, piece.order[2], piece.way, mids[n], 2)
    lax.fori_loop(6, 8, one_block, 0)
    dk_low[...] = (dk_acc[...] * score_scale).astype(jnp.bfloat16)
    dv_low[...] = dv_acc[...].astype(jnp.bfloat16)
    leaving = exchange_start(
        [
            (lambda j: dq_low.at[j], lambda i: dq_out.at[:, columns(i)]),
            (lambda j: dk_low.at[j], lambda i: dk_out.at[i % 2, :, columns(i // 2)]),
            (lambda j: dv_low.at[j], lambda i: dv_out.at[i % 2, :, columns(i // 2)]),
        ],
        me, head_send, head_recv, local, 1,
    )
    for n, piece in enumerate(far):
        scatter.copies[n, 1].wait_recv()
        scatter.copies[n, 2].wait_recv()
        loads[n, 1].wait()
        add_sets(scatter_dims(piece, 0), planes[n], [bases[n], landing[3 * n + 1], landing[3 * n + 2]])
    scatter.drain()
    for copy in leaving:
        copy.wait()


def attend_back(saved, grad_att, grads):
    far = flat_pieces(FAR_PIECES)
    n_far = len(far)
    steps = [(p, 0) for p in far]
    blocks = (8, BLOCK, HEAD_DIM)
    return pl.pallas_call(
        backward_kernel,
        out_shape=[
            jax.ShapeDtypeStruct((BLOCK, 1024), jnp.bfloat16),
            jax.ShapeDtypeStruct((2, BLOCK, 512), jnp.bfloat16),
            jax.ShapeDtypeStruct((2, BLOCK, 512), jnp.bfloat16),
        ]
        + [
            jax.ShapeDtypeStruct((*scatter_dims(p, 0), 16, p.width), jnp.bfloat16) for p in far
        ],
        in_specs=[VMEM] * 5 + [ANY] * 5,
        out_specs=[ANY] * 3 + [VMEM] * n_far,
        scratch_shapes=[pltpu.VMEM(blocks, jnp.bfloat16)] * 4
        + [
            pltpu.VMEM((8, HEAD_DIM, BLOCK), jnp.bfloat16),
            pltpu.VMEM(blocks, jnp.float32),
            pltpu.VMEM(blocks, jnp.float32),
        ]
        + landing_shapes(steps)
        + mid_shapes(steps)
        + mid_shapes(steps)
        + [
            pltpu.SemaphoreType.DMA((n_far, 3)),
            pltpu.SemaphoreType.DMA((n_far, 3)),
            pltpu.SemaphoreType.DMA((n_far, 2)),
            pltpu.SemaphoreType.DMA((4, 8)),
            pltpu.SemaphoreType.DMA((4, 8)),
            pltpu.SemaphoreType.DMA((4,)),
        ],
        compiler_params=pltpu.CompilerParams(
            collective_id=3, has_side_effects=True, vmem_limit_bytes=52 << 20
        ),
        name="attend_back",
    )(*saved, grad_att, *grads)


def contract(left_op, right_op, left_dim, right_dim):
    return lax.dot_general(
        left_op,
        right_op,
        (((left_dim,), (right_dim,)), ((), ())),
        preferred_element_type=jnp.float32,
    )


def rms_scale(values):
    return lax.rsqrt(jnp.mean(values * values, axis=-1, keepdims=True) + eps_norm)


def norm_back(grad_out, values, scale_factor, gain):
    weighted = grad_out * gain
    inner = jnp.mean(weighted * values, axis=-1, keepdims=True)
    grad_in = (
        scale_factor * weighted - values * (scale_factor * scale_factor * scale_factor) * inner
    )
    return (grad_in, grad_out * values * scale_factor)


def rope_tables(places):
    half_dim = HEAD_DIM // 2
    frequency = rope_base ** (-2.0 * jnp.arange(half_dim, dtype=jnp.float32) / HEAD_DIM)
    angles = places.astype(jnp.float32)[:, None] * frequency[None, :]
    cosine = jnp.cos(angles)
    sine_vals = jnp.sin(angles)
    return (
        jnp.concatenate([cosine, cosine], axis=-1),
        jnp.concatenate([sine_vals, sine_vals], axis=-1),
    )


def rotate(values, cosine, sine_vals):
    half_dim = values.shape[-1] // 2
    turned = jnp.concatenate([-values[..., half_dim:], values[..., :half_dim]], axis=-1)
    return values * cosine[:, None, :] + turned * sine_vals[:, None, :]


def rotate_back(grads, cosine, sine_vals):
    half_dim = grads.shape[-1] // 2
    moved = grads * sine_vals[:, None, :]
    return grads * cosine[:, None, :] + jnp.concatenate(
        [moved[..., half_dim:], -moved[..., :half_dim]], axis=-1
    )


def split_columns(shard):
    rows, width = shard.shape
    return jnp.transpose(shard.reshape(rows, CORES, width // CORES), (1, 0, 2))


def other_core(values):
    return lax.ppermute(values, "seq", [(s, s ^ 1) for s in range(16)])


def body(
    tokens,
    positions,
    in_gain,
    q_gain,
    k_gain,
    w_query,
    w_key,
    w_value,
    w_out,
    post_gain,
    w_gate,
    w_up,
    w_down,
    cotangent,
):
    core = lax.axis_index("seq") % 2
    rows = tokens.shape[1]
    both = 2 * rows

    gain_tile = jnp.zeros((8, TILE), jnp.bfloat16)
    gain_tile = gain_tile.at[:, 0].set(in_gain).at[:, 1].set(post_gain)
    gain_tile = gain_tile.at[0, 2].set(q_gain[0]).at[1, 2].set(k_gain[0])
    gain_shard = jnp.broadcast_to(gain_tile[None], (2, 8, TILE))
    shards = (
        [split_columns(w) for w in (w_query, w_key, w_value)]
        + [gain_shard]
        + [split_columns(w) for w in (w_out.T, w_gate, w_up, w_down.T)]
    )
    gathered = gather_weights(shards, [tokens[0], cotangent[0], positions])
    wq, wk, wv, gains = [w.reshape(D, w.shape[-1]) for w in gathered[:4]]
    inputs = gathered[8].reshape(both, D).astype(jnp.float32)
    grad_low = gathered[9].reshape(both, D)
    places = gathered[10].reshape(both)
    gains = gains[:, :4].astype(jnp.float32)
    gain_in = gains[:, 0]
    gain_post = gains[:, 1]
    gain_qk = gains[:, 2].reshape(HEAD_DIM, 8)
    gain_q, gain_k = gain_qk[:, 0], gain_qk[:, 1]

    def own_rows(values):
        return lax.dynamic_slice_in_dim(values, core * rows, rows, 0)

    def sum_cores_own(values):
        away = lax.dynamic_slice_in_dim(values, (1 - core) * rows, rows, 0)
        return own_rows(values) + other_core(away)

    scale_in = rms_scale(inputs)
    normed = (inputs * scale_in * gain_in).astype(jnp.bfloat16)
    query_pre = jnp.dot(normed, wq, preferred_element_type=jnp.float32).reshape(both, -1, HEAD_DIM)
    key_pre = jnp.dot(normed, wk, preferred_element_type=jnp.float32).reshape(both, -1, HEAD_DIM)
    value_low = jnp.dot(normed, wv, preferred_element_type=jnp.float32).astype(jnp.bfloat16)
    query_scale, key_scale = rms_scale(query_pre), rms_scale(key_pre)
    cosine, sine_vals = rope_tables(places)
    query_low = rotate(query_pre * query_scale * gain_q, cosine, sine_vals).astype(jnp.bfloat16)
    key_low = rotate(key_pre * key_scale * gain_k, cosine, sine_vals).astype(jnp.bfloat16)

    *far_weights, q_all, k_all, v_all, mixed, log_total, attended_low = attend(
        query_low.reshape(both, -1), key_low.reshape(both, -1), value_low, gathered[4:8]
    )
    saved = (q_all, k_all, v_all, mixed, log_total)
    wo, wg, wu, wd = [w.reshape(D, w.shape[-1]) for w in far_weights]
    branch = contract(attended_low, wo, 1, 1)
    middle = inputs + (branch + other_core(branch))
    scale_post = rms_scale(middle)
    hidden_in = (middle * scale_post * gain_post).astype(jnp.bfloat16)
    gate_vals = jnp.dot(hidden_in, wg, preferred_element_type=jnp.float32)
    up_vals = jnp.dot(hidden_in, wu, preferred_element_type=jnp.float32)
    sigma = jax.nn.sigmoid(gate_vals)
    swish = gate_vals * sigma
    act_low = (swish * up_vals).astype(jnp.bfloat16)
    output = (own_rows(middle) + sum_cores_own(contract(act_low, wd, 1, 1))).astype(jnp.bfloat16)

    grad_act = jnp.dot(grad_low, wd, preferred_element_type=jnp.float32)
    slope = sigma * (1.0 + gate_vals * (1.0 - sigma))
    grad_gate = (grad_act * up_vals * slope).astype(jnp.bfloat16)
    grad_up = (grad_act * swish).astype(jnp.bfloat16)
    grad_hidden = contract(grad_gate, wg, 1, 1) + contract(grad_up, wu, 1, 1)
    grad_hidden = grad_hidden + other_core(grad_hidden)
    grad_mid_in, post_terms = norm_back(grad_hidden, middle, scale_post, gain_post)
    grad_middle = grad_low.astype(jnp.float32) + grad_mid_in
    branch_grad = grad_middle.astype(jnp.bfloat16)
    grad_att = jnp.dot(branch_grad, wo, preferred_element_type=jnp.float32).astype(jnp.bfloat16)
    far_grads = [
        contract(branch_grad, attended_low, 0, 0),
        contract(hidden_in, grad_gate, 0, 0),
        contract(hidden_in, grad_up, 0, 0),
        contract(grad_low, act_low, 0, 0),
    ]

    def by_chip(grad):
        return grad.astype(jnp.bfloat16).reshape(2, 4, 4, 2, 16, grad.shape[-1])

    grad_query, key_parts, value_parts, *planes = attend_back(
        saved, grad_att, [by_chip(g) for g in far_grads]
    )
    query_rot_grad = rotate_back(
        grad_query.reshape(query_pre.shape).astype(jnp.float32), cosine, sine_vals
    )
    query_pre_grad, q_terms = norm_back(query_rot_grad, query_pre, query_scale, gain_q)
    key_sum = key_parts[0].astype(jnp.float32) + key_parts[1].astype(jnp.float32)
    key_rot_grad = rotate_back(key_sum.reshape(key_pre.shape), cosine, sine_vals)
    key_pre_grad, k_terms = norm_back(key_rot_grad, key_pre, key_scale, gain_k)
    query_grad_low = query_pre_grad.reshape(both, -1).astype(jnp.bfloat16)
    key_grad_low = key_pre_grad.reshape(both, -1).astype(jnp.bfloat16)
    value_grad_low = (
        value_parts[0].astype(jnp.float32) + value_parts[1].astype(jnp.float32)
    ).astype(jnp.bfloat16)
    grad_normed = sum_cores_own(
        contract(query_grad_low, wq, 1, 1)
        + contract(key_grad_low, wk, 1, 1)
        + contract(value_grad_low, wv, 1, 1)
    )
    grad_in_part, in_terms = norm_back(
        grad_normed, own_rows(inputs), own_rows(scale_in), gain_in
    )
    input_grad = (own_rows(grad_middle) + grad_in_part).astype(jnp.bfloat16)

    qk_part = jnp.stack([jnp.sum(q_terms, axis=(0, 1)), jnp.sum(k_terms, axis=(0, 1))], axis=1)
    qk_part = jnp.pad(qk_part, ((0, 0), (0, 6))).reshape(D)
    gain_part = jnp.stack(
        [jnp.sum(in_terms, axis=0), jnp.sum(own_rows(post_terms), axis=0), qk_part], axis=1
    )
    gain_part = jnp.pad(gain_part, ((0, 0), (0, TILE - 3)))
    near_grads = [
        contract(normed, query_grad_low, 0, 0),
        contract(normed, key_grad_low, 0, 0),
        contract(normed, value_grad_low, 0, 0),
        gain_part,
    ]
    sums = scatter_grads(
        [by_chip(g) for g in near_grads], planes, [1024, 512, 512, TILE, 1024, 1536, 1536, 1536]
    )
    wide = [jnp.concatenate([s[0], s[1]], axis=1) for s in sums[:3] + sums[4:]]
    gain_sum = sums[3][0] + sums[3][1]
    return (
        output[None],
        input_grad[None],
        gain_sum[:, 0],
        gain_sum[0:1, 2],
        gain_sum[1:2, 2],
        wide[0],
        wide[1],
        wide[2],
        wide[3].T,
        gain_sum[:, 1],
        wide[4],
        wide[5],
        wide[6].T,
    )


def solution(mesh):
    placed = (
        P("dp", "seq", None),
        P("dp", "seq"),
        P(("dp", "seq")),
        P(("dp", "seq")),
        P(("dp", "seq")),
        P(("dp", "seq"), None),
        P(("dp", "seq"), None),
        P(("dp", "seq"), None),
        P(None, ("dp", "seq")),
        P(("dp", "seq")),
        P(("dp", "seq"), None),
        P(("dp", "seq"), None),
        P(None, ("dp", "seq")),
        P("dp", "seq", None),
    )
    return jax.shard_map(
        body,
        mesh=mesh,
        in_specs=placed,
        out_specs=(
            P("dp", "seq", None),
            P("dp", "seq", None),
            P(("dp", "seq")),
            P(("dp", "seq")),
            P(("dp", "seq")),
            P(("dp", "seq"), None),
            P(("dp", "seq"), None),
            P(("dp", "seq"), None),
            P(None, ("dp", "seq")),
            P(("dp", "seq")),
            P(("dp", "seq"), None),
            P(("dp", "seq"), None),
            P(None, ("dp", "seq")),
        ),
        check_vma=False,
    )
```

```python
import functools
import math

import jax
import jax.numpy as jnp
from jax import lax
from jax.experimental import pallas as pl
from jax.experimental.pallas import tpu as pltpu
from jax.sharding import PartitionSpec as P

HEADS = 16
KV_HEADS = 8
HEAD_DIM = 128
D = 1024
FF = 3072
BLOCK = 256
CORES = 2

TILE = 128

eps_norm = 1e-06
rope_base = 1000000.0
score_scale = 1.0 / math.sqrt(HEAD_DIM)
log2e = math.log2(math.e)


def place():
    dp = lax.axis_index("dp")
    seq = lax.axis_index("seq")
    return dp // 4, dp % 4, seq // 4, (seq // 2) % 2, seq % 2


def device(yh, z, x, yl, c):
    return {"dp": yh * 4 + z, "seq": x * 4 + yl * 2 + c}


def sibling():
    yh, z, x, yl, c = place()
    return device(yh, z, x, yl, 1 - c)


def neighbour(axis, step):
    yh, z, x, yl, c = place()
    if axis == "x":
        return device(yh, z, (x + step + 4) % 4, yl, c)
    if axis == "z":
        return device(yh, (z + step + 4) % 4, x, yl, c)
    y = (yh * 2 + yl + step + 4) % 4
    return device(y // 2, z, x, y % 2, c)


ORDERS = (("x", "y", "z"), ("y", "z", "x"), ("z", "x", "y"))


def chip_set(whole_axes, axis, step):
    yh, z, x, yl, _ = place()
    iz, ix, iyh, iyl = z, x, yh, yl
    if axis == "x":
        ix = (x + step + 4) % 4
    elif axis == "z":
        iz = (z + step + 4) % 4
    else:
        y = (yh * 2 + yl + step + 4) % 4
        iyh, iyl = y // 2, y % 2
    every = slice(None)
    if "x" in whole_axes:
        ix = every
    if "z" in whole_axes:
        iz = every
    if "y" in whole_axes:
        iyh, iyl = every, every
    return (iyh, iz, ix, iyl)


def set_dims(whole_axes):
    dims = ()
    if "y" in whole_axes:
        dims += (2,)
    if "z" in whole_axes:
        dims += (4,)
    if "x" in whole_axes:
        dims += (4,)
    if "y" in whole_axes:
        dims += (2,)
    return dims


NEAR_PIECES = (
    (((0, 0, 3),), ((0, 3, 3),)),
    (((1, 0, 3),), ((2, 0, 3),)),
    (((0, 6, 2), (1, 3, 1)), ((2, 3, 1), (3, 0, 1))),
)
FAR_PIECES = (
    (((4, 0, 8),), ((5, 0, 7),)),
    (((5, 7, 5), (6, 0, 2)), ((6, 2, 8),)),
    (((6, 10, 2), (7, 0, 5)), ((7, 5, 7),)),
)
NEAR = 4
LIMIT = 60 << 20


class Piece:
    def __init__(self, colour, half, array, first, tiles):
        self.name = (array, first)
        self.order = ORDERS[colour]
        self.way = 1 if half == 0 else -1
        self.array = array
        self.width = tiles * TILE
        self.cols = pl.ds(first * TILE, self.width)


def flat_pieces(pieces):
    return [
        Piece(colour, half, *piece)
        for colour in range(3)
        for half in range(2)
        for piece in pieces[colour][half]
    ]


def greet(others):
    barrier = pltpu.get_barrier_semaphore()
    for other in others:
        pl.semaphore_signal(barrier, inc=1, device_id=other)
    pl.semaphore_wait(barrier, len(others))


def torus_neighbours():
    return [neighbour(axis, step) for axis in ("x", "y", "z") for step in (1, -1)]


def sequence_chip(number):
    yh, z, x, yl, c = place()
    return device(yh, z, number // 2, number % 2, c)


def sequence_others():
    yh, z, x, yl, c = place()
    me = x * 2 + yl
    return [sequence_chip((me + step) % 8) for step in range(1, 8)]


HBM = pl.BlockSpec(memory_space=pltpu.HBM)
VMEM = pl.BlockSpec(memory_space=pltpu.VMEM)


def load_all(pairs, sems):
    copies = [pltpu.make_async_copy(a, b, sems.at[n]) for n, (a, b) in enumerate(pairs)]
    for copy in copies:
        copy.start()
    return copies


def nt(left, right):
    return lax.dot_general(left, right, (((1,), (1,)), ((), ())), preferred_element_type=jnp.float32)


def rms_scale(values):
    return lax.rsqrt(jnp.mean(values * values, axis=-1, keepdims=True) + eps_norm)


def norm_back(grad_out, values, scale_factor, gain):
    weighted = grad_out * gain
    inner = jnp.mean(weighted * values, axis=-1, keepdims=True)
    grad_in = (
        scale_factor * weighted - values * (scale_factor * scale_factor * scale_factor) * inner
    )
    return (grad_in, grad_out * values * scale_factor)


def rope_pair(tab):
    table = tab[...].reshape(BLOCK, HEAD_DIM)
    turned = pltpu.roll(table, HEAD_DIM // 2, 1)
    low = lax.broadcasted_iota(jnp.int32, (BLOCK, HEAD_DIM), 1) < HEAD_DIM // 2
    return jnp.where(low, table, turned), jnp.where(low, -turned, table)


class Gather:
    def __init__(self, outs, send, recv):
        self.outs, self.send, self.recv = outs, send, recv
        self.copies = {}

    def start(self, n, piece, phase, which):
        axis, whole = piece.order[phase], piece.order[:phase]
        step, offset = ((piece.way, 0), (-piece.way, 0), (piece.way, -piece.way))[which]
        ref = self.outs[piece.array].at[
            (*chip_set(whole, axis, offset), slice(None), slice(None), piece.cols)
        ]
        copy = pltpu.make_async_remote_copy(
            ref, ref, self.send.at[n, which], self.recv.at[n, which],
            device_id=neighbour(axis, step),
        )
        copy.start()
        self.copies[n, which] = copy

    def begin(self, active):
        for which in (0, 1):
            for n, piece, phase in active:
                self.start(n, piece, phase, which)

    def forward(self, active):
        for n, piece, phase in active:
            self.copies[n, 0].wait_recv()
            self.start(n, piece, phase, 2)

    def arrive(self, active):
        for n, _, _ in active:
            self.copies[n, 1].wait_recv()
            self.copies[n, 2].wait_recv()

    def drain(self):
        for copy in self.copies.values():
            copy.wait_send()


def gather_kernel(n_w, n_p, *refs):
    gain_rows, shards, pairs_in = refs[0], list(refs[1:n_w]), refs[n_w : n_w + n_p]
    outs = refs[n_w + n_p : 2 * n_w + n_p]
    pairs = refs[2 * n_w + n_p : 2 * (n_w + n_p)]
    gain_tile, send, recv, pair_send, pair_recv, local = refs[2 * (n_w + n_p) :]
    yh, z, x, yl, c = place()
    sib = sibling()
    rows = jnp.concatenate([gain_rows[...].astype(jnp.float32), jnp.zeros((TILE - 8, TILE), jnp.float32)])
    tile = rows.T[:8].astype(jnp.bfloat16)
    gain_tile[0] = tile
    gain_tile[1] = tile
    shards.insert(NEAR - 1, gain_tile)
    greet(torus_neighbours() + [sib])
    units, others = [], []
    for k in range(n_w):
        mine = outs[k].at[yh, z, x, yl, c]
        own = pltpu.make_async_copy(shards[k].at[c], mine, local.at[k])
        own.start()
        away = pltpu.make_async_remote_copy(
            shards[k].at[1 - c], mine, pair_send.at[k], pair_recv.at[k], device_id=sib
        )
        away.start()
        units.append((own, away))
    for k in range(n_p):
        own = pltpu.make_async_copy(pairs_in[k], pairs[k].at[c], local.at[n_w + k])
        own.start()
        away = pltpu.make_async_remote_copy(
            pairs_in[k], pairs[k].at[c], pair_send.at[n_w + k], pair_recv.at[n_w + k], device_id=sib
        )
        away.start()
        others.append((own, away))
    near, far = flat_pieces(NEAR_PIECES), flat_pieces(FAR_PIECES)
    gather = Gather(outs, send, recv)
    for own, away in units[:NEAR]:
        own.wait()
        away.wait_recv()
    base = 3 * len(near)
    for stage in range(3):
        active = [(stage * len(near) + n, piece, stage) for n, piece in enumerate(near)]
        if stage == 1:
            for own, away in units[NEAR:]:
                own.wait()
                away.wait_recv()
        if stage >= 1:
            active += [
                (base + (stage - 1) * len(far) + n, piece, stage - 1) for n, piece in enumerate(far)
            ]
        gather.begin(active)
        gather.forward(active)
        gather.arrive(active)
    gather.drain()
    for own, away in units:
        away.wait_send()
    for own, away in others:
        own.wait()
        away.wait()


def gather_weights(gain_rows, shards, pairs):
    n_w, n_p = len(shards) + 1, len(pairs)
    count = 3 * len(flat_pieces(NEAR_PIECES)) + 2 * len(flat_pieces(FAR_PIECES))
    widths = [w.shape[-1] for w in shards]
    widths.insert(NEAR - 1, TILE)
    return pl.pallas_call(
        functools.partial(gather_kernel, n_w, n_p),
        out_shape=[jax.ShapeDtypeStruct((2, 4, 4, 2, 2, 8, w), jnp.bfloat16) for w in widths]
        + [jax.ShapeDtypeStruct((2, *p.shape), p.dtype) for p in pairs],
        in_specs=[VMEM] * (n_w + n_p),
        out_specs=[HBM] * (n_w + n_p),
        scratch_shapes=[
            pltpu.VMEM((2, 8, TILE), jnp.bfloat16),
            pltpu.SemaphoreType.DMA((count, 3)),
            pltpu.SemaphoreType.DMA((count, 3)),
            pltpu.SemaphoreType.DMA((n_w + n_p,)),
            pltpu.SemaphoreType.DMA((n_w + n_p,)),
            pltpu.SemaphoreType.DMA((n_w + n_p,)),
        ],
        compiler_params=pltpu.CompilerParams(
            collective_id=0, has_side_effects=True, vmem_limit_bytes=LIMIT
        ),
        name="gather_weights",
    )(gain_rows, *shards, *pairs)


def kept_index(kept, axis, step):
    iyh, iz, ix, iyl = chip_set(tuple(a for a in kept if a != axis), axis, step)
    index = ()
    if "y" in kept:
        index += (iyh,)
    if "z" in kept:
        index += (iz,)
    if "x" in kept:
        index += (ix,)
    if "y" in kept:
        index += (iyl,)
    return index


def add_sets(dims, target, terms):
    def one(flat_index, _):
        index, rest = [], flat_index
        for size in reversed(dims):
            index.insert(0, rest % size)
            rest = rest // size
        at = tuple(index)
        total = terms[0][at].astype(jnp.float32)
        for term in terms[1:]:
            total = total + term[at].astype(jnp.float32)
        target[at] = total.astype(jnp.bfloat16)
        return 0

    if dims:
        lax.fori_loop(0, math.prod(dims), one, 0)
    else:
        total = terms[0][...].astype(jnp.float32)
        for term in terms[1:]:
            total = total + term[...].astype(jnp.float32)
        target[...] = total.astype(jnp.bfloat16)


class Scatter:
    def __init__(self, landing, send, recv):
        self.landing, self.send, self.recv = landing, send, recv
        self.copies = {}

    def start(self, n, axis, step, source, which):
        copy = pltpu.make_async_remote_copy(
            source, self.landing[3 * n + which], self.send.at[n, which], self.recv.at[n, which],
            device_id=neighbour(axis, step),
        )
        copy.start()
        self.copies[n, which] = copy

    def drain(self):
        for copy in self.copies.values():
            copy.wait_send()


def scatter_dims(piece, phase):
    return set_dims(piece.order[: 2 - phase])


def landing_shapes(steps):
    return [
        pltpu.VMEM((*scatter_dims(piece, phase), 16, piece.width), jnp.bfloat16)
        for piece, phase in steps
        for _ in range(3)
    ]


def mid_shapes(steps):
    return [
        pltpu.VMEM((*scatter_dims(piece, phase), 16, piece.width), jnp.bfloat16)
        for piece, phase in steps
    ]


def grad_spot(grads, piece, offset):
    return grads[piece.array].at[
        (*chip_set(piece.order[:2], piece.order[2], offset), slice(None), piece.cols)
    ]


def last_kernel(*refs):
    near, far = flat_pieces(NEAR_PIECES), flat_pieces(FAR_PIECES)
    n_near, n_far, n_w = len(near), len(far), len(LAST_WIDTHS)
    steps = last_steps()
    n_steps = len(steps)
    gq_in, kparts_in, vparts_in, qpre_in, kpre_in, normed_in, tab_in, rows_in, x_in = refs[:9]
    wq_in, wk_in, wv_in, gmid_in, post_in = refs[9:14]
    planes_in, refs = refs[14 : 14 + n_far], refs[14 + n_far :]
    outs, refs = refs[:n_w], refs[n_w:]
    in_gain_out, post_gain_out, q_gain_out, k_gain_out, input_grad = refs[:5]
    refs = refs[5:]
    gq, kparts, vparts, qpre, kpre, normed, tab, rows, x_ref = refs[:9]
    wq, wk, wv, gmid, post = refs[9:14]
    planes, refs = refs[14 : 14 + n_far], refs[14 + n_far :]
    dq, dk, dv, normed_t, pair_out, pair_in, gain_got = refs[:7]
    refs = refs[7:]
    grads, refs = refs[:NEAR], refs[NEAR:]
    fin, refs = refs[: n_w + 1], refs[n_w + 1 :]
    landing, refs = refs[: 3 * n_steps], refs[3 * n_steps :]
    mids, refs = refs[:n_steps], refs[n_steps:]
    results, refs = refs[:n_steps], refs[n_steps:]
    send, recv, pair_send, pair_recv, local, load = refs
    yh, z, x, yl, c = place()
    sib = sibling()
    loads = load_all(
        [
            (gq_in, gq), (kparts_in, kparts), (vparts_in, vparts), (qpre_in, qpre), (kpre_in, kpre),
            (normed_in, normed), (tab_in, tab), (rows_in, rows), (x_in, x_ref), (wq_in, wq),
            (wk_in, wk), (wv_in, wv), (gmid_in, gmid), (post_in, post),
        ]
        + list(zip(planes_in, planes)),
        load,
    )
    greet(torus_neighbours() + [sib])
    for n in range(9):
        loads[n].wait()
    cosine, sine = rope_pair(tab)
    gain_q, gain_k = rows[2:3, :HEAD_DIM], rows[3:4, :HEAD_DIM]

    def head_back(grad, values, gain):
        grad = grad * cosine - pltpu.roll(grad, HEAD_DIM // 2, 1) * sine
        grad_in, terms = norm_back(grad, values, rms_scale(values), gain)
        return grad_in.astype(jnp.bfloat16), jnp.sum(terms, axis=0, keepdims=True)

    q_part = jnp.zeros((1, HEAD_DIM), jnp.float32)
    k_part = jnp.zeros((1, HEAD_DIM), jnp.float32)
    for h in range(8):
        at = slice(h * HEAD_DIM, (h + 1) * HEAD_DIM)
        dq[:, at], part = head_back(gq[:, at].astype(jnp.float32), qpre[:, at], gain_q)
        q_part = q_part + part
    for h in range(4):
        at = slice(h * HEAD_DIM, (h + 1) * HEAD_DIM)
        grad = kparts[0, :, at].astype(jnp.float32) + kparts[1, :, at].astype(jnp.float32)
        dk[:, at], part = head_back(grad, kpre[:, at], gain_k)
        k_part = k_part + part
    dv[...] = (vparts[0].astype(jnp.float32) + vparts[1].astype(jnp.float32)).astype(jnp.bfloat16)
    normed_t[...] = normed[...].T

    def weight_grads(n, _):
        lhs = normed_t[pl.ds(pl.multiple_of(n * 256, 256), 256), :]
        for grad, factor in ((grads[0], dq), (grads[1], dk), (grads[2], dv)):
            width = factor.shape[1]
            block = jnp.dot(lhs, factor[...], preferred_element_type=jnp.float32)
            grad[n // 2, pl.ds(n % 2 * 2, 2)] = block.astype(jnp.bfloat16).reshape(2, 4, 2, 16, width)
        return 0

    lax.fori_loop(0, 4, weight_grads, 0)
    scatter = Scatter(landing, send, recv)
    number = {(piece.name, phase): n for n, (piece, phase) in enumerate(steps)}

    def source(piece, phase, offset):
        if phase == 0:
            return grad_spot(grads, piece, offset)
        axis, kept = piece.order[2 - phase], piece.order[: 3 - phase]
        if phase == 1 and (piece.name, 0) not in number:
            held = planes[[p.name for p in far].index(piece.name)]
        else:
            held = results[number[piece.name, phase - 1]]
        return held.at[(*kept_index(kept, axis, offset), slice(None), slice(None))]

    def begin(active):
        for which in (0, 1):
            for piece, phase in active:
                axis = piece.order[2 - phase]
                offset, step = ((2, piece.way), (-piece.way, -piece.way))[which]
                scatter.start(number[piece.name, phase], axis, step, source(piece, phase, offset), which)

    def middle(active):
        for piece, phase in active:
            n = number[piece.name, phase]
            scatter.copies[n, 0].wait_recv()
            add_sets(
                scatter_dims(piece, phase), mids[n], [source(piece, phase, piece.way), landing[3 * n]]
            )
            scatter.start(n, piece.order[2 - phase], piece.way, mids[n], 2)

    def end(active):
        for piece, phase in active:
            n = number[piece.name, phase]
            scatter.copies[n, 1].wait_recv()
            scatter.copies[n, 2].wait_recv()
            base, dims = source(piece, phase, 0), scatter_dims(piece, phase)
            if phase < 2:
                add_sets(dims, results[n], [base, landing[3 * n + 1], landing[3 * n + 2]])
            else:
                total = (
                    base[...].astype(jnp.float32)
                    + landing[3 * n + 1][...].astype(jnp.float32)
                    + landing[3 * n + 2][...].astype(jnp.float32)
                )
                fin[piece.array][0, :, piece.cols] = total[:8]
                fin[piece.array][1, :, piece.cols] = total[8:]

    weights_first = [(piece, 0) for piece in near if piece.array != NEAR - 1]
    gains_first = [(piece, 0) for piece in near if piece.array == NEAR - 1]
    begin(weights_first)
    for n in range(9, 14 + n_far):
        loads[n].wait()
    begin([(piece, 1) for piece in far])

    def grad_normed(rows_at):
        return (
            nt(dq[rows_at, :], wq[...]) + nt(dk[rows_at, :], wk[...]) + nt(dv[rows_at, :], wv[...])
        )

    away = pl.ds(pl.multiple_of((1 - c) * 128, 128), 128)
    own = pl.ds(pl.multiple_of(c * 128, 128), 128)
    pair_out[...] = grad_normed(away).astype(jnp.bfloat16)
    swap = pltpu.make_async_remote_copy(
        pair_out, pair_in, pair_send.at[n_w + 1], pair_recv.at[n_w + 1], device_id=sib
    )
    swap.start()
    grad = grad_normed(own)
    values = x_ref[c].astype(jnp.float32)
    swap.wait_recv()
    grad = grad + pair_in[...].astype(jnp.float32)
    grad_in, terms = norm_back(grad, values, rms_scale(values), rows[0:1, :])
    input_grad[...] = (gmid[...] + grad_in).astype(jnp.bfloat16)
    in_part = jnp.sum(terms, axis=0, keepdims=True)
    spread = (
        lax.broadcasted_iota(jnp.int32, (HEAD_DIM, D), 1)
        == 8 * lax.broadcasted_iota(jnp.int32, (HEAD_DIM, D), 0)
    ).astype(jnp.bfloat16)
    qk = jnp.concatenate([q_part, k_part, jnp.zeros((6, HEAD_DIM), jnp.float32)]).astype(jnp.bfloat16)
    qk = jnp.dot(qk, spread, preferred_element_type=jnp.float32)
    gain_rows = jnp.concatenate(
        [in_part, post[0:1, :], qk[0:2], jnp.zeros((TILE - 4, D), jnp.float32)]
    )
    grads[NEAR - 1][...] = gain_rows.T.astype(jnp.bfloat16).reshape(2, 4, 4, 2, 16, TILE)
    begin(gains_first)
    stages = [
        [(piece, stage) for piece in near] + ([(piece, stage + 1) for piece in far] if stage < 2 else [])
        for stage in range(3)
    ]
    for stage, active in enumerate(stages):
        if stage > 0:
            begin(active)
        middle(active)
        end(active)
    copies = []
    for k in range(n_w + 1):
        if k == NEAR - 1:
            target = gain_got
        else:
            out = outs[k if k < NEAR else k - 1]
            width = out.shape[1] // 2
            target = out.at[:, pl.ds(pl.multiple_of(c * width, TILE), width)]
        swap_k = pltpu.make_async_remote_copy(
            fin[k].at[1 - c], target, pair_send.at[k], pair_recv.at[k], device_id=sib
        )
        swap_k.start()
        copies.append(swap_k)
        if k != NEAR - 1:
            keep = pltpu.make_async_copy(fin[k].at[c], target, local.at[k])
            keep.start()
            copies.append(keep)
    scatter.drain()
    swap.wait_send()
    for copy in copies:
        copy.wait()
    gain_sum = fin[NEAR - 1][c] + gain_got[...]
    gain_rows = jnp.concatenate([gain_sum, jnp.zeros((TILE - 8, TILE), jnp.float32)]).T
    in_gain_out[...] = gain_rows[0:1, :8]
    post_gain_out[...] = gain_rows[1:2, :8]
    q_gain_out[...] = gain_rows[2:3, :1]
    k_gain_out[...] = gain_rows[3:4, :1]


LAST_WIDTHS = (1024, 512, 512, 1024, 1536, 1536, 1536)


def last_steps():
    near, far = flat_pieces(NEAR_PIECES), flat_pieces(FAR_PIECES)
    return [(p, ph) for ph in range(3) for p in near] + [(p, ph) for ph in (1, 2) for p in far]


def finish(arrays, planes):
    steps = last_steps()
    n_w = len(LAST_WIDTHS)
    fin_widths = list(LAST_WIDTHS)
    fin_widths.insert(NEAR - 1, TILE)
    loaded = [*arrays, *planes]
    return pl.pallas_call(
        last_kernel,
        out_shape=[jax.ShapeDtypeStruct((8, 2 * w), jnp.float32) for w in LAST_WIDTHS]
        + [jax.ShapeDtypeStruct((1, n), jnp.float32) for n in (8, 8, 1, 1)]
        + [jax.ShapeDtypeStruct((128, D), jnp.bfloat16)],
        in_specs=[HBM] * len(loaded),
        out_specs=[HBM] * n_w + [VMEM] * 5,
        scratch_shapes=[pltpu.VMEM(a.shape, a.dtype) for a in loaded]
        + [
            pltpu.VMEM((BLOCK, 1024), jnp.bfloat16),
            pltpu.VMEM((BLOCK, 512), jnp.bfloat16),
            pltpu.VMEM((BLOCK, 512), jnp.bfloat16),
            pltpu.VMEM((D, BLOCK), jnp.bfloat16),
            pltpu.VMEM((128, D), jnp.bfloat16),
            pltpu.VMEM((128, D), jnp.bfloat16),
            pltpu.VMEM((8, TILE), jnp.float32),
        ]
        + [pltpu.VMEM((2, 4, 4, 2, 16, w), jnp.bfloat16) for w in fin_widths[:NEAR]]
        + [pltpu.VMEM((2, 8, w), jnp.float32) for w in fin_widths]
        + landing_shapes(steps)
        + mid_shapes(steps)
        + mid_shapes(steps)
        + [
            pltpu.SemaphoreType.DMA((len(steps), 3)),
            pltpu.SemaphoreType.DMA((len(steps), 3)),
            pltpu.SemaphoreType.DMA((n_w + 2,)),
            pltpu.SemaphoreType.DMA((n_w + 2,)),
            pltpu.SemaphoreType.DMA((n_w + 1,)),
            pltpu.SemaphoreType.DMA((len(loaded),)),
        ],
        compiler_params=pltpu.CompilerParams(
            collective_id=1, has_side_effects=True, vmem_limit_bytes=LIMIT
        ),
        name="finish",
    )(*loaded)


def columns(head):
    return pl.ds(pl.multiple_of(head * HEAD_DIM, HEAD_DIM), HEAD_DIM)


def exchange_start(moves, me, send, recv, local, first):
    copies = []
    for step in range(1, 8):
        there = (me + step) % 8
        for n, (source, target) in enumerate(moves):
            copy = pltpu.make_async_remote_copy(
                source(there), target(me), send.at[first + n, step], recv.at[first + n, step],
                device_id=sequence_chip(there),
            )
            copy.start()
            copies.append(copy)
    for n, (source, target) in enumerate(moves):
        copy = pltpu.make_async_copy(source(me), target(me), local.at[first + n])
        copy.start()
        copies.append(copy)
    return copies


def forward_kernel(*refs):
    x_in, tab_in, gains_in, wq_in, wk_in, wv_in = refs[:6]
    weights, refs = refs[10:14], refs[14:]
    q_out, k_out, v_out, o32_out, lse_ref, attended, normed_out, qpre_out, kpre_out, rows_ref = refs[:10]
    x_ref, tab, gains, wq, wk, wv, normed, qpre, kpre, q_low, k_low, v_low = refs[10:22]
    q_ref, k_ref, v_ref, o32_ref, o_low, scores, vt = refs[22:29]
    send, recv, head_send, head_recv, local, load, store = refs[29:]
    yh, z, x, yl, c = place()
    me = x * 2 + yl
    loads = load_all(
        [(x_in, x_ref), (gains_in, gains), (tab_in, tab), (wq_in, wq), (wk_in, wk), (wv_in, wv)], load
    )
    far = flat_pieces(FAR_PIECES)
    greet(torus_neighbours() + sequence_others())
    gather = Gather([None] * NEAR + list(weights), send, recv)
    active = [(n, piece, 2) for n, piece in enumerate(far)]
    gather.begin(active)
    for copy in loads:
        copy.wait()

    gain_rows = gains[...].astype(jnp.float32).T[:8]
    pick = (
        lax.broadcasted_iota(jnp.int32, (D, HEAD_DIM), 0)
        == 8 * lax.broadcasted_iota(jnp.int32, (D, HEAD_DIM), 1)
    ).astype(jnp.bfloat16)
    head_gains = jnp.dot(gain_rows.astype(jnp.bfloat16), pick, preferred_element_type=jnp.float32)
    rows_ref[...] = gain_rows
    rows_ref[2:4, :HEAD_DIM] = head_gains[2:4]
    gain_q, gain_k = head_gains[2:3], head_gains[3:4]
    values = x_ref[...].reshape(BLOCK, D).astype(jnp.float32)
    normed[...] = (values * rms_scale(values) * gain_rows[0:1]).astype(jnp.bfloat16)
    cosine, sine = rope_pair(tab)

    def head(pre, gain):
        unit = pre * rms_scale(pre) * gain
        return (unit * cosine + pltpu.roll(unit, HEAD_DIM // 2, 1) * sine).astype(jnp.bfloat16)

    for weight, pre_ref, low_ref, gain in ((wq, qpre, q_low, gain_q), (wk, kpre, k_low, gain_k)):
        for n in range(weight.shape[1] // 256):
            at = slice(n * 256, n * 256 + 256)
            pre = jnp.dot(normed[...], weight[:, at], preferred_element_type=jnp.float32)
            pre_ref[:, at] = pre
            low_ref[:, n * 256 : n * 256 + 128] = head(pre[:, :128], gain)
            low_ref[:, n * 256 + 128 : n * 256 + 256] = head(pre[:, 128:], gain)
    v_low[...] = jnp.dot(normed[...], wv[...], preferred_element_type=jnp.float32).astype(jnp.bfloat16)
    arriving = exchange_start(
        [
            (lambda j: q_low.at[:, columns(j)], lambda i: q_ref.at[i]),
            (lambda j: k_low.at[:, columns(j // 2)], lambda i: k_ref.at[i]),
            (lambda j: v_low.at[:, columns(j // 2)], lambda i: v_ref.at[i]),
        ],
        me, head_send, head_recv, local, 0,
    )
    stores = [
        pltpu.make_async_copy(a, b, store.at[n])
        for n, (a, b) in enumerate(
            ((normed, normed_out), (qpre, qpre_out), (kpre, kpre_out), (q_ref, q_out), (k_ref, k_out),
             (v_ref, v_out), (o32_ref, o32_out))
        )
    ]
    for copy in stores[:3]:
        copy.start()
    for copy in arriving:
        copy.wait()
    for copy in stores[3:6]:
        copy.start()
    for j in range(8):
        vt[j] = v_ref[j].T

    def one_block(i, _):
        q = q_ref[i]

        def score(j, top):
            s = nt(k_ref[j], q) * (score_scale * log2e)
            scores[j] = s
            return jnp.maximum(top, jnp.max(s, axis=0, keepdims=True))

        top = lax.fori_loop(0, i + 1, score, jnp.full((1, BLOCK), -1e30, jnp.float32))

        def weigh(j, carry):
            total, mixed = carry
            p = jnp.exp2(scores[j] - top)
            total = total + jnp.sum(p, axis=0, keepdims=True)
            mixed = mixed + jnp.dot(vt[j], p.astype(jnp.bfloat16), preferred_element_type=jnp.float32)
            return total, mixed

        total, mixed = lax.fori_loop(
            0, i + 1, weigh,
            (jnp.zeros((1, BLOCK), jnp.float32), jnp.zeros((HEAD_DIM, BLOCK), jnp.float32)),
        )
        out = (mixed / total).T
        o32_ref[i] = out
        o_low[i] = out.astype(jnp.bfloat16)
        lse_ref[i] = top + jnp.log2(total)
        return 0

    lax.fori_loop(0, 6, one_block, 0)
    gather.forward(active)
    lax.fori_loop(6, 8, one_block, 0)
    leaving = exchange_start(
        [(lambda j: o_low.at[j], lambda i: attended.at[:, columns(i)])],
        me, head_send, head_recv, local, 3,
    )
    stores[6].start()
    gather.arrive(active)
    gather.drain()
    for copy in stores:
        copy.wait()
    for copy in leaving:
        copy.wait()


def attend(near, weights):
    blocks = (8, BLOCK, HEAD_DIM)
    n_far = len(flat_pieces(FAR_PIECES))
    n_near = len(near)
    low, wide = jnp.bfloat16, jnp.float32
    return pl.pallas_call(
        forward_kernel,
        out_shape=[jax.ShapeDtypeStruct(w.shape, w.dtype) for w in weights]
        + [jax.ShapeDtypeStruct(blocks, low)] * 3
        + [
            jax.ShapeDtypeStruct(blocks, wide),
            jax.ShapeDtypeStruct((8, 1, BLOCK), wide),
            jax.ShapeDtypeStruct((BLOCK, 1024), low),
            jax.ShapeDtypeStruct((BLOCK, D), low),
            jax.ShapeDtypeStruct((BLOCK, 1024), wide),
            jax.ShapeDtypeStruct((BLOCK, 512), wide),
            jax.ShapeDtypeStruct((8, D), wide),
        ],
        in_specs=[HBM] * (n_near + 4),
        out_specs=[HBM] * 8 + [VMEM] + [HBM] * 4 + [VMEM],
        input_output_aliases={n_near + n: n for n in range(4)},
        scratch_shapes=[
            pltpu.VMEM((2, 128, D), low),
            pltpu.VMEM((2, 128, HEAD_DIM), wide),
            pltpu.VMEM((D, TILE), low),
            pltpu.VMEM((D, 1024), low),
            pltpu.VMEM((D, 512), low),
            pltpu.VMEM((D, 512), low),
            pltpu.VMEM((BLOCK, D), low),
            pltpu.VMEM((BLOCK, 1024), wide),
            pltpu.VMEM((BLOCK, 512), wide),
            pltpu.VMEM((BLOCK, 1024), low),
            pltpu.VMEM((BLOCK, 512), low),
            pltpu.VMEM((BLOCK, 512), low),
        ]
        + [pltpu.VMEM(blocks, low)] * 3
        + [
            pltpu.VMEM(blocks, wide),
            pltpu.VMEM(blocks, low),
            pltpu.VMEM((8, BLOCK, BLOCK), wide),
            pltpu.VMEM((8, HEAD_DIM, BLOCK), low),
            pltpu.SemaphoreType.DMA((n_far, 3)),
            pltpu.SemaphoreType.DMA((n_far, 3)),
            pltpu.SemaphoreType.DMA((4, 8)),
            pltpu.SemaphoreType.DMA((4, 8)),
            pltpu.SemaphoreType.DMA((4,)),
            pltpu.SemaphoreType.DMA((6,)),
            pltpu.SemaphoreType.DMA((7,)),
        ],
        compiler_params=pltpu.CompilerParams(
            collective_id=2, has_side_effects=True, vmem_limit_bytes=LIMIT
        ),
        name="attend",
    )(*near, *weights)


def backward_kernel(*refs):
    far = flat_pieces(FAR_PIECES)
    n_far = len(far)
    q_in, k_in, v_in, o32_in, lse_in, do_in = refs[:6]
    grads = [None] * NEAR + list(refs[6:10])
    dq_out, dk_out, dv_out = refs[10:13]
    planes_out, refs = refs[13 : 13 + n_far], refs[13 + n_far :]
    q_ref, k_ref, v_ref, o32_ref, lse_ref = refs[:5]
    do_ref, dq_low, dk_low, dv_low, kt, dk_acc, dv_acc = refs[5:12]
    planes, refs = refs[12 : 12 + n_far], refs[12 + n_far :]
    landing, refs = refs[: 3 * n_far], refs[3 * n_far :]
    mids, bases, refs = refs[:n_far], refs[n_far : 2 * n_far], refs[2 * n_far :]
    send, recv, load, head_send, head_recv, local, saved_load, store = refs
    yh, z, x, yl, c = place()
    me = x * 2 + yl
    saved = load_all(
        [(q_in, q_ref), (k_in, k_ref), (v_in, v_ref), (o32_in, o32_ref), (lse_in, lse_ref)], saved_load
    )
    loads = {}
    for n, piece in enumerate(far):
        for m, (offset, target) in enumerate(((piece.way, mids[n]), (0, bases[n]))):
            loads[n, m] = pltpu.make_async_copy(grad_spot(grads, piece, offset), target, load.at[n, m])
            loads[n, m].start()
    greet(torus_neighbours() + sequence_others())
    arriving = exchange_start(
        [(lambda j: do_in.at[:, columns(j)], lambda i: do_ref.at[i])],
        me, head_send, head_recv, local, 0,
    )
    scatter = Scatter(landing, send, recv)
    for which in (0, 1):
        for n, piece in enumerate(far):
            offset, step = ((2, piece.way), (-piece.way, -piece.way))[which]
            scatter.start(n, piece.order[2], step, grad_spot(grads, piece, offset), which)
    for copy in saved:
        copy.wait()
    for j in range(8):
        kt[j] = k_ref[j].T
    dk_acc[...] = jnp.zeros_like(dk_acc)
    dv_acc[...] = jnp.zeros_like(dv_acc)
    for copy in arriving:
        copy.wait()

    def one_block(i, _):
        q, do, lse = q_ref[i], do_ref[i], lse_ref[i]
        delta = jnp.sum((do.astype(jnp.float32) * o32_ref[i]).T, axis=0, keepdims=True)

        def one_pair(j, dqt):
            p = jnp.exp2(nt(k_ref[j], q) * (score_scale * log2e) - lse)
            dp = nt(v_ref[j], do)
            ds = (p * (dp - delta)).astype(jnp.bfloat16)
            dv_acc[j] += jnp.dot(p.astype(jnp.bfloat16), do, preferred_element_type=jnp.float32)
            dk_acc[j] += jnp.dot(ds, q, preferred_element_type=jnp.float32)
            return dqt + jnp.dot(kt[j], ds, preferred_element_type=jnp.float32)

        dqt = lax.fori_loop(0, i + 1, one_pair, jnp.zeros((HEAD_DIM, BLOCK), jnp.float32))
        dq_low[i] = (dqt * score_scale).T.astype(jnp.bfloat16)
        return 0

    lax.fori_loop(0, 6, one_block, 0)
    for n, piece in enumerate(far):
        scatter.copies[n, 0].wait_recv()
        loads[n, 0].wait()
        add_sets(scatter_dims(piece, 0), mids[n], [mids[n], landing[3 * n]])
        scatter.start(n, piece.order[2], piece.way, mids[n], 2)
    lax.fori_loop(6, 8, one_block, 0)
    dk_low[...] = (dk_acc[...] * score_scale).astype(jnp.bfloat16)
    dv_low[...] = dv_acc[...].astype(jnp.bfloat16)
    leaving = exchange_start(
        [
            (lambda j: dq_low.at[j], lambda i: dq_out.at[:, columns(i)]),
            (lambda j: dk_low.at[j], lambda i: dk_out.at[i % 2, :, columns(i // 2)]),
            (lambda j: dv_low.at[j], lambda i: dv_out.at[i % 2, :, columns(i // 2)]),
        ],
        me, head_send, head_recv, local, 1,
    )
    for n, piece in enumerate(far):
        scatter.copies[n, 1].wait_recv()
        scatter.copies[n, 2].wait_recv()
        loads[n, 1].wait()
        add_sets(scatter_dims(piece, 0), planes[n], [bases[n], landing[3 * n + 1], landing[3 * n + 2]])
        keep = pltpu.make_async_copy(planes[n], planes_out[n], store.at[n])
        keep.start()
        leaving.append(keep)
    scatter.drain()
    for copy in leaving:
        copy.wait()


def attend_back(saved, grad_att, grads):
    far = flat_pieces(FAR_PIECES)
    n_far = len(far)
    steps = [(p, 0) for p in far]
    blocks = (8, BLOCK, HEAD_DIM)
    return pl.pallas_call(
        backward_kernel,
        out_shape=[
            jax.ShapeDtypeStruct((BLOCK, 1024), jnp.bfloat16),
            jax.ShapeDtypeStruct((2, BLOCK, 512), jnp.bfloat16),
            jax.ShapeDtypeStruct((2, BLOCK, 512), jnp.bfloat16),
        ]
        + [
            jax.ShapeDtypeStruct((*scatter_dims(p, 0), 16, p.width), jnp.bfloat16) for p in far
        ],
        in_specs=[HBM] * 10,
        out_specs=[HBM] * (3 + n_far),
        scratch_shapes=[pltpu.VMEM(a.shape, a.dtype) for a in saved]
        + [pltpu.VMEM(blocks, jnp.bfloat16)] * 4
        + [
            pltpu.VMEM((8, HEAD_DIM, BLOCK), jnp.bfloat16),
            pltpu.VMEM(blocks, jnp.float32),
            pltpu.VMEM(blocks, jnp.float32),
        ]
        + mid_shapes(steps)
        + landing_shapes(steps)
        + mid_shapes(steps)
        + mid_shapes(steps)
        + [
            pltpu.SemaphoreType.DMA((n_far, 3)),
            pltpu.SemaphoreType.DMA((n_far, 3)),
            pltpu.SemaphoreType.DMA((n_far, 2)),
            pltpu.SemaphoreType.DMA((4, 8)),
            pltpu.SemaphoreType.DMA((4, 8)),
            pltpu.SemaphoreType.DMA((4,)),
            pltpu.SemaphoreType.DMA((5,)),
            pltpu.SemaphoreType.DMA((n_far,)),
        ],
        compiler_params=pltpu.CompilerParams(
            collective_id=3, has_side_effects=True, vmem_limit_bytes=LIMIT
        ),
        name="attend_back",
    )(*saved, grad_att, *grads)


def middle_kernel(*refs):
    att_in, x_in, g_in, rows_in, wo_in, wg_in, wu_in, wd_in = refs[:8]
    output, grad_att_out, gmid_out, post_out = refs[8:12]
    dwo_out, dwg_out, dwu_out, dwd_out = refs[12:16]
    att, x_ref, g_ref, rows, wo, wg, wu, wd = refs[16:24]
    (branch, middle, hidden, hidden_t, g_t, grad_act, act, gate_grad, up_grad, grad_hidden, branch_t,
     down_own, grad_att, dwo, dwg, dwu, dwd) = refs[24:41]
    out1, in1, out2, in2, out3, in3 = refs[41:47]
    pair_send, pair_recv, load, store = refs[47:]
    yh, z, x, yl, c = place()
    sib = sibling()
    loads = load_all(
        [(att_in, att), (wo_in, wo), (g_in, g_ref), (wd_in, wd), (x_in, x_ref), (rows_in, rows),
         (wg_in, wg), (wu_in, wu)], load
    )
    greet([sib])
    swaps = []

    def swap(source, target):
        n = len(swaps)
        copy = pltpu.make_async_remote_copy(
            source, target, pair_send.at[n], pair_recv.at[n], device_id=sib
        )
        copy.start()
        swaps.append(copy)
        return copy

    def part(n, width=256):
        return pl.ds(n * width, width)

    loads[0].wait()
    loads[1].wait()
    first = []
    for n in range(4):
        block = nt(att[...], wo[part(n), :])
        branch[:, part(n)] = block
        out1[n] = block.astype(jnp.bfloat16)
        first.append(swap(out1.at[n], in1.at[n]))
    loads[2].wait()
    loads[3].wait()
    g_low = g_ref[...].reshape(BLOCK, D)
    for n in range(6):
        grad_act[:, part(n)] = jnp.dot(g_low, wd[:, part(n)], preferred_element_type=jnp.float32)
    g_t[...] = g_low.T
    loads[4].wait()
    loads[5].wait()
    for n in range(4):
        first[n].wait_recv()
        middle[:, part(n)] = (
            x_ref[...].reshape(BLOCK, D)[:, n * 256 : n * 256 + 256].astype(jnp.float32)
            + (branch[:, part(n)] + in1[n].astype(jnp.float32))
        )
    gain = rows[1:2, :]
    scale = rms_scale(middle[...])
    hidden[...] = (middle[...] * scale * gain).astype(jnp.bfloat16)
    loads[6].wait()
    loads[7].wait()
    for n in range(6):
        gate = jnp.dot(hidden[...], wg[:, part(n)], preferred_element_type=jnp.float32)
        up = jnp.dot(hidden[...], wu[:, part(n)], preferred_element_type=jnp.float32)
        sigma = jax.nn.sigmoid(gate)
        swish = gate * sigma
        grad = grad_act[:, part(n)]
        act[:, part(n)] = (swish * up).astype(jnp.bfloat16)
        gate_grad[:, part(n)] = (grad * up * (sigma * (1.0 + gate * (1.0 - sigma)))).astype(jnp.bfloat16)
        up_grad[:, part(n)] = (grad * swish).astype(jnp.bfloat16)
    second = []
    for n in range(4):
        block = nt(gate_grad[...], wg[part(n), :]) + nt(up_grad[...], wu[part(n), :])
        grad_hidden[:, part(n)] = block
        out2[n] = block.astype(jnp.bfloat16)
        second.append(swap(out2.at[n], in2.at[n]))
    away = pl.ds(pl.multiple_of((1 - c) * 128, 128), 128)
    own = pl.ds(pl.multiple_of(c * 128, 128), 128)
    out3[...] = nt(act[away, :], wd[...]).astype(jnp.bfloat16)
    third = swap(out3, in3)
    down_own[...] = nt(act[own, :], wd[...])
    hidden_t[...] = hidden[...].T
    stores = []

    def keep(source, target):
        copy = pltpu.make_async_copy(source, target, store.at[len(stores)])
        copy.start()
        stores.append(copy)

    for lhs, rhs, grads, target in (
        (hidden_t, gate_grad, dwg, dwg_out), (hidden_t, up_grad, dwu, dwu_out), (g_t, act, dwd, dwd_out)
    ):
        for n in range(4):
            grads[part(n), :] = jnp.dot(
                lhs[part(n), :], rhs[...], preferred_element_type=jnp.float32
            ).astype(jnp.bfloat16)
        keep(grads, target)
    for n in range(4):
        second[n].wait_recv()
        grad_hidden[:, part(n)] = grad_hidden[:, part(n)] + in2[n].astype(jnp.float32)
    grad_in, terms = norm_back(grad_hidden[...], middle[...], scale, gain)
    grad_hidden[...] = terms
    post_out[...] = jnp.broadcast_to(jnp.sum(grad_hidden[own, :], axis=0, keepdims=True), (8, D))
    grad_hidden[...] = g_low.astype(jnp.float32) + grad_in
    gmid_out[...] = grad_hidden[own, :]
    branch_grad = grad_hidden[...].astype(jnp.bfloat16)
    branch_t[...] = branch_grad.T
    for n in range(4):
        grad_att[:, part(n)] = jnp.dot(
            branch_grad, wo[:, part(n)], preferred_element_type=jnp.float32
        ).astype(jnp.bfloat16)
    keep(grad_att, grad_att_out)
    for n in range(4):
        dwo[part(n), :] = jnp.dot(
            branch_t[part(n), :], att[...], preferred_element_type=jnp.float32
        ).astype(jnp.bfloat16)
    keep(dwo, dwo_out)
    third.wait_recv()
    output[...] = (
        middle[own, :] + (down_own[...] + in3[...].astype(jnp.float32))
    ).astype(jnp.bfloat16)
    for copy in swaps:
        copy.wait_send()
    for copy in stores:
        copy.wait()


def feed_forward(arrays):
    low, wide = jnp.bfloat16, jnp.float32
    shapes = [(D, 1024), (D, 1536), (D, 1536), (D, 1536)]
    return pl.pallas_call(
        middle_kernel,
        out_shape=[
            jax.ShapeDtypeStruct((128, D), low),
            jax.ShapeDtypeStruct((BLOCK, 1024), low),
            jax.ShapeDtypeStruct((128, D), wide),
            jax.ShapeDtypeStruct((8, D), wide),
        ]
        + [jax.ShapeDtypeStruct(s, low) for s in shapes],
        in_specs=[HBM] * 8,
        out_specs=[VMEM, HBM, VMEM, VMEM] + [HBM] * 4,
        scratch_shapes=[pltpu.VMEM(a.shape, a.dtype) for a in arrays]
        + [
            pltpu.VMEM((BLOCK, D), wide),
            pltpu.VMEM((BLOCK, D), wide),
            pltpu.VMEM((BLOCK, D), low),
            pltpu.VMEM((D, BLOCK), low),
            pltpu.VMEM((D, BLOCK), low),
            pltpu.VMEM((BLOCK, 1536), wide),
            pltpu.VMEM((BLOCK, 1536), low),
            pltpu.VMEM((BLOCK, 1536), low),
            pltpu.VMEM((BLOCK, 1536), low),
            pltpu.VMEM((BLOCK, D), wide),
            pltpu.VMEM((D, BLOCK), low),
            pltpu.VMEM((128, D), wide),
            pltpu.VMEM((BLOCK, 1024), low),
        ]
        + [pltpu.VMEM(s, low) for s in shapes]
        + [pltpu.VMEM((4, BLOCK, 256), low)] * 4
        + [pltpu.VMEM((128, D), low)] * 2
        + [
            pltpu.SemaphoreType.DMA((9,)),
            pltpu.SemaphoreType.DMA((9,)),
            pltpu.SemaphoreType.DMA((8,)),
            pltpu.SemaphoreType.DMA((5,)),
        ],
        compiler_params=pltpu.CompilerParams(
            collective_id=4, has_side_effects=True, vmem_limit_bytes=LIMIT
        ),
        name="feed_forward",
    )(*arrays)


def results_kernel(n, *refs):
    for source, target in zip(refs[:n], refs[n:]):
        target[...] = source[...]


def results(arrays):
    n = len(arrays)
    return pl.pallas_call(
        functools.partial(results_kernel, n),
        out_shape=[jax.ShapeDtypeStruct(a.shape, a.dtype) for a in arrays],
        in_specs=[VMEM] * n,
        out_specs=[VMEM] * n,
        name="results",
    )(*arrays)


def split_columns(shard):
    rows, width = shard.shape
    return jnp.transpose(shard.reshape(rows, CORES, width // CORES), (1, 0, 2))


def body(
    tokens,
    positions,
    in_gain,
    q_gain,
    k_gain,
    w_query,
    w_key,
    w_value,
    w_out,
    post_gain,
    w_gate,
    w_up,
    w_down,
    cotangent,
):
    half = HEAD_DIM // 2
    frequency = rope_base ** (-2.0 * jnp.arange(half, dtype=jnp.float32) / HEAD_DIM)
    angles = positions[0].astype(jnp.float32)[:, None] * frequency[None, :]
    table = jnp.concatenate([jnp.cos(angles), jnp.sin(angles)], axis=-1)
    gain_rows = jnp.stack(
        [jnp.pad(g, (0, TILE - g.shape[0])) for g in (in_gain, post_gain, q_gain, k_gain)]
    )
    gain_rows = jnp.pad(gain_rows, ((0, 4), (0, 0)))
    shards = [
        split_columns(w) for w in (w_query, w_key, w_value, w_out.T, w_gate, w_up, w_down.T)
    ]
    gathered = gather_weights(gain_rows, shards, [tokens[0], cotangent[0], table])

    def whole(weight):
        return weight.reshape(D, weight.shape[-1])

    wq, wk, wv, gains = [whole(w) for w in gathered[:4]]
    x_pair, g_pair, tables = gathered[8:]
    *far, q_all, k_all, v_all, mixed, log_total, attended, normed, q_pre, k_pre, rows = attend(
        [x_pair, tables, gains, wq, wk, wv], gathered[4:8]
    )
    wo, wg, wu, wd = [whole(w) for w in far]
    output, grad_att, grad_middle, post_part, *far_grads = feed_forward(
        [attended, x_pair, g_pair, rows, wo, wg, wu, wd]
    )
    grad_query, key_parts, value_parts, *planes = attend_back(
        (q_all, k_all, v_all, mixed, log_total),
        grad_att,
        [g.reshape(2, 4, 4, 2, 16, g.shape[-1]) for g in far_grads],
    )
    last = finish(
        [grad_query, key_parts, value_parts, q_pre, k_pre, normed, tables, rows, x_pair, wq, wk, wv,
         grad_middle, post_part],
        planes,
    )
    *sums, in_gain_grad, post_gain_grad, q_gain_grad, k_gain_grad, input_grad, output = results(
        [*last, output]
    )
    return (
        output[None],
        input_grad[None],
        in_gain_grad[0],
        q_gain_grad[0],
        k_gain_grad[0],
        sums[0],
        sums[1],
        sums[2],
        sums[3].T,
        post_gain_grad[0],
        sums[4],
        sums[5],
        sums[6].T,
    )


def solution(mesh):
    placed = (
        P("dp", "seq", None),
        P("dp", "seq"),
        P(("dp", "seq")),
        P(("dp", "seq")),
        P(("dp", "seq")),
        P(("dp", "seq"), None),
        P(("dp", "seq"), None),
        P(("dp", "seq"), None),
        P(None, ("dp", "seq")),
        P(("dp", "seq")),
        P(("dp", "seq"), None),
        P(("dp", "seq"), None),
        P(None, ("dp", "seq")),
        P("dp", "seq", None),
    )
    return jax.shard_map(
        body,
        mesh=mesh,
        in_specs=placed,
        out_specs=(
            P("dp", "seq", None),
            P("dp", "seq", None),
            P(("dp", "seq")),
            P(("dp", "seq")),
            P(("dp", "seq")),
            P(("dp", "seq"), None),
            P(("dp", "seq"), None),
            P(("dp", "seq"), None),
            P(None, ("dp", "seq")),
            P(("dp", "seq")),
            P(("dp", "seq"), None),
            P(("dp", "seq"), None),
            P(None, ("dp", "seq")),
        ),
        check_vma=False,
    )
```

```python
import functools
import math

import jax
import jax.numpy as jnp
from jax import lax
from jax.experimental import pallas as pl
from jax.experimental.pallas import tpu as pltpu
from jax.sharding import PartitionSpec as P

HEADS = 16
KV_HEADS = 8
HEAD_DIM = 128
D = 1024
FF = 3072
BLOCK = 256
CORES = 2

TILE = 128

eps_norm = 1e-06
rope_base = 1000000.0
score_scale = 1.0 / math.sqrt(HEAD_DIM)
log2e = math.log2(math.e)


def place():
    dp = lax.axis_index("dp")
    seq = lax.axis_index("seq")
    return dp // 4, dp % 4, seq // 4, (seq // 2) % 2, seq % 2


def device(yh, z, x, yl, c):
    return {"dp": yh * 4 + z, "seq": x * 4 + yl * 2 + c}


def sibling():
    yh, z, x, yl, c = place()
    return device(yh, z, x, yl, 1 - c)


def neighbour(axis, step):
    yh, z, x, yl, c = place()
    if axis == "x":
        return device(yh, z, (x + step + 4) % 4, yl, c)
    if axis == "z":
        return device(yh, (z + step + 4) % 4, x, yl, c)
    y = (yh * 2 + yl + step + 4) % 4
    return device(y // 2, z, x, y % 2, c)


ORDERS = (("x", "y", "z"), ("y", "z", "x"), ("z", "x", "y"))


def chip_set(whole_axes, axis, step):
    yh, z, x, yl, _ = place()
    iz, ix, iyh, iyl = z, x, yh, yl
    if axis == "x":
        ix = (x + step + 4) % 4
    elif axis == "z":
        iz = (z + step + 4) % 4
    else:
        y = (yh * 2 + yl + step + 4) % 4
        iyh, iyl = y // 2, y % 2
    every = slice(None)
    if "x" in whole_axes:
        ix = every
    if "z" in whole_axes:
        iz = every
    if "y" in whole_axes:
        iyh, iyl = every, every
    return (iyh, iz, ix, iyl)


def set_dims(whole_axes):
    dims = ()
    if "y" in whole_axes:
        dims += (2,)
    if "z" in whole_axes:
        dims += (4,)
    if "x" in whole_axes:
        dims += (4,)
    if "y" in whole_axes:
        dims += (2,)
    return dims


NEAR_PIECES = (
    (((0, 0, 3),), ((0, 3, 3),)),
    (((1, 0, 3),), ((2, 0, 3),)),
    (((0, 6, 2), (1, 3, 1)), ((2, 3, 1), (3, 0, 1))),
)
FAR_PIECES = (
    (((5, 0, 10),), ((6, 0, 10),)),
    (((4, 0, 6),), ((7, 0, 6),)),
    (((7, 6, 6),), ((4, 6, 2), (5, 10, 2), (6, 10, 2))),
)
NEAR = 4
LIMIT = 60 << 20


class Piece:
    def __init__(self, colour, half, array, first, tiles):
        self.name = (array, first)
        self.order = ORDERS[colour]
        self.way = 1 if half == 0 else -1
        self.array = array
        self.width = tiles * TILE
        self.cols = pl.ds(first * TILE, self.width)


def flat_pieces(pieces):
    return [
        Piece(colour, half, *piece)
        for colour in range(3)
        for half in range(2)
        for piece in pieces[colour][half]
    ]


def greet(others):
    barrier = pltpu.get_barrier_semaphore()
    for other in others:
        pl.semaphore_signal(barrier, inc=1, device_id=other)
    pl.semaphore_wait(barrier, len(others))


def torus_neighbours():
    return [neighbour(axis, step) for axis in ("x", "y", "z") for step in (1, -1)]


def sequence_chip(number):
    yh, z, x, yl, c = place()
    return device(yh, z, number // 2, number % 2, c)


def sequence_others():
    yh, z, x, yl, c = place()
    me = x * 2 + yl
    return [sequence_chip((me + step) % 8) for step in range(1, 8)]


HBM = pl.BlockSpec(memory_space=pltpu.HBM)
VMEM = pl.BlockSpec(memory_space=pltpu.VMEM)


def load_all(pairs, sems):
    copies = [pltpu.make_async_copy(a, b, sems.at[n]) for n, (a, b) in enumerate(pairs)]
    for copy in copies:
        copy.start()
    return copies


def nt(left, right):
    return lax.dot_general(left, right, (((1,), (1,)), ((), ())), preferred_element_type=jnp.float32)


def rms_scale(values):
    return lax.rsqrt(jnp.mean(values * values, axis=-1, keepdims=True) + eps_norm)


def norm_back(grad_out, values, scale_factor, gain):
    weighted = grad_out * gain
    inner = jnp.mean(weighted * values, axis=-1, keepdims=True)
    grad_in = (
        scale_factor * weighted - values * (scale_factor * scale_factor * scale_factor) * inner
    )
    return (grad_in, grad_out * values * scale_factor)


def rope_pair(tab):
    table = tab[...].reshape(BLOCK, HEAD_DIM)
    turned = pltpu.roll(table, HEAD_DIM // 2, 1)
    low = lax.broadcasted_iota(jnp.int32, (BLOCK, HEAD_DIM), 1) < HEAD_DIM // 2
    return jnp.where(low, table, turned), jnp.where(low, -turned, table)


class Gather:
    def __init__(self, outs, send, recv):
        self.outs, self.send, self.recv = outs, send, recv
        self.copies = {}

    def start(self, n, piece, phase, which):
        axis, whole = piece.order[phase], piece.order[:phase]
        step, offset = ((piece.way, 0), (-piece.way, 0), (piece.way, -piece.way))[which]
        ref = self.outs[piece.array].at[
            (*chip_set(whole, axis, offset), slice(None), slice(None), piece.cols)
        ]
        copy = pltpu.make_async_remote_copy(
            ref, ref, self.send.at[n, which], self.recv.at[n, which],
            device_id=neighbour(axis, step),
        )
        copy.start()
        self.copies[n, which] = copy

    def begin(self, active):
        for which in (0, 1):
            for n, piece, phase in active:
                self.start(n, piece, phase, which)

    def forward(self, active):
        for n, piece, phase in active:
            self.copies[n, 0].wait_recv()
            self.start(n, piece, phase, 2)

    def arrive(self, active):
        for n, _, _ in active:
            self.copies[n, 1].wait_recv()
            self.copies[n, 2].wait_recv()

    def advance(self, active, following):
        for (n, _, _), (m, piece, phase) in zip(active, following):
            self.copies[n, 1].wait_recv()
            self.copies[n, 2].wait_recv()
            self.start(m, piece, phase, 0)
            self.start(m, piece, phase, 1)

    def drain(self):
        for copy in self.copies.values():
            copy.wait_send()


def kept_index(kept, axis, step):
    iyh, iz, ix, iyl = chip_set(tuple(a for a in kept if a != axis), axis, step)
    index = ()
    if "y" in kept:
        index += (iyh,)
    if "z" in kept:
        index += (iz,)
    if "x" in kept:
        index += (ix,)
    if "y" in kept:
        index += (iyl,)
    return index


def add_sets(dims, target, terms):
    def one(flat_index, _):
        index, rest = [], flat_index
        for size in reversed(dims):
            index.insert(0, rest % size)
            rest = rest // size
        at = tuple(index)
        total = terms[0][at].astype(jnp.float32)
        for term in terms[1:]:
            total = total + term[at].astype(jnp.float32)
        target[at] = total.astype(jnp.bfloat16)
        return 0

    if dims:
        lax.fori_loop(0, math.prod(dims), one, 0)
    else:
        total = terms[0][...].astype(jnp.float32)
        for term in terms[1:]:
            total = total + term[...].astype(jnp.float32)
        target[...] = total.astype(jnp.bfloat16)


class Scatter:
    def __init__(self, steps, grads, landing, mids, results, fin, send, recv):
        self.grads, self.landing, self.mids, self.results = grads, landing, mids, results
        self.fin, self.send, self.recv = fin, send, recv
        self.number = {(piece.name, phase): n for n, (piece, phase) in enumerate(steps)}
        self.copies = {}
        self.loads = {}

    def source(self, piece, phase, offset):
        if phase == 0:
            return grad_spot(self.grads, piece, offset)
        axis, kept = piece.order[2 - phase], piece.order[: 3 - phase]
        held = self.results[self.number[piece.name, phase - 1]]
        return held.at[(*kept_index(kept, axis, offset), slice(None), slice(None))]

    def load(self, piece, sems):
        n = self.number[piece.name, 0]
        for m, (offset, target) in enumerate(((piece.way, self.mids[n]), (0, self.results[n]))):
            self.loads[n, m] = pltpu.make_async_copy(
                grad_spot(self.grads, piece, offset), target, sems.at[m]
            )
            self.loads[n, m].start()

    def start(self, piece, phase, which):
        n = self.number[piece.name, phase]
        way = piece.way
        offset, step = ((2, way), (-way, -way), (way, way))[which]
        source = self.mids[n] if which == 2 else self.source(piece, phase, offset)
        copy = pltpu.make_async_remote_copy(
            source, self.landing[3 * n + which], self.send.at[n, which], self.recv.at[n, which],
            device_id=neighbour(piece.order[2 - phase], step),
        )
        copy.start()
        self.copies[n, which] = copy

    def begin(self, pieces, phase):
        for which in (0, 1):
            for piece in pieces:
                self.start(piece, phase, which)

    def middle(self, pieces, phase):
        for piece in pieces:
            n = self.number[piece.name, phase]
            self.copies[n, 0].wait_recv()
            own = self.source(piece, phase, piece.way)
            if (n, 0) in self.loads:
                self.loads[n, 0].wait()
                own = self.mids[n]
            add_sets(scatter_dims(piece, phase), self.mids[n], [own, self.landing[3 * n]])
            self.start(piece, phase, 2)

    def end(self, pieces, phase):
        for piece in pieces:
            n = self.number[piece.name, phase]
            self.copies[n, 1].wait_recv()
            self.copies[n, 2].wait_recv()
            base = self.source(piece, phase, 0)
            if (n, 1) in self.loads:
                self.loads[n, 1].wait()
                base = self.results[n]
            terms = [base, self.landing[3 * n + 1], self.landing[3 * n + 2]]
            if phase < 2:
                add_sets(scatter_dims(piece, phase), self.results[n], terms)
                self.start(piece, phase + 1, 0)
                self.start(piece, phase + 1, 1)
            else:
                total = terms[0][...].astype(jnp.float32)
                for term in terms[1:]:
                    total = total + term[...].astype(jnp.float32)
                self.fin[piece.array][0, :, piece.cols] = total[:8]
                self.fin[piece.array][1, :, piece.cols] = total[8:]

    def drain(self):
        for copy in self.copies.values():
            copy.wait_send()


def scatter_dims(piece, phase):
    return set_dims(piece.order[: 2 - phase])


def landing_shapes(steps):
    return [
        pltpu.VMEM((*scatter_dims(piece, phase), 16, piece.width), jnp.bfloat16)
        for piece, phase in steps
        for _ in range(3)
    ]


def mid_shapes(steps):
    return [
        pltpu.VMEM((*scatter_dims(piece, phase), 16, piece.width), jnp.bfloat16)
        for piece, phase in steps
    ]


def grad_spot(grads, piece, offset):
    return grads[piece.array].at[
        (*chip_set(piece.order[:2], piece.order[2], offset), slice(None), piece.cols)
    ]


def columns(head):
    return pl.ds(pl.multiple_of(head * HEAD_DIM, HEAD_DIM), HEAD_DIM)


def exchange_start(moves, me, send, recv, local, first):
    copies = []
    for step in range(1, 8):
        there = (me + step) % 8
        for n, (source, target) in enumerate(moves):
            copy = pltpu.make_async_remote_copy(
                source(there), target(me), send.at[first + n, step], recv.at[first + n, step],
                device_id=sequence_chip(there),
            )
            copy.start()
            copies.append(copy)
    for n, (source, target) in enumerate(moves):
        copy = pltpu.make_async_copy(source(me), target(me), local.at[first + n])
        copy.start()
        copies.append(copy)
    return copies


def forward_kernel(*refs):
    gain_in, shards, (x_in, g_in, tab_in), refs = refs[0], list(refs[1:8]), refs[8:11], refs[11:]
    weights, (x_out, g_out, tab_out), refs = refs[:8], refs[8:11], refs[11:]
    q_out, k_out, v_out, o32_out, lse_ref, attended, normed_out, qpre_out, kpre_out, rows_ref = refs[:10]
    x_ref, tab, gains, wq, wk, wv, normed, qpre, kpre, q_low, k_low, v_low = refs[10:22]
    q_ref, k_ref, v_ref, o32_ref, o_low, scores, vt, gain_tile = refs[22:30]
    send, recv, head_send, head_recv, local, load, store, pair_send, pair_recv, pair_local = refs[30:]
    yh, z, x, yl, c = place()
    me = x * 2 + yl
    sib = sibling()
    tile_rows = jnp.concatenate([gain_in[...].astype(jnp.float32), jnp.zeros((TILE - 8, TILE), jnp.float32)])
    tile = tile_rows.T[:8].astype(jnp.bfloat16)
    gain_tile[0] = tile
    gain_tile[1] = tile
    shards.insert(NEAR - 1, gain_tile)
    greet(torus_neighbours() + sequence_others() + [sib])
    units = []
    for k in range(8):
        mine = weights[k].at[yh, z, x, yl, c]
        own = pltpu.make_async_copy(shards[k].at[c], mine, pair_local.at[k])
        away = pltpu.make_async_remote_copy(
            shards[k].at[1 - c], mine, pair_send.at[k], pair_recv.at[k], device_id=sib
        )
        units.append((own, away))
    for k, (source, target) in enumerate(((x_in, x_ref), (tab_in, tab), (g_in, g_out))):
        own = pltpu.make_async_copy(source, target.at[c], pair_local.at[8 + k])
        away = pltpu.make_async_remote_copy(
            source, target.at[c], pair_send.at[8 + k], pair_recv.at[8 + k], device_id=sib
        )
        units.append((own, away))
    for own, away in units:
        own.start()
        away.start()

    def met(some):
        for own, away in some:
            own.wait()
            away.wait_recv()

    near, far = flat_pieces(NEAR_PIECES), flat_pieces(FAR_PIECES)
    gather = Gather(weights, send, recv)

    def steps(pieces, first, phase):
        return [(first + phase * len(pieces) + n, piece, phase) for n, piece in enumerate(pieces)]

    near0, near1, near2 = (steps(near, 0, phase) for phase in range(3))
    far0, far1, far2 = (steps(far, 3 * len(near), phase) for phase in range(3))
    met(units[:NEAR])
    gather.begin(near0)
    met(units[NEAR:8])
    gather.begin(far0)
    gather.forward(near0)
    gather.advance(near0, near1)
    gather.forward(far0)
    gather.forward(near1)
    gather.advance(near1, near2)
    gather.advance(far0, far1)
    gather.forward(near2)
    gather.forward(far1)
    gather.arrive(near2)
    pieces_in = [(weights[3], gains), (weights[0], wq), (weights[1], wk), (weights[2], wv)]
    loads = load_all(pieces_in, load)
    gather.advance(far1[:2], far2[:2])
    gather.advance(far1[2:3], far2[2:3])
    gather.advance(far1[4:5], far2[4:5])
    met(units[8:])
    for copy in loads:
        copy.wait()

    gain_rows = gains[...].reshape(D, TILE).astype(jnp.float32).T[:8]
    pick = (
        lax.broadcasted_iota(jnp.int32, (D, HEAD_DIM), 0)
        == 8 * lax.broadcasted_iota(jnp.int32, (D, HEAD_DIM), 1)
    ).astype(jnp.bfloat16)
    head_gains = jnp.dot(gain_rows.astype(jnp.bfloat16), pick, preferred_element_type=jnp.float32)
    rows_ref[...] = gain_rows
    rows_ref[2:4, :HEAD_DIM] = head_gains[2:4]
    gain_q, gain_k = head_gains[2:3], head_gains[3:4]
    values = x_ref[...].reshape(BLOCK, D).astype(jnp.float32)
    normed[...] = (values * rms_scale(values) * gain_rows[0:1]).astype(jnp.bfloat16)
    cosine, sine = rope_pair(tab)

    def matrix(ref, at):
        value = ref[:, :, :, :, :, :, at]
        return value.reshape(D, value.shape[-1])

    def head(pre, gain):
        unit = pre * rms_scale(pre) * gain
        return (unit * cosine + pltpu.roll(unit, HEAD_DIM // 2, 1) * sine).astype(jnp.bfloat16)

    for weight, pre_ref, low_ref, gain in ((wq, qpre, q_low, gain_q), (wk, kpre, k_low, gain_k)):
        for n in range(weight.shape[-1] // 256):
            at = slice(n * 256, n * 256 + 256)
            pre = jnp.dot(normed[...], matrix(weight, at), preferred_element_type=jnp.float32)
            pre_ref[:, at] = pre
            low_ref[:, n * 256 : n * 256 + 128] = head(pre[:, :128], gain)
            low_ref[:, n * 256 + 128 : n * 256 + 256] = head(pre[:, 128:], gain)
    v_low[...] = jnp.dot(normed[...], matrix(wv, slice(None)), preferred_element_type=jnp.float32).astype(jnp.bfloat16)
    arriving = exchange_start(
        [
            (lambda j: q_low.at[:, columns(j)], lambda i: q_ref.at[i]),
            (lambda j: k_low.at[:, columns(j // 2)], lambda i: k_ref.at[i]),
            (lambda j: v_low.at[:, columns(j // 2)], lambda i: v_ref.at[i]),
        ],
        me, head_send, head_recv, local, 0,
    )
    stores = [
        pltpu.make_async_copy(a, b, store.at[n])
        for n, (a, b) in enumerate(
            ((normed, normed_out), (qpre, qpre_out), (kpre, kpre_out), (q_ref, q_out), (k_ref, k_out),
             (v_ref, v_out), (o32_ref, o32_out), (x_ref, x_out), (tab, tab_out))
        )
    ]
    for copy in stores[:3] + stores[7:]:
        copy.start()
    for copy in arriving:
        copy.wait()
    gather.advance(far1[3:4], far2[3:4])
    gather.advance(far1[5:6], far2[5:6])
    gather.advance(far1[6:7], far2[6:7])
    gather.advance(far1[7:8], far2[7:8])
    gather.forward(far2[:2])
    for copy in stores[3:6]:
        copy.start()
    for j in range(8):
        vt[j] = v_ref[j].T

    def one_block(i, _):
        q = q_ref[i]

        def score(j, top):
            s = nt(k_ref[j], q) * (score_scale * log2e)
            scores[j] = s
            return jnp.maximum(top, jnp.max(s, axis=0, keepdims=True))

        top = lax.fori_loop(0, i + 1, score, jnp.full((1, BLOCK), -1e30, jnp.float32))

        def weigh(j, carry):
            total, mixed = carry
            p = jnp.exp2(scores[j] - top)
            total = total + jnp.sum(p, axis=0, keepdims=True)
            mixed = mixed + jnp.dot(vt[j], p.astype(jnp.bfloat16), preferred_element_type=jnp.float32)
            return total, mixed

        total, mixed = lax.fori_loop(
            0, i + 1, weigh,
            (jnp.zeros((1, BLOCK), jnp.float32), jnp.zeros((HEAD_DIM, BLOCK), jnp.float32)),
        )
        out = (mixed / total).T
        o32_ref[i] = out
        o_low[i] = out.astype(jnp.bfloat16)
        lse_ref[i] = top + jnp.log2(total)
        return 0

    lax.fori_loop(0, 6, one_block, 0)
    gather.forward(far2[2:])
    lax.fori_loop(6, 8, one_block, 0)
    leaving = exchange_start(
        [(lambda j: o_low.at[j], lambda i: attended.at[:, columns(i)])],
        me, head_send, head_recv, local, 3,
    )
    stores[6].start()
    gather.arrive(far2)
    gather.drain()
    for copy in stores:
        copy.wait()
    for copy in leaving:
        copy.wait()
    for _, away in units:
        away.wait_send()


def attend(gain_rows, shards, pairs):
    blocks = (8, BLOCK, HEAD_DIM)
    count = 3 * (len(flat_pieces(NEAR_PIECES)) + len(flat_pieces(FAR_PIECES)))
    low, wide = jnp.bfloat16, jnp.float32
    widths = [w.shape[-1] for w in shards]
    widths.insert(NEAR - 1, TILE)
    whole = [(2, 4, 4, 2, 2, 8, w) for w in widths]
    return pl.pallas_call(
        forward_kernel,
        out_shape=[jax.ShapeDtypeStruct(w, low) for w in whole]
        + [jax.ShapeDtypeStruct((2, *p.shape), p.dtype) for p in pairs]
        + [jax.ShapeDtypeStruct(blocks, low)] * 3
        + [
            jax.ShapeDtypeStruct(blocks, wide),
            jax.ShapeDtypeStruct((8, 1, BLOCK), wide),
            jax.ShapeDtypeStruct((BLOCK, 1024), low),
            jax.ShapeDtypeStruct((BLOCK, D), low),
            jax.ShapeDtypeStruct((BLOCK, 1024), wide),
            jax.ShapeDtypeStruct((BLOCK, 512), wide),
            jax.ShapeDtypeStruct((8, D), wide),
        ],
        in_specs=[VMEM] * 11,
        out_specs=[HBM] * 15 + [VMEM] + [HBM] * 4 + [VMEM],
        scratch_shapes=[
            pltpu.VMEM((2, 128, D), low),
            pltpu.VMEM((2, 128, HEAD_DIM), wide),
            pltpu.VMEM(whole[3], low),
            pltpu.VMEM(whole[0], low),
            pltpu.VMEM(whole[1], low),
            pltpu.VMEM(whole[2], low),
            pltpu.VMEM((BLOCK, D), low),
            pltpu.VMEM((BLOCK, 1024), wide),
            pltpu.VMEM((BLOCK, 512), wide),
            pltpu.VMEM((BLOCK, 1024), low),
            pltpu.VMEM((BLOCK, 512), low),
            pltpu.VMEM((BLOCK, 512), low),
        ]
        + [pltpu.VMEM(blocks, low)] * 3
        + [
            pltpu.VMEM(blocks, wide),
            pltpu.VMEM(blocks, low),
            pltpu.VMEM((8, BLOCK, BLOCK), wide),
            pltpu.VMEM((8, HEAD_DIM, BLOCK), low),
            pltpu.VMEM((2, 8, TILE), low),
            pltpu.SemaphoreType.DMA((count, 3)),
            pltpu.SemaphoreType.DMA((count, 3)),
            pltpu.SemaphoreType.DMA((4, 8)),
            pltpu.SemaphoreType.DMA((4, 8)),
            pltpu.SemaphoreType.DMA((4,)),
            pltpu.SemaphoreType.DMA((4,)),
            pltpu.SemaphoreType.DMA((9,)),
            pltpu.SemaphoreType.DMA((11,)),
            pltpu.SemaphoreType.DMA((11,)),
            pltpu.SemaphoreType.DMA((11,)),
        ],
        compiler_params=pltpu.CompilerParams(
            collective_id=2, has_side_effects=True, vmem_limit_bytes=LIMIT
        ),
        name="attend",
    )(gain_rows, *shards, *pairs)


LAST_WIDTHS = (1024, 512, 512, 1024, 1536, 1536, 1536)


def scatter_steps():
    pieces = flat_pieces(NEAR_PIECES) + flat_pieces(FAR_PIECES)
    return [(piece, phase) for piece in pieces for phase in range(3)]


def backward_kernel(*refs):
    near, far = flat_pieces(NEAR_PIECES), flat_pieces(FAR_PIECES)
    n_w, steps = len(LAST_WIDTHS), scatter_steps()
    n_steps = len(steps)
    ins, far_grads, do_in, refs = refs[:16], refs[16:20], refs[20], refs[21:]
    outs, refs = refs[:n_w], refs[n_w:]
    in_gain_out, post_gain_out, q_gain_out, k_gain_out, input_grad = refs[:5]
    held, refs = refs[5:21], refs[21:]
    q_ref, k_ref, v_ref, o32_ref, lse_ref, qpre, kpre, normed, tab, rows, x_ref = held[:11]
    wq, wk, wv, gmid, post = held[11:]
    do_ref, dq_low, dk_low, dv_low, kt, dk_acc, dv_acc = refs[:7]
    gq, kparts, vparts, dq, dk, dv, normed_t, pair_out, pair_in, gain_got = refs[7:17]
    refs = refs[17:]
    grads, refs = refs[:NEAR], refs[NEAR:]
    fin, refs = refs[: n_w + 1], refs[n_w + 1 :]
    landing, refs = refs[: 3 * n_steps], refs[3 * n_steps :]
    mids, refs = refs[:n_steps], refs[n_steps:]
    results, refs = refs[:n_steps], refs[n_steps:]
    send, recv, pair_send, pair_recv, local, load, far_load, head_send, head_recv, head_local = refs
    yh, z, x, yl, c = place()
    me = x * 2 + yl
    sib = sibling()
    scatter = Scatter(steps, list(grads) + list(far_grads), landing, mids, results, fin, send, recv)
    loads = load_all(list(zip(ins, held)), load)
    for n, piece in enumerate(far):
        scatter.load(piece, far_load.at[n])
    greet(torus_neighbours() + sequence_others() + [sib])
    arriving = exchange_start(
        [(lambda j: do_in.at[:, columns(j)], lambda i: do_ref.at[i])],
        me, head_send, head_recv, head_local, 0,
    )
    scatter.begin(far[:2], 0)
    scatter.begin(far[2:], 0)
    for copy in loads[:5]:
        copy.wait()
    for j in range(8):
        kt[j] = k_ref[j].T
    dk_acc[...] = jnp.zeros_like(dk_acc)
    dv_acc[...] = jnp.zeros_like(dv_acc)
    for copy in arriving:
        copy.wait()

    def one_block(i, _):
        q, do, lse = q_ref[i], do_ref[i], lse_ref[i]
        delta = jnp.sum((do.astype(jnp.float32) * o32_ref[i]).T, axis=0, keepdims=True)

        def one_pair(j, dqt):
            p = jnp.exp2(nt(k_ref[j], q) * (score_scale * log2e) - lse)
            dp = nt(v_ref[j], do)
            ds = (p * (dp - delta)).astype(jnp.bfloat16)
            dv_acc[j] += jnp.dot(p.astype(jnp.bfloat16), do, preferred_element_type=jnp.float32)
            dk_acc[j] += jnp.dot(ds, q, preferred_element_type=jnp.float32)
            return dqt + jnp.dot(kt[j], ds, preferred_element_type=jnp.float32)

        dqt = lax.fori_loop(0, i + 1, one_pair, jnp.zeros((HEAD_DIM, BLOCK), jnp.float32))
        dq_low[i] = (dqt * score_scale).T.astype(jnp.bfloat16)
        return 0

    lax.fori_loop(0, 6, one_block, 0)
    scatter.middle(far[:2], 0)
    scatter.middle(far[2:], 0)
    lax.fori_loop(6, 8, one_block, 0)
    dk_low[...] = (dk_acc[...] * score_scale).astype(jnp.bfloat16)
    dv_low[...] = dv_acc[...].astype(jnp.bfloat16)
    arriving = exchange_start(
        [
            (lambda j: dq_low.at[j], lambda i: gq.at[:, columns(i)]),
            (lambda j: dk_low.at[j], lambda i: kparts.at[i % 2, :, columns(i // 2)]),
            (lambda j: dv_low.at[j], lambda i: vparts.at[i % 2, :, columns(i // 2)]),
        ],
        me, head_send, head_recv, head_local, 1,
    )
    scatter.end(far[:2], 0)
    scatter.end(far[2:], 0)
    for copy in loads[5:]:
        copy.wait()
    normed_t[...] = normed[...].T
    for copy in arriving:
        copy.wait()
    cosine, sine = rope_pair(tab)
    gain_q, gain_k = rows[2:3, :HEAD_DIM], rows[3:4, :HEAD_DIM]

    def head_back(grad, values, gain):
        grad = grad * cosine - pltpu.roll(grad, HEAD_DIM // 2, 1) * sine
        grad_in, terms = norm_back(grad, values, rms_scale(values), gain)
        return grad_in.astype(jnp.bfloat16), jnp.sum(terms, axis=0, keepdims=True)

    q_part = jnp.zeros((1, HEAD_DIM), jnp.float32)
    k_part = jnp.zeros((1, HEAD_DIM), jnp.float32)
    for h in range(8):
        at = slice(h * HEAD_DIM, (h + 1) * HEAD_DIM)
        dq[:, at], part = head_back(gq[:, at].astype(jnp.float32), qpre[:, at], gain_q)
        q_part = q_part + part
    for h in range(4):
        at = slice(h * HEAD_DIM, (h + 1) * HEAD_DIM)
        grad = kparts[0, :, at].astype(jnp.float32) + kparts[1, :, at].astype(jnp.float32)
        dk[:, at], part = head_back(grad, kpre[:, at], gain_k)
        k_part = k_part + part
    dv[...] = (vparts[0].astype(jnp.float32) + vparts[1].astype(jnp.float32)).astype(jnp.bfloat16)

    def weight_grads(n, _):
        lhs = normed_t[pl.ds(pl.multiple_of(n * 256, 256), 256), :]
        for grad, factor in ((grads[0], dq), (grads[1], dk), (grads[2], dv)):
            width = factor.shape[1]
            block = jnp.dot(lhs, factor[...], preferred_element_type=jnp.float32)
            grad[n // 2, pl.ds(n % 2 * 2, 2)] = block.astype(jnp.bfloat16).reshape(2, 4, 2, 16, width)
        return 0

    lax.fori_loop(0, 4, weight_grads, 0)
    weights = [piece for piece in near if piece.array != NEAR - 1]
    gains = [piece for piece in near if piece.array == NEAR - 1]
    scatter.begin(weights, 0)

    def grad_normed(rows_at):
        return (
            nt(dq[rows_at, :], wq[...]) + nt(dk[rows_at, :], wk[...]) + nt(dv[rows_at, :], wv[...])
        )

    away = pl.ds(pl.multiple_of((1 - c) * 128, 128), 128)
    own = pl.ds(pl.multiple_of(c * 128, 128), 128)
    pair_out[...] = grad_normed(away).astype(jnp.bfloat16)
    swap = pltpu.make_async_remote_copy(
        pair_out, pair_in, pair_send.at[n_w + 1], pair_recv.at[n_w + 1], device_id=sib
    )
    swap.start()
    grad = grad_normed(own)
    values = x_ref[c].astype(jnp.float32)
    swap.wait_recv()
    grad = grad + pair_in[...].astype(jnp.float32)
    grad_in, terms = norm_back(grad, values, rms_scale(values), rows[0:1, :])
    input_grad[...] = (gmid[...] + grad_in).astype(jnp.bfloat16)
    in_part = jnp.sum(terms, axis=0, keepdims=True)
    spread = (
        lax.broadcasted_iota(jnp.int32, (HEAD_DIM, D), 1)
        == 8 * lax.broadcasted_iota(jnp.int32, (HEAD_DIM, D), 0)
    ).astype(jnp.bfloat16)
    qk = jnp.concatenate([q_part, k_part, jnp.zeros((6, HEAD_DIM), jnp.float32)]).astype(jnp.bfloat16)
    qk = jnp.dot(qk, spread, preferred_element_type=jnp.float32)
    gain_rows = jnp.concatenate(
        [in_part, post[0:1, :], qk[0:2], jnp.zeros((TILE - 4, D), jnp.float32)]
    )
    grads[NEAR - 1][...] = gain_rows.T.astype(jnp.bfloat16).reshape(2, 4, 4, 2, 16, TILE)
    scatter.begin(gains, 0)

    copies = []

    def deliver(k):
        if k == NEAR - 1:
            target = gain_got
        else:
            out = outs[k if k < NEAR else k - 1]
            width = out.shape[1] // 2
            target = out.at[:, pl.ds(pl.multiple_of(c * width, TILE), width)]
            keep = pltpu.make_async_copy(fin[k].at[c], target, local.at[k])
            keep.start()
            copies.append(keep)
        away_k = pltpu.make_async_remote_copy(
            fin[k].at[1 - c], target, pair_send.at[k], pair_recv.at[k], device_id=sib
        )
        away_k.start()
        copies.append(away_k)

    near = weights + gains
    scatter.middle(near, 0)
    scatter.middle(far, 1)
    scatter.end(near, 0)
    scatter.end(far, 1)
    scatter.middle(near, 1)
    scatter.middle(far, 2)
    scatter.end(near, 1)
    scatter.middle(near, 2)
    scatter.end(far, 2)
    for k in range(NEAR, 8):
        deliver(k)
    scatter.end(near, 2)
    for k in range(NEAR):
        deliver(k)
    scatter.drain()
    swap.wait_send()
    for copy in copies:
        copy.wait()
    gain_sum = fin[NEAR - 1][c] + gain_got[...]
    gain_rows = jnp.concatenate([gain_sum, jnp.zeros((TILE - 8, TILE), jnp.float32)]).T
    in_gain_out[...] = gain_rows[0:1, :8]
    post_gain_out[...] = gain_rows[1:2, :8]
    q_gain_out[...] = gain_rows[2:3, :1]
    k_gain_out[...] = gain_rows[3:4, :1]


def attend_back(arrays, far_grads, grad_att):
    steps = scatter_steps()
    blocks = (8, BLOCK, HEAD_DIM)
    low, wide = jnp.bfloat16, jnp.float32
    n_w = len(LAST_WIDTHS)
    fin_widths = list(LAST_WIDTHS)
    fin_widths.insert(NEAR - 1, TILE)
    far = flat_pieces(FAR_PIECES)
    return pl.pallas_call(
        backward_kernel,
        out_shape=[jax.ShapeDtypeStruct((8, 2 * w), wide) for w in LAST_WIDTHS]
        + [jax.ShapeDtypeStruct((1, n), wide) for n in (8, 8, 1, 1)]
        + [jax.ShapeDtypeStruct((128, D), low)],
        in_specs=[HBM] * (len(arrays) + 5),
        out_specs=[HBM] * n_w + [VMEM] * 5,
        scratch_shapes=[pltpu.VMEM(a.shape, a.dtype) for a in arrays]
        + [pltpu.VMEM(blocks, low)] * 4
        + [
            pltpu.VMEM((8, HEAD_DIM, BLOCK), low),
            pltpu.VMEM(blocks, wide),
            pltpu.VMEM(blocks, wide),
            pltpu.VMEM((BLOCK, 1024), low),
            pltpu.VMEM((2, BLOCK, 512), low),
            pltpu.VMEM((2, BLOCK, 512), low),
            pltpu.VMEM((BLOCK, 1024), low),
            pltpu.VMEM((BLOCK, 512), low),
            pltpu.VMEM((BLOCK, 512), low),
            pltpu.VMEM((D, BLOCK), low),
            pltpu.VMEM((128, D), low),
            pltpu.VMEM((128, D), low),
            pltpu.VMEM((8, TILE), wide),
        ]
        + [pltpu.VMEM((2, 4, 4, 2, 16, w), low) for w in fin_widths[:NEAR]]
        + [pltpu.VMEM((2, 8, w), wide) for w in fin_widths]
        + landing_shapes(steps)
        + mid_shapes(steps)
        + mid_shapes(steps)
        + [
            pltpu.SemaphoreType.DMA((len(steps), 3)),
            pltpu.SemaphoreType.DMA((len(steps), 3)),
            pltpu.SemaphoreType.DMA((n_w + 2,)),
            pltpu.SemaphoreType.DMA((n_w + 2,)),
            pltpu.SemaphoreType.DMA((n_w + 1,)),
            pltpu.SemaphoreType.DMA((len(arrays),)),
            pltpu.SemaphoreType.DMA((len(far), 2)),
            pltpu.SemaphoreType.DMA((4, 8)),
            pltpu.SemaphoreType.DMA((4, 8)),
            pltpu.SemaphoreType.DMA((4,)),
        ],
        compiler_params=pltpu.CompilerParams(
            collective_id=3, has_side_effects=True, vmem_limit_bytes=LIMIT
        ),
        name="attend_back",
    )(*arrays, *far_grads, grad_att)


def middle_kernel(*refs):
    att_in, x_in, g_in, rows_in, wo_in, wg_in, wu_in, wd_in = refs[:8]
    output, grad_att_out, gmid_out, post_out = refs[8:12]
    dwo_out, dwg_out, dwu_out, dwd_out = refs[12:16]
    att, x_ref, g_ref, rows, wo, wg, wu, wd = refs[16:24]
    (branch, middle, hidden, hidden_t, g_t, grad_act, act, gate_grad, up_grad, grad_hidden, branch_t,
     down_own, grad_att, dwo, dwg, dwu, dwd) = refs[24:41]
    out1, in1, out2, in2, out3, in3 = refs[41:47]
    pair_send, pair_recv, load, store = refs[47:]
    yh, z, x, yl, c = place()
    sib = sibling()
    loads = load_all(
        [(att_in, att), (wo_in, wo), (g_in, g_ref), (wd_in, wd), (x_in, x_ref), (rows_in, rows),
         (wg_in, wg), (wu_in, wu)], load
    )
    greet([sib])
    swaps = []

    def swap(source, target):
        n = len(swaps)
        copy = pltpu.make_async_remote_copy(
            source, target, pair_send.at[n], pair_recv.at[n], device_id=sib
        )
        copy.start()
        swaps.append(copy)
        return copy

    def part(n, width=256):
        return pl.ds(n * width, width)

    loads[0].wait()
    loads[1].wait()
    first = []
    for n in range(4):
        block = nt(att[...], wo[part(n), :])
        branch[:, part(n)] = block
        out1[n] = block.astype(jnp.bfloat16)
        first.append(swap(out1.at[n], in1.at[n]))
    loads[2].wait()
    loads[3].wait()
    g_low = g_ref[...].reshape(BLOCK, D)
    for n in range(6):
        grad_act[:, part(n)] = jnp.dot(g_low, wd[:, part(n)], preferred_element_type=jnp.float32)
    g_t[...] = g_low.T
    loads[4].wait()
    loads[5].wait()
    for n in range(4):
        first[n].wait_recv()
        middle[:, part(n)] = (
            x_ref[...].reshape(BLOCK, D)[:, n * 256 : n * 256 + 256].astype(jnp.float32)
            + (branch[:, part(n)] + in1[n].astype(jnp.float32))
        )
    gain = rows[1:2, :]
    scale = rms_scale(middle[...])
    hidden[...] = (middle[...] * scale * gain).astype(jnp.bfloat16)
    loads[6].wait()
    loads[7].wait()
    for n in range(6):
        gate = jnp.dot(hidden[...], wg[:, part(n)], preferred_element_type=jnp.float32)
        up = jnp.dot(hidden[...], wu[:, part(n)], preferred_element_type=jnp.float32)
        sigma = jax.nn.sigmoid(gate)
        swish = gate * sigma
        grad = grad_act[:, part(n)]
        act[:, part(n)] = (swish * up).astype(jnp.bfloat16)
        gate_grad[:, part(n)] = (grad * up * (sigma * (1.0 + gate * (1.0 - sigma)))).astype(jnp.bfloat16)
        up_grad[:, part(n)] = (grad * swish).astype(jnp.bfloat16)
    second = []
    for n in range(4):
        block = nt(gate_grad[...], wg[part(n), :]) + nt(up_grad[...], wu[part(n), :])
        grad_hidden[:, part(n)] = block
        out2[n] = block.astype(jnp.bfloat16)
        second.append(swap(out2.at[n], in2.at[n]))
    away = pl.ds(pl.multiple_of((1 - c) * 128, 128), 128)
    own = pl.ds(pl.multiple_of(c * 128, 128), 128)
    out3[...] = nt(act[away, :], wd[...]).astype(jnp.bfloat16)
    third = swap(out3, in3)
    down_own[...] = nt(act[own, :], wd[...])
    hidden_t[...] = hidden[...].T
    stores = []

    def keep(source, target):
        copy = pltpu.make_async_copy(source, target, store.at[len(stores)])
        copy.start()
        stores.append(copy)

    for lhs, rhs, grads, target in (
        (hidden_t, gate_grad, dwg, dwg_out), (hidden_t, up_grad, dwu, dwu_out), (g_t, act, dwd, dwd_out)
    ):
        for n in range(4):
            grads[part(n), :] = jnp.dot(
                lhs[part(n), :], rhs[...], preferred_element_type=jnp.float32
            ).astype(jnp.bfloat16)
        keep(grads, target)
    for n in range(4):
        second[n].wait_recv()
        grad_hidden[:, part(n)] = grad_hidden[:, part(n)] + in2[n].astype(jnp.float32)
    grad_in, terms = norm_back(grad_hidden[...], middle[...], scale, gain)
    grad_hidden[...] = terms
    post_out[...] = jnp.broadcast_to(jnp.sum(grad_hidden[own, :], axis=0, keepdims=True), (8, D))
    grad_hidden[...] = g_low.astype(jnp.float32) + grad_in
    gmid_out[...] = grad_hidden[own, :]
    branch_grad = grad_hidden[...].astype(jnp.bfloat16)
    branch_t[...] = branch_grad.T
    for n in range(4):
        grad_att[:, part(n)] = jnp.dot(
            branch_grad, wo[:, part(n)], preferred_element_type=jnp.float32
        ).astype(jnp.bfloat16)
    keep(grad_att, grad_att_out)
    for n in range(4):
        dwo[part(n), :] = jnp.dot(
            branch_t[part(n), :], att[...], preferred_element_type=jnp.float32
        ).astype(jnp.bfloat16)
    keep(dwo, dwo_out)
    third.wait_recv()
    output[...] = (
        middle[own, :] + (down_own[...] + in3[...].astype(jnp.float32))
    ).astype(jnp.bfloat16)
    for copy in swaps:
        copy.wait_send()
    for copy in stores:
        copy.wait()


def feed_forward(arrays):
    low, wide = jnp.bfloat16, jnp.float32
    shapes = [(D, 1024), (D, 1536), (D, 1536), (D, 1536)]
    return pl.pallas_call(
        middle_kernel,
        out_shape=[
            jax.ShapeDtypeStruct((128, D), low),
            jax.ShapeDtypeStruct((BLOCK, 1024), low),
            jax.ShapeDtypeStruct((128, D), wide),
            jax.ShapeDtypeStruct((8, D), wide),
        ]
        + [jax.ShapeDtypeStruct(s, low) for s in shapes],
        in_specs=[HBM] * 8,
        out_specs=[VMEM, HBM, VMEM, VMEM] + [HBM] * 4,
        scratch_shapes=[pltpu.VMEM(a.shape, a.dtype) for a in arrays]
        + [
            pltpu.VMEM((BLOCK, D), wide),
            pltpu.VMEM((BLOCK, D), wide),
            pltpu.VMEM((BLOCK, D), low),
            pltpu.VMEM((D, BLOCK), low),
            pltpu.VMEM((D, BLOCK), low),
            pltpu.VMEM((BLOCK, 1536), wide),
            pltpu.VMEM((BLOCK, 1536), low),
            pltpu.VMEM((BLOCK, 1536), low),
            pltpu.VMEM((BLOCK, 1536), low),
            pltpu.VMEM((BLOCK, D), wide),
            pltpu.VMEM((D, BLOCK), low),
            pltpu.VMEM((128, D), wide),
            pltpu.VMEM((BLOCK, 1024), low),
        ]
        + [pltpu.VMEM(s, low) for s in shapes]
        + [pltpu.VMEM((4, BLOCK, 256), low)] * 4
        + [pltpu.VMEM((128, D), low)] * 2
        + [
            pltpu.SemaphoreType.DMA((9,)),
            pltpu.SemaphoreType.DMA((9,)),
            pltpu.SemaphoreType.DMA((8,)),
            pltpu.SemaphoreType.DMA((5,)),
        ],
        compiler_params=pltpu.CompilerParams(
            collective_id=4, has_side_effects=True, vmem_limit_bytes=LIMIT
        ),
        name="feed_forward",
    )(*arrays)


def results_kernel(n, *refs):
    for source, target in zip(refs[:n], refs[n:]):
        target[...] = source[...]


def results(arrays):
    n = len(arrays)
    return pl.pallas_call(
        functools.partial(results_kernel, n),
        out_shape=[jax.ShapeDtypeStruct(a.shape, a.dtype) for a in arrays],
        in_specs=[VMEM] * n,
        out_specs=[VMEM] * n,
        name="results",
    )(*arrays)


def split_columns(shard):
    rows, width = shard.shape
    return jnp.transpose(shard.reshape(rows, CORES, width // CORES), (1, 0, 2))


def body(
    tokens,
    positions,
    in_gain,
    q_gain,
    k_gain,
    w_query,
    w_key,
    w_value,
    w_out,
    post_gain,
    w_gate,
    w_up,
    w_down,
    cotangent,
):
    half = HEAD_DIM // 2
    frequency = rope_base ** (-2.0 * jnp.arange(half, dtype=jnp.float32) / HEAD_DIM)
    angles = positions[0].astype(jnp.float32)[:, None] * frequency[None, :]
    table = jnp.concatenate([jnp.cos(angles), jnp.sin(angles)], axis=-1)
    gain_rows = jnp.stack(
        [jnp.pad(g, (0, TILE - g.shape[0])) for g in (in_gain, post_gain, q_gain, k_gain)]
    )
    gain_rows = jnp.pad(gain_rows, ((0, 4), (0, 0)))
    shards = [
        split_columns(w) for w in (w_query, w_key, w_value, w_out.T, w_gate, w_up, w_down.T)
    ]
    *gathered, x_pair, g_pair, tables, q_all, k_all, v_all, mixed, log_total, attended, normed, q_pre, k_pre, rows = attend(
        gain_rows, shards, [tokens[0], cotangent[0], table]
    )
    wq, wk, wv, _, wo, wg, wu, wd = [w.reshape(D, w.shape[-1]) for w in gathered]
    output, grad_att, grad_middle, post_part, *far_grads = feed_forward(
        [attended, x_pair, g_pair, rows, wo, wg, wu, wd]
    )
    last = attend_back(
        [q_all, k_all, v_all, mixed, log_total, q_pre, k_pre, normed, tables, rows, x_pair, wq, wk, wv,
         grad_middle, post_part],
        [g.reshape(2, 4, 4, 2, 16, g.shape[-1]) for g in far_grads],
        grad_att,
    )
    *sums, in_gain_grad, post_gain_grad, q_gain_grad, k_gain_grad, input_grad, output = results(
        [*last, output]
    )
    return (
        output[None],
        input_grad[None],
        in_gain_grad[0],
        q_gain_grad[0],
        k_gain_grad[0],
        sums[0],
        sums[1],
        sums[2],
        sums[3].T,
        post_gain_grad[0],
        sums[4],
        sums[5],
        sums[6].T,
    )


def solution(mesh):
    placed = (
        P("dp", "seq", None),
        P("dp", "seq"),
        P(("dp", "seq")),
        P(("dp", "seq")),
        P(("dp", "seq")),
        P(("dp", "seq"), None),
        P(("dp", "seq"), None),
        P(("dp", "seq"), None),
        P(None, ("dp", "seq")),
        P(("dp", "seq")),
        P(("dp", "seq"), None),
        P(("dp", "seq"), None),
        P(None, ("dp", "seq")),
        P("dp", "seq", None),
    )
    return jax.shard_map(
        body,
        mesh=mesh,
        in_specs=placed,
        out_specs=(
            P("dp", "seq", None),
            P("dp", "seq", None),
            P(("dp", "seq")),
            P(("dp", "seq")),
            P(("dp", "seq")),
            P(("dp", "seq"), None),
            P(("dp", "seq"), None),
            P(("dp", "seq"), None),
            P(None, ("dp", "seq")),
            P(("dp", "seq")),
            P(("dp", "seq"), None),
            P(("dp", "seq"), None),
            P(None, ("dp", "seq")),
        ),
        check_vma=False,
    )
```

```python
import functools
import math

import jax
import jax.numpy as jnp
from jax import lax
from jax.experimental import pallas as pl
from jax.experimental.pallas import tpu as pltpu
from jax.sharding import PartitionSpec as P

HEADS = 16
KV_HEADS = 8
HEAD_DIM = 128
D = 1024
FF = 3072
BLOCK = 256
CORES = 2

TILE = 128

eps_norm = 1e-06
rope_base = 1000000.0
score_scale = 1.0 / math.sqrt(HEAD_DIM)
log2e = math.log2(math.e)


def place():
    dp = lax.axis_index("dp")
    seq = lax.axis_index("seq")
    return dp // 4, dp % 4, seq // 4, (seq // 2) % 2, seq % 2


def device(yh, z, x, yl, c):
    return {"dp": yh * 4 + z, "seq": x * 4 + yl * 2 + c}


def sibling():
    yh, z, x, yl, c = place()
    return device(yh, z, x, yl, 1 - c)


def neighbour(axis, step):
    yh, z, x, yl, c = place()
    if axis == "x":
        return device(yh, z, (x + step + 4) % 4, yl, c)
    if axis == "z":
        return device(yh, (z + step + 4) % 4, x, yl, c)
    y = (yh * 2 + yl + step + 4) % 4
    return device(y // 2, z, x, y % 2, c)


ORDERS = (("x", "y", "z"), ("y", "z", "x"), ("z", "x", "y"))


def chip_set(whole_axes, axis, step):
    yh, z, x, yl, _ = place()
    iz, ix, iyh, iyl = z, x, yh, yl
    if axis == "x":
        ix = (x + step + 4) % 4
    elif axis == "z":
        iz = (z + step + 4) % 4
    else:
        y = (yh * 2 + yl + step + 4) % 4
        iyh, iyl = y // 2, y % 2
    every = slice(None)
    if "x" in whole_axes:
        ix = every
    if "z" in whole_axes:
        iz = every
    if "y" in whole_axes:
        iyh, iyl = every, every
    return (iyh, iz, ix, iyl)


def set_dims(whole_axes):
    dims = ()
    if "y" in whole_axes:
        dims += (2,)
    if "z" in whole_axes:
        dims += (4,)
    if "x" in whole_axes:
        dims += (4,)
    if "y" in whole_axes:
        dims += (2,)
    return dims


NEAR, FAR = 0, 1
WIDE = (2176, 5632)
LIMIT = 60 << 20


class Part:
    def __init__(self, array, number, order, first, tiles):
        self.array, self.number, self.order = array, number, order
        self.start, self.width = first * TILE, tiles * TILE
        self.cols = pl.ds(self.start, self.width)
        cut = (tiles + 1) // 2 * TILE
        self.halves = ((0, 1, 0, cut), (1, -1, cut, self.width - cut))


def parts_of(array, tiles):
    parts, first = [], 0
    for number, count in enumerate(tiles):
        parts.append(Part(array, number, ORDERS[number], first, count))
        first += count
    return parts


def near_parts():
    return parts_of(NEAR, (6, 6, 5))


def far_parts():
    return parts_of(FAR, (20, 12, 12))


def greet(others):
    barrier = pltpu.get_barrier_semaphore()
    for other in others:
        pl.semaphore_signal(barrier, inc=1, device_id=other)
    pl.semaphore_wait(barrier, len(others))


def ring_device(axis, step, other):
    yh, z, x, yl, c = place()
    core = (c + other) % 2
    if axis == "x":
        return device(yh, z, (x + step + 4) % 4, yl, core)
    if axis == "z":
        return device(yh, (z + step + 4) % 4, x, yl, core)
    y = (yh * 2 + yl + step + 4) % 4
    return device(y // 2, z, x, y % 2, core)


def ring_devices():
    return [ring_device(axis, step, other) for axis in "xyz" for step in (1, 2, 3) for other in (0, 1)]


def sequence_chip(number):
    yh, z, x, yl, c = place()
    return device(yh, z, number // 2, number % 2, c)


def sequence_others():
    yh, z, x, yl, c = place()
    me = x * 2 + yl
    return [sequence_chip((me + step) % 8) for step in range(1, 8)]


HBM = pl.BlockSpec(memory_space=pltpu.HBM)
VMEM = pl.BlockSpec(memory_space=pltpu.VMEM)


def load_all(pairs, sems):
    copies = [pltpu.make_async_copy(a, b, sems.at[n]) for n, (a, b) in enumerate(pairs)]
    for copy in copies:
        copy.start()
    return copies


def nt(left, right):
    return lax.dot_general(left, right, (((1,), (1,)), ((), ())), preferred_element_type=jnp.float32)


def rms_scale(values):
    return lax.rsqrt(jnp.mean(values * values, axis=-1, keepdims=True) + eps_norm)


def norm_back(grad_out, values, scale_factor, gain):
    weighted = grad_out * gain
    inner = jnp.mean(weighted * values, axis=-1, keepdims=True)
    grad_in = (
        scale_factor * weighted - values * (scale_factor * scale_factor * scale_factor) * inner
    )
    return (grad_in, grad_out * values * scale_factor)


def rope_pair(tab):
    table = tab[...].reshape(BLOCK, HEAD_DIM)
    turned = pltpu.roll(table, HEAD_DIM // 2, 1)
    low = lax.broadcasted_iota(jnp.int32, (BLOCK, HEAD_DIM), 1) < HEAD_DIM // 2
    return jnp.where(low, table, turned), jnp.where(low, -turned, table)


class Gather:
    def __init__(self, units, outs, base, send, recv, local):
        self.units, self.outs, self.base = units, outs, base
        self.send, self.recv, self.local = send, recv, local
        self.copies = {}

    def remote(self, key, slot, source, target, device_id):
        copy = pltpu.make_async_remote_copy(
            source, target, self.send.at[slot], self.recv.at[slot], device_id=device_id
        )
        copy.start()
        self.copies[key] = copy

    def slot(self, part, n):
        return self.base[part.array] + part.number * GATHER_SLOTS + n

    def spread(self, parts):
        yh, z, x, yl, c = place()
        for part in parts:
            target = self.outs[part.array].at[yh, z, x, yl, c, :, part.cols]
            for step in range(4):
                for other in range(2):
                    source = self.units[part.array].at[(c + other) % 2, :, part.cols]
                    key = (part.array, part.number, 0, step, other)
                    if step == 0 and other == 0:
                        copy = pltpu.make_async_copy(
                            source, target, self.local.at[part.array * 3 + part.number]
                        )
                        copy.start()
                        self.copies[key] = copy
                    else:
                        slot = self.slot(part, step * 2 + other - 1)
                        self.remote(key, slot, source, target, ring_device(part.order[0], step, other))

    def settle(self, part):
        for step in range(4):
            for other in range(2):
                copy = self.copies[part.array, part.number, 0, step, other]
                if step == 0 and other == 0:
                    copy.wait()
                else:
                    copy.wait_recv()

    def block(self, part, phase, offset, first, width):
        index = chip_set(part.order[:phase], part.order[phase], offset)
        cols = pl.ds(part.start + first, width)
        return self.outs[part.array].at[(*index, slice(None), slice(None), cols)]

    def direct(self, part):
        ref = self.block(part, 1, 0, 0, part.width)
        for step in (1, 2, 3):
            key = (part.array, part.number, 1, step)
            self.remote(key, self.slot(part, 6 + step), ref, ref, ring_device(part.order[1], step, 0))

    def landed(self, part):
        for step in (1, 2, 3):
            self.copies[part.array, part.number, 1, step].wait_recv()

    def ring(self, part, phase, which):
        for half, way, first, width in part.halves:
            step, offset = ((way, 0), (-way, 0), (way, -way))[which]
            key = (part.array, part.number, phase, which, half)
            if which == 2:
                self.copies[part.array, part.number, phase, 0, half].wait_recv()
            ref = self.block(part, phase, offset, first, width)
            slot = self.slot(part, 7 + 6 * (phase - 1) + 2 * which + half)
            self.remote(key, slot, ref, ref, ring_device(part.order[phase], step, 0))

    def begin(self, parts, phase):
        for part in parts:
            self.ring(part, phase, 0)
            self.ring(part, phase, 1)

    def forward(self, parts, phase):
        for part in parts:
            self.ring(part, phase, 2)

    def arrive(self, parts, phase):
        for part in parts:
            for which in (1, 2):
                for half in (0, 1):
                    self.copies[part.array, part.number, phase, which, half].wait_recv()

    def drain(self):
        for key, copy in self.copies.items():
            if key[2:] != (0, 0, 0):
                copy.wait_send()


GATHER_SLOTS = 19


def kept_index(kept, axis, step):
    iyh, iz, ix, iyl = chip_set(tuple(a for a in kept if a != axis), axis, step)
    index = ()
    if "y" in kept:
        index += (iyh,)
    if "z" in kept:
        index += (iz,)
    if "x" in kept:
        index += (ix,)
    if "y" in kept:
        index += (iyl,)
    return index


def add_sets(dims, terms, store):
    def one(flat_index, _):
        index, rest = [], flat_index
        for size in reversed(dims):
            index.insert(0, rest % size)
            rest = rest // size
        at = tuple(index)
        total = terms[0][at].astype(jnp.float32)
        for term in terms[1:]:
            total = total + term[at].astype(jnp.float32)
        store(at, total)
        return 0

    lax.fori_loop(0, math.prod(dims), one, 0)


def scatter_shapes():
    low, shapes = jnp.bfloat16, []
    for part in near_parts() + far_parts():
        plane, line = set_dims(part.order[:2]), set_dims(part.order[:1])
        for _, _, _, width in part.halves:
            shapes += [pltpu.VMEM((*plane, 16, width), low)] * 4
            if part.array == FAR:
                shapes += [pltpu.VMEM((*line, 16, width), low)] * 4
        if part.array == NEAR:
            shapes += [pltpu.VMEM((*line, 16, part.width), low)] * 3
        shapes += [pltpu.VMEM((8, 8, part.width), low)]
        shapes += [pltpu.VMEM((*plane, 16, part.width), low)]
        shapes += [pltpu.VMEM((*line, 2, 8, part.width), low)]
    return shapes


class Scatter:
    def __init__(self, grads, fin, refs, send, recv):
        self.grads, self.fin, self.send, self.recv = grads, fin, send, recv
        self.copies, self.loads = {}, {}
        self.land, self.mids, self.plane, self.line = {}, {}, {}, {}
        refs = list(refs)
        for part in near_parts() + far_parts():
            name = (part.array, part.number)
            for half in (0, 1):
                for phase in (0, 1) if part.array == FAR else (0,):
                    self.land[name, phase, half] = [refs.pop(0) for _ in range(3)]
                    self.mids[name, phase, half] = refs.pop(0)
            if part.array == NEAR:
                self.land[name, 1] = [refs.pop(0) for _ in range(3)]
            self.land[name, 2] = refs.pop(0)
            self.plane[name] = refs.pop(0)
            self.line[name] = refs.pop(0)

    def remote(self, key, part, n, source, target, device_id):
        slot = (part.array * 3 + part.number) * GATHER_SLOTS + n
        copy = pltpu.make_async_remote_copy(
            source, target, self.send.at[slot], self.recv.at[slot], device_id=device_id
        )
        copy.start()
        self.copies[key] = copy

    def source(self, part, phase, offset, first, width):
        if phase == 0:
            index = chip_set(part.order[:2], part.order[2], offset)
            cols = pl.ds(part.start + first, width)
            return self.grads[part.array].at[(*index, slice(None), cols)]
        index = kept_index(part.order[:2], part.order[1], offset)
        return self.plane[part.array, part.number].at[(*index, slice(None), pl.ds(first, width))]

    def load(self, part, sems):
        name = (part.array, part.number)
        every = (slice(None),) * (len(set_dims(part.order[:2])) + 1)
        for half, way, first, width in part.halves:
            target = self.plane[name].at[(*every, pl.ds(first, width))]
            for m, (offset, place_to) in enumerate(((way, self.mids[name, 0, half]), (0, target))):
                copy = pltpu.make_async_copy(
                    self.source(part, 0, offset, first, width), place_to, sems.at[2 * half + m]
                )
                copy.start()
                self.loads[name, half, m] = copy

    def ring(self, part, phase, which):
        name = (part.array, part.number)
        for half, way, first, width in part.halves:
            offset, step = ((2, way), (-way, -way))[which]
            self.remote(
                (name, phase, which, half), part, 6 * phase + 2 * which + half,
                self.source(part, phase, offset, first, width), self.land[name, phase, half][which],
                ring_device(part.order[2 - phase], step, 0),
            )

    def begin(self, parts, phase):
        for part in parts:
            self.ring(part, phase, 0)
        for part in parts:
            self.ring(part, phase, 1)

    def middle(self, parts, phase):
        for part in parts:
            name = (part.array, part.number)
            for half, way, first, width in part.halves:
                self.copies[name, phase, 0, half].wait_recv()
                mid = self.mids[name, phase, half]
                own = self.source(part, phase, way, first, width)
                if (name, half, 0) in self.loads and phase == 0:
                    self.loads[name, half, 0].wait()
                    own = mid

                def store(at, total, mid=mid):
                    mid[at] = total.astype(jnp.bfloat16)

                add_sets(set_dims(part.order[: 2 - phase]), [own, self.land[name, phase, half][0]], store)
                self.remote(
                    (name, phase, 2, half), part, 6 * phase + 4 + half, mid,
                    self.land[name, phase, half][2], ring_device(part.order[2 - phase], way, 0),
                )

    def end(self, parts, phase):
        for part in parts:
            name = (part.array, part.number)
            for half, way, first, width in part.halves:
                self.copies[name, phase, 1, half].wait_recv()
                self.copies[name, phase, 2, half].wait_recv()
                base = self.source(part, phase, 0, first, width)
                cols = pl.ds(first, width)
                if phase == 0:
                    plane = self.plane[name]
                    if (name, half, 1) in self.loads:
                        self.loads[name, half, 1].wait()
                        base = plane.at[(*(slice(None),) * (len(plane.shape) - 1), cols)]

                    def store(at, total, plane=plane, cols=cols):
                        plane[(*at, slice(None), cols)] = total.astype(jnp.bfloat16)

                else:
                    line = self.line[name]

                    def store(at, total, line=line, cols=cols):
                        line[(*at, 0, slice(None), cols)] = total[:8].astype(jnp.bfloat16)
                        line[(*at, 1, slice(None), cols)] = total[8:].astype(jnp.bfloat16)

                add_sets(
                    set_dims(part.order[: 2 - phase]), [base, *self.land[name, phase, half][1:]], store
                )

    def direct(self, parts):
        for part in parts:
            name = (part.array, part.number)
            for step in (1, 2, 3):
                self.remote(
                    (name, 1, step), part, 5 + step, self.source(part, 1, step, 0, part.width),
                    self.land[name, 1][step - 1], ring_device(part.order[1], step, 0),
                )

    def landed(self, parts):
        for part in parts:
            name = (part.array, part.number)
            for step in (1, 2, 3):
                self.copies[name, 1, step].wait_recv()
            line = self.line[name]

            def store(at, total, line=line):
                line[(*at, 0)] = total[:8].astype(jnp.bfloat16)
                line[(*at, 1)] = total[8:].astype(jnp.bfloat16)

            add_sets(
                set_dims(part.order[:1]),
                [self.source(part, 1, 0, 0, part.width), *self.land[name, 1]], store,
            )

    def deliver(self, parts):
        c = place()[4]
        for part in parts:
            name, axis = (part.array, part.number), part.order[0]
            for step in range(4):
                for other in range(2):
                    if step or other:
                        source = self.line[name].at[
                            (*kept_index(part.order[:1], axis, step), (c + other) % 2)
                        ]
                        self.remote(
                            (name, 2, step, other), part, 11 + step * 2 + other, source,
                            self.land[name, 2].at[step * 2 + other], ring_device(axis, step, other),
                        )

    def finish(self, parts):
        c = place()[4]
        for part in parts:
            name, axis = (part.array, part.number), part.order[0]
            for other in range(2):
                total = None
                for step in range(4):
                    if step or other:
                        self.copies[name, 2, step, other].wait_recv()
                        term = self.land[name, 2][step * 2 + other]
                    else:
                        term = self.line[name][(*kept_index(part.order[:1], axis, 0), c)]
                    term = term.astype(jnp.float32)
                    total = term if total is None else total + term
                self.fin[part.array][(c + other) % 2, :, part.cols] = total

    def drain(self):
        for copy in self.copies.values():
            copy.wait_send()


def columns(head):
    return pl.ds(pl.multiple_of(head * HEAD_DIM, HEAD_DIM), HEAD_DIM)


def exchange_start(moves, me, send, recv, local, first):
    copies = []
    for step in range(1, 8):
        there = (me + step) % 8
        for n, (source, target) in enumerate(moves):
            copy = pltpu.make_async_remote_copy(
                source(there), target(me), send.at[first + n, step], recv.at[first + n, step],
                device_id=sequence_chip(there),
            )
            copy.start()
            copies.append(copy)
    for n, (source, target) in enumerate(moves):
        copy = pltpu.make_async_copy(source(me), target(me), local.at[first + n])
        copy.start()
        copies.append(copy)
    return copies


FAR_SPANS = ((0, 1024), (1024, 1536), (2560, 1536), (4096, 1536))


def middle_shapes():
    low, wide = jnp.bfloat16, jnp.float32
    return [
        pltpu.VMEM((BLOCK, D), wide),
        pltpu.VMEM((BLOCK, D), wide),
        pltpu.VMEM((BLOCK, D), low),
        pltpu.VMEM((D, BLOCK), low),
        pltpu.VMEM((D, BLOCK), low),
        pltpu.VMEM((BLOCK, 1536), wide),
        pltpu.VMEM((BLOCK, 1536), low),
        pltpu.VMEM((BLOCK, 1536), low),
        pltpu.VMEM((BLOCK, 1536), low),
        pltpu.VMEM((BLOCK, D), wide),
        pltpu.VMEM((128, D), wide),
        pltpu.VMEM((BLOCK, 1024), low),
        pltpu.VMEM((D, WIDE[FAR]), low),
        pltpu.VMEM((4, BLOCK, 256), low),
        pltpu.VMEM((4, BLOCK, 256), low),
        pltpu.VMEM((4, BLOCK, 256), low),
        pltpu.VMEM((4, BLOCK, 256), low),
        pltpu.VMEM((128, D), low),
        pltpu.VMEM((128, D), low),
    ]


def middle_layer(att, x_ref, g_low, rows, w_far, refs, outs, pair_send, pair_recv, sems, c, sib):
    output, grad_att_out, gmid_out, post_out, dw_out = outs
    (branch, middle, hidden, g_t, hidden_t, grad_act, act, gate_grad, up_grad, grad_hidden,
     down_own, grad_att, dw, out1, in1, out2, in2, out3, in3) = refs
    branch_t = hidden_t
    swaps = []

    def swap(source, target):
        n = 3 + len(swaps)
        copy = pltpu.make_async_remote_copy(
            source, target, pair_send.at[n], pair_recv.at[n], device_id=sib
        )
        copy.start()
        swaps.append(copy)
        return copy

    def part(n, width=256):
        return pl.ds(n * width, width)

    def far_rows(n, which):
        first, width = FAR_SPANS[which]
        half = n % 2 * 2
        return w_far[n // 2, half : half + 2, :, :, :, :, first : first + width].reshape(256, width)

    def far_cols(which, n):
        first = FAR_SPANS[which][0] + n * 256
        return w_far[:, :, :, :, :, :, first : first + 256].reshape(D, 256)

    first = []
    for n in range(4):
        block = nt(att[...], far_rows(n, 0))
        branch[:, part(n)] = block
        out1[n] = block.astype(jnp.bfloat16)
        first.append(swap(out1.at[n], in1.at[n]))
    for n in range(6):
        grad_act[:, part(n)] = jnp.dot(g_low, far_cols(3, n), preferred_element_type=jnp.float32)
    for n in range(4):
        first[n].wait_recv()
        middle[:, part(n)] = (
            x_ref[...].reshape(BLOCK, D)[:, n * 256 : n * 256 + 256].astype(jnp.float32)
            + (branch[:, part(n)] + in1[n].astype(jnp.float32))
        )
    gain = rows[1:2, :]
    scale = rms_scale(middle[...])
    hidden[...] = (middle[...] * scale * gain).astype(jnp.bfloat16)
    for n in range(6):
        gate = jnp.dot(hidden[...], far_cols(1, n), preferred_element_type=jnp.float32)
        up = jnp.dot(hidden[...], far_cols(2, n), preferred_element_type=jnp.float32)
        sigma = jax.nn.sigmoid(gate)
        swish = gate * sigma
        grad = grad_act[:, part(n)]
        act[:, part(n)] = (swish * up).astype(jnp.bfloat16)
        gate_grad[:, part(n)] = (grad * up * (sigma * (1.0 + gate * (1.0 - sigma)))).astype(jnp.bfloat16)
        up_grad[:, part(n)] = (grad * swish).astype(jnp.bfloat16)
    second = []
    for n in range(4):
        block = nt(gate_grad[...], far_rows(n, 1)) + nt(up_grad[...], far_rows(n, 2))
        grad_hidden[:, part(n)] = block
        out2[n] = block.astype(jnp.bfloat16)
        second.append(swap(out2.at[n], in2.at[n]))
    away = pl.ds(pl.multiple_of((1 - c) * 128, 128), 128)
    own = pl.ds(pl.multiple_of(c * 128, 128), 128)
    for n in range(4):
        out3[:, part(n)] = nt(act[away, :], far_rows(n, 3)).astype(jnp.bfloat16)
    third = swap(out3, in3)
    for n in range(4):
        down_own[:, part(n)] = nt(act[own, :], far_rows(n, 3))
    hidden_t[...] = hidden[...].T
    stores = []

    def keep(source, target):
        copy = pltpu.make_async_copy(source, target, sems.at[6 + len(stores)])
        copy.start()
        stores.append(copy)

    for lhs, rhs, (first, width) in (
        (hidden_t, gate_grad, FAR_SPANS[1]), (hidden_t, up_grad, FAR_SPANS[2]), (g_t, act, FAR_SPANS[3])
    ):
        for n in range(4):
            dw[part(n), first : first + width] = jnp.dot(
                lhs[part(n), :], rhs[...], preferred_element_type=jnp.float32
            ).astype(jnp.bfloat16)
        keep(dw.at[:, pl.ds(first, width)], dw_out.at[:, pl.ds(first, width)])
    for n in range(4):
        second[n].wait_recv()
        grad_hidden[:, part(n)] = grad_hidden[:, part(n)] + in2[n].astype(jnp.float32)
    grad_in, terms = norm_back(grad_hidden[...], middle[...], scale, gain)
    grad_hidden[...] = terms
    post_out[...] = jnp.broadcast_to(jnp.sum(grad_hidden[own, :], axis=0, keepdims=True), (8, D))
    grad_hidden[...] = g_low.astype(jnp.float32) + grad_in
    gmid_out[...] = grad_hidden[own, :]
    branch_grad = grad_hidden[...].astype(jnp.bfloat16)
    branch_t[...] = branch_grad.T
    for n in range(4):
        grad_att[:, part(n)] = jnp.dot(
            branch_grad, far_cols(0, n), preferred_element_type=jnp.float32
        ).astype(jnp.bfloat16)
    keep(grad_att, grad_att_out)
    for n in range(4):
        dw[part(n), :1024] = jnp.dot(
            branch_t[part(n), :], att[...], preferred_element_type=jnp.float32
        ).astype(jnp.bfloat16)
    keep(dw.at[:, pl.ds(0, 1024)], dw_out.at[:, pl.ds(0, 1024)])
    third.wait_recv()
    output[...] = (
        middle[own, :] + (down_own[...] + in3[...].astype(jnp.float32))
    ).astype(jnp.bfloat16)
    for copy in swaps:
        copy.wait_send()
    for copy in stores:
        copy.wait()


def forward_kernel(*refs):
    gains_in, shards, (x_in, g_in, cos_in, sin_in), refs = refs[:4], refs[4:11], refs[11:15], refs[15:]
    near_out, x_out, tab_out, q_out, k_out, v_out, o32_out, lse_ref, normed_out = refs[:9]
    qpre_out, kpre_out, rows_ref, output, grad_att_out, gmid_out, post_out, dw_out = refs[9:17]
    x_ref, g_ref, tab, w_near, w_far, normed, qpre, kpre, q_low, k_low, v_low = refs[17:28]
    q_ref, k_ref, v_ref, o32_ref, o_low, att, vt, near_unit, far_unit, tab_own = refs[28:38]
    middle_refs, refs = refs[38:57], refs[57:]
    send, recv, head_send, head_recv, local, load, store, pair_send, pair_recv, pair_local, own = refs
    weights = (w_near, w_far)
    yh, z, x, yl, c = place()
    me = x * 2 + yl
    sib = sibling()
    lanes = lax.broadcasted_iota(jnp.int32, (TILE, TILE), 1)
    rows = lax.broadcasted_iota(jnp.int32, (TILE, TILE), 0)
    tile = jnp.zeros((TILE, TILE), jnp.float32)
    for n, gain in enumerate(gains_in):
        value = gain[...].astype(jnp.float32)
        if value.shape[1] == 1:
            tile = jnp.where((rows == n) & (lanes == 0), value, tile)
        else:
            value = jnp.concatenate([value, jnp.zeros((1, TILE - 8), jnp.float32)], axis=1)
            tile = jnp.where(rows == n, value, tile)
    tile = tile.T[:8].astype(jnp.bfloat16)
    for unit, group, first in ((near_unit, shards[:3], 0), (far_unit, shards[3:], 0)):
        for shard in group:
            width = shard.shape[1] // 2
            for half in range(2):
                unit[half, :, first : first + width] = shard[:, half * width : (half + 1) * width]
            first += width
    near_unit[0, :, 2048:] = tile
    near_unit[1, :, 2048:] = tile
    tab_own[...] = jnp.concatenate([cos_in[...], sin_in[...]], axis=1)
    greet(ring_devices() + sequence_others() + [sib])
    near, far = near_parts(), far_parts()
    gather = Gather((near_unit, far_unit), weights, (0, 3 * GATHER_SLOTS), send, recv, own)
    gather.spread(near)
    pairs = []
    for k, (source, target) in enumerate(((x_in, x_ref), (tab_own, tab), (g_in, g_ref))):
        keep = pltpu.make_async_copy(source, target.at[c], pair_local.at[k])
        away = pltpu.make_async_remote_copy(
            source, target.at[c], pair_send.at[k], pair_recv.at[k], device_id=sib
        )
        keep.start()
        away.start()
        pairs.append((keep, away))
    gather.spread(far)
    for part in near:
        gather.settle(part)
        gather.direct(part)
    for part in near:
        gather.landed(part)
        gather.begin([part], 2)
    for part in far:
        gather.settle(part)
        gather.begin([part], 1)
    gather.forward(near, 2)
    gather.forward(far, 1)
    gather.arrive(far[:1], 1)
    gather.begin(far[:1], 2)
    gather.arrive(near, 2)
    keep_near = pltpu.make_async_copy(w_near, near_out, load.at[0])
    keep_near.start()
    gather.arrive(far[1:], 1)
    gather.ring(far[1], 2, 0)
    gather.ring(far[2], 2, 0)
    for keep, away in pairs:
        keep.wait()
        away.wait_recv()

    def matrix(first, width):
        return w_near[:, :, :, :, :, :, first : first + width].reshape(D, width)

    gain_rows = matrix(2048, TILE).astype(jnp.float32).T[:8]
    pick = (
        lax.broadcasted_iota(jnp.int32, (D, HEAD_DIM), 0)
        == 8 * lax.broadcasted_iota(jnp.int32, (D, HEAD_DIM), 1)
    ).astype(jnp.bfloat16)
    head_gains = jnp.dot(gain_rows.astype(jnp.bfloat16), pick, preferred_element_type=jnp.float32)
    rows_ref[...] = gain_rows
    rows_ref[2:4, :HEAD_DIM] = head_gains[2:4]
    gain_q, gain_k = head_gains[2:3], head_gains[3:4]
    values = x_ref[...].reshape(BLOCK, D).astype(jnp.float32)
    normed[...] = (values * rms_scale(values) * gain_rows[0:1]).astype(jnp.bfloat16)
    cosine, sine = rope_pair(tab)

    def head(pre, gain):
        unit = pre * rms_scale(pre) * gain
        return (unit * cosine + pltpu.roll(unit, HEAD_DIM // 2, 1) * sine).astype(jnp.bfloat16)

    for first, pre_ref, low_ref, gain in ((0, qpre, q_low, gain_q), (1024, kpre, k_low, gain_k)):
        for n in range(pre_ref.shape[1] // 256):
            at = slice(n * 256, n * 256 + 256)
            pre = jnp.dot(normed[...], matrix(first + n * 256, 256), preferred_element_type=jnp.float32)
            pre_ref[:, at] = pre
            low_ref[:, n * 256 : n * 256 + 128] = head(pre[:, :128], gain)
            low_ref[:, n * 256 + 128 : n * 256 + 256] = head(pre[:, 128:], gain)
    v_low[...] = jnp.dot(normed[...], matrix(1536, 512), preferred_element_type=jnp.float32).astype(jnp.bfloat16)
    arriving = exchange_start(
        [
            (lambda j: q_low.at[:, columns(j)], lambda i: q_ref.at[i]),
            (lambda j: k_low.at[:, columns(j // 2)], lambda i: k_ref.at[i]),
            (lambda j: v_low.at[:, columns(j // 2)], lambda i: v_ref.at[i]),
        ],
        me, head_send, head_recv, local, 0,
    )
    stores = [
        pltpu.make_async_copy(a, b, store.at[n])
        for n, (a, b) in enumerate(
            ((normed, normed_out), (qpre, qpre_out), (kpre, kpre_out), (q_ref, q_out), (k_ref, k_out),
             (v_ref, v_out), (o32_ref, o32_out), (x_ref, x_out), (tab, tab_out))
        )
    ]
    for copy in stores[:3] + stores[7:]:
        copy.start()
    for copy in arriving:
        copy.wait()
    gather.forward(far[:1], 2)
    gather.ring(far[1], 2, 1)
    gather.ring(far[2], 2, 1)
    for copy in stores[3:6]:
        copy.start()
    for j in range(8):
        vt[j] = v_ref[j].T

    def one_block(i, _):
        q = q_ref[i]

        def weigh(j, carry):
            total, mixed = carry
            p = jnp.exp2(nt(k_ref[j], q) * (score_scale * log2e))
            total = total + jnp.sum(p, axis=0, keepdims=True)
            mixed = mixed + jnp.dot(vt[j], p.astype(jnp.bfloat16), preferred_element_type=jnp.float32)
            return total, mixed

        carry = (jnp.zeros((1, BLOCK), jnp.float32), jnp.zeros((HEAD_DIM, BLOCK), jnp.float32))
        carry = lax.fori_loop(
            0, (i + 1) // 2, lambda t, carry: weigh(2 * t + 1, weigh(2 * t, carry)), carry
        )
        total, mixed = lax.fori_loop(i // 2 * 2 + (i % 2) * 2, i + 1, weigh, carry)
        out = (mixed / total).T
        o32_ref[i] = out
        o_low[i] = out.astype(jnp.bfloat16)
        lse_ref[i] = jnp.log2(total)
        return 0

    lax.fori_loop(0, 6, one_block, 0)
    gather.forward(far[1:], 2)
    lax.fori_loop(6, 8, one_block, 0)
    leaving = exchange_start(
        [(lambda j: o_low.at[j], lambda i: att.at[:, columns(i)])],
        me, head_send, head_recv, local, 3,
    )
    stores[6].start()
    g_low = g_ref[...].reshape(BLOCK, D)
    g_t = middle_refs[3]
    g_t[...] = g_low.T
    gather.arrive(far, 2)
    for copy in leaving:
        copy.wait()
    middle_layer(
        att, x_ref, g_low, rows_ref, w_far, middle_refs, (output, grad_att_out, gmid_out, post_out, dw_out),
        pair_send, pair_recv, own, c, sib,
    )
    gather.drain()
    for copy in stores:
        copy.wait()
    keep_near.wait()
    for _, away in pairs:
        away.wait_send()


def attend(gains, shards, tokens):
    blocks = (8, BLOCK, HEAD_DIM)
    low, wide = jnp.bfloat16, jnp.float32
    whole = [(2, 4, 4, 2, 2, 8, w) for w in WIDE]
    return pl.pallas_call(
        forward_kernel,
        out_shape=[
            jax.ShapeDtypeStruct(whole[NEAR], low),
            jax.ShapeDtypeStruct((2, 128, D), low),
            jax.ShapeDtypeStruct((2, 128, HEAD_DIM), wide),
        ]
        + [jax.ShapeDtypeStruct(blocks, low)] * 3
        + [
            jax.ShapeDtypeStruct(blocks, wide),
            jax.ShapeDtypeStruct((8, 1, BLOCK), wide),
            jax.ShapeDtypeStruct((BLOCK, D), low),
            jax.ShapeDtypeStruct((BLOCK, 1024), wide),
            jax.ShapeDtypeStruct((BLOCK, 512), wide),
            jax.ShapeDtypeStruct((8, D), wide),
            jax.ShapeDtypeStruct((128, D), low),
            jax.ShapeDtypeStruct((BLOCK, 1024), low),
            jax.ShapeDtypeStruct((128, D), wide),
            jax.ShapeDtypeStruct((8, D), wide),
            jax.ShapeDtypeStruct((D, WIDE[FAR]), low),
        ],
        in_specs=[VMEM] * 15,
        out_specs=[HBM] * 7 + [VMEM] + [HBM] * 3 + [VMEM, VMEM, HBM, VMEM, VMEM, HBM],
        scratch_shapes=[
            pltpu.VMEM((2, 128, D), low),
            pltpu.VMEM((2, 128, D), low),
            pltpu.VMEM((2, 128, HEAD_DIM), wide),
            pltpu.VMEM(whole[NEAR], low),
            pltpu.VMEM(whole[FAR], low),
            pltpu.VMEM((BLOCK, D), low),
            pltpu.VMEM((BLOCK, 1024), wide),
            pltpu.VMEM((BLOCK, 512), wide),
            pltpu.VMEM((BLOCK, 1024), low),
            pltpu.VMEM((BLOCK, 512), low),
            pltpu.VMEM((BLOCK, 512), low),
        ]
        + [pltpu.VMEM(blocks, low)] * 3
        + [
            pltpu.VMEM(blocks, wide),
            pltpu.VMEM(blocks, low),
            pltpu.VMEM((BLOCK, 1024), low),
            pltpu.VMEM((8, HEAD_DIM, BLOCK), low),
            pltpu.VMEM((2, 8, WIDE[0]), low),
            pltpu.VMEM((2, 8, WIDE[1]), low),
            pltpu.VMEM((128, HEAD_DIM), wide),
        ]
        + middle_shapes()
        + [
            pltpu.SemaphoreType.DMA((6 * GATHER_SLOTS,)),
            pltpu.SemaphoreType.DMA((6 * GATHER_SLOTS,)),
            pltpu.SemaphoreType.DMA((4, 8)),
            pltpu.SemaphoreType.DMA((4, 8)),
            pltpu.SemaphoreType.DMA((4,)),
            pltpu.SemaphoreType.DMA((1,)),
            pltpu.SemaphoreType.DMA((9,)),
            pltpu.SemaphoreType.DMA((12,)),
            pltpu.SemaphoreType.DMA((12,)),
            pltpu.SemaphoreType.DMA((3,)),
            pltpu.SemaphoreType.DMA((11,)),
        ],
        compiler_params=pltpu.CompilerParams(
            collective_id=2, has_side_effects=True, vmem_limit_bytes=LIMIT
        ),
        name="attend",
    )(*gains, *shards, *tokens)


def backward_kernel(*refs):
    near, far = near_parts(), far_parts()
    n_scatter = len(scatter_shapes())
    ins, far_grad, do_in, refs = refs[:14], refs[14], refs[15], refs[16:]
    fin, input_grad, held, refs = refs[:2], refs[2], refs[3:17], refs[17:]
    q_ref, k_ref, v_ref, o32_ref, lse_ref, qpre, kpre, normed, tab, rows, x_ref = held[:11]
    w_near, gmid, post = held[11:]
    do_ref, dq_low, dk_low, dv_low, kt, dk_acc, dv_acc = refs[:7]
    gq, kparts, vparts, dqkv, normed_t, pair_out, pair_in, near_grad = refs[7:15]
    places, refs = refs[15 : 15 + n_scatter], refs[15 + n_scatter :]
    send, recv, pair_send, pair_recv, load, far_load, head_send, head_recv, head_local = refs
    yh, z, x, yl, c = place()
    me = x * 2 + yl
    sib = sibling()
    scatter = Scatter((near_grad, far_grad), fin, places, send, recv)
    loads = load_all(list(zip(ins, held)), load)
    for n, part in enumerate(far):
        scatter.load(part, far_load.at[n])
    greet(ring_devices() + sequence_others() + [sib])
    arriving = exchange_start(
        [(lambda j: do_in.at[:, columns(j)], lambda i: do_ref.at[i])],
        me, head_send, head_recv, head_local, 0,
    )
    scatter.begin(far[:1], 0)
    scatter.begin(far[1:], 0)
    for copy in loads[:5]:
        copy.wait()
    for j in range(8):
        kt[j] = k_ref[j].T
    dk_acc[...] = jnp.zeros_like(dk_acc)
    dv_acc[...] = jnp.zeros_like(dv_acc)
    for copy in arriving:
        copy.wait()

    def one_block(i, _):
        q, do, lse = q_ref[i], do_ref[i], lse_ref[i]
        delta = jnp.sum((do.astype(jnp.float32) * o32_ref[i]).T, axis=0, keepdims=True)

        def one_pair(j, dqt):
            p = jnp.exp2(nt(k_ref[j], q) * (score_scale * log2e) - lse)
            dp = nt(v_ref[j], do)
            ds = (p * (dp - delta)).astype(jnp.bfloat16)
            dv_acc[j] += jnp.dot(p.astype(jnp.bfloat16), do, preferred_element_type=jnp.float32)
            dk_acc[j] += jnp.dot(ds, q, preferred_element_type=jnp.float32)
            return dqt + jnp.dot(kt[j], ds, preferred_element_type=jnp.float32)

        dqt = lax.fori_loop(
            0, (i + 1) // 2, lambda t, carry: one_pair(2 * t + 1, one_pair(2 * t, carry)),
            jnp.zeros((HEAD_DIM, BLOCK), jnp.float32),
        )
        dqt = lax.fori_loop(i // 2 * 2 + (i % 2) * 2, i + 1, one_pair, dqt)
        dq_low[i] = (dqt * score_scale).T.astype(jnp.bfloat16)
        return 0

    lax.fori_loop(0, 6, one_block, 0)
    scatter.middle(far[:1], 0)
    scatter.middle(far[1:], 0)
    lax.fori_loop(6, 8, one_block, 0)
    dk_low[...] = (dk_acc[...] * score_scale).astype(jnp.bfloat16)
    dv_low[...] = dv_acc[...].astype(jnp.bfloat16)
    arriving = exchange_start(
        [
            (lambda j: dq_low.at[j], lambda i: gq.at[:, columns(i)]),
            (lambda j: dk_low.at[j], lambda i: kparts.at[i % 2, :, columns(i // 2)]),
            (lambda j: dv_low.at[j], lambda i: vparts.at[i % 2, :, columns(i // 2)]),
        ],
        me, head_send, head_recv, head_local, 1,
    )
    scatter.end(far[:1], 0)
    scatter.begin(far[:1], 1)
    scatter.end(far[1:], 0)
    scatter.begin(far[1:], 1)
    for copy in loads[5:]:
        copy.wait()
    normed_t[...] = normed[...].T
    for copy in arriving:
        copy.wait()
    cosine, sine = rope_pair(tab)
    gain_q, gain_k = rows[2:3, :HEAD_DIM], rows[3:4, :HEAD_DIM]

    def head_back(grad, values, gain):
        grad = grad * cosine - pltpu.roll(grad, HEAD_DIM // 2, 1) * sine
        grad_in, terms = norm_back(grad, values, rms_scale(values), gain)
        return grad_in.astype(jnp.bfloat16), jnp.sum(terms, axis=0, keepdims=True)

    q_part = jnp.zeros((1, HEAD_DIM), jnp.float32)
    k_part = jnp.zeros((1, HEAD_DIM), jnp.float32)
    for h in range(8):
        at = slice(h * HEAD_DIM, (h + 1) * HEAD_DIM)
        dqkv[:, at], part = head_back(gq[:, at].astype(jnp.float32), qpre[:, at], gain_q)
        q_part = q_part + part
    for h in range(4):
        at = slice(h * HEAD_DIM, (h + 1) * HEAD_DIM)
        grad = kparts[0, :, at].astype(jnp.float32) + kparts[1, :, at].astype(jnp.float32)
        low_at = slice(1024 + h * HEAD_DIM, 1024 + (h + 1) * HEAD_DIM)
        dqkv[:, low_at], part = head_back(grad, kpre[:, at], gain_k)
        k_part = k_part + part
    dqkv[:, 1536:] = (vparts[0].astype(jnp.float32) + vparts[1].astype(jnp.float32)).astype(jnp.bfloat16)

    def weight_grads(n, _):
        lhs = normed_t[pl.ds(pl.multiple_of(n * 256, 256), 256), :]
        for first in range(0, 2048, 512):
            block = jnp.dot(lhs, dqkv[:, first : first + 512], preferred_element_type=jnp.float32)
            near_grad[n // 2, pl.ds(n % 2 * 2, 2), :, :, :, first : first + 512] = block.astype(
                jnp.bfloat16
            ).reshape(2, 4, 2, 16, 512)
        return 0

    lax.fori_loop(0, 4, weight_grads, 0)
    scatter.begin(near[:2], 0)

    def grad_normed(rows_at):
        return nt(dqkv[rows_at, :], w_near[:, :2048])

    away = pl.ds(pl.multiple_of((1 - c) * 128, 128), 128)
    own = pl.ds(pl.multiple_of(c * 128, 128), 128)
    pair_out[...] = grad_normed(away).astype(jnp.bfloat16)
    swap = pltpu.make_async_remote_copy(
        pair_out, pair_in, pair_send.at[0], pair_recv.at[0], device_id=sib
    )
    swap.start()
    grad = grad_normed(own)
    values = x_ref[c].astype(jnp.float32)
    swap.wait_recv()
    grad = grad + pair_in[...].astype(jnp.float32)
    grad_in, terms = norm_back(grad, values, rms_scale(values), rows[0:1, :])
    input_grad[...] = (gmid[...] + grad_in).astype(jnp.bfloat16)
    in_part = jnp.sum(terms, axis=0, keepdims=True)
    spread = (
        lax.broadcasted_iota(jnp.int32, (HEAD_DIM, D), 1)
        == 8 * lax.broadcasted_iota(jnp.int32, (HEAD_DIM, D), 0)
    ).astype(jnp.bfloat16)
    qk = jnp.concatenate([q_part, k_part, jnp.zeros((6, HEAD_DIM), jnp.float32)]).astype(jnp.bfloat16)
    qk = jnp.dot(qk, spread, preferred_element_type=jnp.float32)
    gain_rows = jnp.concatenate(
        [in_part, post[0:1, :], qk[0:2], jnp.zeros((TILE - 4, D), jnp.float32)]
    )
    near_grad[:, :, :, :, :, 2048:] = gain_rows.T.astype(jnp.bfloat16).reshape(2, 4, 4, 2, 16, TILE)
    scatter.begin(near[2:], 0)
    scatter.middle(near, 0)
    scatter.middle(far, 1)
    for part in near:
        scatter.end([part], 0)
        scatter.direct([part])
    for part in far:
        scatter.end([part], 1)
        scatter.deliver([part])
    for part in near:
        scatter.landed([part])
        scatter.deliver([part])
    scatter.finish(far)
    scatter.finish(near)
    scatter.drain()
    swap.wait_send()


def attend_back(arrays, far_grad, grad_att):
    blocks = (8, BLOCK, HEAD_DIM)
    low, wide = jnp.bfloat16, jnp.float32
    return pl.pallas_call(
        backward_kernel,
        out_shape=[jax.ShapeDtypeStruct((2, 8, w), wide) for w in WIDE]
        + [jax.ShapeDtypeStruct((128, D), low)],
        in_specs=[HBM] * (len(arrays) + 2),
        out_specs=[VMEM] * 3,
        scratch_shapes=[pltpu.VMEM(a.shape, a.dtype) for a in arrays]
        + [pltpu.VMEM(blocks, low)] * 4
        + [
            pltpu.VMEM((8, HEAD_DIM, BLOCK), low),
            pltpu.VMEM(blocks, wide),
            pltpu.VMEM(blocks, wide),
            pltpu.VMEM((BLOCK, 1024), low),
            pltpu.VMEM((2, BLOCK, 512), low),
            pltpu.VMEM((2, BLOCK, 512), low),
            pltpu.VMEM((BLOCK, 2048), low),
            pltpu.VMEM((D, BLOCK), low),
            pltpu.VMEM((128, D), low),
            pltpu.VMEM((128, D), low),
            pltpu.VMEM((2, 4, 4, 2, 16, WIDE[0]), low),
        ]
        + scatter_shapes()
        + [
            pltpu.SemaphoreType.DMA((6 * GATHER_SLOTS,)),
            pltpu.SemaphoreType.DMA((6 * GATHER_SLOTS,)),
            pltpu.SemaphoreType.DMA((1,)),
            pltpu.SemaphoreType.DMA((1,)),
            pltpu.SemaphoreType.DMA((len(arrays),)),
            pltpu.SemaphoreType.DMA((3, 4)),
            pltpu.SemaphoreType.DMA((4, 8)),
            pltpu.SemaphoreType.DMA((4, 8)),
            pltpu.SemaphoreType.DMA((4,)),
        ],
        compiler_params=pltpu.CompilerParams(
            collective_id=3, has_side_effects=True, vmem_limit_bytes=LIMIT
        ),
        name="attend_back",
    )(*arrays, far_grad, grad_att)


def results_kernel(near, far, grad_in, out_in, *refs):
    (q, k, v, in_gain, post_gain, q_gain, k_gain, w_out, gate, up, down, grad, out) = refs
    for source, group in ((near, ((q, 0), (k, 1024), (v, 1536))), (far, zip((w_out, gate, up, down), [s for s, _ in FAR_SPANS]))):
        for target, first in group:
            width = target.shape[1] // 2
            for half in range(2):
                target[:, half * width : (half + 1) * width] = source[half, :, first : first + width]
    gains = near[0, :, 2048:] + near[1, :, 2048:]
    gains = jnp.concatenate([gains, jnp.zeros((TILE - 8, TILE), jnp.float32)]).T
    in_gain[...] = gains[0:1, :8]
    post_gain[...] = gains[1:2, :8]
    q_gain[...] = gains[2:3, :1]
    k_gain[...] = gains[3:4, :1]
    grad[...] = grad_in[...]
    out[...] = out_in[...]


def results(arrays):
    shapes = [(8, 2048), (8, 1024), (8, 1024), (1, 8), (1, 8), (1, 1), (1, 1)]
    shapes += [(8, 2 * width) for _, width in FAR_SPANS]
    return pl.pallas_call(
        results_kernel,
        out_shape=[jax.ShapeDtypeStruct(s, jnp.float32) for s in shapes]
        + [jax.ShapeDtypeStruct((128, D), jnp.bfloat16)] * 2,
        in_specs=[VMEM] * 4,
        out_specs=[VMEM] * 13,
        name="results",
    )(*arrays)


def body(
    tokens,
    positions,
    in_gain,
    q_gain,
    k_gain,
    w_query,
    w_key,
    w_value,
    w_out,
    post_gain,
    w_gate,
    w_up,
    w_down,
    cotangent,
):
    half = HEAD_DIM // 2
    frequency = rope_base ** (-2.0 * jnp.arange(half, dtype=jnp.float32) / HEAD_DIM)
    angles = positions[0].astype(jnp.float32)[:, None] * frequency[None, :]
    gains = [g[None] for g in (in_gain, post_gain, q_gain, k_gain)]
    shards = [w_query, w_key, w_value, w_out.T, w_gate, w_up, w_down.T]
    (near, x_pair, tables, q_all, k_all, v_all, mixed, log_total, normed, q_pre, k_pre, rows, output,
     grad_att, grad_middle, post_part, far_grad) = attend(
        gains, shards, [tokens[0], cotangent[0], jnp.cos(angles), jnp.sin(angles)]
    )
    near_sum, far_sum, input_grad = attend_back(
        [q_all, k_all, v_all, mixed, log_total, q_pre, k_pre, normed, tables, rows, x_pair,
         near.reshape(D, WIDE[NEAR]), grad_middle, post_part],
        far_grad.reshape(2, 4, 4, 2, 16, WIDE[FAR]),
        grad_att,
    )
    (query, key, value, in_gain_grad, post_gain_grad, q_gain_grad, k_gain_grad, out_grad, gate, up, down,
     input_grad, output) = results([near_sum, far_sum, input_grad, output])
    return (
        output[None],
        input_grad[None],
        in_gain_grad[0],
        q_gain_grad[0],
        k_gain_grad[0],
        query,
        key,
        value,
        out_grad.T,
        post_gain_grad[0],
        gate,
        up,
        down.T,
    )


def solution(mesh):
    placed = (
        P("dp", "seq", None),
        P("dp", "seq"),
        P(("dp", "seq")),
        P(("dp", "seq")),
        P(("dp", "seq")),
        P(("dp", "seq"), None),
        P(("dp", "seq"), None),
        P(("dp", "seq"), None),
        P(None, ("dp", "seq")),
        P(("dp", "seq")),
        P(("dp", "seq"), None),
        P(("dp", "seq"), None),
        P(None, ("dp", "seq")),
        P("dp", "seq", None),
    )
    return jax.shard_map(
        body,
        mesh=mesh,
        in_specs=placed,
        out_specs=(
            P("dp", "seq", None),
            P("dp", "seq", None),
            P(("dp", "seq")),
            P(("dp", "seq")),
            P(("dp", "seq")),
            P(("dp", "seq"), None),
            P(("dp", "seq"), None),
            P(("dp", "seq"), None),
            P(None, ("dp", "seq")),
            P(("dp", "seq")),
            P(("dp", "seq"), None),
            P(("dp", "seq"), None),
            P(None, ("dp", "seq")),
        ),
        check_vma=False,
    )
```

```python
import functools
import math

import jax
import jax.numpy as jnp
from jax import lax
from jax.experimental import pallas as pl
from jax.experimental.pallas import tpu as pltpu
from jax.sharding import PartitionSpec as P

HEADS = 16
KV_HEADS = 8
HEAD_DIM = 128
D = 1024
FF = 3072
BLOCK = 256
CORES = 2

TILE = 128

eps_norm = 1e-06
rope_base = 1000000.0
score_scale = 1.0 / math.sqrt(HEAD_DIM)
log2e = math.log2(math.e)


def place():
    dp = lax.axis_index("dp")
    seq = lax.axis_index("seq")
    return dp // 4, dp % 4, seq // 4, (seq // 2) % 2, seq % 2


def device(yh, z, x, yl, c):
    return {"dp": yh * 4 + z, "seq": x * 4 + yl * 2 + c}


def sibling():
    yh, z, x, yl, c = place()
    return device(yh, z, x, yl, 1 - c)


def neighbour(axis, step):
    yh, z, x, yl, c = place()
    if axis == "x":
        return device(yh, z, (x + step + 4) % 4, yl, c)
    if axis == "z":
        return device(yh, (z + step + 4) % 4, x, yl, c)
    y = (yh * 2 + yl + step + 4) % 4
    return device(y // 2, z, x, y % 2, c)


ORDERS = (("x", "y", "z"), ("y", "z", "x"), ("z", "x", "y"))


def chip_set(whole_axes, axis, step):
    yh, z, x, yl, _ = place()
    iz, ix, iyh, iyl = z, x, yh, yl
    if axis == "x":
        ix = (x + step + 4) % 4
    elif axis == "z":
        iz = (z + step + 4) % 4
    else:
        y = (yh * 2 + yl + step + 4) % 4
        iyh, iyl = y // 2, y % 2
    every = slice(None)
    if "x" in whole_axes:
        ix = every
    if "z" in whole_axes:
        iz = every
    if "y" in whole_axes:
        iyh, iyl = every, every
    return (iyh, iz, ix, iyl)


def set_dims(whole_axes):
    dims = ()
    if "y" in whole_axes:
        dims += (2,)
    if "z" in whole_axes:
        dims += (4,)
    if "x" in whole_axes:
        dims += (4,)
    if "y" in whole_axes:
        dims += (2,)
    return dims


NEAR, FAR = 0, 1
WIDE = (2176, 5632)
LIMIT = 60 << 20


class Part:
    def __init__(self, array, number, order, first, tiles):
        self.array, self.number, self.order = array, number, order
        self.start, self.width = first * TILE, tiles * TILE
        self.cols = pl.ds(self.start, self.width)
        cut = (tiles + 1) // 2 * TILE
        self.halves = ((0, 1, 0, cut), (1, -1, cut, self.width - cut))


def parts_of(array, tiles):
    parts, first = [], 0
    for number, count in enumerate(tiles):
        parts.append(Part(array, number, ORDERS[number], first, count))
        first += count
    return parts


def near_parts():
    return parts_of(NEAR, (6, 6, 5))


def far_parts():
    return parts_of(FAR, (20, 12, 12))


def greet(others):
    barrier = pltpu.get_barrier_semaphore()
    for other in others:
        pl.semaphore_signal(barrier, inc=1, device_id=other)
    pl.semaphore_wait(barrier, len(others))


def ring_device(axis, step, other):
    yh, z, x, yl, c = place()
    core = (c + other) % 2
    if axis == "x":
        return device(yh, z, (x + step + 4) % 4, yl, core)
    if axis == "z":
        return device(yh, (z + step + 4) % 4, x, yl, core)
    y = (yh * 2 + yl + step + 4) % 4
    return device(y // 2, z, x, y % 2, core)


def ring_devices():
    return [ring_device(axis, step, other) for axis in "xyz" for step in (1, 2, 3) for other in (0, 1)]


HBM = pl.BlockSpec(memory_space=pltpu.HBM)
VMEM = pl.BlockSpec(memory_space=pltpu.VMEM)


def load_all(pairs, sems):
    copies = [pltpu.make_async_copy(a, b, sems.at[n]) for n, (a, b) in enumerate(pairs)]
    for copy in copies:
        copy.start()
    return copies


def nt(left, right):
    return lax.dot_general(left, right, (((1,), (1,)), ((), ())), preferred_element_type=jnp.float32)


def rms_scale(values):
    return lax.rsqrt(jnp.mean(values * values, axis=-1, keepdims=True) + eps_norm)


def norm_back(grad_out, values, scale_factor, gain):
    weighted = grad_out * gain
    inner = jnp.mean(weighted * values, axis=-1, keepdims=True)
    grad_in = (
        scale_factor * weighted - values * (scale_factor * scale_factor * scale_factor) * inner
    )
    return (grad_in, grad_out * values * scale_factor)


def rope_pair(tab):
    table = tab[...].reshape(BLOCK, HEAD_DIM)
    turned = pltpu.roll(table, HEAD_DIM // 2, 1)
    low = lax.broadcasted_iota(jnp.int32, (BLOCK, HEAD_DIM), 1) < HEAD_DIM // 2
    return jnp.where(low, table, turned), jnp.where(low, -turned, table)


class Gather:
    def __init__(self, units, outs, base, send, recv, local):
        self.units, self.outs, self.base = units, outs, base
        self.send, self.recv, self.local = send, recv, local
        self.copies = {}

    def remote(self, key, slot, source, target, device_id):
        copy = pltpu.make_async_remote_copy(
            source, target, self.send.at[slot], self.recv.at[slot], device_id=device_id
        )
        copy.start()
        self.copies[key] = copy

    def slot(self, part, n):
        return self.base[part.array] + part.number * GATHER_SLOTS + n

    def spread(self, parts):
        yh, z, x, yl, c = place()
        for part in parts:
            target = self.outs[part.array].at[yh, z, x, yl, c, :, part.cols]
            for step in range(4):
                for other in range(2):
                    source = self.units[part.array].at[(c + other) % 2, :, part.cols]
                    key = (part.array, part.number, 0, step, other)
                    if step == 0 and other == 0:
                        copy = pltpu.make_async_copy(
                            source, target, self.local.at[part.array * 3 + part.number]
                        )
                        copy.start()
                        self.copies[key] = copy
                    else:
                        slot = self.slot(part, step * 2 + other - 1)
                        self.remote(key, slot, source, target, ring_device(part.order[0], step, other))

    def settle(self, part):
        for step in range(4):
            for other in range(2):
                copy = self.copies[part.array, part.number, 0, step, other]
                if step == 0 and other == 0:
                    copy.wait()
                else:
                    copy.wait_recv()

    def block(self, part, phase, offset, first, width):
        index = chip_set(part.order[:phase], part.order[phase], offset)
        cols = pl.ds(part.start + first, width)
        return self.outs[part.array].at[(*index, slice(None), slice(None), cols)]

    def direct(self, part):
        ref = self.block(part, 1, 0, 0, part.width)
        for step in (1, 2, 3):
            key = (part.array, part.number, 1, step)
            self.remote(key, self.slot(part, 6 + step), ref, ref, ring_device(part.order[1], step, 0))

    def landed(self, part):
        for step in (1, 2, 3):
            self.copies[part.array, part.number, 1, step].wait_recv()

    def ring(self, part, phase, which):
        for half, way, first, width in part.halves:
            step, offset = ((way, 0), (-way, 0), (way, -way))[which]
            key = (part.array, part.number, phase, which, half)
            if which == 2:
                self.copies[part.array, part.number, phase, 0, half].wait_recv()
            ref = self.block(part, phase, offset, first, width)
            slot = self.slot(part, 7 + 6 * (phase - 1) + 2 * which + half)
            self.remote(key, slot, ref, ref, ring_device(part.order[phase], step, 0))

    def begin(self, parts, phase):
        for part in parts:
            self.ring(part, phase, 0)
            self.ring(part, phase, 1)

    def forward(self, parts, phase):
        for part in parts:
            self.ring(part, phase, 2)

    def arrive(self, parts, phase):
        for part in parts:
            for which in (1, 2):
                for half in (0, 1):
                    self.copies[part.array, part.number, phase, which, half].wait_recv()

    def drain(self):
        for key, copy in self.copies.items():
            if key[2:] != (0, 0, 0):
                copy.wait_send()


GATHER_SLOTS = 19


def kept_index(kept, axis, step):
    iyh, iz, ix, iyl = chip_set(tuple(a for a in kept if a != axis), axis, step)
    index = ()
    if "y" in kept:
        index += (iyh,)
    if "z" in kept:
        index += (iz,)
    if "x" in kept:
        index += (ix,)
    if "y" in kept:
        index += (iyl,)
    return index


def add_sets(dims, terms, store):
    def one(flat_index, _):
        index, rest = [], flat_index
        for size in reversed(dims):
            index.insert(0, rest % size)
            rest = rest // size
        at = tuple(index)
        total = terms[0][at].astype(jnp.float32)
        for term in terms[1:]:
            total = total + term[at].astype(jnp.float32)
        store(at, total)
        return 0

    lax.fori_loop(0, math.prod(dims), one, 0)


def scatter_shapes():
    low, shapes = jnp.bfloat16, []
    for part in near_parts() + far_parts():
        plane, line = set_dims(part.order[:2]), set_dims(part.order[:1])
        for _, _, _, width in part.halves:
            shapes += [pltpu.VMEM((*plane, 16, width), low)] * 4
            if part.array == FAR:
                shapes += [pltpu.VMEM((*line, 16, width), low)] * 4
        if part.array == NEAR:
            shapes += [pltpu.VMEM((*line, 16, part.width), low)] * 3
        shapes += [pltpu.VMEM((8, 8, part.width), low)]
        shapes += [pltpu.VMEM((*plane, 16, part.width), low)]
        shapes += [pltpu.VMEM((*line, 2, 8, part.width), low)]
    return shapes


class Scatter:
    def __init__(self, grads, fin, refs, send, recv):
        self.grads, self.fin, self.send, self.recv = grads, fin, send, recv
        self.copies, self.loads = {}, {}
        self.land, self.mids, self.plane, self.line = {}, {}, {}, {}
        refs = list(refs)
        for part in near_parts() + far_parts():
            name = (part.array, part.number)
            for half in (0, 1):
                for phase in (0, 1) if part.array == FAR else (0,):
                    self.land[name, phase, half] = [refs.pop(0) for _ in range(3)]
                    self.mids[name, phase, half] = refs.pop(0)
            if part.array == NEAR:
                self.land[name, 1] = [refs.pop(0) for _ in range(3)]
            self.land[name, 2] = refs.pop(0)
            self.plane[name] = refs.pop(0)
            self.line[name] = refs.pop(0)

    def remote(self, key, part, n, source, target, device_id):
        slot = (part.array * 3 + part.number) * GATHER_SLOTS + n
        copy = pltpu.make_async_remote_copy(
            source, target, self.send.at[slot], self.recv.at[slot], device_id=device_id
        )
        copy.start()
        self.copies[key] = copy

    def source(self, part, phase, offset, first, width):
        if phase == 0:
            index = chip_set(part.order[:2], part.order[2], offset)
            cols = pl.ds(part.start + first, width)
            return self.grads[part.array].at[(*index, slice(None), cols)]
        index = kept_index(part.order[:2], part.order[1], offset)
        return self.plane[part.array, part.number].at[(*index, slice(None), pl.ds(first, width))]

    def load(self, part, sems):
        name = (part.array, part.number)
        every = (slice(None),) * (len(set_dims(part.order[:2])) + 1)
        for half, way, first, width in part.halves:
            target = self.plane[name].at[(*every, pl.ds(first, width))]
            for m, (offset, place_to) in enumerate(((way, self.mids[name, 0, half]), (0, target))):
                copy = pltpu.make_async_copy(
                    self.source(part, 0, offset, first, width), place_to, sems.at[2 * half + m]
                )
                copy.start()
                self.loads[name, half, m] = copy

    def ring(self, part, phase, which):
        name = (part.array, part.number)
        for half, way, first, width in part.halves:
            offset, step = ((2, way), (-way, -way))[which]
            self.remote(
                (name, phase, which, half), part, 6 * phase + 2 * which + half,
                self.source(part, phase, offset, first, width), self.land[name, phase, half][which],
                ring_device(part.order[2 - phase], step, 0),
            )

    def begin(self, parts, phase):
        for part in parts:
            self.ring(part, phase, 0)
        for part in parts:
            self.ring(part, phase, 1)

    def middle(self, parts, phase):
        for part in parts:
            name = (part.array, part.number)
            for half, way, first, width in part.halves:
                self.copies[name, phase, 0, half].wait_recv()
                mid = self.mids[name, phase, half]
                own = self.source(part, phase, way, first, width)
                if (name, half, 0) in self.loads and phase == 0:
                    self.loads[name, half, 0].wait()
                    own = mid

                def store(at, total, mid=mid):
                    mid[at] = total.astype(jnp.bfloat16)

                add_sets(set_dims(part.order[: 2 - phase]), [own, self.land[name, phase, half][0]], store)
                self.remote(
                    (name, phase, 2, half), part, 6 * phase + 4 + half, mid,
                    self.land[name, phase, half][2], ring_device(part.order[2 - phase], way, 0),
                )

    def end(self, parts, phase):
        for part in parts:
            name = (part.array, part.number)
            for half, way, first, width in part.halves:
                self.copies[name, phase, 1, half].wait_recv()
                self.copies[name, phase, 2, half].wait_recv()
                base = self.source(part, phase, 0, first, width)
                cols = pl.ds(first, width)
                if phase == 0:
                    plane = self.plane[name]
                    if (name, half, 1) in self.loads:
                        self.loads[name, half, 1].wait()
                        base = plane.at[(*(slice(None),) * (len(plane.shape) - 1), cols)]

                    def store(at, total, plane=plane, cols=cols):
                        plane[(*at, slice(None), cols)] = total.astype(jnp.bfloat16)

                else:
                    line = self.line[name]

                    def store(at, total, line=line, cols=cols):
                        line[(*at, 0, slice(None), cols)] = total[:8].astype(jnp.bfloat16)
                        line[(*at, 1, slice(None), cols)] = total[8:].astype(jnp.bfloat16)

                add_sets(
                    set_dims(part.order[: 2 - phase]), [base, *self.land[name, phase, half][1:]], store
                )

    def direct(self, parts):
        for part in parts:
            name = (part.array, part.number)
            for step in (1, 2, 3):
                self.remote(
                    (name, 1, step), part, 5 + step, self.source(part, 1, step, 0, part.width),
                    self.land[name, 1][step - 1], ring_device(part.order[1], step, 0),
                )

    def landed(self, parts):
        for part in parts:
            name = (part.array, part.number)
            for step in (1, 2, 3):
                self.copies[name, 1, step].wait_recv()
            line = self.line[name]

            def store(at, total, line=line):
                line[(*at, 0)] = total[:8].astype(jnp.bfloat16)
                line[(*at, 1)] = total[8:].astype(jnp.bfloat16)

            add_sets(
                set_dims(part.order[:1]),
                [self.source(part, 1, 0, 0, part.width), *self.land[name, 1]], store,
            )

    def deliver(self, parts):
        c = place()[4]
        for part in parts:
            name, axis = (part.array, part.number), part.order[0]
            for step in range(4):
                for other in range(2):
                    if step or other:
                        source = self.line[name].at[
                            (*kept_index(part.order[:1], axis, step), (c + other) % 2)
                        ]
                        self.remote(
                            (name, 2, step, other), part, 11 + step * 2 + other, source,
                            self.land[name, 2].at[step * 2 + other], ring_device(axis, step, other),
                        )

    def finish(self, parts):
        c = place()[4]
        for part in parts:
            name, axis = (part.array, part.number), part.order[0]
            for other in range(2):
                total = None
                for step in range(4):
                    if step or other:
                        self.copies[name, 2, step, other].wait_recv()
                        term = self.land[name, 2][step * 2 + other]
                    else:
                        term = self.line[name][(*kept_index(part.order[:1], axis, 0), c)]
                    term = term.astype(jnp.float32)
                    total = term if total is None else total + term
                self.fin[part.array][(c + other) % 2, :, part.cols] = total

    def drain(self):
        for copy in self.copies.values():
            copy.wait_send()


def columns(head, heads=1):
    width = heads * HEAD_DIM
    return pl.ds(pl.multiple_of(head * width, width), width)


def y_partner():
    yh, z, x, yl, c = place()
    return device(yh, z, x, 1 - yl, c)


def along_x(n, source, target, send, recv, local):
    x = place()[2]
    copies = [pltpu.make_async_copy(source(x), target(x), local.at[n])]
    for step in (1, 2, 3):
        copies.append(
            pltpu.make_async_remote_copy(
                source((x + step) % 4), target(x), send.at[n, step], recv.at[n, step],
                device_id=ring_device("x", step, 0),
            )
        )
    for copy in copies[1:] + copies[:1]:
        copy.start()
    return copies


FAR_SPANS = ((0, 1024), (1024, 1536), (2560, 1536), (4096, 1536))


def middle_shapes():
    low, wide = jnp.bfloat16, jnp.float32
    return [
        pltpu.VMEM((BLOCK, D), wide),
        pltpu.VMEM((BLOCK, D), wide),
        pltpu.VMEM((BLOCK, D), low),
        pltpu.VMEM((D, BLOCK), low),
        pltpu.VMEM((D, BLOCK), low),
        pltpu.VMEM((BLOCK, 1536), wide),
        pltpu.VMEM((BLOCK, 1536), low),
        pltpu.VMEM((BLOCK, 1536), low),
        pltpu.VMEM((BLOCK, 1536), low),
        pltpu.VMEM((BLOCK, D), wide),
        pltpu.VMEM((128, D), wide),
        pltpu.VMEM((BLOCK, 1024), low),
        pltpu.VMEM((D, WIDE[FAR]), low),
        pltpu.VMEM((4, BLOCK, 256), low),
        pltpu.VMEM((4, BLOCK, 256), low),
        pltpu.VMEM((4, BLOCK, 256), low),
        pltpu.VMEM((4, BLOCK, 256), low),
        pltpu.VMEM((128, D), low),
        pltpu.VMEM((128, D), low),
    ]


def middle_layer(att, x_ref, g_low, rows, w_far, refs, outs, pair_send, pair_recv, sems, c, sib):
    output, grad_att_out, gmid_out, post_out, dw_out = outs
    (branch, middle, hidden, g_t, hidden_t, grad_act, act, gate_grad, up_grad, grad_hidden,
     down_own, grad_att, dw, out1, in1, out2, in2, out3, in3) = refs
    branch_t = hidden_t
    swaps = []

    def swap(source, target):
        n = 3 + len(swaps)
        copy = pltpu.make_async_remote_copy(
            source, target, pair_send.at[n], pair_recv.at[n], device_id=sib
        )
        copy.start()
        swaps.append(copy)
        return copy

    def part(n, width=256):
        return pl.ds(n * width, width)

    def far_rows(n, which):
        first, width = FAR_SPANS[which]
        half = n % 2 * 2
        return w_far[n // 2, half : half + 2, :, :, :, :, first : first + width].reshape(256, width)

    def far_cols(which, n):
        first = FAR_SPANS[which][0] + n * 256
        return w_far[:, :, :, :, :, :, first : first + 256].reshape(D, 256)

    first = []
    for n in range(4):
        block = nt(att[...], far_rows(n, 0))
        branch[:, part(n)] = block
        out1[n] = block.astype(jnp.bfloat16)
        first.append(swap(out1.at[n], in1.at[n]))
    for n in range(6):
        grad_act[:, part(n)] = jnp.dot(g_low, far_cols(3, n), preferred_element_type=jnp.float32)
    for n in range(4):
        first[n].wait_recv()
        middle[:, part(n)] = (
            x_ref[...].reshape(BLOCK, D)[:, n * 256 : n * 256 + 256].astype(jnp.float32)
            + (branch[:, part(n)] + in1[n].astype(jnp.float32))
        )
    gain = rows[1:2, :]
    scale = rms_scale(middle[...])
    hidden[...] = (middle[...] * scale * gain).astype(jnp.bfloat16)
    for n in range(6):
        gate = jnp.dot(hidden[...], far_cols(1, n), preferred_element_type=jnp.float32)
        up = jnp.dot(hidden[...], far_cols(2, n), preferred_element_type=jnp.float32)
        sigma = jax.nn.sigmoid(gate)
        swish = gate * sigma
        grad = grad_act[:, part(n)]
        act[:, part(n)] = (swish * up).astype(jnp.bfloat16)
        gate_grad[:, part(n)] = (grad * up * (sigma * (1.0 + gate * (1.0 - sigma)))).astype(jnp.bfloat16)
        up_grad[:, part(n)] = (grad * swish).astype(jnp.bfloat16)
    second = []
    for n in range(4):
        block = nt(gate_grad[...], far_rows(n, 1)) + nt(up_grad[...], far_rows(n, 2))
        grad_hidden[:, part(n)] = block
        out2[n] = block.astype(jnp.bfloat16)
        second.append(swap(out2.at[n], in2.at[n]))
    away = pl.ds(pl.multiple_of((1 - c) * 128, 128), 128)
    own = pl.ds(pl.multiple_of(c * 128, 128), 128)
    for n in range(4):
        out3[:, part(n)] = nt(act[away, :], far_rows(n, 3)).astype(jnp.bfloat16)
    third = swap(out3, in3)
    for n in range(4):
        down_own[:, part(n)] = nt(act[own, :], far_rows(n, 3))
    hidden_t[...] = hidden[...].T
    stores = []

    def keep(source, target):
        copy = pltpu.make_async_copy(source, target, sems.at[6 + len(stores)])
        copy.start()
        stores.append(copy)

    for lhs, rhs, (first, width) in (
        (hidden_t, gate_grad, FAR_SPANS[1]), (hidden_t, up_grad, FAR_SPANS[2]), (g_t, act, FAR_SPANS[3])
    ):
        for n in range(4):
            dw[part(n), first : first + width] = jnp.dot(
                lhs[part(n), :], rhs[...], preferred_element_type=jnp.float32
            ).astype(jnp.bfloat16)
        keep(dw.at[:, pl.ds(first, width)], dw_out.at[:, pl.ds(first, width)])
    for n in range(4):
        second[n].wait_recv()
        grad_hidden[:, part(n)] = grad_hidden[:, part(n)] + in2[n].astype(jnp.float32)
    grad_in, terms = norm_back(grad_hidden[...], middle[...], scale, gain)
    grad_hidden[...] = terms
    post_out[...] = jnp.broadcast_to(jnp.sum(grad_hidden[own, :], axis=0, keepdims=True), (8, D))
    grad_hidden[...] = g_low.astype(jnp.float32) + grad_in
    gmid_out[...] = grad_hidden[own, :]
    branch_grad = grad_hidden[...].astype(jnp.bfloat16)
    branch_t[...] = branch_grad.T
    for n in range(4):
        grad_att[:, part(n)] = jnp.dot(
            branch_grad, far_cols(0, n), preferred_element_type=jnp.float32
        ).astype(jnp.bfloat16)
    keep(grad_att, grad_att_out)
    for n in range(4):
        dw[part(n), :1024] = jnp.dot(
            branch_t[part(n), :], att[...], preferred_element_type=jnp.float32
        ).astype(jnp.bfloat16)
    keep(dw.at[:, pl.ds(0, 1024)], dw_out.at[:, pl.ds(0, 1024)])
    third.wait_recv()
    output[...] = (
        middle[own, :] + (down_own[...] + in3[...].astype(jnp.float32))
    ).astype(jnp.bfloat16)
    for copy in swaps:
        copy.wait_send()
    for copy in stores:
        copy.wait()


def forward_kernel(*refs):
    gains_in, shards, (x_in, g_in, cos_in, sin_in), refs = refs[:4], refs[4:11], refs[11:15], refs[15:]
    near_out, x_out, tab_out, q_out, k_out, v_out, o32_out, lse_ref, normed_out = refs[:9]
    qpre_out, kpre_out, rows_ref, output, grad_att_out, gmid_out, post_out, dw_out = refs[9:17]
    x_ref, g_ref, tab, w_near, w_far, normed, qpre, kpre, q_low, k_low, v_low = refs[17:28]
    q_ref, k_ref, v_ref, o32_ref, o_low, att, vt, near_unit, far_unit, tab_own = refs[28:38]
    middle_refs, refs = refs[38:57], refs[57:]
    send, recv, head_send, head_recv, local, load, store, pair_send, pair_recv, pair_local, own = refs
    weights = (w_near, w_far)
    yh, z, x, yl, c = place()
    sib = sibling()
    lanes = lax.broadcasted_iota(jnp.int32, (TILE, TILE), 1)
    rows = lax.broadcasted_iota(jnp.int32, (TILE, TILE), 0)
    tile = jnp.zeros((TILE, TILE), jnp.float32)
    for n, gain in enumerate(gains_in):
        value = gain[...].astype(jnp.float32)
        if value.shape[1] == 1:
            tile = jnp.where((rows == n) & (lanes == 0), value, tile)
        else:
            value = jnp.concatenate([value, jnp.zeros((1, TILE - 8), jnp.float32)], axis=1)
            tile = jnp.where(rows == n, value, tile)
    tile = tile.T[:8].astype(jnp.bfloat16)
    for unit, group, first in ((near_unit, shards[:3], 0), (far_unit, shards[3:], 0)):
        for shard in group:
            width = shard.shape[1] // 2
            for half in range(2):
                unit[half, :, first : first + width] = shard[:, half * width : (half + 1) * width]
            first += width
    near_unit[0, :, 2048:] = tile
    near_unit[1, :, 2048:] = tile
    tab_own[...] = jnp.concatenate([cos_in[...], sin_in[...]], axis=1)
    greet(ring_devices() + [sib])
    near, far = near_parts(), far_parts()
    gather = Gather((near_unit, far_unit), weights, (0, 3 * GATHER_SLOTS), send, recv, own)
    gather.spread(near)
    pairs = []
    for k, (source, target) in enumerate(((x_in, x_ref), (tab_own, tab), (g_in, g_ref))):
        keep = pltpu.make_async_copy(source, target.at[c], pair_local.at[k])
        away = pltpu.make_async_remote_copy(
            source, target.at[c], pair_send.at[k], pair_recv.at[k], device_id=sib
        )
        keep.start()
        away.start()
        pairs.append((keep, away))
    gather.spread(far)
    for part in near:
        gather.settle(part)
        gather.direct(part)
    for part in near:
        gather.landed(part)
        gather.begin([part], 2)
    for part in far:
        gather.settle(part)
        gather.begin([part], 1)
    gather.forward(near, 2)
    gather.forward(far, 1)
    gather.arrive(far[:1], 1)
    gather.begin(far[:1], 2)
    gather.arrive(near, 2)
    keep_near = pltpu.make_async_copy(w_near, near_out, load.at[0])
    keep_near.start()
    gather.arrive(far[1:], 1)
    gather.ring(far[1], 2, 0)
    gather.ring(far[2], 2, 0)
    for keep, away in pairs:
        keep.wait()
        away.wait_recv()

    def matrix(first, width):
        return w_near[:, :, :, :, :, :, first : first + width].reshape(D, width)

    gain_rows = matrix(2048, TILE).astype(jnp.float32).T[:8]
    pick = (
        lax.broadcasted_iota(jnp.int32, (D, HEAD_DIM), 0)
        == 8 * lax.broadcasted_iota(jnp.int32, (D, HEAD_DIM), 1)
    ).astype(jnp.bfloat16)
    head_gains = jnp.dot(gain_rows.astype(jnp.bfloat16), pick, preferred_element_type=jnp.float32)
    rows_ref[...] = gain_rows
    rows_ref[2:4, :HEAD_DIM] = head_gains[2:4]
    gain_q, gain_k = head_gains[2:3], head_gains[3:4]
    values = x_ref[...].reshape(BLOCK, D).astype(jnp.float32)
    normed[...] = (values * rms_scale(values) * gain_rows[0:1]).astype(jnp.bfloat16)
    cosine, sine = rope_pair(tab)

    def head(pre, gain):
        unit = pre * rms_scale(pre) * gain
        return (unit * cosine + pltpu.roll(unit, HEAD_DIM // 2, 1) * sine).astype(jnp.bfloat16)

    for first, pre_ref, low_ref, gain in ((0, qpre, q_low, gain_q), (1024, kpre, k_low, gain_k)):
        for n in range(pre_ref.shape[1] // 256):
            at = slice(n * 256, n * 256 + 256)
            pre = jnp.dot(normed[...], matrix(first + n * 256, 256), preferred_element_type=jnp.float32)
            pre_ref[:, at] = pre
            low_ref[:, n * 256 : n * 256 + 128] = head(pre[:, :128], gain)
            low_ref[:, n * 256 + 128 : n * 256 + 256] = head(pre[:, 128:], gain)
    v_low[...] = jnp.dot(normed[...], matrix(1536, 512), preferred_element_type=jnp.float32).astype(jnp.bfloat16)
    pairs_kv = ((k_low, k_ref), (v_low, v_ref))
    ring_kv = [
        along_x(
            n, lambda t, low=low: low.at[:, columns(t)], lambda t, ref=ref: ref.at[2 * t + yl],
            head_send, head_recv, local,
        )
        for n, (low, ref) in enumerate(pairs_kv)
    ]
    relays = []

    def relay(n, step, source, target):
        copy = pltpu.make_async_remote_copy(
            source, target, head_send.at[4 + n, step], head_recv.at[4 + n, step], device_id=y_partner()
        )
        copy.start()
        relays.append(copy)

    for n, (low, ref) in enumerate(pairs_kv):
        relay(n, 0, low.at[:, columns(x)], ref.at[2 * x + yl])
    ring_q = along_x(
        2, lambda t: q_low.at[:, columns(t, 2)], lambda t: q_ref.at[t], head_send, head_recv, local
    )
    stores = [
        pltpu.make_async_copy(a, b, store.at[n])
        for n, (a, b) in enumerate(
            ((normed, normed_out), (qpre, qpre_out), (kpre, kpre_out), (q_ref, q_out), (k_ref, k_out),
             (v_ref, v_out), (o32_ref, o32_out), (x_ref, x_out), (tab, tab_out))
        )
    ]
    for copy in stores[:3] + stores[7:]:
        copy.start()
    for step in (1, 3, 2):
        there = 2 * ((x - step + 4) % 4) + yl
        for n, (_, ref) in enumerate(pairs_kv):
            ring_kv[n][step].wait_recv()
            relay(n, step, ref.at[there], ref.at[there])
    for copies in (*ring_kv, ring_q):
        copies[0].wait()
    for step in (1, 2, 3):
        ring_q[step].wait_recv()
    for copy in relays:
        copy.wait_recv()
    gather.forward(far[:1], 2)
    gather.ring(far[1], 2, 1)
    gather.ring(far[2], 2, 1)
    for copy in stores[3:6]:
        copy.start()
    for j in range(8):
        vt[j] = v_ref[j].T

    def one_block(n, _):
        queries = (q_ref[n, :, :HEAD_DIM], q_ref[n, :, HEAD_DIM:])

        def weigh(j, carry):
            after = []
            for q, (total, mixed) in zip(queries, carry):
                p = jnp.exp2(nt(k_ref[j], q) * (score_scale * log2e))
                total = total + jnp.sum(p, axis=0, keepdims=True)
                mixed = mixed + jnp.dot(
                    vt[j], p.astype(jnp.bfloat16), preferred_element_type=jnp.float32
                )
                after.append((total, mixed))
            return tuple(after)

        start = (jnp.zeros((1, BLOCK), jnp.float32), jnp.zeros((HEAD_DIM, BLOCK), jnp.float32))
        carry = lax.fori_loop(0, 2 * n + yl + 1, weigh, (start, start))
        for h, (total, mixed) in enumerate(carry):
            out = (mixed / total).T
            o32_ref[n, :, h * HEAD_DIM : (h + 1) * HEAD_DIM] = out
            o_low[n, :, h * HEAD_DIM : (h + 1) * HEAD_DIM] = out.astype(jnp.bfloat16)
            lse_ref[n, h] = jnp.log2(total)
        return 0

    lax.fori_loop(0, 3, one_block, 0)
    gather.forward(far[1:], 2)
    lax.fori_loop(3, 4, one_block, 0)
    leaving = along_x(
        3, lambda t: o_low.at[t], lambda t: att.at[:, columns(t, 2)], head_send, head_recv, local
    )
    stores[6].start()
    g_low = g_ref[...].reshape(BLOCK, D)
    g_t = middle_refs[3]
    g_t[...] = g_low.T
    gather.arrive(far, 2)
    for copy in leaving:
        copy.wait()
    middle_layer(
        att, x_ref, g_low, rows_ref, w_far, middle_refs, (output, grad_att_out, gmid_out, post_out, dw_out),
        pair_send, pair_recv, own, c, sib,
    )
    gather.drain()
    for copy in stores:
        copy.wait()
    keep_near.wait()
    for _, away in pairs:
        away.wait_send()
    for copies in (*ring_kv, ring_q):
        for copy in copies[1:]:
            copy.wait_send()
    for copy in relays:
        copy.wait_send()


def attend(gains, shards, tokens):
    blocks, pairs = (8, BLOCK, HEAD_DIM), (4, BLOCK, 2 * HEAD_DIM)
    low, wide = jnp.bfloat16, jnp.float32
    whole = [(2, 4, 4, 2, 2, 8, w) for w in WIDE]
    return pl.pallas_call(
        forward_kernel,
        out_shape=[
            jax.ShapeDtypeStruct(whole[NEAR], low),
            jax.ShapeDtypeStruct((2, 128, D), low),
            jax.ShapeDtypeStruct((2, 128, HEAD_DIM), wide),
        ]
        + [
            jax.ShapeDtypeStruct(pairs, low),
            jax.ShapeDtypeStruct(blocks, low),
            jax.ShapeDtypeStruct(blocks, low),
            jax.ShapeDtypeStruct(pairs, wide),
            jax.ShapeDtypeStruct((4, 2, 1, BLOCK), wide),
            jax.ShapeDtypeStruct((BLOCK, D), low),
            jax.ShapeDtypeStruct((BLOCK, 1024), wide),
            jax.ShapeDtypeStruct((BLOCK, 512), wide),
            jax.ShapeDtypeStruct((8, D), wide),
            jax.ShapeDtypeStruct((128, D), low),
            jax.ShapeDtypeStruct((BLOCK, 1024), low),
            jax.ShapeDtypeStruct((128, D), wide),
            jax.ShapeDtypeStruct((8, D), wide),
            jax.ShapeDtypeStruct((D, WIDE[FAR]), low),
        ],
        in_specs=[VMEM] * 15,
        out_specs=[HBM] * 7 + [VMEM] + [HBM] * 3 + [VMEM, VMEM, HBM, VMEM, VMEM, HBM],
        scratch_shapes=[
            pltpu.VMEM((2, 128, D), low),
            pltpu.VMEM((2, 128, D), low),
            pltpu.VMEM((2, 128, HEAD_DIM), wide),
            pltpu.VMEM(whole[NEAR], low),
            pltpu.VMEM(whole[FAR], low),
            pltpu.VMEM((BLOCK, D), low),
            pltpu.VMEM((BLOCK, 1024), wide),
            pltpu.VMEM((BLOCK, 512), wide),
            pltpu.VMEM((BLOCK, 1024), low),
            pltpu.VMEM((BLOCK, 512), low),
            pltpu.VMEM((BLOCK, 512), low),
        ]
        + [
            pltpu.VMEM(pairs, low),
            pltpu.VMEM(blocks, low),
            pltpu.VMEM(blocks, low),
            pltpu.VMEM(pairs, wide),
            pltpu.VMEM(pairs, low),
            pltpu.VMEM((BLOCK, 1024), low),
            pltpu.VMEM((8, HEAD_DIM, BLOCK), low),
            pltpu.VMEM((2, 8, WIDE[0]), low),
            pltpu.VMEM((2, 8, WIDE[1]), low),
            pltpu.VMEM((128, HEAD_DIM), wide),
        ]
        + middle_shapes()
        + [
            pltpu.SemaphoreType.DMA((6 * GATHER_SLOTS,)),
            pltpu.SemaphoreType.DMA((6 * GATHER_SLOTS,)),
            pltpu.SemaphoreType.DMA((6, 4)),
            pltpu.SemaphoreType.DMA((6, 4)),
            pltpu.SemaphoreType.DMA((4,)),
            pltpu.SemaphoreType.DMA((1,)),
            pltpu.SemaphoreType.DMA((9,)),
            pltpu.SemaphoreType.DMA((12,)),
            pltpu.SemaphoreType.DMA((12,)),
            pltpu.SemaphoreType.DMA((3,)),
            pltpu.SemaphoreType.DMA((11,)),
        ],
        compiler_params=pltpu.CompilerParams(
            collective_id=2, has_side_effects=True, vmem_limit_bytes=LIMIT
        ),
        name="attend",
    )(*gains, *shards, *tokens)


def backward_kernel(*refs):
    near, far = near_parts(), far_parts()
    n_scatter = len(scatter_shapes())
    ins, far_grad, do_in, refs = refs[:14], refs[14], refs[15], refs[16:]
    fin, input_grad, held, refs = refs[:2], refs[2], refs[3:17], refs[17:]
    q_ref, k_ref, v_ref, o32_ref, lse_ref, qpre, kpre, normed, tab, rows, x_ref = held[:11]
    w_near, gmid, post = held[11:]
    do_ref, dq_low, dk_low, dv_low, kt, dk_acc, dv_acc, k_in, v_in, k_sum, v_sum = refs[:11]
    gq, k_part_in, v_part_in, dqkv, normed_t, pair_out, pair_in, near_grad = refs[11:19]
    places, refs = refs[19 : 19 + n_scatter], refs[19 + n_scatter :]
    send, recv, pair_send, pair_recv, load, far_load, head_send, head_recv, head_local = refs
    yh, z, x, yl, c = place()
    sib = sibling()
    scatter = Scatter((near_grad, far_grad), fin, places, send, recv)
    loads = load_all(list(zip(ins, held)), load)
    for n, part in enumerate(far):
        scatter.load(part, far_load.at[n])
    greet(ring_devices() + [sib])
    arriving = along_x(
        0, lambda t: do_in.at[:, columns(t, 2)], lambda t: do_ref.at[t], head_send, head_recv, head_local
    )
    scatter.begin(far[:1], 0)
    scatter.begin(far[1:], 0)
    for copy in loads[:5]:
        copy.wait()
    for j in range(8):
        kt[j] = k_ref[j].T
    dk_acc[...] = jnp.zeros_like(dk_acc)
    dv_acc[...] = jnp.zeros_like(dv_acc)
    for copy in arriving:
        copy.wait()

    def one_block(n, _):
        heads = []
        for h in range(2):
            at = slice(h * HEAD_DIM, (h + 1) * HEAD_DIM)
            q, do = q_ref[n, :, at], do_ref[n, :, at]
            delta = jnp.sum((do.astype(jnp.float32) * o32_ref[n, :, at]).T, axis=0, keepdims=True)
            heads.append((q, do, lse_ref[n, h], delta))

        def one_pair(j, dqts):
            after, dk_term, dv_term = [], 0.0, 0.0
            for (q, do, lse, delta), dqt in zip(heads, dqts):
                p = jnp.exp2(nt(k_ref[j], q) * (score_scale * log2e) - lse)
                ds = (p * (nt(v_ref[j], do) - delta)).astype(jnp.bfloat16)
                dv_term += jnp.dot(p.astype(jnp.bfloat16), do, preferred_element_type=jnp.float32)
                dk_term += jnp.dot(ds, q, preferred_element_type=jnp.float32)
                after.append(dqt + jnp.dot(kt[j], ds, preferred_element_type=jnp.float32))
            dv_acc[j // 2, j % 2] += dv_term
            dk_acc[j // 2, j % 2] += dk_term
            return tuple(after)

        start = jnp.zeros((HEAD_DIM, BLOCK), jnp.float32)
        dqts = lax.fori_loop(0, 2 * n + yl + 1, one_pair, (start, start))
        for h, dqt in enumerate(dqts):
            dq_low[n, :, h * HEAD_DIM : (h + 1) * HEAD_DIM] = (dqt * score_scale).T.astype(jnp.bfloat16)
        return 0

    lax.fori_loop(0, 3, one_block, 0)
    scatter.middle(far[:1], 0)
    scatter.middle(far[1:], 0)
    lax.fori_loop(3, 4, one_block, 0)
    sums = ((dk_acc, dk_low, k_in, k_sum, k_part_in, score_scale), (dv_acc, dv_low, v_in, v_sum, v_part_in, 1.0))
    across = {}
    for n, (acc, low, landing, _, _, scale) in enumerate(sums):
        low[...] = (acc[:, 1 - yl] * scale).astype(jnp.bfloat16)
        for step in (1, 2, 3, 0):
            there = (x + step) % 4
            copy = pltpu.make_async_remote_copy(
                low.at[there], landing.at[there], head_send.at[4 + n, step], head_recv.at[4 + n, step],
                device_id=y_partner(),
            )
            copy.start()
            across[n, step] = copy
    ring_q = along_x(
        1, lambda t: dq_low.at[t], lambda t: gq.at[:, columns(t, 2)], head_send, head_recv, head_local
    )
    ring_kv = []
    for step in (1, 2, 3, 0):
        there = (x + step) % 4
        for n, (acc, _, landing, total, part_in, scale) in enumerate(sums):
            across[n, step].wait_recv()
            total[there] = (
                acc[there, yl] * scale + landing[there].astype(jnp.float32)
            ).astype(jnp.bfloat16)
            target = part_in.at[:, columns(x)]
            if step == 0:
                copy = pltpu.make_async_copy(total.at[there], target, head_local.at[2 + n])
            else:
                copy = pltpu.make_async_remote_copy(
                    total.at[there], target, head_send.at[2 + n, step], head_recv.at[2 + n, step],
                    device_id=ring_device("x", step, 0),
                )
            copy.start()
            ring_kv.append(copy)
    arriving_late = ring_q + ring_kv
    scatter.end(far[:1], 0)
    scatter.begin(far[:1], 1)
    scatter.end(far[1:], 0)
    scatter.begin(far[1:], 1)
    for copy in loads[5:]:
        copy.wait()
    normed_t[...] = normed[...].T
    for copy in arriving_late:
        copy.wait()
    cosine, sine = rope_pair(tab)
    gain_q, gain_k = rows[2:3, :HEAD_DIM], rows[3:4, :HEAD_DIM]

    def head_back(grad, values, gain):
        grad = grad * cosine - pltpu.roll(grad, HEAD_DIM // 2, 1) * sine
        grad_in, terms = norm_back(grad, values, rms_scale(values), gain)
        return grad_in.astype(jnp.bfloat16), jnp.sum(terms, axis=0, keepdims=True)

    q_part = jnp.zeros((1, HEAD_DIM), jnp.float32)
    k_part = jnp.zeros((1, HEAD_DIM), jnp.float32)
    for h in range(8):
        at = slice(h * HEAD_DIM, (h + 1) * HEAD_DIM)
        dqkv[:, at], part = head_back(gq[:, at].astype(jnp.float32), qpre[:, at], gain_q)
        q_part = q_part + part
    for h in range(4):
        at = slice(h * HEAD_DIM, (h + 1) * HEAD_DIM)
        grad = k_part_in[:, at].astype(jnp.float32)
        low_at = slice(1024 + h * HEAD_DIM, 1024 + (h + 1) * HEAD_DIM)
        dqkv[:, low_at], part = head_back(grad, kpre[:, at], gain_k)
        k_part = k_part + part
    dqkv[:, 1536:] = v_part_in[...]

    def weight_grads(n, _):
        lhs = normed_t[pl.ds(pl.multiple_of(n * 256, 256), 256), :]
        for first in range(0, 2048, 512):
            block = jnp.dot(lhs, dqkv[:, first : first + 512], preferred_element_type=jnp.float32)
            near_grad[n // 2, pl.ds(n % 2 * 2, 2), :, :, :, first : first + 512] = block.astype(
                jnp.bfloat16
            ).reshape(2, 4, 2, 16, 512)
        return 0

    lax.fori_loop(0, 4, weight_grads, 0)
    scatter.begin(near[:2], 0)

    def grad_normed(rows_at):
        return nt(dqkv[rows_at, :], w_near[:, :2048])

    away = pl.ds(pl.multiple_of((1 - c) * 128, 128), 128)
    own = pl.ds(pl.multiple_of(c * 128, 128), 128)
    pair_out[...] = grad_normed(away).astype(jnp.bfloat16)
    swap = pltpu.make_async_remote_copy(
        pair_out, pair_in, pair_send.at[0], pair_recv.at[0], device_id=sib
    )
    swap.start()
    grad = grad_normed(own)
    values = x_ref[c].astype(jnp.float32)
    swap.wait_recv()
    grad = grad + pair_in[...].astype(jnp.float32)
    grad_in, terms = norm_back(grad, values, rms_scale(values), rows[0:1, :])
    input_grad[...] = (gmid[...] + grad_in).astype(jnp.bfloat16)
    in_part = jnp.sum(terms, axis=0, keepdims=True)
    spread = (
        lax.broadcasted_iota(jnp.int32, (HEAD_DIM, D), 1)
        == 8 * lax.broadcasted_iota(jnp.int32, (HEAD_DIM, D), 0)
    ).astype(jnp.bfloat16)
    qk = jnp.concatenate([q_part, k_part, jnp.zeros((6, HEAD_DIM), jnp.float32)]).astype(jnp.bfloat16)
    qk = jnp.dot(qk, spread, preferred_element_type=jnp.float32)
    gain_rows = jnp.concatenate(
        [in_part, post[0:1, :], qk[0:2], jnp.zeros((TILE - 4, D), jnp.float32)]
    )
    near_grad[:, :, :, :, :, 2048:] = gain_rows.T.astype(jnp.bfloat16).reshape(2, 4, 4, 2, 16, TILE)
    scatter.begin(near[2:], 0)
    scatter.middle(near, 0)
    scatter.middle(far, 1)
    for part in near:
        scatter.end([part], 0)
        scatter.direct([part])
    for part in far:
        scatter.end([part], 1)
        scatter.deliver([part])
    for part in near:
        scatter.landed([part])
        scatter.deliver([part])
    scatter.finish(far)
    scatter.finish(near)
    scatter.drain()
    swap.wait_send()
    for copy in across.values():
        copy.wait_send()


def attend_back(arrays, far_grad, grad_att):
    blocks, pairs, split = (8, BLOCK, HEAD_DIM), (4, BLOCK, 2 * HEAD_DIM), (4, BLOCK, HEAD_DIM)
    low, wide = jnp.bfloat16, jnp.float32
    return pl.pallas_call(
        backward_kernel,
        out_shape=[jax.ShapeDtypeStruct((2, 8, w), wide) for w in WIDE]
        + [jax.ShapeDtypeStruct((128, D), low)],
        in_specs=[HBM] * (len(arrays) + 2),
        out_specs=[VMEM] * 3,
        scratch_shapes=[pltpu.VMEM(a.shape, a.dtype) for a in arrays]
        + [pltpu.VMEM(pairs, low)] * 2
        + [pltpu.VMEM(split, low)] * 2
        + [
            pltpu.VMEM((8, HEAD_DIM, BLOCK), low),
            pltpu.VMEM((4, 2, BLOCK, HEAD_DIM), wide),
            pltpu.VMEM((4, 2, BLOCK, HEAD_DIM), wide),
        ]
        + [pltpu.VMEM(split, low)] * 4
        + [
            pltpu.VMEM((BLOCK, 1024), low),
            pltpu.VMEM((BLOCK, 512), low),
            pltpu.VMEM((BLOCK, 512), low),
            pltpu.VMEM((BLOCK, 2048), low),
            pltpu.VMEM((D, BLOCK), low),
            pltpu.VMEM((128, D), low),
            pltpu.VMEM((128, D), low),
            pltpu.VMEM((2, 4, 4, 2, 16, WIDE[0]), low),
        ]
        + scatter_shapes()
        + [
            pltpu.SemaphoreType.DMA((6 * GATHER_SLOTS,)),
            pltpu.SemaphoreType.DMA((6 * GATHER_SLOTS,)),
            pltpu.SemaphoreType.DMA((1,)),
            pltpu.SemaphoreType.DMA((1,)),
            pltpu.SemaphoreType.DMA((len(arrays),)),
            pltpu.SemaphoreType.DMA((3, 4)),
            pltpu.SemaphoreType.DMA((6, 4)),
            pltpu.SemaphoreType.DMA((6, 4)),
            pltpu.SemaphoreType.DMA((4,)),
        ],
        compiler_params=pltpu.CompilerParams(
            collective_id=3, has_side_effects=True, vmem_limit_bytes=LIMIT
        ),
        name="attend_back",
    )(*arrays, far_grad, grad_att)


def results_kernel(near, far, grad_in, out_in, *refs):
    (q, k, v, in_gain, post_gain, q_gain, k_gain, w_out, gate, up, down, grad, out) = refs
    for source, group in ((near, ((q, 0), (k, 1024), (v, 1536))), (far, zip((w_out, gate, up, down), [s for s, _ in FAR_SPANS]))):
        for target, first in group:
            width = target.shape[1] // 2
            for half in range(2):
                target[:, half * width : (half + 1) * width] = source[half, :, first : first + width]
    gains = near[0, :, 2048:] + near[1, :, 2048:]
    gains = jnp.concatenate([gains, jnp.zeros((TILE - 8, TILE), jnp.float32)]).T
    in_gain[...] = gains[0:1, :8]
    post_gain[...] = gains[1:2, :8]
    q_gain[...] = gains[2:3, :1]
    k_gain[...] = gains[3:4, :1]
    grad[...] = grad_in[...]
    out[...] = out_in[...]


def results(arrays):
    shapes = [(8, 2048), (8, 1024), (8, 1024), (1, 8), (1, 8), (1, 1), (1, 1)]
    shapes += [(8, 2 * width) for _, width in FAR_SPANS]
    return pl.pallas_call(
        results_kernel,
        out_shape=[jax.ShapeDtypeStruct(s, jnp.float32) for s in shapes]
        + [jax.ShapeDtypeStruct((128, D), jnp.bfloat16)] * 2,
        in_specs=[VMEM] * 4,
        out_specs=[VMEM] * 13,
        name="results",
    )(*arrays)


def body(
    tokens,
    positions,
    in_gain,
    q_gain,
    k_gain,
    w_query,
    w_key,
    w_value,
    w_out,
    post_gain,
    w_gate,
    w_up,
    w_down,
    cotangent,
):
    half = HEAD_DIM // 2
    frequency = rope_base ** (-2.0 * jnp.arange(half, dtype=jnp.float32) / HEAD_DIM)
    angles = positions[0].astype(jnp.float32)[:, None] * frequency[None, :]
    gains = [g[None] for g in (in_gain, post_gain, q_gain, k_gain)]
    shards = [w_query, w_key, w_value, w_out.T, w_gate, w_up, w_down.T]
    (near, x_pair, tables, q_all, k_all, v_all, mixed, log_total, normed, q_pre, k_pre, rows, output,
     grad_att, grad_middle, post_part, far_grad) = attend(
        gains, shards, [tokens[0], cotangent[0], jnp.cos(angles), jnp.sin(angles)]
    )
    near_sum, far_sum, input_grad = attend_back(
        [q_all, k_all, v_all, mixed, log_total, q_pre, k_pre, normed, tables, rows, x_pair,
         near.reshape(D, WIDE[NEAR]), grad_middle, post_part],
        far_grad.reshape(2, 4, 4, 2, 16, WIDE[FAR]),
        grad_att,
    )
    (query, key, value, in_gain_grad, post_gain_grad, q_gain_grad, k_gain_grad, out_grad, gate, up, down,
     input_grad, output) = results([near_sum, far_sum, input_grad, output])
    return (
        output[None],
        input_grad[None],
        in_gain_grad[0],
        q_gain_grad[0],
        k_gain_grad[0],
        query,
        key,
        value,
        out_grad.T,
        post_gain_grad[0],
        gate,
        up,
        down.T,
    )


def solution(mesh):
    placed = (
        P("dp", "seq", None),
        P("dp", "seq"),
        P(("dp", "seq")),
        P(("dp", "seq")),
        P(("dp", "seq")),
        P(("dp", "seq"), None),
        P(("dp", "seq"), None),
        P(("dp", "seq"), None),
        P(None, ("dp", "seq")),
        P(("dp", "seq")),
        P(("dp", "seq"), None),
        P(("dp", "seq"), None),
        P(None, ("dp", "seq")),
        P("dp", "seq", None),
    )
    return jax.shard_map(
        body,
        mesh=mesh,
        in_specs=placed,
        out_specs=(
            P("dp", "seq", None),
            P("dp", "seq", None),
            P(("dp", "seq")),
            P(("dp", "seq")),
            P(("dp", "seq")),
            P(("dp", "seq"), None),
            P(("dp", "seq"), None),
            P(("dp", "seq"), None),
            P(None, ("dp", "seq")),
            P(("dp", "seq")),
            P(("dp", "seq"), None),
            P(("dp", "seq"), None),
            P(None, ("dp", "seq")),
        ),
        check_vma=False,
    )
```

```python
import functools
import math

import jax
import jax.numpy as jnp
from jax import lax
from jax.experimental import pallas as pl
from jax.experimental.pallas import tpu as pltpu
from jax.sharding import PartitionSpec as P

HEADS = 16
KV_HEADS = 8
HEAD_DIM = 128
D = 1024
FF = 3072
BLOCK = 256
CORES = 2

TILE = 128

eps_norm = 1e-06
rope_base = 1000000.0
score_scale = 1.0 / math.sqrt(HEAD_DIM)
log2e = math.log2(math.e)


def place():
    dp = lax.axis_index("dp")
    seq = lax.axis_index("seq")
    return dp // 4, dp % 4, seq // 4, (seq // 2) % 2, seq % 2


def device(yh, z, x, yl, c):
    return {"dp": yh * 4 + z, "seq": x * 4 + yl * 2 + c}


def sibling():
    yh, z, x, yl, c = place()
    return device(yh, z, x, yl, 1 - c)


def neighbour(axis, step):
    yh, z, x, yl, c = place()
    if axis == "x":
        return device(yh, z, (x + step + 4) % 4, yl, c)
    if axis == "z":
        return device(yh, (z + step + 4) % 4, x, yl, c)
    y = (yh * 2 + yl + step + 4) % 4
    return device(y // 2, z, x, y % 2, c)


ORDERS = (("x", "y", "z"), ("y", "z", "x"), ("z", "x", "y"))


def chip_set(whole_axes, axis, step):
    yh, z, x, yl, _ = place()
    iz, ix, iyh, iyl = z, x, yh, yl
    if axis == "x":
        ix = (x + step + 4) % 4
    elif axis == "z":
        iz = (z + step + 4) % 4
    else:
        y = (yh * 2 + yl + step + 4) % 4
        iyh, iyl = y // 2, y % 2
    every = slice(None)
    if "x" in whole_axes:
        ix = every
    if "z" in whole_axes:
        iz = every
    if "y" in whole_axes:
        iyh, iyl = every, every
    return (iyh, iz, ix, iyl)


def set_dims(whole_axes):
    dims = ()
    if "y" in whole_axes:
        dims += (2,)
    if "z" in whole_axes:
        dims += (4,)
    if "x" in whole_axes:
        dims += (4,)
    if "y" in whole_axes:
        dims += (2,)
    return dims


NEAR, FAR = 0, 1
WIDE = (2176, 5632)
LIMIT = 60 << 20


class Part:
    def __init__(self, array, number, order, first, tiles):
        self.array, self.number, self.order = array, number, order
        self.start, self.width = first * TILE, tiles * TILE
        self.cols = pl.ds(self.start, self.width)
        cut = (tiles + 1) // 2 * TILE
        self.halves = ((0, 1, 0, cut), (1, -1, cut, self.width - cut))


def parts_of(array, tiles):
    parts, first = [], 0
    for number, count in enumerate(tiles):
        parts.append(Part(array, number, ORDERS[number], first, count))
        first += count
    return parts


def near_parts():
    return parts_of(NEAR, (6, 6, 5))


def far_parts(tiles=(17, 14, 13)):
    return parts_of(FAR, tiles)


def greet(others):
    barrier = pltpu.get_barrier_semaphore()
    for other in others:
        pl.semaphore_signal(barrier, inc=1, device_id=other)
    pl.semaphore_wait(barrier, len(others))


def ring_device(axis, step, other):
    yh, z, x, yl, c = place()
    core = (c + other) % 2
    if axis == "x":
        return device(yh, z, (x + step + 4) % 4, yl, core)
    if axis == "z":
        return device(yh, (z + step + 4) % 4, x, yl, core)
    y = (yh * 2 + yl + step + 4) % 4
    return device(y // 2, z, x, y % 2, core)


def ring_devices():
    return [ring_device(axis, step, other) for axis in "xyz" for step in (1, 2, 3) for other in (0, 1)]


HBM = pl.BlockSpec(memory_space=pltpu.HBM)
VMEM = pl.BlockSpec(memory_space=pltpu.VMEM)


def load_all(pairs, sems):
    copies = [pltpu.make_async_copy(a, b, sems.at[n]) for n, (a, b) in enumerate(pairs)]
    for copy in copies:
        copy.start()
    return copies


def nt(left, right):
    return lax.dot_general(left, right, (((1,), (1,)), ((), ())), preferred_element_type=jnp.float32)


def rms_scale(values):
    return lax.rsqrt(jnp.mean(values * values, axis=-1, keepdims=True) + eps_norm)


def norm_back(grad_out, values, scale_factor, gain):
    weighted = grad_out * gain
    inner = jnp.mean(weighted * values, axis=-1, keepdims=True)
    grad_in = (
        scale_factor * weighted - values * (scale_factor * scale_factor * scale_factor) * inner
    )
    return (grad_in, grad_out * values * scale_factor)


def rope_pair(tab):
    table = tab[...].reshape(BLOCK, HEAD_DIM)
    turned = pltpu.roll(table, HEAD_DIM // 2, 1)
    low = lax.broadcasted_iota(jnp.int32, (BLOCK, HEAD_DIM), 1) < HEAD_DIM // 2
    return jnp.where(low, table, turned), jnp.where(low, -turned, table)


class Gather:
    def __init__(self, units, outs, base, send, recv, local):
        self.units, self.outs, self.base = units, outs, base
        self.send, self.recv, self.local = send, recv, local
        self.copies = {}

    def remote(self, key, slot, source, target, device_id):
        copy = pltpu.make_async_remote_copy(
            source, target, self.send.at[slot], self.recv.at[slot], device_id=device_id
        )
        copy.start()
        self.copies[key] = copy

    def slot(self, part, n):
        return self.base[part.array] + part.number * GATHER_SLOTS + n

    def spread(self, parts):
        yh, z, x, yl, c = place()
        for part in parts:
            target = self.outs[part.array].at[yh, z, x, yl, c, :, part.cols]
            for step in range(4):
                for other in range(2):
                    source = self.units[part.array].at[(c + other) % 2, :, part.cols]
                    key = (part.array, part.number, 0, step, other)
                    if step == 0 and other == 0:
                        copy = pltpu.make_async_copy(
                            source, target, self.local.at[part.array * 3 + part.number]
                        )
                        copy.start()
                        self.copies[key] = copy
                    else:
                        slot = self.slot(part, step * 2 + other - 1)
                        self.remote(key, slot, source, target, ring_device(part.order[0], step, other))

    def settle(self, part):
        for step in range(4):
            for other in range(2):
                copy = self.copies[part.array, part.number, 0, step, other]
                if step == 0 and other == 0:
                    copy.wait()
                else:
                    copy.wait_recv()

    def block(self, part, phase, offset, first, width):
        index = chip_set(part.order[:phase], part.order[phase], offset)
        cols = pl.ds(part.start + first, width)
        return self.outs[part.array].at[(*index, slice(None), slice(None), cols)]

    def direct(self, part):
        ref = self.block(part, 1, 0, 0, part.width)
        for step in (1, 2, 3):
            key = (part.array, part.number, 1, step)
            self.remote(key, self.slot(part, 6 + step), ref, ref, ring_device(part.order[1], step, 0))

    def landed(self, part):
        for step in (1, 2, 3):
            self.copies[part.array, part.number, 1, step].wait_recv()

    def ring(self, part, phase, which):
        for half, way, first, width in part.halves:
            step, offset = ((way, 0), (-way, 0), (way, -way))[which]
            key = (part.array, part.number, phase, which, half)
            if which == 2:
                self.copies[part.array, part.number, phase, 0, half].wait_recv()
            ref = self.block(part, phase, offset, first, width)
            slot = self.slot(part, 7 + 6 * (phase - 1) + 2 * which + half)
            self.remote(key, slot, ref, ref, ring_device(part.order[phase], step, 0))

    def begin(self, parts, phase):
        for part in parts:
            self.ring(part, phase, 0)
            self.ring(part, phase, 1)

    def forward(self, parts, phase):
        for part in parts:
            self.ring(part, phase, 2)

    def arrive(self, parts, phase):
        for part in parts:
            for which in (1, 2):
                for half in (0, 1):
                    self.copies[part.array, part.number, phase, which, half].wait_recv()

    def drain(self):
        for key, copy in self.copies.items():
            if key[2:] != (0, 0, 0):
                copy.wait_send()


GATHER_SLOTS = 19


def kept_index(kept, axis, step):
    iyh, iz, ix, iyl = chip_set(tuple(a for a in kept if a != axis), axis, step)
    index = ()
    if "y" in kept:
        index += (iyh,)
    if "z" in kept:
        index += (iz,)
    if "x" in kept:
        index += (ix,)
    if "y" in kept:
        index += (iyl,)
    return index


def add_sets(dims, terms, store):
    def one(flat_index, _):
        index, rest = [], flat_index
        for size in reversed(dims):
            index.insert(0, rest % size)
            rest = rest // size
        at = tuple(index)
        total = terms[0][at].astype(jnp.float32)
        for term in terms[1:]:
            total = total + term[at].astype(jnp.float32)
        store(at, total)
        return 0

    lax.fori_loop(0, math.prod(dims), one, 0)


def scatter_shapes():
    low, shapes = jnp.bfloat16, []
    for part in near_parts() + far_parts():
        plane, line = set_dims(part.order[:2]), set_dims(part.order[:1])
        for _, _, _, width in part.halves:
            shapes += [pltpu.VMEM((*plane, 16, width), low)] * 4
            if part.array == FAR:
                shapes += [pltpu.VMEM((*line, 16, width), low)] * 4
        if part.array == NEAR:
            shapes += [pltpu.VMEM((*line, 16, part.width), low)] * 3
        shapes += [pltpu.VMEM((8, 8, part.width), low)]
        shapes += [pltpu.VMEM((*plane, 16, part.width), low)]
        shapes += [pltpu.VMEM((*line, 2, 8, part.width), low)]
    return shapes


class Scatter:
    def __init__(self, grads, fin, refs, send, recv):
        self.grads, self.fin, self.send, self.recv = grads, fin, send, recv
        self.copies, self.loads = {}, {}
        self.land, self.mids, self.plane, self.line = {}, {}, {}, {}
        refs = list(refs)
        for part in near_parts() + far_parts():
            name = (part.array, part.number)
            for half in (0, 1):
                for phase in (0, 1) if part.array == FAR else (0,):
                    self.land[name, phase, half] = [refs.pop(0) for _ in range(3)]
                    self.mids[name, phase, half] = refs.pop(0)
            if part.array == NEAR:
                self.land[name, 1] = [refs.pop(0) for _ in range(3)]
            self.land[name, 2] = refs.pop(0)
            self.plane[name] = refs.pop(0)
            self.line[name] = refs.pop(0)

    def remote(self, key, part, n, source, target, device_id):
        slot = (part.array * 3 + part.number) * GATHER_SLOTS + n
        copy = pltpu.make_async_remote_copy(
            source, target, self.send.at[slot], self.recv.at[slot], device_id=device_id
        )
        copy.start()
        self.copies[key] = copy

    def source(self, part, phase, offset, first, width):
        if phase == 0:
            index = chip_set(part.order[:2], part.order[2], offset)
            cols = pl.ds(part.start + first, width)
            return self.grads[part.array].at[(*index, slice(None), cols)]
        index = kept_index(part.order[:2], part.order[1], offset)
        return self.plane[part.array, part.number].at[(*index, slice(None), pl.ds(first, width))]

    def load(self, part, sems):
        name = (part.array, part.number)
        every = (slice(None),) * (len(set_dims(part.order[:2])) + 1)
        for half, way, first, width in part.halves:
            target = self.plane[name].at[(*every, pl.ds(first, width))]
            for m, (offset, place_to) in enumerate(((way, self.mids[name, 0, half]), (0, target))):
                copy = pltpu.make_async_copy(
                    self.source(part, 0, offset, first, width), place_to, sems.at[2 * half + m]
                )
                copy.start()
                self.loads[name, half, m] = copy

    def ring(self, part, phase, which):
        name = (part.array, part.number)
        for half, way, first, width in part.halves:
            offset, step = ((2, way), (-way, -way))[which]
            self.remote(
                (name, phase, which, half), part, 6 * phase + 2 * which + half,
                self.source(part, phase, offset, first, width), self.land[name, phase, half][which],
                ring_device(part.order[2 - phase], step, 0),
            )

    def begin(self, parts, phase):
        for part in parts:
            self.ring(part, phase, 0)
        for part in parts:
            self.ring(part, phase, 1)

    def middle(self, parts, phase):
        for part in parts:
            name = (part.array, part.number)
            for half, way, first, width in part.halves:
                self.copies[name, phase, 0, half].wait_recv()
                mid = self.mids[name, phase, half]
                own = self.source(part, phase, way, first, width)
                if (name, half, 0) in self.loads and phase == 0:
                    self.loads[name, half, 0].wait()
                    own = mid

                def store(at, total, mid=mid):
                    mid[at] = total.astype(jnp.bfloat16)

                add_sets(set_dims(part.order[: 2 - phase]), [own, self.land[name, phase, half][0]], store)
                self.remote(
                    (name, phase, 2, half), part, 6 * phase + 4 + half, mid,
                    self.land[name, phase, half][2], ring_device(part.order[2 - phase], way, 0),
                )

    def end(self, parts, phase):
        for part in parts:
            name = (part.array, part.number)
            for half, way, first, width in part.halves:
                self.copies[name, phase, 1, half].wait_recv()
                self.copies[name, phase, 2, half].wait_recv()
                base = self.source(part, phase, 0, first, width)
                cols = pl.ds(first, width)
                if phase == 0:
                    plane = self.plane[name]
                    if (name, half, 1) in self.loads:
                        self.loads[name, half, 1].wait()
                        base = plane.at[(*(slice(None),) * (len(plane.shape) - 1), cols)]

                    def store(at, total, plane=plane, cols=cols):
                        plane[(*at, slice(None), cols)] = total.astype(jnp.bfloat16)

                else:
                    line = self.line[name]

                    def store(at, total, line=line, cols=cols):
                        line[(*at, 0, slice(None), cols)] = total[:8].astype(jnp.bfloat16)
                        line[(*at, 1, slice(None), cols)] = total[8:].astype(jnp.bfloat16)

                add_sets(
                    set_dims(part.order[: 2 - phase]), [base, *self.land[name, phase, half][1:]], store
                )

    def direct(self, parts):
        for part in parts:
            name = (part.array, part.number)
            for step in (1, 2, 3):
                self.remote(
                    (name, 1, step), part, 5 + step, self.source(part, 1, step, 0, part.width),
                    self.land[name, 1][step - 1], ring_device(part.order[1], step, 0),
                )

    def landed(self, parts):
        for part in parts:
            name = (part.array, part.number)
            for step in (1, 2, 3):
                self.copies[name, 1, step].wait_recv()
            line = self.line[name]

            def store(at, total, line=line):
                line[(*at, 0)] = total[:8].astype(jnp.bfloat16)
                line[(*at, 1)] = total[8:].astype(jnp.bfloat16)

            add_sets(
                set_dims(part.order[:1]),
                [self.source(part, 1, 0, 0, part.width), *self.land[name, 1]], store,
            )

    def deliver(self, parts):
        c = place()[4]
        for part in parts:
            name, axis = (part.array, part.number), part.order[0]
            for step in range(4):
                for other in range(2):
                    if step or other:
                        source = self.line[name].at[
                            (*kept_index(part.order[:1], axis, step), (c + other) % 2)
                        ]
                        self.remote(
                            (name, 2, step, other), part, 11 + step * 2 + other, source,
                            self.land[name, 2].at[step * 2 + other], ring_device(axis, step, other),
                        )

    def finish(self, parts):
        c = place()[4]
        for part in parts:
            name, axis = (part.array, part.number), part.order[0]
            for other in range(2):
                total = None
                for step in range(4):
                    if step or other:
                        self.copies[name, 2, step, other].wait_recv()
                        term = self.land[name, 2][step * 2 + other]
                    else:
                        term = self.line[name][(*kept_index(part.order[:1], axis, 0), c)]
                    term = term.astype(jnp.float32)
                    total = term if total is None else total + term
                self.fin[part.array][(c + other) % 2, :, part.cols] = total

    def drain(self):
        for copy in self.copies.values():
            copy.wait_send()


def columns(head, heads=1):
    width = heads * HEAD_DIM
    return pl.ds(pl.multiple_of(head * width, width), width)


def y_partner():
    yh, z, x, yl, c = place()
    return device(yh, z, x, 1 - yl, c)


def along_x(n, source, target, send, recv, local):
    x = place()[2]
    copies = [pltpu.make_async_copy(source(x), target(x), local.at[n])]
    for step in (1, 2, 3):
        copies.append(
            pltpu.make_async_remote_copy(
                source((x + step) % 4), target(x), send.at[n, step], recv.at[n, step],
                device_id=ring_device("x", step, 0),
            )
        )
    for copy in copies[1:] + copies[:1]:
        copy.start()
    return copies


FAR_SPANS = ((3072, 1024), (0, 1536), (1536, 1536), (4096, 1536))


def middle_shapes():
    low, wide = jnp.bfloat16, jnp.float32
    return [
        pltpu.VMEM((BLOCK, D), wide),
        pltpu.VMEM((BLOCK, D), wide),
        pltpu.VMEM((BLOCK, D), low),
        pltpu.VMEM((D, BLOCK), low),
        pltpu.VMEM((D, BLOCK), low),
        pltpu.VMEM((BLOCK, 1536), wide),
        pltpu.VMEM((BLOCK, 1536), low),
        pltpu.VMEM((BLOCK, 1536), low),
        pltpu.VMEM((BLOCK, 1536), low),
        pltpu.VMEM((BLOCK, D), wide),
        pltpu.VMEM((128, D), wide),
        pltpu.VMEM((BLOCK, 1024), low),
        pltpu.VMEM((D, WIDE[FAR]), low),
        pltpu.VMEM((4, BLOCK, 256), low),
        pltpu.VMEM((4, BLOCK, 256), low),
        pltpu.VMEM((4, BLOCK, 256), low),
        pltpu.VMEM((4, BLOCK, 256), low),
        pltpu.VMEM((128, D), low),
        pltpu.VMEM((128, D), low),
    ]


def middle_layer(gather, far, att, x_ref, g_low, rows, w_far, refs, outs, pair_send, pair_recv, sems, c, sib):
    output, grad_att_out, gmid_out, post_out, dw_out = outs
    (branch, middle, hidden, g_t, hidden_t, grad_act, act, gate_grad, up_grad, grad_hidden,
     down_own, grad_att, dw, out1, in1, out2, in2, out3, in3) = refs
    branch_t = hidden_t
    swaps = []

    def swap(source, target):
        n = 3 + len(swaps)
        copy = pltpu.make_async_remote_copy(
            source, target, pair_send.at[n], pair_recv.at[n], device_id=sib
        )
        copy.start()
        swaps.append(copy)
        return copy

    def part(n, width=256):
        return pl.ds(n * width, width)

    def far_rows(n, which):
        first, width = FAR_SPANS[which]
        half = n % 2 * 2
        return w_far[n // 2, half : half + 2, :, :, :, :, first : first + width].reshape(256, width)

    def far_cols(which, n):
        first = FAR_SPANS[which][0] + n * 256
        return w_far[:, :, :, :, :, :, first : first + 256].reshape(D, 256)

    first = []
    for n in range(4):
        block = nt(att[...], far_rows(n, 0))
        branch[:, part(n)] = block
        out1[n] = block.astype(jnp.bfloat16)
        first.append(swap(out1.at[n], in1.at[n]))
    gather.arrive(far[2:], 2)
    for n in range(6):
        grad_act[:, part(n)] = jnp.dot(g_low, far_cols(3, n), preferred_element_type=jnp.float32)
    for n in range(4):
        first[n].wait_recv()
        middle[:, part(n)] = (
            x_ref[...].reshape(BLOCK, D)[:, n * 256 : n * 256 + 256].astype(jnp.float32)
            + (branch[:, part(n)] + in1[n].astype(jnp.float32))
        )
    gain = rows[1:2, :]
    scale = rms_scale(middle[...])
    hidden[...] = (middle[...] * scale * gain).astype(jnp.bfloat16)
    gather.arrive(far[:1], 2)
    for n in range(6):
        gate = jnp.dot(hidden[...], far_cols(1, n), preferred_element_type=jnp.float32)
        up = jnp.dot(hidden[...], far_cols(2, n), preferred_element_type=jnp.float32)
        sigma = jax.nn.sigmoid(gate)
        swish = gate * sigma
        grad = grad_act[:, part(n)]
        act[:, part(n)] = (swish * up).astype(jnp.bfloat16)
        gate_grad[:, part(n)] = (grad * up * (sigma * (1.0 + gate * (1.0 - sigma)))).astype(jnp.bfloat16)
        up_grad[:, part(n)] = (grad * swish).astype(jnp.bfloat16)
    second = []
    for n in range(4):
        block = nt(gate_grad[...], far_rows(n, 1)) + nt(up_grad[...], far_rows(n, 2))
        grad_hidden[:, part(n)] = block
        out2[n] = block.astype(jnp.bfloat16)
        second.append(swap(out2.at[n], in2.at[n]))
    away = pl.ds(pl.multiple_of((1 - c) * 128, 128), 128)
    own = pl.ds(pl.multiple_of(c * 128, 128), 128)
    for n in range(4):
        out3[:, part(n)] = nt(act[away, :], far_rows(n, 3)).astype(jnp.bfloat16)
    third = swap(out3, in3)
    for n in range(4):
        down_own[:, part(n)] = nt(act[own, :], far_rows(n, 3))
    hidden_t[...] = hidden[...].T
    stores = []

    def keep(source, target):
        copy = pltpu.make_async_copy(source, target, sems.at[6 + len(stores)])
        copy.start()
        stores.append(copy)

    for lhs, rhs, (first, width) in (
        (hidden_t, gate_grad, FAR_SPANS[1]), (hidden_t, up_grad, FAR_SPANS[2]), (g_t, act, FAR_SPANS[3])
    ):
        for n in range(4):
            dw[part(n), first : first + width] = jnp.dot(
                lhs[part(n), :], rhs[...], preferred_element_type=jnp.float32
            ).astype(jnp.bfloat16)
        keep(dw.at[:, pl.ds(first, width)], dw_out.at[:, pl.ds(first, width)])
    for n in range(4):
        second[n].wait_recv()
        grad_hidden[:, part(n)] = grad_hidden[:, part(n)] + in2[n].astype(jnp.float32)
    grad_in, terms = norm_back(grad_hidden[...], middle[...], scale, gain)
    grad_hidden[...] = terms
    post_out[...] = jnp.broadcast_to(jnp.sum(grad_hidden[own, :], axis=0, keepdims=True), (8, D))
    grad_hidden[...] = g_low.astype(jnp.float32) + grad_in
    gmid_out[...] = grad_hidden[own, :]
    branch_grad = grad_hidden[...].astype(jnp.bfloat16)
    branch_t[...] = branch_grad.T
    for n in range(4):
        grad_att[:, part(n)] = jnp.dot(
            branch_grad, far_cols(0, n), preferred_element_type=jnp.float32
        ).astype(jnp.bfloat16)
    keep(grad_att, grad_att_out)
    for n in range(4):
        dw[part(n), pl.ds(*FAR_SPANS[0])] = jnp.dot(
            branch_t[part(n), :], att[...], preferred_element_type=jnp.float32
        ).astype(jnp.bfloat16)
    keep(dw.at[:, pl.ds(*FAR_SPANS[0])], dw_out.at[:, pl.ds(*FAR_SPANS[0])])
    third.wait_recv()
    output[...] = (
        middle[own, :] + (down_own[...] + in3[...].astype(jnp.float32))
    ).astype(jnp.bfloat16)
    for copy in swaps:
        copy.wait_send()
    for copy in stores:
        copy.wait()


def forward_kernel(*refs):
    gains_in, shards, (x_in, g_in, cos_in, sin_in), refs = refs[:4], refs[4:11], refs[11:15], refs[15:]
    near_out, x_out, tab_out, q_out, k_out, v_out, o32_out, lse_ref, normed_out = refs[:9]
    qpre_out, kpre_out, rows_ref, output, grad_att_out, gmid_out, post_out, dw_out = refs[9:17]
    x_ref, g_ref, tab, w_near, w_far, normed, qpre, kpre, q_low, k_low, v_low = refs[17:28]
    q_ref, k_ref, v_ref, o32_ref, o_low, att, vt, near_unit, far_unit, tab_own = refs[28:38]
    middle_refs, refs = refs[38:57], refs[57:]
    send, recv, head_send, head_recv, local, load, store, pair_send, pair_recv, pair_local, own = refs
    weights = (w_near, w_far)
    yh, z, x, yl, c = place()
    sib = sibling()
    lanes = lax.broadcasted_iota(jnp.int32, (TILE, TILE), 1)
    rows = lax.broadcasted_iota(jnp.int32, (TILE, TILE), 0)
    tile = jnp.zeros((TILE, TILE), jnp.float32)
    for n, gain in enumerate(gains_in):
        value = gain[...].astype(jnp.float32)
        if value.shape[1] == 1:
            tile = jnp.where((rows == n) & (lanes == 0), value, tile)
        else:
            value = jnp.concatenate([value, jnp.zeros((1, TILE - 8), jnp.float32)], axis=1)
            tile = jnp.where(rows == n, value, tile)
    tile = tile.T[:8].astype(jnp.bfloat16)
    places = [(near_unit, 0), (near_unit, 1024), (near_unit, 1536)]
    places += [(far_unit, first) for first, _ in FAR_SPANS]
    for shard, (unit, first) in zip(shards, places):
        width = shard.shape[1] // 2
        for half in range(2):
            unit[half, :, first : first + width] = shard[:, half * width : (half + 1) * width]
    near_unit[0, :, 2048:] = tile
    near_unit[1, :, 2048:] = tile
    tab_own[...] = jnp.concatenate([cos_in[...], sin_in[...]], axis=1)
    greet(ring_devices() + [sib])
    near, far = near_parts(), far_parts((21, 11, 12))
    gather = Gather((near_unit, far_unit), weights, (0, 3 * GATHER_SLOTS), send, recv, own)
    gather.spread(near)
    pairs = []
    for k, (source, target) in enumerate(((x_in, x_ref), (tab_own, tab), (g_in, g_ref))):
        keep = pltpu.make_async_copy(source, target.at[c], pair_local.at[k])
        away = pltpu.make_async_remote_copy(
            source, target.at[c], pair_send.at[k], pair_recv.at[k], device_id=sib
        )
        keep.start()
        away.start()
        pairs.append((keep, away))
    gather.spread(far)
    for part in near:
        gather.settle(part)
        gather.direct(part)
    gather.settle(far[0])
    gather.begin(far[:1], 1)
    for part in near:
        gather.landed(part)
        gather.begin([part], 2)
    for part in far[1:]:
        gather.settle(part)
        gather.begin([part], 1)
    gather.forward(near, 2)
    gather.forward(far, 1)
    gather.arrive(far[:1], 1)
    gather.begin(far[:1], 2)
    gather.arrive(near, 2)
    keep_near = pltpu.make_async_copy(w_near, near_out, load.at[0])
    keep_near.start()
    gather.arrive(far[1:], 1)
    gather.ring(far[1], 2, 0)
    gather.ring(far[2], 2, 0)
    for keep, away in pairs:
        keep.wait()
        away.wait_recv()

    def matrix(first, width):
        return w_near[:, :, :, :, :, :, first : first + width].reshape(D, width)

    gain_rows = matrix(2048, TILE).astype(jnp.float32).T[:8]
    pick = (
        lax.broadcasted_iota(jnp.int32, (D, HEAD_DIM), 0)
        == 8 * lax.broadcasted_iota(jnp.int32, (D, HEAD_DIM), 1)
    ).astype(jnp.bfloat16)
    head_gains = jnp.dot(gain_rows.astype(jnp.bfloat16), pick, preferred_element_type=jnp.float32)
    rows_ref[...] = gain_rows
    rows_ref[2:4, :HEAD_DIM] = head_gains[2:4]
    gain_q, gain_k = head_gains[2:3], head_gains[3:4]
    values = x_ref[...].reshape(BLOCK, D).astype(jnp.float32)
    normed[...] = (values * rms_scale(values) * gain_rows[0:1]).astype(jnp.bfloat16)
    cosine, sine = rope_pair(tab)

    def head(pre, gain):
        unit = pre * rms_scale(pre) * gain
        return (unit * cosine + pltpu.roll(unit, HEAD_DIM // 2, 1) * sine).astype(jnp.bfloat16)

    for first, pre_ref, low_ref, gain in ((0, qpre, q_low, gain_q), (1024, kpre, k_low, gain_k)):
        for n in range(pre_ref.shape[1] // 256):
            at = slice(n * 256, n * 256 + 256)
            pre = jnp.dot(normed[...], matrix(first + n * 256, 256), preferred_element_type=jnp.float32)
            pre_ref[:, at] = pre
            low_ref[:, n * 256 : n * 256 + 128] = head(pre[:, :128], gain)
            low_ref[:, n * 256 + 128 : n * 256 + 256] = head(pre[:, 128:], gain)
    v_low[...] = jnp.dot(normed[...], matrix(1536, 512), preferred_element_type=jnp.float32).astype(jnp.bfloat16)
    pairs_kv = ((k_low, k_ref), (v_low, v_ref))
    ring_kv = [
        along_x(
            n, lambda t, low=low: low.at[:, columns(t)], lambda t, ref=ref: ref.at[2 * t + yl],
            head_send, head_recv, local,
        )
        for n, (low, ref) in enumerate(pairs_kv)
    ]
    relays = []

    def relay(n, step, source, target):
        copy = pltpu.make_async_remote_copy(
            source, target, head_send.at[4 + n, step], head_recv.at[4 + n, step], device_id=y_partner()
        )
        copy.start()
        relays.append(copy)

    for n, (low, ref) in enumerate(pairs_kv):
        relay(n, 0, low.at[:, columns(x)], ref.at[2 * x + yl])
    ring_q = along_x(
        2, lambda t: q_low.at[:, columns(t, 2)], lambda t: q_ref.at[t], head_send, head_recv, local
    )
    stores = [
        pltpu.make_async_copy(a, b, store.at[n])
        for n, (a, b) in enumerate(
            ((normed, normed_out), (qpre, qpre_out), (kpre, kpre_out), (q_ref, q_out), (k_ref, k_out),
             (v_ref, v_out), (o32_ref, o32_out), (x_ref, x_out), (tab, tab_out))
        )
    ]
    for copy in stores[:3] + stores[7:]:
        copy.start()
    for step in (1, 3, 2):
        there = 2 * ((x - step + 4) % 4) + yl
        for n, (_, ref) in enumerate(pairs_kv):
            ring_kv[n][step].wait_recv()
            relay(n, step, ref.at[there], ref.at[there])
    for copies in (*ring_kv, ring_q):
        copies[0].wait()
    for step in (1, 2, 3):
        ring_q[step].wait_recv()
    for copy in relays:
        copy.wait_recv()
    gather.forward(far[:1], 2)
    gather.ring(far[1], 2, 1)
    gather.ring(far[2], 2, 1)
    gather.forward(far[1:], 2)
    for copy in stores[3:6]:
        copy.start()
    for j in range(8):
        vt[j] = v_ref[j].T

    def one_block(n, _):
        queries = (q_ref[n, :, :HEAD_DIM], q_ref[n, :, HEAD_DIM:])

        def weigh(j, carry):
            after = []
            for q, (total, mixed) in zip(queries, carry):
                p = jnp.exp2(nt(k_ref[j], q) * (score_scale * log2e))
                total = total + jnp.sum(p, axis=0, keepdims=True)
                mixed = mixed + jnp.dot(
                    vt[j], p.astype(jnp.bfloat16), preferred_element_type=jnp.float32
                )
                after.append((total, mixed))
            return tuple(after)

        start = (jnp.zeros((1, BLOCK), jnp.float32), jnp.zeros((HEAD_DIM, BLOCK), jnp.float32))
        carry = lax.fori_loop(0, 2 * n + yl + 1, weigh, (start, start))
        for h, (total, mixed) in enumerate(carry):
            out = (mixed / total).T
            o32_ref[n, :, h * HEAD_DIM : (h + 1) * HEAD_DIM] = out
            o_low[n, :, h * HEAD_DIM : (h + 1) * HEAD_DIM] = out.astype(jnp.bfloat16)
            lse_ref[n, h] = jnp.log2(total)
        return 0

    lax.fori_loop(0, 3, one_block, 0)
    lax.fori_loop(3, 4, one_block, 0)
    leaving = along_x(
        3, lambda t: o_low.at[t], lambda t: att.at[:, columns(t, 2)], head_send, head_recv, local
    )
    stores[6].start()
    g_low = g_ref[...].reshape(BLOCK, D)
    g_t = middle_refs[3]
    g_t[...] = g_low.T
    gather.arrive(far[1:2], 2)
    for copy in leaving:
        copy.wait()
    middle_layer(
        gather, far, att, x_ref, g_low, rows_ref, w_far, middle_refs, (output, grad_att_out, gmid_out, post_out, dw_out),
        pair_send, pair_recv, own, c, sib,
    )
    gather.drain()
    for copy in stores:
        copy.wait()
    keep_near.wait()
    for _, away in pairs:
        away.wait_send()
    for copies in (*ring_kv, ring_q):
        for copy in copies[1:]:
            copy.wait_send()
    for copy in relays:
        copy.wait_send()


def attend(gains, shards, tokens):
    blocks, pairs = (8, BLOCK, HEAD_DIM), (4, BLOCK, 2 * HEAD_DIM)
    low, wide = jnp.bfloat16, jnp.float32
    whole = [(2, 4, 4, 2, 2, 8, w) for w in WIDE]
    return pl.pallas_call(
        forward_kernel,
        out_shape=[
            jax.ShapeDtypeStruct(whole[NEAR], low),
            jax.ShapeDtypeStruct((2, 128, D), low),
            jax.ShapeDtypeStruct((2, 128, HEAD_DIM), wide),
        ]
        + [
            jax.ShapeDtypeStruct(pairs, low),
            jax.ShapeDtypeStruct(blocks, low),
            jax.ShapeDtypeStruct(blocks, low),
            jax.ShapeDtypeStruct(pairs, wide),
            jax.ShapeDtypeStruct((4, 2, 1, BLOCK), wide),
            jax.ShapeDtypeStruct((BLOCK, D), low),
            jax.ShapeDtypeStruct((BLOCK, 1024), wide),
            jax.ShapeDtypeStruct((BLOCK, 512), wide),
            jax.ShapeDtypeStruct((8, D), wide),
            jax.ShapeDtypeStruct((128, D), low),
            jax.ShapeDtypeStruct((BLOCK, 1024), low),
            jax.ShapeDtypeStruct((128, D), wide),
            jax.ShapeDtypeStruct((8, D), wide),
            jax.ShapeDtypeStruct((D, WIDE[FAR]), low),
        ],
        in_specs=[VMEM] * 15,
        out_specs=[HBM] * 7 + [VMEM] + [HBM] * 3 + [VMEM, VMEM, HBM, VMEM, VMEM, HBM],
        scratch_shapes=[
            pltpu.VMEM((2, 128, D), low),
            pltpu.VMEM((2, 128, D), low),
            pltpu.VMEM((2, 128, HEAD_DIM), wide),
            pltpu.VMEM(whole[NEAR], low),
            pltpu.VMEM(whole[FAR], low),
            pltpu.VMEM((BLOCK, D), low),
            pltpu.VMEM((BLOCK, 1024), wide),
            pltpu.VMEM((BLOCK, 512), wide),
            pltpu.VMEM((BLOCK, 1024), low),
            pltpu.VMEM((BLOCK, 512), low),
            pltpu.VMEM((BLOCK, 512), low),
        ]
        + [
            pltpu.VMEM(pairs, low),
            pltpu.VMEM(blocks, low),
            pltpu.VMEM(blocks, low),
            pltpu.VMEM(pairs, wide),
            pltpu.VMEM(pairs, low),
            pltpu.VMEM((BLOCK, 1024), low),
            pltpu.VMEM((8, HEAD_DIM, BLOCK), low),
            pltpu.VMEM((2, 8, WIDE[0]), low),
            pltpu.VMEM((2, 8, WIDE[1]), low),
            pltpu.VMEM((128, HEAD_DIM), wide),
        ]
        + middle_shapes()
        + [
            pltpu.SemaphoreType.DMA((6 * GATHER_SLOTS,)),
            pltpu.SemaphoreType.DMA((6 * GATHER_SLOTS,)),
            pltpu.SemaphoreType.DMA((6, 4)),
            pltpu.SemaphoreType.DMA((6, 4)),
            pltpu.SemaphoreType.DMA((4,)),
            pltpu.SemaphoreType.DMA((1,)),
            pltpu.SemaphoreType.DMA((9,)),
            pltpu.SemaphoreType.DMA((12,)),
            pltpu.SemaphoreType.DMA((12,)),
            pltpu.SemaphoreType.DMA((3,)),
            pltpu.SemaphoreType.DMA((11,)),
        ],
        compiler_params=pltpu.CompilerParams(
            collective_id=2, has_side_effects=True, vmem_limit_bytes=LIMIT
        ),
        name="attend",
    )(*gains, *shards, *tokens)


def backward_kernel(*refs):
    near, far = near_parts(), far_parts()
    n_scatter = len(scatter_shapes())
    ins, far_grad, do_in, refs = refs[:14], refs[14], refs[15], refs[16:]
    fin, input_grad, held, refs = refs[:2], refs[2], refs[3:17], refs[17:]
    q_ref, k_ref, v_ref, o32_ref, lse_ref, qpre, kpre, normed, tab, rows, x_ref = held[:11]
    w_near, gmid, post = held[11:]
    do_ref, dq_low, dk_low, dv_low, kt, dk_acc, dv_acc, k_in, v_in, k_sum, v_sum = refs[:11]
    gq, k_part_in, v_part_in, dqkv, normed_t, pair_out, pair_in, near_grad = refs[11:19]
    places, refs = refs[19 : 19 + n_scatter], refs[19 + n_scatter :]
    send, recv, pair_send, pair_recv, load, far_load, head_send, head_recv, head_local = refs
    yh, z, x, yl, c = place()
    sib = sibling()
    scatter = Scatter((near_grad, far_grad), fin, places, send, recv)
    loads = load_all(list(zip(ins, held)), load)
    for n, part in enumerate(far):
        scatter.load(part, far_load.at[n])
    greet(ring_devices() + [sib])
    arriving = along_x(
        0, lambda t: do_in.at[:, columns(t, 2)], lambda t: do_ref.at[t], head_send, head_recv, head_local
    )
    scatter.begin(far[:1], 0)
    scatter.begin(far[1:], 0)
    for copy in loads[:5]:
        copy.wait()
    for j in range(8):
        kt[j] = k_ref[j].T
    dk_acc[...] = jnp.zeros_like(dk_acc)
    dv_acc[...] = jnp.zeros_like(dv_acc)
    for copy in arriving:
        copy.wait()

    def one_block(n, _):
        heads = []
        for h in range(2):
            at = slice(h * HEAD_DIM, (h + 1) * HEAD_DIM)
            q, do = q_ref[n, :, at], do_ref[n, :, at]
            delta = jnp.sum((do.astype(jnp.float32) * o32_ref[n, :, at]).T, axis=0, keepdims=True)
            heads.append((q, do, lse_ref[n, h], delta))

        def one_pair(j, dqts):
            after, dk_term, dv_term = [], 0.0, 0.0
            for (q, do, lse, delta), dqt in zip(heads, dqts):
                p = jnp.exp2(nt(k_ref[j], q) * (score_scale * log2e) - lse)
                ds = (p * (nt(v_ref[j], do) - delta)).astype(jnp.bfloat16)
                dv_term += jnp.dot(p.astype(jnp.bfloat16), do, preferred_element_type=jnp.float32)
                dk_term += jnp.dot(ds, q, preferred_element_type=jnp.float32)
                after.append(dqt + jnp.dot(kt[j], ds, preferred_element_type=jnp.float32))
            dv_acc[j // 2, j % 2] += dv_term
            dk_acc[j // 2, j % 2] += dk_term
            return tuple(after)

        start = jnp.zeros((HEAD_DIM, BLOCK), jnp.float32)
        dqts = lax.fori_loop(0, 2 * n + yl + 1, one_pair, (start, start))
        for h, dqt in enumerate(dqts):
            dq_low[n, :, h * HEAD_DIM : (h + 1) * HEAD_DIM] = (dqt * score_scale).T.astype(jnp.bfloat16)
        return 0

    lax.fori_loop(0, 3, one_block, 0)
    scatter.middle(far[:1], 0)
    scatter.middle(far[1:], 0)
    lax.fori_loop(3, 4, one_block, 0)
    sums = ((dk_acc, dk_low, k_in, k_sum, k_part_in, score_scale), (dv_acc, dv_low, v_in, v_sum, v_part_in, 1.0))
    across = {}
    for n, (acc, low, landing, _, _, scale) in enumerate(sums):
        low[...] = (acc[:, 1 - yl] * scale).astype(jnp.bfloat16)
        for step in (1, 2, 3, 0):
            there = (x + step) % 4
            copy = pltpu.make_async_remote_copy(
                low.at[there], landing.at[there], head_send.at[4 + n, step], head_recv.at[4 + n, step],
                device_id=y_partner(),
            )
            copy.start()
            across[n, step] = copy
    ring_q = along_x(
        1, lambda t: dq_low.at[t], lambda t: gq.at[:, columns(t, 2)], head_send, head_recv, head_local
    )
    ring_kv = []
    for step in (1, 2, 3, 0):
        there = (x + step) % 4
        for n, (acc, _, landing, total, part_in, scale) in enumerate(sums):
            across[n, step].wait_recv()
            total[there] = (
                acc[there, yl] * scale + landing[there].astype(jnp.float32)
            ).astype(jnp.bfloat16)
            target = part_in.at[:, columns(x)]
            if step == 0:
                copy = pltpu.make_async_copy(total.at[there], target, head_local.at[2 + n])
            else:
                copy = pltpu.make_async_remote_copy(
                    total.at[there], target, head_send.at[2 + n, step], head_recv.at[2 + n, step],
                    device_id=ring_device("x", step, 0),
                )
            copy.start()
            ring_kv.append(copy)
    for copy in loads[5:]:
        copy.wait()
    normed_t[...] = normed[...].T
    cosine, sine = rope_pair(tab)
    gain_q, gain_k = rows[2:3, :HEAD_DIM], rows[3:4, :HEAD_DIM]

    def head_back(grad, values, gain):
        grad = grad * cosine - pltpu.roll(grad, HEAD_DIM // 2, 1) * sine
        grad_in, terms = norm_back(grad, values, rms_scale(values), gain)
        return grad_in.astype(jnp.bfloat16), jnp.sum(terms, axis=0, keepdims=True)

    def weight_grads(first):
        def one(n, _):
            lhs = normed_t[pl.ds(pl.multiple_of(n * 256, 256), 256), :]
            for at in (first, first + 512):
                block = jnp.dot(lhs, dqkv[:, at : at + 512], preferred_element_type=jnp.float32)
                near_grad[n // 2, pl.ds(n % 2 * 2, 2), :, :, :, at : at + 512] = block.astype(
                    jnp.bfloat16
                ).reshape(2, 4, 2, 16, 512)
            return 0

        lax.fori_loop(0, 4, one, 0)

    for copy in ring_q:
        copy.wait()
    q_part = jnp.zeros((1, HEAD_DIM), jnp.float32)
    k_part = jnp.zeros((1, HEAD_DIM), jnp.float32)
    for h in range(8):
        at = slice(h * HEAD_DIM, (h + 1) * HEAD_DIM)
        dqkv[:, at], part = head_back(gq[:, at].astype(jnp.float32), qpre[:, at], gain_q)
        q_part = q_part + part
    weight_grads(0)
    scatter.begin(near[:1], 0)
    scatter.end(far[:1], 0)
    scatter.begin(far[:1], 1)
    scatter.end(far[1:], 0)
    scatter.begin(far[1:], 1)
    for copy in ring_kv:
        copy.wait()
    for h in range(4):
        at = slice(h * HEAD_DIM, (h + 1) * HEAD_DIM)
        low_at = slice(1024 + h * HEAD_DIM, 1024 + (h + 1) * HEAD_DIM)
        dqkv[:, low_at], part = head_back(k_part_in[:, at].astype(jnp.float32), kpre[:, at], gain_k)
        k_part = k_part + part
    dqkv[:, 1536:] = v_part_in[...]
    weight_grads(1024)
    scatter.begin(near[1:2], 0)

    def grad_normed(rows_at):
        return nt(dqkv[rows_at, :], w_near[:, :2048])

    away = pl.ds(pl.multiple_of((1 - c) * 128, 128), 128)
    own = pl.ds(pl.multiple_of(c * 128, 128), 128)
    pair_out[...] = grad_normed(away).astype(jnp.bfloat16)
    swap = pltpu.make_async_remote_copy(
        pair_out, pair_in, pair_send.at[0], pair_recv.at[0], device_id=sib
    )
    swap.start()
    grad = grad_normed(own)
    values = x_ref[c].astype(jnp.float32)
    swap.wait_recv()
    grad = grad + pair_in[...].astype(jnp.float32)
    grad_in, terms = norm_back(grad, values, rms_scale(values), rows[0:1, :])
    input_grad[...] = (gmid[...] + grad_in).astype(jnp.bfloat16)
    in_part = jnp.sum(terms, axis=0, keepdims=True)
    spread = (
        lax.broadcasted_iota(jnp.int32, (HEAD_DIM, D), 1)
        == 8 * lax.broadcasted_iota(jnp.int32, (HEAD_DIM, D), 0)
    ).astype(jnp.bfloat16)
    qk = jnp.concatenate([q_part, k_part, jnp.zeros((6, HEAD_DIM), jnp.float32)]).astype(jnp.bfloat16)
    qk = jnp.dot(qk, spread, preferred_element_type=jnp.float32)
    gain_rows = jnp.concatenate(
        [in_part, post[0:1, :], qk[0:2], jnp.zeros((TILE - 4, D), jnp.float32)]
    )
    near_grad[:, :, :, :, :, 2048:] = gain_rows.T.astype(jnp.bfloat16).reshape(2, 4, 4, 2, 16, TILE)
    scatter.begin(near[2:], 0)
    scatter.middle(near, 0)
    scatter.middle(far, 1)
    for part in near:
        scatter.end([part], 0)
        scatter.direct([part])
    for part in far:
        scatter.end([part], 1)
        scatter.deliver([part])
    for part in near:
        scatter.landed([part])
        scatter.deliver([part])
    scatter.finish(far)
    scatter.finish(near)
    scatter.drain()
    swap.wait_send()
    for copy in across.values():
        copy.wait_send()


def attend_back(arrays, far_grad, grad_att):
    blocks, pairs, split = (8, BLOCK, HEAD_DIM), (4, BLOCK, 2 * HEAD_DIM), (4, BLOCK, HEAD_DIM)
    low, wide = jnp.bfloat16, jnp.float32
    return pl.pallas_call(
        backward_kernel,
        out_shape=[jax.ShapeDtypeStruct((2, 8, w), wide) for w in WIDE]
        + [jax.ShapeDtypeStruct((128, D), low)],
        in_specs=[HBM] * (len(arrays) + 2),
        out_specs=[VMEM] * 3,
        scratch_shapes=[pltpu.VMEM(a.shape, a.dtype) for a in arrays]
        + [pltpu.VMEM(pairs, low)] * 2
        + [pltpu.VMEM(split, low)] * 2
        + [
            pltpu.VMEM((8, HEAD_DIM, BLOCK), low),
            pltpu.VMEM((4, 2, BLOCK, HEAD_DIM), wide),
            pltpu.VMEM((4, 2, BLOCK, HEAD_DIM), wide),
        ]
        + [pltpu.VMEM(split, low)] * 4
        + [
            pltpu.VMEM((BLOCK, 1024), low),
            pltpu.VMEM((BLOCK, 512), low),
            pltpu.VMEM((BLOCK, 512), low),
            pltpu.VMEM((BLOCK, 2048), low),
            pltpu.VMEM((D, BLOCK), low),
            pltpu.VMEM((128, D), low),
            pltpu.VMEM((128, D), low),
            pltpu.VMEM((2, 4, 4, 2, 16, WIDE[0]), low),
        ]
        + scatter_shapes()
        + [
            pltpu.SemaphoreType.DMA((6 * GATHER_SLOTS,)),
            pltpu.SemaphoreType.DMA((6 * GATHER_SLOTS,)),
            pltpu.SemaphoreType.DMA((1,)),
            pltpu.SemaphoreType.DMA((1,)),
            pltpu.SemaphoreType.DMA((len(arrays),)),
            pltpu.SemaphoreType.DMA((3, 4)),
            pltpu.SemaphoreType.DMA((6, 4)),
            pltpu.SemaphoreType.DMA((6, 4)),
            pltpu.SemaphoreType.DMA((4,)),
        ],
        compiler_params=pltpu.CompilerParams(
            collective_id=3, has_side_effects=True, vmem_limit_bytes=LIMIT
        ),
        name="attend_back",
    )(*arrays, far_grad, grad_att)


def results_kernel(near, far, grad_in, out_in, *refs):
    (q, k, v, in_gain, post_gain, q_gain, k_gain, w_out, gate, up, down, grad, out) = refs
    for source, group in ((near, ((q, 0), (k, 1024), (v, 1536))), (far, zip((w_out, gate, up, down), [s for s, _ in FAR_SPANS]))):
        for target, first in group:
            width = target.shape[1] // 2
            for half in range(2):
                target[:, half * width : (half + 1) * width] = source[half, :, first : first + width]
    gains = near[0, :, 2048:] + near[1, :, 2048:]
    gains = jnp.concatenate([gains, jnp.zeros((TILE - 8, TILE), jnp.float32)]).T
    in_gain[...] = gains[0:1, :8]
    post_gain[...] = gains[1:2, :8]
    q_gain[...] = gains[2:3, :1]
    k_gain[...] = gains[3:4, :1]
    grad[...] = grad_in[...]
    out[...] = out_in[...]


def results(arrays):
    shapes = [(8, 2048), (8, 1024), (8, 1024), (1, 8), (1, 8), (1, 1), (1, 1)]
    shapes += [(8, 2 * width) for _, width in FAR_SPANS]
    return pl.pallas_call(
        results_kernel,
        out_shape=[jax.ShapeDtypeStruct(s, jnp.float32) for s in shapes]
        + [jax.ShapeDtypeStruct((128, D), jnp.bfloat16)] * 2,
        in_specs=[VMEM] * 4,
        out_specs=[VMEM] * 13,
        name="results",
    )(*arrays)


def body(
    tokens,
    positions,
    in_gain,
    q_gain,
    k_gain,
    w_query,
    w_key,
    w_value,
    w_out,
    post_gain,
    w_gate,
    w_up,
    w_down,
    cotangent,
):
    half = HEAD_DIM // 2
    frequency = rope_base ** (-2.0 * jnp.arange(half, dtype=jnp.float32) / HEAD_DIM)
    angles = positions[0].astype(jnp.float32)[:, None] * frequency[None, :]
    gains = [g[None] for g in (in_gain, post_gain, q_gain, k_gain)]
    shards = [w_query, w_key, w_value, w_out.T, w_gate, w_up, w_down.T]
    (near, x_pair, tables, q_all, k_all, v_all, mixed, log_total, normed, q_pre, k_pre, rows, output,
     grad_att, grad_middle, post_part, far_grad) = attend(
        gains, shards, [tokens[0], cotangent[0], jnp.cos(angles), jnp.sin(angles)]
    )
    near_sum, far_sum, input_grad = attend_back(
        [q_all, k_all, v_all, mixed, log_total, q_pre, k_pre, normed, tables, rows, x_pair,
         near.reshape(D, WIDE[NEAR]), grad_middle, post_part],
        far_grad.reshape(2, 4, 4, 2, 16, WIDE[FAR]),
        grad_att,
    )
    (query, key, value, in_gain_grad, post_gain_grad, q_gain_grad, k_gain_grad, out_grad, gate, up, down,
     input_grad, output) = results([near_sum, far_sum, input_grad, output])
    return (
        output[None],
        input_grad[None],
        in_gain_grad[0],
        q_gain_grad[0],
        k_gain_grad[0],
        query,
        key,
        value,
        out_grad.T,
        post_gain_grad[0],
        gate,
        up,
        down.T,
    )


def solution(mesh):
    placed = (
        P("dp", "seq", None),
        P("dp", "seq"),
        P(("dp", "seq")),
        P(("dp", "seq")),
        P(("dp", "seq")),
        P(("dp", "seq"), None),
        P(("dp", "seq"), None),
        P(("dp", "seq"), None),
        P(None, ("dp", "seq")),
        P(("dp", "seq")),
        P(("dp", "seq"), None),
        P(("dp", "seq"), None),
        P(None, ("dp", "seq")),
        P("dp", "seq", None),
    )
    return jax.shard_map(
        body,
        mesh=mesh,
        in_specs=placed,
        out_specs=(
            P("dp", "seq", None),
            P("dp", "seq", None),
            P(("dp", "seq")),
            P(("dp", "seq")),
            P(("dp", "seq")),
            P(("dp", "seq"), None),
            P(("dp", "seq"), None),
            P(("dp", "seq"), None),
            P(None, ("dp", "seq")),
            P(("dp", "seq")),
            P(("dp", "seq"), None),
            P(("dp", "seq"), None),
            P(None, ("dp", "seq")),
        ),
        check_vma=False,
    )
```

```python
import functools
import math

import jax
import jax.numpy as jnp
from jax import lax
from jax.experimental import pallas as pl
from jax.experimental.pallas import tpu as pltpu
from jax.sharding import PartitionSpec as P

HEADS = 16
KV_HEADS = 8
HEAD_DIM = 128
D = 1024
FF = 3072
BLOCK = 256
CORES = 2

TILE = 128

eps_norm = 1e-06
rope_base = 1000000.0
score_scale = 1.0 / math.sqrt(HEAD_DIM)
log2e = math.log2(math.e)


def place():
    dp = lax.axis_index("dp")
    seq = lax.axis_index("seq")
    return dp // 4, dp % 4, seq // 4, (seq // 2) % 2, seq % 2


def device(yh, z, x, yl, c):
    return {"dp": yh * 4 + z, "seq": x * 4 + yl * 2 + c}


def sibling():
    yh, z, x, yl, c = place()
    return device(yh, z, x, yl, 1 - c)


def neighbour(axis, step):
    yh, z, x, yl, c = place()
    if axis == "x":
        return device(yh, z, (x + step + 4) % 4, yl, c)
    if axis == "z":
        return device(yh, (z + step + 4) % 4, x, yl, c)
    y = (yh * 2 + yl + step + 4) % 4
    return device(y // 2, z, x, y % 2, c)


ORDERS = (("x", "y", "z"), ("y", "z", "x"), ("z", "x", "y"))


def chip_set(whole_axes, axis, step):
    yh, z, x, yl, _ = place()
    iz, ix, iyh, iyl = z, x, yh, yl
    if axis == "x":
        ix = (x + step + 4) % 4
    elif axis == "z":
        iz = (z + step + 4) % 4
    else:
        y = (yh * 2 + yl + step + 4) % 4
        iyh, iyl = y // 2, y % 2
    every = slice(None)
    if "x" in whole_axes:
        ix = every
    if "z" in whole_axes:
        iz = every
    if "y" in whole_axes:
        iyh, iyl = every, every
    return (iyh, iz, ix, iyl)


def set_dims(whole_axes):
    dims = ()
    if "y" in whole_axes:
        dims += (2,)
    if "z" in whole_axes:
        dims += (4,)
    if "x" in whole_axes:
        dims += (4,)
    if "y" in whole_axes:
        dims += (2,)
    return dims


NEAR, FAR = 0, 1
WIDE = (2176, 5632)
LIMIT = 60 << 20


class Part:
    def __init__(self, array, number, order, first, tiles):
        self.array, self.number, self.order = array, number, order
        self.start, self.width = first * TILE, tiles * TILE
        self.cols = pl.ds(self.start, self.width)
        cut = (tiles + 1) // 2 * TILE
        self.halves = ((0, 1, 0, cut), (1, -1, cut, self.width - cut))


def parts_of(array, tiles):
    parts, first = [], 0
    for number, count in enumerate(tiles):
        parts.append(Part(array, number, ORDERS[number], first, count))
        first += count
    return parts


def near_parts():
    return parts_of(NEAR, (6, 6, 5))


def far_parts(tiles=(17, 14, 13)):
    return parts_of(FAR, tiles)


def greet(others):
    barrier = pltpu.get_barrier_semaphore()
    for other in others:
        pl.semaphore_signal(barrier, inc=1, device_id=other)
    pl.semaphore_wait(barrier, len(others))


def ring_device(axis, step, other):
    yh, z, x, yl, c = place()
    core = (c + other) % 2
    if axis == "x":
        return device(yh, z, (x + step + 4) % 4, yl, core)
    if axis == "z":
        return device(yh, (z + step + 4) % 4, x, yl, core)
    y = (yh * 2 + yl + step + 4) % 4
    return device(y // 2, z, x, y % 2, core)


def ring_devices():
    return [ring_device(axis, step, other) for axis in "xyz" for step in (1, 2, 3) for other in (0, 1)]


HBM = pl.BlockSpec(memory_space=pltpu.HBM)
VMEM = pl.BlockSpec(memory_space=pltpu.VMEM)


def load_all(pairs, sems):
    copies = [pltpu.make_async_copy(a, b, sems.at[n]) for n, (a, b) in enumerate(pairs)]
    for copy in copies:
        copy.start()
    return copies


def nt(left, right):
    return lax.dot_general(left, right, (((1,), (1,)), ((), ())), preferred_element_type=jnp.float32)


def rms_scale(values):
    return lax.rsqrt(jnp.mean(values * values, axis=-1, keepdims=True) + eps_norm)


def norm_back(grad_out, values, scale_factor, gain):
    weighted = grad_out * gain
    inner = jnp.mean(weighted * values, axis=-1, keepdims=True)
    grad_in = (
        scale_factor * weighted - values * (scale_factor * scale_factor * scale_factor) * inner
    )
    return (grad_in, grad_out * values * scale_factor)


def rope_pair(tab):
    table = tab[...].reshape(BLOCK, HEAD_DIM)
    turned = pltpu.roll(table, HEAD_DIM // 2, 1)
    low = lax.broadcasted_iota(jnp.int32, (BLOCK, HEAD_DIM), 1) < HEAD_DIM // 2
    return jnp.where(low, table, turned), jnp.where(low, -turned, table)


class Gather:
    def __init__(self, units, outs, base, send, recv, local):
        self.units, self.outs, self.base = units, outs, base
        self.send, self.recv, self.local = send, recv, local
        self.copies = {}

    def remote(self, key, slot, source, target, device_id):
        copy = pltpu.make_async_remote_copy(
            source, target, self.send.at[slot], self.recv.at[slot], device_id=device_id
        )
        copy.start()
        self.copies[key] = copy

    def slot(self, part, n):
        return self.base[part.array] + part.number * GATHER_SLOTS + n

    def spread(self, parts):
        yh, z, x, yl, c = place()
        for part in parts:
            target = self.outs[part.array].at[yh, z, x, yl, c, :, part.cols]
            for step in range(4):
                for other in range(2):
                    source = self.units[part.array].at[(c + other) % 2, :, part.cols]
                    key = (part.array, part.number, 0, step, other)
                    if step == 0 and other == 0:
                        copy = pltpu.make_async_copy(
                            source, target, self.local.at[part.array * 3 + part.number]
                        )
                        copy.start()
                        self.copies[key] = copy
                    else:
                        slot = self.slot(part, step * 2 + other - 1)
                        self.remote(key, slot, source, target, ring_device(part.order[0], step, other))

    def settle(self, part):
        for step in range(4):
            for other in range(2):
                copy = self.copies[part.array, part.number, 0, step, other]
                if step == 0 and other == 0:
                    copy.wait()
                else:
                    copy.wait_recv()

    def block(self, part, phase, offset, first, width):
        index = chip_set(part.order[:phase], part.order[phase], offset)
        cols = pl.ds(part.start + first, width)
        return self.outs[part.array].at[(*index, slice(None), slice(None), cols)]

    def direct(self, part):
        ref = self.block(part, 1, 0, 0, part.width)
        for step in (1, 2, 3):
            key = (part.array, part.number, 1, step)
            self.remote(key, self.slot(part, 6 + step), ref, ref, ring_device(part.order[1], step, 0))

    def landed(self, part):
        for step in (1, 2, 3):
            self.copies[part.array, part.number, 1, step].wait_recv()

    def ring(self, part, phase, which):
        for half, way, first, width in part.halves:
            step, offset = ((way, 0), (-way, 0), (way, -way))[which]
            key = (part.array, part.number, phase, which, half)
            if which == 2:
                self.copies[part.array, part.number, phase, 0, half].wait_recv()
            ref = self.block(part, phase, offset, first, width)
            slot = self.slot(part, 7 + 6 * (phase - 1) + 2 * which + half)
            self.remote(key, slot, ref, ref, ring_device(part.order[phase], step, 0))

    def begin(self, parts, phase):
        for part in parts:
            self.ring(part, phase, 0)
            self.ring(part, phase, 1)

    def forward(self, parts, phase):
        for part in parts:
            self.ring(part, phase, 2)

    def arrive(self, parts, phase):
        for part in parts:
            for which in (1, 2):
                for half in (0, 1):
                    self.copies[part.array, part.number, phase, which, half].wait_recv()

    def drain(self):
        for key, copy in self.copies.items():
            if key[2:] != (0, 0, 0):
                copy.wait_send()


GATHER_SLOTS = 19


def kept_index(kept, axis, step):
    iyh, iz, ix, iyl = chip_set(tuple(a for a in kept if a != axis), axis, step)
    index = ()
    if "y" in kept:
        index += (iyh,)
    if "z" in kept:
        index += (iz,)
    if "x" in kept:
        index += (ix,)
    if "y" in kept:
        index += (iyl,)
    return index


def add_sets(dims, terms, store):
    def one(flat_index, _):
        index, rest = [], flat_index
        for size in reversed(dims):
            index.insert(0, rest % size)
            rest = rest // size
        at = tuple(index)
        total = terms[0][at].astype(jnp.float32)
        for term in terms[1:]:
            total = total + term[at].astype(jnp.float32)
        store(at, total)
        return 0

    lax.fori_loop(0, math.prod(dims), one, 0)


def scatter_shapes():
    low, shapes = jnp.bfloat16, []
    for part in near_parts() + far_parts():
        plane, line = set_dims(part.order[:2]), set_dims(part.order[:1])
        for _, _, _, width in part.halves:
            shapes += [pltpu.VMEM((*plane, 16, width), low)] * 4
            if part.array == FAR:
                shapes += [pltpu.VMEM((*line, 16, width), low)] * 4
        if part.array == NEAR:
            shapes += [pltpu.VMEM((*line, 16, part.width), low)] * 3
        shapes += [pltpu.VMEM((8, 8, part.width), low)]
        shapes += [pltpu.VMEM((*plane, 16, part.width), low)]
        shapes += [pltpu.VMEM((*line, 2, 8, part.width), low)]
    return shapes


class Scatter:
    def __init__(self, grads, fin, refs, send, recv):
        self.grads, self.fin, self.send, self.recv = grads, fin, send, recv
        self.copies, self.loads = {}, {}
        self.land, self.mids, self.plane, self.line = {}, {}, {}, {}
        refs = list(refs)
        for part in near_parts() + far_parts():
            name = (part.array, part.number)
            for half in (0, 1):
                for phase in (0, 1) if part.array == FAR else (0,):
                    self.land[name, phase, half] = [refs.pop(0) for _ in range(3)]
                    self.mids[name, phase, half] = refs.pop(0)
            if part.array == NEAR:
                self.land[name, 1] = [refs.pop(0) for _ in range(3)]
            self.land[name, 2] = refs.pop(0)
            self.plane[name] = refs.pop(0)
            self.line[name] = refs.pop(0)

    def remote(self, key, part, n, source, target, device_id):
        slot = (part.array * 3 + part.number) * GATHER_SLOTS + n
        copy = pltpu.make_async_remote_copy(
            source, target, self.send.at[slot], self.recv.at[slot], device_id=device_id
        )
        copy.start()
        self.copies[key] = copy

    def source(self, part, phase, offset, first, width):
        if phase == 0:
            index = chip_set(part.order[:2], part.order[2], offset)
            cols = pl.ds(part.start + first, width)
            return self.grads[part.array].at[(*index, slice(None), cols)]
        index = kept_index(part.order[:2], part.order[1], offset)
        return self.plane[part.array, part.number].at[(*index, slice(None), pl.ds(first, width))]

    def load(self, part, sems):
        name = (part.array, part.number)
        every = (slice(None),) * (len(set_dims(part.order[:2])) + 1)
        for half, way, first, width in part.halves:
            target = self.plane[name].at[(*every, pl.ds(first, width))]
            for m, (offset, place_to) in enumerate(((way, self.mids[name, 0, half]), (0, target))):
                copy = pltpu.make_async_copy(
                    self.source(part, 0, offset, first, width), place_to, sems.at[2 * half + m]
                )
                copy.start()
                self.loads[name, half, m] = copy

    def ring(self, part, phase, which, halves=(0, 1)):
        name = (part.array, part.number)
        for half, way, first, width in part.halves:
            if half not in halves:
                continue
            offset, step = ((2, way), (-way, -way))[which]
            self.remote(
                (name, phase, which, half), part, 6 * phase + 2 * which + half,
                self.source(part, phase, offset, first, width), self.land[name, phase, half][which],
                ring_device(part.order[2 - phase], step, 0),
            )

    def begin(self, parts, phase, halves=(0, 1)):
        for part in parts:
            self.ring(part, phase, 0, halves)
        for part in parts:
            self.ring(part, phase, 1, halves)

    def middle(self, parts, phase):
        for part in parts:
            name = (part.array, part.number)
            for half, way, first, width in part.halves:
                self.copies[name, phase, 0, half].wait_recv()
                mid = self.mids[name, phase, half]
                own = self.source(part, phase, way, first, width)
                if (name, half, 0) in self.loads and phase == 0:
                    self.loads[name, half, 0].wait()
                    own = mid

                def store(at, total, mid=mid):
                    mid[at] = total.astype(jnp.bfloat16)

                add_sets(set_dims(part.order[: 2 - phase]), [own, self.land[name, phase, half][0]], store)
                self.remote(
                    (name, phase, 2, half), part, 6 * phase + 4 + half, mid,
                    self.land[name, phase, half][2], ring_device(part.order[2 - phase], way, 0),
                )

    def end(self, parts, phase):
        for part in parts:
            name = (part.array, part.number)
            for half, way, first, width in part.halves:
                self.copies[name, phase, 1, half].wait_recv()
                self.copies[name, phase, 2, half].wait_recv()
                base = self.source(part, phase, 0, first, width)
                cols = pl.ds(first, width)
                if phase == 0:
                    plane = self.plane[name]
                    if (name, half, 1) in self.loads:
                        self.loads[name, half, 1].wait()
                        base = plane.at[(*(slice(None),) * (len(plane.shape) - 1), cols)]

                    def store(at, total, plane=plane, cols=cols):
                        plane[(*at, slice(None), cols)] = total.astype(jnp.bfloat16)

                else:
                    line = self.line[name]

                    def store(at, total, line=line, cols=cols):
                        line[(*at, 0, slice(None), cols)] = total[:8].astype(jnp.bfloat16)
                        line[(*at, 1, slice(None), cols)] = total[8:].astype(jnp.bfloat16)

                add_sets(
                    set_dims(part.order[: 2 - phase]), [base, *self.land[name, phase, half][1:]], store
                )

    def direct(self, parts):
        for part in parts:
            name = (part.array, part.number)
            for step in (1, 2, 3):
                self.remote(
                    (name, 1, step), part, 5 + step, self.source(part, 1, step, 0, part.width),
                    self.land[name, 1][step - 1], ring_device(part.order[1], step, 0),
                )

    def landed(self, parts):
        for part in parts:
            name = (part.array, part.number)
            for step in (1, 2, 3):
                self.copies[name, 1, step].wait_recv()
            line = self.line[name]

            def store(at, total, line=line):
                line[(*at, 0)] = total[:8].astype(jnp.bfloat16)
                line[(*at, 1)] = total[8:].astype(jnp.bfloat16)

            add_sets(
                set_dims(part.order[:1]),
                [self.source(part, 1, 0, 0, part.width), *self.land[name, 1]], store,
            )

    def deliver(self, parts):
        c = place()[4]
        for part in parts:
            name, axis = (part.array, part.number), part.order[0]
            for step in range(4):
                for other in range(2):
                    if step or other:
                        source = self.line[name].at[
                            (*kept_index(part.order[:1], axis, step), (c + other) % 2)
                        ]
                        self.remote(
                            (name, 2, step, other), part, 11 + step * 2 + other, source,
                            self.land[name, 2].at[step * 2 + other], ring_device(axis, step, other),
                        )

    def finish(self, parts):
        c = place()[4]
        for part in parts:
            name, axis = (part.array, part.number), part.order[0]
            for other in range(2):
                total = None
                for step in range(4):
                    if step or other:
                        self.copies[name, 2, step, other].wait_recv()
                        term = self.land[name, 2][step * 2 + other]
                    else:
                        term = self.line[name][(*kept_index(part.order[:1], axis, 0), c)]
                    term = term.astype(jnp.float32)
                    total = term if total is None else total + term
                self.fin[part.array][(c + other) % 2, :, part.cols] = total

    def drain(self):
        for copy in self.copies.values():
            copy.wait_send()


def columns(head, heads=1):
    width = heads * HEAD_DIM
    return pl.ds(pl.multiple_of(head * width, width), width)


def y_partner():
    yh, z, x, yl, c = place()
    return device(yh, z, x, 1 - yl, c)


def along_x(n, source, target, send, recv, local):
    copies = moves_along_x(n, source, target, send, recv, local)
    for copy in copies[1:] + copies[:1]:
        copy.start()
    return copies


def moves_along_x(n, source, target, send, recv, local):
    x = place()[2]
    copies = [pltpu.make_async_copy(source(x), target(x), local.at[n])]
    for step in (1, 2, 3):
        copies.append(
            pltpu.make_async_remote_copy(
                source((x + step) % 4), target(x), send.at[n, step], recv.at[n, step],
                device_id=ring_device("x", step, 0),
            )
        )
    return copies


FAR_SPANS = ((3072, 1024), (0, 1536), (1536, 1536), (4096, 1536))


def middle_shapes():
    low, wide = jnp.bfloat16, jnp.float32
    return [
        pltpu.VMEM((BLOCK, D), wide),
        pltpu.VMEM((BLOCK, D), wide),
        pltpu.VMEM((BLOCK, D), low),
        pltpu.VMEM((D, BLOCK), low),
        pltpu.VMEM((D, BLOCK), low),
        pltpu.VMEM((BLOCK, 1536), wide),
        pltpu.VMEM((BLOCK, 1536), low),
        pltpu.VMEM((BLOCK, 1536), low),
        pltpu.VMEM((BLOCK, 1536), low),
        pltpu.VMEM((BLOCK, D), wide),
        pltpu.VMEM((128, D), wide),
        pltpu.VMEM((BLOCK, 1024), low),
        pltpu.VMEM((D, WIDE[FAR]), low),
        pltpu.VMEM((4, BLOCK, 256), low),
        pltpu.VMEM((4, BLOCK, 256), low),
        pltpu.VMEM((4, BLOCK, 256), low),
        pltpu.VMEM((4, BLOCK, 256), low),
        pltpu.VMEM((128, D), low),
        pltpu.VMEM((128, D), low),
    ]


def middle_layer(gather, far, att, x_ref, g_low, rows, w_far, refs, outs, pair_send, pair_recv, sems, c, sib):
    output, grad_att_out, gmid_out, post_out, dw_out = outs
    (branch, middle, hidden, g_t, hidden_t, grad_act, act, gate_grad, up_grad, grad_hidden,
     down_own, grad_att, dw, out1, in1, out2, in2, out3, in3) = refs
    branch_t = hidden_t
    swaps = []

    def swap(source, target):
        n = 3 + len(swaps)
        copy = pltpu.make_async_remote_copy(
            source, target, pair_send.at[n], pair_recv.at[n], device_id=sib
        )
        copy.start()
        swaps.append(copy)
        return copy

    def part(n, width=256):
        return pl.ds(n * width, width)

    def far_rows(n, which):
        first, width = FAR_SPANS[which]
        half = n % 2 * 2
        return w_far[n // 2, half : half + 2, :, :, :, :, first : first + width].reshape(256, width)

    def far_cols(which, n):
        first = FAR_SPANS[which][0] + n * 256
        return w_far[:, :, :, :, :, :, first : first + 256].reshape(D, 256)

    first = []
    for n in range(4):
        block = nt(att[...], far_rows(n, 0))
        branch[:, part(n)] = block
        out1[n] = block.astype(jnp.bfloat16)
        first.append(swap(out1.at[n], in1.at[n]))
    gather.arrive(far[2:], 2)
    for n in range(6):
        grad_act[:, part(n)] = jnp.dot(g_low, far_cols(3, n), preferred_element_type=jnp.float32)
    for n in range(4):
        first[n].wait_recv()
        middle[:, part(n)] = (
            x_ref[...].reshape(BLOCK, D)[:, n * 256 : n * 256 + 256].astype(jnp.float32)
            + (branch[:, part(n)] + in1[n].astype(jnp.float32))
        )
    gain = rows[1:2, :]
    scale = rms_scale(middle[...])
    hidden[...] = (middle[...] * scale * gain).astype(jnp.bfloat16)
    gather.arrive(far[:1], 2)
    for n in range(6):
        gate = jnp.dot(hidden[...], far_cols(1, n), preferred_element_type=jnp.float32)
        up = jnp.dot(hidden[...], far_cols(2, n), preferred_element_type=jnp.float32)
        sigma = jax.nn.sigmoid(gate)
        swish = gate * sigma
        grad = grad_act[:, part(n)]
        act[:, part(n)] = (swish * up).astype(jnp.bfloat16)
        gate_grad[:, part(n)] = (grad * up * (sigma * (1.0 + gate * (1.0 - sigma)))).astype(jnp.bfloat16)
        up_grad[:, part(n)] = (grad * swish).astype(jnp.bfloat16)
    second = []
    for n in range(4):
        block = nt(gate_grad[...], far_rows(n, 1)) + nt(up_grad[...], far_rows(n, 2))
        grad_hidden[:, part(n)] = block
        out2[n] = block.astype(jnp.bfloat16)
        second.append(swap(out2.at[n], in2.at[n]))
    away = pl.ds(pl.multiple_of((1 - c) * 128, 128), 128)
    own = pl.ds(pl.multiple_of(c * 128, 128), 128)
    for n in range(4):
        out3[:, part(n)] = nt(act[away, :], far_rows(n, 3)).astype(jnp.bfloat16)
    third = swap(out3, in3)
    for n in range(4):
        down_own[:, part(n)] = nt(act[own, :], far_rows(n, 3))
    hidden_t[...] = hidden[...].T
    stores = []

    def keep(source, target):
        copy = pltpu.make_async_copy(source, target, sems.at[6 + len(stores)])
        copy.start()
        stores.append(copy)

    for lhs, rhs, (first, width) in (
        (hidden_t, gate_grad, FAR_SPANS[1]), (hidden_t, up_grad, FAR_SPANS[2]), (g_t, act, FAR_SPANS[3])
    ):
        for n in range(4):
            dw[part(n), first : first + width] = jnp.dot(
                lhs[part(n), :], rhs[...], preferred_element_type=jnp.float32
            ).astype(jnp.bfloat16)
        keep(dw.at[:, pl.ds(first, width)], dw_out.at[:, pl.ds(first, width)])
    for n in range(4):
        second[n].wait_recv()
        grad_hidden[:, part(n)] = grad_hidden[:, part(n)] + in2[n].astype(jnp.float32)
    grad_in, terms = norm_back(grad_hidden[...], middle[...], scale, gain)
    grad_hidden[...] = terms
    post_out[...] = jnp.broadcast_to(jnp.sum(grad_hidden[own, :], axis=0, keepdims=True), (8, D))
    grad_hidden[...] = g_low.astype(jnp.float32) + grad_in
    gmid_out[...] = grad_hidden[own, :]
    branch_grad = grad_hidden[...].astype(jnp.bfloat16)
    branch_t[...] = branch_grad.T
    for n in range(4):
        grad_att[:, part(n)] = jnp.dot(
            branch_grad, far_cols(0, n), preferred_element_type=jnp.float32
        ).astype(jnp.bfloat16)
    keep(grad_att, grad_att_out)
    for n in range(4):
        dw[part(n), pl.ds(*FAR_SPANS[0])] = jnp.dot(
            branch_t[part(n), :], att[...], preferred_element_type=jnp.float32
        ).astype(jnp.bfloat16)
    keep(dw.at[:, pl.ds(*FAR_SPANS[0])], dw_out.at[:, pl.ds(*FAR_SPANS[0])])
    third.wait_recv()
    output[...] = (
        middle[own, :] + (down_own[...] + in3[...].astype(jnp.float32))
    ).astype(jnp.bfloat16)
    for copy in swaps:
        copy.wait_send()
    for copy in stores:
        copy.wait()


def forward_kernel(*refs):
    gains_in, shards, (x_in, g_in, cos_in, sin_in), refs = refs[:4], refs[4:11], refs[11:15], refs[15:]
    near_out, x_out, tab_out, q_out, k_out, v_out, o32_out, lse_ref, normed_out = refs[:9]
    qpre_out, kpre_out, rows_ref, output, grad_att_out, gmid_out, post_out, dw_out = refs[9:17]
    x_ref, g_ref, tab, w_near, w_far, normed, qpre, kpre, q_low, k_low, v_low = refs[17:28]
    q_ref, k_ref, v_ref, o32_ref, o_low, att, vt, near_unit, far_unit, tab_own = refs[28:38]
    middle_refs, refs = refs[38:57], refs[57:]
    send, recv, head_send, head_recv, local, load, store, pair_send, pair_recv, pair_local, own = refs
    weights = (w_near, w_far)
    yh, z, x, yl, c = place()
    sib = sibling()
    lanes = lax.broadcasted_iota(jnp.int32, (TILE, TILE), 1)
    rows = lax.broadcasted_iota(jnp.int32, (TILE, TILE), 0)
    tile = jnp.zeros((TILE, TILE), jnp.float32)
    for n, gain in enumerate(gains_in):
        value = gain[...].astype(jnp.float32)
        if value.shape[1] == 1:
            tile = jnp.where((rows == n) & (lanes == 0), value, tile)
        else:
            value = jnp.concatenate([value, jnp.zeros((1, TILE - 8), jnp.float32)], axis=1)
            tile = jnp.where(rows == n, value, tile)
    tile = tile.T[:8].astype(jnp.bfloat16)
    places = [(near_unit, 0), (near_unit, 1024), (near_unit, 1536)]
    places += [(far_unit, first) for first, _ in FAR_SPANS]
    for shard, (unit, first) in zip(shards, places):
        width = shard.shape[1] // 2
        for half in range(2):
            unit[half, :, first : first + width] = shard[:, half * width : (half + 1) * width]
    near_unit[0, :, 2048:] = tile
    near_unit[1, :, 2048:] = tile
    tab_own[...] = jnp.concatenate([cos_in[...], sin_in[...]], axis=1)
    greet(ring_devices() + [sib])
    near, far = near_parts(), far_parts((21, 11, 12))
    gather = Gather((near_unit, far_unit), weights, (0, 3 * GATHER_SLOTS), send, recv, own)
    gather.spread(near)
    pairs = []
    for k, (source, target) in enumerate(((x_in, x_ref), (tab_own, tab), (g_in, g_ref))):
        keep = pltpu.make_async_copy(source, target.at[c], pair_local.at[k])
        away = pltpu.make_async_remote_copy(
            source, target.at[c], pair_send.at[k], pair_recv.at[k], device_id=sib
        )
        keep.start()
        away.start()
        pairs.append((keep, away))
    gather.spread(far)
    for part in near:
        gather.settle(part)
        gather.direct(part)
    gather.settle(far[0])
    gather.begin(far[:1], 1)
    for part in near:
        gather.landed(part)
        gather.begin([part], 2)
    for part in far[1:]:
        gather.settle(part)
        gather.begin([part], 1)
    gather.forward(near, 2)
    gather.forward(far, 1)
    gather.arrive(far[:1], 1)
    gather.begin(far[:1], 2)
    gather.arrive(near, 2)
    keep_near = pltpu.make_async_copy(w_near, near_out, load.at[0])
    keep_near.start()
    gather.arrive(far[1:], 1)
    gather.ring(far[1], 2, 0)
    gather.ring(far[2], 2, 0)
    for keep, away in pairs:
        keep.wait()
        away.wait_recv()

    def matrix(first, width):
        return w_near[:, :, :, :, :, :, first : first + width].reshape(D, width)

    gain_rows = matrix(2048, TILE).astype(jnp.float32).T[:8]
    pick = (
        lax.broadcasted_iota(jnp.int32, (D, HEAD_DIM), 0)
        == 8 * lax.broadcasted_iota(jnp.int32, (D, HEAD_DIM), 1)
    ).astype(jnp.bfloat16)
    head_gains = jnp.dot(gain_rows.astype(jnp.bfloat16), pick, preferred_element_type=jnp.float32)
    rows_ref[...] = gain_rows
    rows_ref[2:4, :HEAD_DIM] = head_gains[2:4]
    gain_q, gain_k = head_gains[2:3], head_gains[3:4]
    values = x_ref[...].reshape(BLOCK, D).astype(jnp.float32)
    normed[...] = (values * rms_scale(values) * gain_rows[0:1]).astype(jnp.bfloat16)
    cosine, sine = rope_pair(tab)

    def head(pre, gain):
        unit = pre * rms_scale(pre) * gain
        return (unit * cosine + pltpu.roll(unit, HEAD_DIM // 2, 1) * sine).astype(jnp.bfloat16)

    for first, pre_ref, low_ref, gain in ((0, qpre, q_low, gain_q), (1024, kpre, k_low, gain_k)):
        for n in range(pre_ref.shape[1] // 256):
            at = slice(n * 256, n * 256 + 256)
            pre = jnp.dot(normed[...], matrix(first + n * 256, 256), preferred_element_type=jnp.float32)
            pre_ref[:, at] = pre
            low_ref[:, n * 256 : n * 256 + 128] = head(pre[:, :128], gain)
            low_ref[:, n * 256 + 128 : n * 256 + 256] = head(pre[:, 128:], gain)
    v_low[...] = jnp.dot(normed[...], matrix(1536, 512), preferred_element_type=jnp.float32).astype(jnp.bfloat16)
    pairs_kv = ((k_low, k_ref), (v_low, v_ref))
    ring_kv = [
        along_x(
            n, lambda t, low=low: low.at[:, columns(t)], lambda t, ref=ref: ref.at[2 * t + yl],
            head_send, head_recv, local,
        )
        for n, (low, ref) in enumerate(pairs_kv)
    ]
    relays = []

    def relay(n, step, source, target):
        copy = pltpu.make_async_remote_copy(
            source, target, head_send.at[4 + n, step], head_recv.at[4 + n, step], device_id=y_partner()
        )
        copy.start()
        relays.append(copy)

    for n, (low, ref) in enumerate(pairs_kv):
        relay(n, 0, low.at[:, columns(x)], ref.at[2 * x + yl])
    ring_q = along_x(
        2, lambda t: q_low.at[:, columns(t, 2)], lambda t: q_ref.at[t], head_send, head_recv, local
    )
    stores = [
        pltpu.make_async_copy(a, b, store.at[n])
        for n, (a, b) in enumerate(
            ((normed, normed_out), (qpre, qpre_out), (kpre, kpre_out), (q_ref, q_out), (k_ref, k_out),
             (v_ref, v_out), (o32_ref, o32_out), (x_ref, x_out), (tab, tab_out))
        )
    ]
    for copy in stores[:3] + stores[7:]:
        copy.start()
    for step in (1, 3, 2):
        there = 2 * ((x - step + 4) % 4) + yl
        for n, (_, ref) in enumerate(pairs_kv):
            ring_kv[n][step].wait_recv()
            relay(n, step, ref.at[there], ref.at[there])
    for copies in (*ring_kv, ring_q):
        copies[0].wait()
    for step in (1, 2, 3):
        ring_q[step].wait_recv()
    for copy in relays:
        copy.wait_recv()
    gather.forward(far[:1], 2)
    gather.ring(far[1], 2, 1)
    gather.ring(far[2], 2, 1)
    gather.forward(far[1:], 2)
    for copy in stores[3:6]:
        copy.start()
    for j in range(8):
        vt[j] = v_ref[j].T

    def one_block(n, _):
        queries = (q_ref[n, :, :HEAD_DIM], q_ref[n, :, HEAD_DIM:])

        def weigh(j, carry):
            after = []
            for q, (total, mixed) in zip(queries, carry):
                p = jnp.exp2(nt(k_ref[j], q) * (score_scale * log2e))
                total = total + jnp.sum(p, axis=0, keepdims=True)
                mixed = mixed + jnp.dot(
                    vt[j], p.astype(jnp.bfloat16), preferred_element_type=jnp.float32
                )
                after.append((total, mixed))
            return tuple(after)

        start = (jnp.zeros((1, BLOCK), jnp.float32), jnp.zeros((HEAD_DIM, BLOCK), jnp.float32))
        carry = lax.fori_loop(0, 2 * n + yl + 1, weigh, (start, start))
        for h, (total, mixed) in enumerate(carry):
            out = (mixed / total).T
            o32_ref[n, :, h * HEAD_DIM : (h + 1) * HEAD_DIM] = out
            o_low[n, :, h * HEAD_DIM : (h + 1) * HEAD_DIM] = out.astype(jnp.bfloat16)
            lse_ref[n, h] = jnp.log2(total)
        return 0

    leaving = moves_along_x(
        3, lambda t: o_low.at[t], lambda t: att.at[:, columns(t, 2)], head_send, head_recv, local
    )
    for step in (2, 1, 3, 0):
        one_block((x + step) % 4, 0)
        leaving[step].start()
    stores[6].start()
    g_low = g_ref[...].reshape(BLOCK, D)
    g_t = middle_refs[3]
    g_t[...] = g_low.T
    gather.arrive(far[1:2], 2)
    for copy in leaving:
        copy.wait()
    middle_layer(
        gather, far, att, x_ref, g_low, rows_ref, w_far, middle_refs, (output, grad_att_out, gmid_out, post_out, dw_out),
        pair_send, pair_recv, own, c, sib,
    )
    gather.drain()
    for copy in stores:
        copy.wait()
    keep_near.wait()
    for _, away in pairs:
        away.wait_send()
    for copies in (*ring_kv, ring_q):
        for copy in copies[1:]:
            copy.wait_send()
    for copy in relays:
        copy.wait_send()


def attend(gains, shards, tokens):
    blocks, pairs = (8, BLOCK, HEAD_DIM), (4, BLOCK, 2 * HEAD_DIM)
    low, wide = jnp.bfloat16, jnp.float32
    whole = [(2, 4, 4, 2, 2, 8, w) for w in WIDE]
    return pl.pallas_call(
        forward_kernel,
        out_shape=[
            jax.ShapeDtypeStruct(whole[NEAR], low),
            jax.ShapeDtypeStruct((2, 128, D), low),
            jax.ShapeDtypeStruct((2, 128, HEAD_DIM), wide),
        ]
        + [
            jax.ShapeDtypeStruct(pairs, low),
            jax.ShapeDtypeStruct(blocks, low),
            jax.ShapeDtypeStruct(blocks, low),
            jax.ShapeDtypeStruct(pairs, wide),
            jax.ShapeDtypeStruct((4, 2, 1, BLOCK), wide),
            jax.ShapeDtypeStruct((BLOCK, D), low),
            jax.ShapeDtypeStruct((BLOCK, 1024), wide),
            jax.ShapeDtypeStruct((BLOCK, 512), wide),
            jax.ShapeDtypeStruct((8, D), wide),
            jax.ShapeDtypeStruct((128, D), low),
            jax.ShapeDtypeStruct((BLOCK, 1024), low),
            jax.ShapeDtypeStruct((128, D), wide),
            jax.ShapeDtypeStruct((8, D), wide),
            jax.ShapeDtypeStruct((D, WIDE[FAR]), low),
        ],
        in_specs=[VMEM] * 15,
        out_specs=[HBM] * 7 + [VMEM] + [HBM] * 3 + [VMEM, VMEM, HBM, VMEM, VMEM, HBM],
        scratch_shapes=[
            pltpu.VMEM((2, 128, D), low),
            pltpu.VMEM((2, 128, D), low),
            pltpu.VMEM((2, 128, HEAD_DIM), wide),
            pltpu.VMEM(whole[NEAR], low),
            pltpu.VMEM(whole[FAR], low),
            pltpu.VMEM((BLOCK, D), low),
            pltpu.VMEM((BLOCK, 1024), wide),
            pltpu.VMEM((BLOCK, 512), wide),
            pltpu.VMEM((BLOCK, 1024), low),
            pltpu.VMEM((BLOCK, 512), low),
            pltpu.VMEM((BLOCK, 512), low),
        ]
        + [
            pltpu.VMEM(pairs, low),
            pltpu.VMEM(blocks, low),
            pltpu.VMEM(blocks, low),
            pltpu.VMEM(pairs, wide),
            pltpu.VMEM(pairs, low),
            pltpu.VMEM((BLOCK, 1024), low),
            pltpu.VMEM((8, HEAD_DIM, BLOCK), low),
            pltpu.VMEM((2, 8, WIDE[0]), low),
            pltpu.VMEM((2, 8, WIDE[1]), low),
            pltpu.VMEM((128, HEAD_DIM), wide),
        ]
        + middle_shapes()
        + [
            pltpu.SemaphoreType.DMA((6 * GATHER_SLOTS,)),
            pltpu.SemaphoreType.DMA((6 * GATHER_SLOTS,)),
            pltpu.SemaphoreType.DMA((6, 4)),
            pltpu.SemaphoreType.DMA((6, 4)),
            pltpu.SemaphoreType.DMA((4,)),
            pltpu.SemaphoreType.DMA((1,)),
            pltpu.SemaphoreType.DMA((9,)),
            pltpu.SemaphoreType.DMA((12,)),
            pltpu.SemaphoreType.DMA((12,)),
            pltpu.SemaphoreType.DMA((3,)),
            pltpu.SemaphoreType.DMA((11,)),
        ],
        compiler_params=pltpu.CompilerParams(
            collective_id=2, has_side_effects=True, vmem_limit_bytes=LIMIT
        ),
        name="attend",
    )(*gains, *shards, *tokens)


def backward_kernel(*refs):
    near, far = near_parts(), far_parts()
    n_scatter = len(scatter_shapes())
    ins, far_grad, do_in, refs = refs[:14], refs[14], refs[15], refs[16:]
    fin, input_grad, held, refs = refs[:2], refs[2], refs[3:17], refs[17:]
    q_ref, k_ref, v_ref, o32_ref, lse_ref, qpre, kpre, normed, tab, rows, x_ref = held[:11]
    w_near, gmid, post = held[11:]
    do_ref, dq_low, dk_low, dv_low, kt, dk_acc, dv_acc, k_in, v_in, k_sum, v_sum = refs[:11]
    gq, k_part_in, v_part_in, dqkv, normed_t, pair_out, pair_in, near_grad = refs[11:19]
    places, refs = refs[19 : 19 + n_scatter], refs[19 + n_scatter :]
    send, recv, pair_send, pair_recv, load, far_load, head_send, head_recv, head_local = refs
    yh, z, x, yl, c = place()
    sib = sibling()
    scatter = Scatter((near_grad, far_grad), fin, places, send, recv)
    loads = load_all(list(zip(ins, held)), load)
    for n, part in enumerate(far):
        scatter.load(part, far_load.at[n])
    greet(ring_devices() + [sib])
    arriving = along_x(
        0, lambda t: do_in.at[:, columns(t, 2)], lambda t: do_ref.at[t], head_send, head_recv, head_local
    )
    scatter.begin(far[:1], 0)
    scatter.begin(far[1:], 0)
    for copy in loads[:5]:
        copy.wait()
    for j in range(8):
        kt[j] = k_ref[j].T
    dk_acc[...] = jnp.zeros_like(dk_acc)
    dv_acc[...] = jnp.zeros_like(dv_acc)
    for copy in arriving:
        copy.wait()

    def one_block(n, _):
        heads = []
        for h in range(2):
            at = slice(h * HEAD_DIM, (h + 1) * HEAD_DIM)
            q, do = q_ref[n, :, at], do_ref[n, :, at]
            delta = jnp.sum((do.astype(jnp.float32) * o32_ref[n, :, at]).T, axis=0, keepdims=True)
            heads.append((q, do, lse_ref[n, h], delta))

        def one_pair(j, dqts):
            after, dk_term, dv_term = [], 0.0, 0.0
            for (q, do, lse, delta), dqt in zip(heads, dqts):
                p = jnp.exp2(nt(k_ref[j], q) * (score_scale * log2e) - lse)
                ds = (p * (nt(v_ref[j], do) - delta)).astype(jnp.bfloat16)
                dv_term += jnp.dot(p.astype(jnp.bfloat16), do, preferred_element_type=jnp.float32)
                dk_term += jnp.dot(ds, q, preferred_element_type=jnp.float32)
                after.append(dqt + jnp.dot(kt[j], ds, preferred_element_type=jnp.float32))
            dv_acc[j // 2, j % 2] += dv_term
            dk_acc[j // 2, j % 2] += dk_term
            return tuple(after)

        start = jnp.zeros((HEAD_DIM, BLOCK), jnp.float32)
        dqts = lax.fori_loop(0, 2 * n + yl + 1, one_pair, (start, start))
        for h, dqt in enumerate(dqts):
            dq_low[n, :, h * HEAD_DIM : (h + 1) * HEAD_DIM] = (dqt * score_scale).T.astype(jnp.bfloat16)
        return 0

    ring_q = moves_along_x(
        1, lambda t: dq_low.at[t], lambda t: gq.at[:, columns(t, 2)], head_send, head_recv, head_local
    )
    for step in (2, 1, 3):
        one_block((x + step) % 4, 0)
        ring_q[step].start()
    scatter.middle(far[:1], 0)
    scatter.middle(far[1:], 0)
    one_block(x, 0)
    ring_q[0].start()
    sums = ((dk_acc, dk_low, k_in, k_sum, k_part_in, score_scale), (dv_acc, dv_low, v_in, v_sum, v_part_in, 1.0))
    across = {}
    for n, (acc, low, landing, _, _, scale) in enumerate(sums):
        low[...] = (acc[:, 1 - yl] * scale).astype(jnp.bfloat16)
        for step in (1, 2, 3, 0):
            there = (x + step) % 4
            copy = pltpu.make_async_remote_copy(
                low.at[there], landing.at[there], head_send.at[4 + n, step], head_recv.at[4 + n, step],
                device_id=y_partner(),
            )
            copy.start()
            across[n, step] = copy
    ring_kv = []
    for step in (1, 2, 3, 0):
        there = (x + step) % 4
        for n, (acc, _, landing, total, part_in, scale) in enumerate(sums):
            across[n, step].wait_recv()
            total[there] = (
                acc[there, yl] * scale + landing[there].astype(jnp.float32)
            ).astype(jnp.bfloat16)
            target = part_in.at[:, columns(x)]
            if step == 0:
                copy = pltpu.make_async_copy(total.at[there], target, head_local.at[2 + n])
            else:
                copy = pltpu.make_async_remote_copy(
                    total.at[there], target, head_send.at[2 + n, step], head_recv.at[2 + n, step],
                    device_id=ring_device("x", step, 0),
                )
            copy.start()
            ring_kv.append(copy)
    for copy in loads[5:]:
        copy.wait()
    normed_t[...] = normed[...].T
    cosine, sine = rope_pair(tab)
    gain_q, gain_k = rows[2:3, :HEAD_DIM], rows[3:4, :HEAD_DIM]

    def head_back(grad, values, gain):
        grad = grad * cosine - pltpu.roll(grad, HEAD_DIM // 2, 1) * sine
        grad_in, terms = norm_back(grad, values, rms_scale(values), gain)
        return grad_in.astype(jnp.bfloat16), jnp.sum(terms, axis=0, keepdims=True)

    def weight_grads(first):
        def one(n, _):
            lhs = normed_t[pl.ds(pl.multiple_of(n * 256, 256), 256), :]
            for at in (first, first + 512):
                block = jnp.dot(lhs, dqkv[:, at : at + 512], preferred_element_type=jnp.float32)
                near_grad[n // 2, pl.ds(n % 2 * 2, 2), :, :, :, at : at + 512] = block.astype(
                    jnp.bfloat16
                ).reshape(2, 4, 2, 16, 512)
            return 0

        lax.fori_loop(0, 4, one, 0)

    for copy in ring_q:
        copy.wait()
    q_part = jnp.zeros((1, HEAD_DIM), jnp.float32)
    k_part = jnp.zeros((1, HEAD_DIM), jnp.float32)
    for h in range(8):
        at = slice(h * HEAD_DIM, (h + 1) * HEAD_DIM)
        dqkv[:, at], part = head_back(gq[:, at].astype(jnp.float32), qpre[:, at], gain_q)
        q_part = q_part + part
    weight_grads(0)
    scatter.begin(near[:1], 0)
    scatter.end(far[:1], 0)
    scatter.begin(far[:1], 1)
    scatter.end(far[1:], 0)
    scatter.begin(far[1:], 1)
    for copy in ring_kv:
        copy.wait()
    for h in range(4):
        at = slice(h * HEAD_DIM, (h + 1) * HEAD_DIM)
        low_at = slice(1024 + h * HEAD_DIM, 1024 + (h + 1) * HEAD_DIM)
        dqkv[:, low_at], part = head_back(k_part_in[:, at].astype(jnp.float32), kpre[:, at], gain_k)
        k_part = k_part + part
    dqkv[:, 1536:] = v_part_in[...]
    weight_grads(1024)
    scatter.begin(near[1:2], 0)
    scatter.begin(near[2:], 0, (0,))

    def grad_normed(rows_at):
        return nt(dqkv[rows_at, :], w_near[:, :2048])

    away = pl.ds(pl.multiple_of((1 - c) * 128, 128), 128)
    own = pl.ds(pl.multiple_of(c * 128, 128), 128)
    pair_out[...] = grad_normed(away).astype(jnp.bfloat16)
    swap = pltpu.make_async_remote_copy(
        pair_out, pair_in, pair_send.at[0], pair_recv.at[0], device_id=sib
    )
    swap.start()
    grad = grad_normed(own)
    values = x_ref[c].astype(jnp.float32)
    swap.wait_recv()
    grad = grad + pair_in[...].astype(jnp.float32)
    grad_in, terms = norm_back(grad, values, rms_scale(values), rows[0:1, :])
    input_grad[...] = (gmid[...] + grad_in).astype(jnp.bfloat16)
    in_part = jnp.sum(terms, axis=0, keepdims=True)
    spread = (
        lax.broadcasted_iota(jnp.int32, (HEAD_DIM, D), 1)
        == 8 * lax.broadcasted_iota(jnp.int32, (HEAD_DIM, D), 0)
    ).astype(jnp.bfloat16)
    qk = jnp.concatenate([q_part, k_part, jnp.zeros((6, HEAD_DIM), jnp.float32)]).astype(jnp.bfloat16)
    qk = jnp.dot(qk, spread, preferred_element_type=jnp.float32)
    gain_rows = jnp.concatenate(
        [in_part, post[0:1, :], qk[0:2], jnp.zeros((TILE - 4, D), jnp.float32)]
    )
    near_grad[:, :, :, :, :, 2048:] = gain_rows.T.astype(jnp.bfloat16).reshape(2, 4, 4, 2, 16, TILE)
    scatter.begin(near[2:], 0, (1,))
    scatter.middle(near, 0)
    scatter.middle(far, 1)
    for part in near:
        scatter.end([part], 0)
        scatter.direct([part])
    for part in far:
        scatter.end([part], 1)
        scatter.deliver([part])
    for part in near:
        scatter.landed([part])
        scatter.deliver([part])
    scatter.finish(far)
    scatter.finish(near)
    scatter.drain()
    swap.wait_send()
    for copy in across.values():
        copy.wait_send()


def attend_back(arrays, far_grad, grad_att):
    blocks, pairs, split = (8, BLOCK, HEAD_DIM), (4, BLOCK, 2 * HEAD_DIM), (4, BLOCK, HEAD_DIM)
    low, wide = jnp.bfloat16, jnp.float32
    return pl.pallas_call(
        backward_kernel,
        out_shape=[jax.ShapeDtypeStruct((2, 8, w), wide) for w in WIDE]
        + [jax.ShapeDtypeStruct((128, D), low)],
        in_specs=[HBM] * (len(arrays) + 2),
        out_specs=[VMEM] * 3,
        scratch_shapes=[pltpu.VMEM(a.shape, a.dtype) for a in arrays]
        + [pltpu.VMEM(pairs, low)] * 2
        + [pltpu.VMEM(split, low)] * 2
        + [
            pltpu.VMEM((8, HEAD_DIM, BLOCK), low),
            pltpu.VMEM((4, 2, BLOCK, HEAD_DIM), wide),
            pltpu.VMEM((4, 2, BLOCK, HEAD_DIM), wide),
        ]
        + [pltpu.VMEM(split, low)] * 4
        + [
            pltpu.VMEM((BLOCK, 1024), low),
            pltpu.VMEM((BLOCK, 512), low),
            pltpu.VMEM((BLOCK, 512), low),
            pltpu.VMEM((BLOCK, 2048), low),
            pltpu.VMEM((D, BLOCK), low),
            pltpu.VMEM((128, D), low),
            pltpu.VMEM((128, D), low),
            pltpu.VMEM((2, 4, 4, 2, 16, WIDE[0]), low),
        ]
        + scatter_shapes()
        + [
            pltpu.SemaphoreType.DMA((6 * GATHER_SLOTS,)),
            pltpu.SemaphoreType.DMA((6 * GATHER_SLOTS,)),
            pltpu.SemaphoreType.DMA((1,)),
            pltpu.SemaphoreType.DMA((1,)),
            pltpu.SemaphoreType.DMA((len(arrays),)),
            pltpu.SemaphoreType.DMA((3, 4)),
            pltpu.SemaphoreType.DMA((6, 4)),
            pltpu.SemaphoreType.DMA((6, 4)),
            pltpu.SemaphoreType.DMA((4,)),
        ],
        compiler_params=pltpu.CompilerParams(
            collective_id=3, has_side_effects=True, vmem_limit_bytes=LIMIT
        ),
        name="attend_back",
    )(*arrays, far_grad, grad_att)


def results_kernel(near, far, grad_in, out_in, *refs):
    (q, k, v, in_gain, post_gain, q_gain, k_gain, w_out, gate, up, down, grad, out) = refs
    for source, group in ((near, ((q, 0), (k, 1024), (v, 1536))), (far, zip((w_out, gate, up, down), [s for s, _ in FAR_SPANS]))):
        for target, first in group:
            width = target.shape[1] // 2
            for half in range(2):
                target[:, half * width : (half + 1) * width] = source[half, :, first : first + width]
    gains = near[0, :, 2048:] + near[1, :, 2048:]
    gains = jnp.concatenate([gains, jnp.zeros((TILE - 8, TILE), jnp.float32)]).T
    in_gain[...] = gains[0:1, :8]
    post_gain[...] = gains[1:2, :8]
    q_gain[...] = gains[2:3, :1]
    k_gain[...] = gains[3:4, :1]
    grad[...] = grad_in[...]
    out[...] = out_in[...]


def results(arrays):
    shapes = [(8, 2048), (8, 1024), (8, 1024), (1, 8), (1, 8), (1, 1), (1, 1)]
    shapes += [(8, 2 * width) for _, width in FAR_SPANS]
    return pl.pallas_call(
        results_kernel,
        out_shape=[jax.ShapeDtypeStruct(s, jnp.float32) for s in shapes]
        + [jax.ShapeDtypeStruct((128, D), jnp.bfloat16)] * 2,
        in_specs=[VMEM] * 4,
        out_specs=[VMEM] * 13,
        name="results",
    )(*arrays)


def body(
    tokens,
    positions,
    in_gain,
    q_gain,
    k_gain,
    w_query,
    w_key,
    w_value,
    w_out,
    post_gain,
    w_gate,
    w_up,
    w_down,
    cotangent,
):
    half = HEAD_DIM // 2
    frequency = rope_base ** (-2.0 * jnp.arange(half, dtype=jnp.float32) / HEAD_DIM)
    angles = positions[0].astype(jnp.float32)[:, None] * frequency[None, :]
    gains = [g[None] for g in (in_gain, post_gain, q_gain, k_gain)]
    shards = [w_query, w_key, w_value, w_out.T, w_gate, w_up, w_down.T]
    (near, x_pair, tables, q_all, k_all, v_all, mixed, log_total, normed, q_pre, k_pre, rows, output,
     grad_att, grad_middle, post_part, far_grad) = attend(
        gains, shards, [tokens[0], cotangent[0], jnp.cos(angles), jnp.sin(angles)]
    )
    near_sum, far_sum, input_grad = attend_back(
        [q_all, k_all, v_all, mixed, log_total, q_pre, k_pre, normed, tables, rows, x_pair,
         near.reshape(D, WIDE[NEAR]), grad_middle, post_part],
        far_grad.reshape(2, 4, 4, 2, 16, WIDE[FAR]),
        grad_att,
    )
    (query, key, value, in_gain_grad, post_gain_grad, q_gain_grad, k_gain_grad, out_grad, gate, up, down,
     input_grad, output) = results([near_sum, far_sum, input_grad, output])
    return (
        output[None],
        input_grad[None],
        in_gain_grad[0],
        q_gain_grad[0],
        k_gain_grad[0],
        query,
        key,
        value,
        out_grad.T,
        post_gain_grad[0],
        gate,
        up,
        down.T,
    )


def solution(mesh):
    placed = (
        P("dp", "seq", None),
        P("dp", "seq"),
        P(("dp", "seq")),
        P(("dp", "seq")),
        P(("dp", "seq")),
        P(("dp", "seq"), None),
        P(("dp", "seq"), None),
        P(("dp", "seq"), None),
        P(None, ("dp", "seq")),
        P(("dp", "seq")),
        P(("dp", "seq"), None),
        P(("dp", "seq"), None),
        P(None, ("dp", "seq")),
        P("dp", "seq", None),
    )
    return jax.shard_map(
        body,
        mesh=mesh,
        in_specs=placed,
        out_specs=(
            P("dp", "seq", None),
            P("dp", "seq", None),
            P(("dp", "seq")),
            P(("dp", "seq")),
            P(("dp", "seq")),
            P(("dp", "seq"), None),
            P(("dp", "seq"), None),
            P(("dp", "seq"), None),
            P(None, ("dp", "seq")),
            P(("dp", "seq")),
            P(("dp", "seq"), None),
            P(("dp", "seq"), None),
            P(None, ("dp", "seq")),
        ),
        check_vma=False,
    )
```

```python
import functools
import math

import jax
import jax.numpy as jnp
from jax import lax
from jax.experimental import pallas as pl
from jax.experimental.pallas import tpu as pltpu
from jax.sharding import PartitionSpec as P

HEADS = 16
KV_HEADS = 8
HEAD_DIM = 128
D = 1024
FF = 3072
BLOCK = 256
CORES = 2

TILE = 128

eps_norm = 1e-06
rope_base = 1000000.0
score_scale = 1.0 / math.sqrt(HEAD_DIM)
log2e = math.log2(math.e)


def place():
    dp = lax.axis_index("dp")
    seq = lax.axis_index("seq")
    return dp // 4, dp % 4, seq // 4, (seq // 2) % 2, seq % 2


def device(yh, z, x, yl, c):
    return {"dp": yh * 4 + z, "seq": x * 4 + yl * 2 + c}


def sibling():
    yh, z, x, yl, c = place()
    return device(yh, z, x, yl, 1 - c)


def neighbour(axis, step):
    yh, z, x, yl, c = place()
    if axis == "x":
        return device(yh, z, (x + step + 4) % 4, yl, c)
    if axis == "z":
        return device(yh, (z + step + 4) % 4, x, yl, c)
    y = (yh * 2 + yl + step + 4) % 4
    return device(y // 2, z, x, y % 2, c)


ORDERS = (("x", "y", "z"), ("y", "z", "x"), ("z", "x", "y"))


def chip_set(whole_axes, axis, step):
    yh, z, x, yl, _ = place()
    iz, ix, iyh, iyl = z, x, yh, yl
    if axis == "x":
        ix = (x + step + 4) % 4
    elif axis == "z":
        iz = (z + step + 4) % 4
    else:
        y = (yh * 2 + yl + step + 4) % 4
        iyh, iyl = y // 2, y % 2
    every = slice(None)
    if "x" in whole_axes:
        ix = every
    if "z" in whole_axes:
        iz = every
    if "y" in whole_axes:
        iyh, iyl = every, every
    return (iyh, iz, ix, iyl)


def set_dims(whole_axes):
    dims = ()
    if "y" in whole_axes:
        dims += (2,)
    if "z" in whole_axes:
        dims += (4,)
    if "x" in whole_axes:
        dims += (4,)
    if "y" in whole_axes:
        dims += (2,)
    return dims


NEAR, FAR = 0, 1
WIDE = (2176, 5632)
LIMIT = 60 << 20


class Part:
    def __init__(self, array, number, order, first, tiles):
        self.array, self.number, self.order = array, number, order
        self.start, self.width = first * TILE, tiles * TILE
        self.cols = pl.ds(self.start, self.width)
        cut = (tiles + 1) // 2 * TILE
        self.halves = ((0, 1, 0, cut), (1, -1, cut, self.width - cut))


def parts_of(array, tiles):
    parts, first = [], 0
    for number, count in enumerate(tiles):
        parts.append(Part(array, number, ORDERS[number], first, count))
        first += count
    return parts


def near_parts():
    return parts_of(NEAR, (6, 6, 5))


def far_parts(tiles=(17, 14, 13)):
    return parts_of(FAR, tiles)


def greet(others):
    barrier = pltpu.get_barrier_semaphore()
    for other in others:
        pl.semaphore_signal(barrier, inc=1, device_id=other)


def await_greetings(others):
    pl.semaphore_wait(pltpu.get_barrier_semaphore(), len(others))


def ring_device(axis, step, other):
    yh, z, x, yl, c = place()
    core = (c + other) % 2
    if axis == "x":
        return device(yh, z, (x + step + 4) % 4, yl, core)
    if axis == "z":
        return device(yh, (z + step + 4) % 4, x, yl, core)
    y = (yh * 2 + yl + step + 4) % 4
    return device(y // 2, z, x, y % 2, core)


def ring_devices():
    return [ring_device(axis, step, other) for axis in "xyz" for step in (1, 2, 3) for other in (0, 1)]


HBM = pl.BlockSpec(memory_space=pltpu.HBM)
VMEM = pl.BlockSpec(memory_space=pltpu.VMEM)


def load_all(pairs, sems):
    copies = [pltpu.make_async_copy(a, b, sems.at[n]) for n, (a, b) in enumerate(pairs)]
    for copy in copies:
        copy.start()
    return copies


def nt(left, right):
    return lax.dot_general(left, right, (((1,), (1,)), ((), ())), preferred_element_type=jnp.float32)


def rms_scale(values):
    return lax.rsqrt(jnp.mean(values * values, axis=-1, keepdims=True) + eps_norm)


def norm_back(grad_out, values, scale_factor, gain):
    weighted = grad_out * gain
    inner = jnp.mean(weighted * values, axis=-1, keepdims=True)
    grad_in = (
        scale_factor * weighted - values * (scale_factor * scale_factor * scale_factor) * inner
    )
    return (grad_in, grad_out * values * scale_factor)


def rope_pair(tab):
    table = tab[...].reshape(BLOCK, HEAD_DIM)
    turned = pltpu.roll(table, HEAD_DIM // 2, 1)
    low = lax.broadcasted_iota(jnp.int32, (BLOCK, HEAD_DIM), 1) < HEAD_DIM // 2
    return jnp.where(low, table, turned), jnp.where(low, -turned, table)


class Gather:
    def __init__(self, units, outs, base, send, recv, local):
        self.units, self.outs, self.base = units, outs, base
        self.send, self.recv, self.local = send, recv, local
        self.copies = {}

    def remote(self, key, slot, source, target, device_id):
        copy = pltpu.make_async_remote_copy(
            source, target, self.send.at[slot], self.recv.at[slot], device_id=device_id
        )
        copy.start()
        self.copies[key] = copy

    def slot(self, part, n):
        return self.base[part.array] + part.number * GATHER_SLOTS + n

    def spread(self, parts):
        yh, z, x, yl, c = place()
        for part in parts:
            target = self.outs[part.array].at[yh, z, x, yl, c, :, part.cols]
            for step in range(4):
                for other in range(2):
                    source = self.units[part.array].at[(c + other) % 2, :, part.cols]
                    key = (part.array, part.number, 0, step, other)
                    if step == 0 and other == 0:
                        copy = pltpu.make_async_copy(
                            source, target, self.local.at[part.array * 3 + part.number]
                        )
                        copy.start()
                        self.copies[key] = copy
                    else:
                        slot = self.slot(part, step * 2 + other - 1)
                        self.remote(key, slot, source, target, ring_device(part.order[0], step, other))

    def settle(self, part):
        for step in range(4):
            for other in range(2):
                copy = self.copies[part.array, part.number, 0, step, other]
                if step == 0 and other == 0:
                    copy.wait()
                else:
                    copy.wait_recv()

    def block(self, part, phase, offset, first, width):
        index = chip_set(part.order[:phase], part.order[phase], offset)
        cols = pl.ds(part.start + first, width)
        return self.outs[part.array].at[(*index, slice(None), slice(None), cols)]

    def direct(self, part):
        ref = self.block(part, 1, 0, 0, part.width)
        for step in (1, 2, 3):
            key = (part.array, part.number, 1, step)
            self.remote(key, self.slot(part, 6 + step), ref, ref, ring_device(part.order[1], step, 0))

    def landed(self, part):
        for step in (1, 2, 3):
            self.copies[part.array, part.number, 1, step].wait_recv()

    def ring(self, part, phase, which):
        for half, way, first, width in part.halves:
            step, offset = ((way, 0), (-way, 0), (way, -way))[which]
            key = (part.array, part.number, phase, which, half)
            if which == 2:
                self.copies[part.array, part.number, phase, 0, half].wait_recv()
            ref = self.block(part, phase, offset, first, width)
            slot = self.slot(part, 7 + 6 * (phase - 1) + 2 * which + half)
            self.remote(key, slot, ref, ref, ring_device(part.order[phase], step, 0))

    def begin(self, parts, phase):
        for part in parts:
            self.ring(part, phase, 0)
            self.ring(part, phase, 1)

    def forward(self, parts, phase):
        for part in parts:
            self.ring(part, phase, 2)

    def arrive(self, parts, phase):
        for part in parts:
            for which in (1, 2):
                for half in (0, 1):
                    self.copies[part.array, part.number, phase, which, half].wait_recv()

    def drain(self):
        for key, copy in self.copies.items():
            if key[2:] != (0, 0, 0):
                copy.wait_send()


GATHER_SLOTS = 19


def kept_index(kept, axis, step):
    iyh, iz, ix, iyl = chip_set(tuple(a for a in kept if a != axis), axis, step)
    index = ()
    if "y" in kept:
        index += (iyh,)
    if "z" in kept:
        index += (iz,)
    if "x" in kept:
        index += (ix,)
    if "y" in kept:
        index += (iyl,)
    return index


def add_sets(dims, terms, store):
    def one(flat_index, _):
        index, rest = [], flat_index
        for size in reversed(dims):
            index.insert(0, rest % size)
            rest = rest // size
        at = tuple(index)
        total = terms[0][at].astype(jnp.float32)
        for term in terms[1:]:
            total = total + term[at].astype(jnp.float32)
        store(at, total)
        return 0

    lax.fori_loop(0, math.prod(dims), one, 0)


def scatter_shapes():
    low, shapes = jnp.bfloat16, []
    for part in near_parts() + far_parts():
        plane, line = set_dims(part.order[:2]), set_dims(part.order[:1])
        for _, _, _, width in part.halves:
            shapes += [pltpu.VMEM((*plane, 16, width), low)] * 4
            if part.array == FAR:
                shapes += [pltpu.VMEM((*line, 16, width), low)] * 4
        if part.array == NEAR:
            shapes += [pltpu.VMEM((*line, 16, part.width), low)] * 3
        shapes += [pltpu.VMEM((8, 8, part.width), low)]
        shapes += [pltpu.VMEM((*plane, 16, part.width), low)]
        shapes += [pltpu.VMEM((*line, 2, 8, part.width), low)]
    return shapes


class Scatter:
    def __init__(self, grads, fin, refs, send, recv):
        self.grads, self.fin, self.send, self.recv = grads, fin, send, recv
        self.copies, self.loads = {}, {}
        self.land, self.mids, self.plane, self.line = {}, {}, {}, {}
        refs = list(refs)
        for part in near_parts() + far_parts():
            name = (part.array, part.number)
            for half in (0, 1):
                for phase in (0, 1) if part.array == FAR else (0,):
                    self.land[name, phase, half] = [refs.pop(0) for _ in range(3)]
                    self.mids[name, phase, half] = refs.pop(0)
            if part.array == NEAR:
                self.land[name, 1] = [refs.pop(0) for _ in range(3)]
            self.land[name, 2] = refs.pop(0)
            self.plane[name] = refs.pop(0)
            self.line[name] = refs.pop(0)

    def remote(self, key, part, n, source, target, device_id):
        slot = (part.array * 3 + part.number) * GATHER_SLOTS + n
        copy = pltpu.make_async_remote_copy(
            source, target, self.send.at[slot], self.recv.at[slot], device_id=device_id
        )
        copy.start()
        self.copies[key] = copy

    def source(self, part, phase, offset, first, width):
        if phase == 0:
            index = chip_set(part.order[:2], part.order[2], offset)
            cols = pl.ds(part.start + first, width)
            return self.grads[part.array].at[(*index, slice(None), cols)]
        index = kept_index(part.order[:2], part.order[1], offset)
        return self.plane[part.array, part.number].at[(*index, slice(None), pl.ds(first, width))]

    def load(self, part, sems):
        name = (part.array, part.number)
        every = (slice(None),) * (len(set_dims(part.order[:2])) + 1)
        for half, way, first, width in part.halves:
            target = self.plane[name].at[(*every, pl.ds(first, width))]
            for m, (offset, place_to) in enumerate(((way, self.mids[name, 0, half]), (0, target))):
                copy = pltpu.make_async_copy(
                    self.source(part, 0, offset, first, width), place_to, sems.at[2 * half + m]
                )
                copy.start()
                self.loads[name, half, m] = copy

    def ring(self, part, phase, which, halves=(0, 1)):
        name = (part.array, part.number)
        for half, way, first, width in part.halves:
            if half not in halves:
                continue
            offset, step = ((2, way), (-way, -way))[which]
            self.remote(
                (name, phase, which, half), part, 6 * phase + 2 * which + half,
                self.source(part, phase, offset, first, width), self.land[name, phase, half][which],
                ring_device(part.order[2 - phase], step, 0),
            )

    def begin(self, parts, phase, halves=(0, 1)):
        for part in parts:
            self.ring(part, phase, 0, halves)
        for part in parts:
            self.ring(part, phase, 1, halves)

    def middle(self, parts, phase):
        for part in parts:
            name = (part.array, part.number)
            for half, way, first, width in part.halves:
                self.copies[name, phase, 0, half].wait_recv()
                mid = self.mids[name, phase, half]
                own = self.source(part, phase, way, first, width)
                if (name, half, 0) in self.loads and phase == 0:
                    self.loads[name, half, 0].wait()
                    own = mid

                def store(at, total, mid=mid):
                    mid[at] = total.astype(jnp.bfloat16)

                add_sets(set_dims(part.order[: 2 - phase]), [own, self.land[name, phase, half][0]], store)
                self.remote(
                    (name, phase, 2, half), part, 6 * phase + 4 + half, mid,
                    self.land[name, phase, half][2], ring_device(part.order[2 - phase], way, 0),
                )

    def end(self, parts, phase):
        for part in parts:
            name = (part.array, part.number)
            for half, way, first, width in part.halves:
                self.copies[name, phase, 1, half].wait_recv()
                self.copies[name, phase, 2, half].wait_recv()
                base = self.source(part, phase, 0, first, width)
                cols = pl.ds(first, width)
                if phase == 0:
                    plane = self.plane[name]
                    if (name, half, 1) in self.loads:
                        self.loads[name, half, 1].wait()
                        base = plane.at[(*(slice(None),) * (len(plane.shape) - 1), cols)]

                    def store(at, total, plane=plane, cols=cols):
                        plane[(*at, slice(None), cols)] = total.astype(jnp.bfloat16)

                else:
                    line = self.line[name]

                    def store(at, total, line=line, cols=cols):
                        line[(*at, 0, slice(None), cols)] = total[:8].astype(jnp.bfloat16)
                        line[(*at, 1, slice(None), cols)] = total[8:].astype(jnp.bfloat16)

                add_sets(
                    set_dims(part.order[: 2 - phase]), [base, *self.land[name, phase, half][1:]], store
                )

    def direct(self, parts):
        for part in parts:
            name = (part.array, part.number)
            for step in (1, 2, 3):
                self.remote(
                    (name, 1, step), part, 5 + step, self.source(part, 1, step, 0, part.width),
                    self.land[name, 1][step - 1], ring_device(part.order[1], step, 0),
                )

    def landed(self, parts):
        for part in parts:
            name = (part.array, part.number)
            for step in (1, 2, 3):
                self.copies[name, 1, step].wait_recv()
            line = self.line[name]

            def store(at, total, line=line):
                line[(*at, 0)] = total[:8].astype(jnp.bfloat16)
                line[(*at, 1)] = total[8:].astype(jnp.bfloat16)

            add_sets(
                set_dims(part.order[:1]),
                [self.source(part, 1, 0, 0, part.width), *self.land[name, 1]], store,
            )

    def deliver(self, parts):
        c = place()[4]
        for part in parts:
            name, axis = (part.array, part.number), part.order[0]
            for step in range(4):
                for other in range(2):
                    if step or other:
                        source = self.line[name].at[
                            (*kept_index(part.order[:1], axis, step), (c + other) % 2)
                        ]
                        self.remote(
                            (name, 2, step, other), part, 11 + step * 2 + other, source,
                            self.land[name, 2].at[step * 2 + other], ring_device(axis, step, other),
                        )

    def finish(self, parts):
        c = place()[4]
        for part in parts:
            name, axis = (part.array, part.number), part.order[0]
            for other in range(2):
                total = None
                for step in range(4):
                    if step or other:
                        self.copies[name, 2, step, other].wait_recv()
                        term = self.land[name, 2][step * 2 + other]
                    else:
                        term = self.line[name][(*kept_index(part.order[:1], axis, 0), c)]
                    term = term.astype(jnp.float32)
                    total = term if total is None else total + term
                self.fin[part.array][(c + other) % 2, :, part.cols] = total

    def drain(self):
        for copy in self.copies.values():
            copy.wait_send()


def columns(head, heads=1):
    width = heads * HEAD_DIM
    return pl.ds(pl.multiple_of(head * width, width), width)


def y_partner():
    yh, z, x, yl, c = place()
    return device(yh, z, x, 1 - yl, c)


def along_x(n, source, target, send, recv, local):
    copies = moves_along_x(n, source, target, send, recv, local)
    for copy in copies[1:] + copies[:1]:
        copy.start()
    return copies


def moves_along_x(n, source, target, send, recv, local):
    x = place()[2]
    copies = [pltpu.make_async_copy(source(x), target(x), local.at[n])]
    for step in (1, 2, 3):
        copies.append(
            pltpu.make_async_remote_copy(
                source((x + step) % 4), target(x), send.at[n, step], recv.at[n, step],
                device_id=ring_device("x", step, 0),
            )
        )
    return copies


FAR_SPANS = ((3072, 1024), (0, 1536), (1536, 1536), (4096, 1536))


def middle_shapes():
    low, wide = jnp.bfloat16, jnp.float32
    return [
        pltpu.VMEM((BLOCK, D), wide),
        pltpu.VMEM((BLOCK, D), wide),
        pltpu.VMEM((BLOCK, D), low),
        pltpu.VMEM((D, BLOCK), low),
        pltpu.VMEM((D, BLOCK), low),
        pltpu.VMEM((BLOCK, 1536), wide),
        pltpu.VMEM((BLOCK, 1536), low),
        pltpu.VMEM((BLOCK, 1536), low),
        pltpu.VMEM((BLOCK, 1536), low),
        pltpu.VMEM((BLOCK, D), wide),
        pltpu.VMEM((128, D), wide),
        pltpu.VMEM((BLOCK, 1024), low),
        pltpu.VMEM((D, WIDE[FAR]), low),
        pltpu.VMEM((4, BLOCK, 256), low),
        pltpu.VMEM((4, BLOCK, 256), low),
        pltpu.VMEM((4, BLOCK, 256), low),
        pltpu.VMEM((4, BLOCK, 256), low),
        pltpu.VMEM((128, D), low),
        pltpu.VMEM((128, D), low),
    ]


def middle_layer(gather, far, att, x_ref, g_low, rows, w_far, refs, outs, pair_send, pair_recv, sems, c, sib):
    output, grad_att_out, gmid_out, post_out, dw_out = outs
    (branch, middle, hidden, g_t, hidden_t, grad_act, act, gate_grad, up_grad, grad_hidden,
     down_own, grad_att, dw, out1, in1, out2, in2, out3, in3) = refs
    branch_t = hidden_t
    swaps = []

    def swap(source, target):
        n = 3 + len(swaps)
        copy = pltpu.make_async_remote_copy(
            source, target, pair_send.at[n], pair_recv.at[n], device_id=sib
        )
        copy.start()
        swaps.append(copy)
        return copy

    def part(n, width=256):
        return pl.ds(n * width, width)

    def far_rows(n, which):
        first, width = FAR_SPANS[which]
        half = n % 2 * 2
        return w_far[n // 2, half : half + 2, :, :, :, :, first : first + width].reshape(256, width)

    def far_cols(which, n):
        first = FAR_SPANS[which][0] + n * 256
        return w_far[:, :, :, :, :, :, first : first + 256].reshape(D, 256)

    first = []
    for n in range(4):
        block = nt(att[...], far_rows(n, 0))
        branch[:, part(n)] = block
        out1[n] = block.astype(jnp.bfloat16)
        first.append(swap(out1.at[n], in1.at[n]))
    gather.arrive(far[2:], 2)
    for n in range(6):
        grad_act[:, part(n)] = jnp.dot(g_low, far_cols(3, n), preferred_element_type=jnp.float32)
    for n in range(4):
        first[n].wait_recv()
        middle[:, part(n)] = (
            x_ref[...].reshape(BLOCK, D)[:, n * 256 : n * 256 + 256].astype(jnp.float32)
            + (branch[:, part(n)] + in1[n].astype(jnp.float32))
        )
    gain = rows[1:2, :]
    scale = rms_scale(middle[...])
    hidden[...] = (middle[...] * scale * gain).astype(jnp.bfloat16)
    gather.arrive(far[:1], 2)
    for n in range(6):
        gate = jnp.dot(hidden[...], far_cols(1, n), preferred_element_type=jnp.float32)
        up = jnp.dot(hidden[...], far_cols(2, n), preferred_element_type=jnp.float32)
        sigma = jax.nn.sigmoid(gate)
        swish = gate * sigma
        grad = grad_act[:, part(n)]
        act[:, part(n)] = (swish * up).astype(jnp.bfloat16)
        gate_grad[:, part(n)] = (grad * up * (sigma * (1.0 + gate * (1.0 - sigma)))).astype(jnp.bfloat16)
        up_grad[:, part(n)] = (grad * swish).astype(jnp.bfloat16)
    second = []
    for n in range(4):
        block = nt(gate_grad[...], far_rows(n, 1)) + nt(up_grad[...], far_rows(n, 2))
        grad_hidden[:, part(n)] = block
        out2[n] = block.astype(jnp.bfloat16)
        second.append(swap(out2.at[n], in2.at[n]))
    away = pl.ds(pl.multiple_of((1 - c) * 128, 128), 128)
    own = pl.ds(pl.multiple_of(c * 128, 128), 128)
    for n in range(4):
        out3[:, part(n)] = nt(act[away, :], far_rows(n, 3)).astype(jnp.bfloat16)
    third = swap(out3, in3)
    for n in range(4):
        down_own[:, part(n)] = nt(act[own, :], far_rows(n, 3))
    hidden_t[...] = hidden[...].T
    stores = []

    def keep(source, target):
        copy = pltpu.make_async_copy(source, target, sems.at[6 + len(stores)])
        copy.start()
        stores.append(copy)

    for lhs, rhs, (first, width) in (
        (hidden_t, gate_grad, FAR_SPANS[1]), (hidden_t, up_grad, FAR_SPANS[2]), (g_t, act, FAR_SPANS[3])
    ):
        for n in range(4):
            dw[part(n), first : first + width] = jnp.dot(
                lhs[part(n), :], rhs[...], preferred_element_type=jnp.float32
            ).astype(jnp.bfloat16)
        keep(dw.at[:, pl.ds(first, width)], dw_out.at[:, pl.ds(first, width)])
    for n in range(4):
        second[n].wait_recv()
        grad_hidden[:, part(n)] = grad_hidden[:, part(n)] + in2[n].astype(jnp.float32)
    grad_in, terms = norm_back(grad_hidden[...], middle[...], scale, gain)
    grad_hidden[...] = terms
    post_out[...] = jnp.broadcast_to(jnp.sum(grad_hidden[own, :], axis=0, keepdims=True), (8, D))
    grad_hidden[...] = g_low.astype(jnp.float32) + grad_in
    gmid_out[...] = grad_hidden[own, :]
    branch_grad = grad_hidden[...].astype(jnp.bfloat16)
    branch_t[...] = branch_grad.T
    for n in range(4):
        grad_att[:, part(n)] = jnp.dot(
            branch_grad, far_cols(0, n), preferred_element_type=jnp.float32
        ).astype(jnp.bfloat16)
    keep(grad_att, grad_att_out)
    for n in range(4):
        dw[part(n), pl.ds(*FAR_SPANS[0])] = jnp.dot(
            branch_t[part(n), :], att[...], preferred_element_type=jnp.float32
        ).astype(jnp.bfloat16)
    keep(dw.at[:, pl.ds(*FAR_SPANS[0])], dw_out.at[:, pl.ds(*FAR_SPANS[0])])
    third.wait_recv()
    output[...] = (
        middle[own, :] + (down_own[...] + in3[...].astype(jnp.float32))
    ).astype(jnp.bfloat16)
    for copy in swaps:
        copy.wait_send()
    for copy in stores:
        copy.wait()


def forward_kernel(*refs):
    gains_in, shards, (x_in, g_in, cos_in, sin_in), refs = refs[:4], refs[4:11], refs[11:15], refs[15:]
    near_out, x_out, tab_out, q_out, k_out, v_out, o32_out, lse_ref, normed_out = refs[:9]
    qpre_out, kpre_out, rows_ref, output, grad_att_out, gmid_out, post_out, dw_out = refs[9:17]
    x_ref, g_ref, tab, w_near, w_far, normed, qpre, kpre, q_low, k_low, v_low = refs[17:28]
    q_ref, k_ref, v_ref, o32_ref, o_low, att, vt, near_unit, far_unit, tab_own = refs[28:38]
    middle_refs, refs = refs[38:57], refs[57:]
    send, recv, head_send, head_recv, local, load, store, pair_send, pair_recv, pair_local, own = refs
    weights = (w_near, w_far)
    yh, z, x, yl, c = place()
    sib = sibling()
    others = ring_devices() + [sib]
    greet(others)
    lanes = lax.broadcasted_iota(jnp.int32, (TILE, TILE), 1)
    rows = lax.broadcasted_iota(jnp.int32, (TILE, TILE), 0)
    tile = jnp.zeros((TILE, TILE), jnp.float32)
    for n, gain in enumerate(gains_in):
        value = gain[...].astype(jnp.float32)
        if value.shape[1] == 1:
            tile = jnp.where((rows == n) & (lanes == 0), value, tile)
        else:
            value = jnp.concatenate([value, jnp.zeros((1, TILE - 8), jnp.float32)], axis=1)
            tile = jnp.where(rows == n, value, tile)
    tile = tile.T[:8].astype(jnp.bfloat16)
    places = [(near_unit, 0), (near_unit, 1024), (near_unit, 1536)]
    places += [(far_unit, first) for first, _ in FAR_SPANS]
    for shard, (unit, first) in zip(shards, places):
        width = shard.shape[1] // 2
        for half in range(2):
            unit[half, :, first : first + width] = shard[:, half * width : (half + 1) * width]
    near_unit[0, :, 2048:] = tile
    near_unit[1, :, 2048:] = tile
    tab_own[...] = jnp.concatenate([cos_in[...], sin_in[...]], axis=1)
    await_greetings(others)
    near, far = near_parts(), far_parts((21, 11, 12))
    gather = Gather((near_unit, far_unit), weights, (0, 3 * GATHER_SLOTS), send, recv, own)
    gather.spread(near)
    pairs = []
    for k, (source, target) in enumerate(((x_in, x_ref), (tab_own, tab), (g_in, g_ref))):
        keep = pltpu.make_async_copy(source, target.at[c], pair_local.at[k])
        away = pltpu.make_async_remote_copy(
            source, target.at[c], pair_send.at[k], pair_recv.at[k], device_id=sib
        )
        keep.start()
        away.start()
        pairs.append((keep, away))
    gather.spread(far)
    for part in near:
        gather.settle(part)
        gather.direct(part)
    gather.settle(far[0])
    gather.begin(far[:1], 1)
    for part in near:
        gather.landed(part)
        gather.begin([part], 2)
    for part in far[1:]:
        gather.settle(part)
        gather.begin([part], 1)
    gather.forward(near, 2)
    gather.forward(far, 1)
    gather.arrive(far[:1], 1)
    gather.begin(far[:1], 2)
    gather.arrive(near, 2)
    keep_near = pltpu.make_async_copy(w_near, near_out, load.at[0])
    keep_near.start()
    gather.arrive(far[1:], 1)
    gather.ring(far[1], 2, 0)
    gather.ring(far[2], 2, 0)
    for keep, away in pairs:
        keep.wait()
        away.wait_recv()

    def matrix(first, width):
        return w_near[:, :, :, :, :, :, first : first + width].reshape(D, width)

    gain_rows = matrix(2048, TILE).astype(jnp.float32).T[:8]
    pick = (
        lax.broadcasted_iota(jnp.int32, (D, HEAD_DIM), 0)
        == 8 * lax.broadcasted_iota(jnp.int32, (D, HEAD_DIM), 1)
    ).astype(jnp.bfloat16)
    head_gains = jnp.dot(gain_rows.astype(jnp.bfloat16), pick, preferred_element_type=jnp.float32)
    rows_ref[...] = gain_rows
    rows_ref[2:4, :HEAD_DIM] = head_gains[2:4]
    gain_q, gain_k = head_gains[2:3], head_gains[3:4]
    values = x_ref[...].reshape(BLOCK, D).astype(jnp.float32)
    normed[...] = (values * rms_scale(values) * gain_rows[0:1]).astype(jnp.bfloat16)
    cosine, sine = rope_pair(tab)

    def head(pre, gain):
        unit = pre * rms_scale(pre) * gain
        return (unit * cosine + pltpu.roll(unit, HEAD_DIM // 2, 1) * sine).astype(jnp.bfloat16)

    for first, pre_ref, low_ref, gain in ((0, qpre, q_low, gain_q), (1024, kpre, k_low, gain_k)):
        for n in range(pre_ref.shape[1] // 256):
            at = slice(n * 256, n * 256 + 256)
            pre = jnp.dot(normed[...], matrix(first + n * 256, 256), preferred_element_type=jnp.float32)
            pre_ref[:, at] = pre
            low_ref[:, n * 256 : n * 256 + 128] = head(pre[:, :128], gain)
            low_ref[:, n * 256 + 128 : n * 256 + 256] = head(pre[:, 128:], gain)
    v_low[...] = jnp.dot(normed[...], matrix(1536, 512), preferred_element_type=jnp.float32).astype(jnp.bfloat16)
    pairs_kv = ((k_low, k_ref), (v_low, v_ref))
    ring_kv = [
        along_x(
            n, lambda t, low=low: low.at[:, columns(t)], lambda t, ref=ref: ref.at[2 * t + yl],
            head_send, head_recv, local,
        )
        for n, (low, ref) in enumerate(pairs_kv)
    ]
    relays = []

    def relay(n, step, source, target):
        copy = pltpu.make_async_remote_copy(
            source, target, head_send.at[4 + n, step], head_recv.at[4 + n, step], device_id=y_partner()
        )
        copy.start()
        relays.append(copy)

    for n, (low, ref) in enumerate(pairs_kv):
        relay(n, 0, low.at[:, columns(x)], ref.at[2 * x + yl])
    ring_q = along_x(
        2, lambda t: q_low.at[:, columns(t, 2)], lambda t: q_ref.at[t], head_send, head_recv, local
    )
    stores = [
        pltpu.make_async_copy(a, b, store.at[n])
        for n, (a, b) in enumerate(
            ((normed, normed_out), (qpre, qpre_out), (kpre, kpre_out), (q_ref, q_out), (k_ref, k_out),
             (v_ref, v_out), (o32_ref, o32_out), (x_ref, x_out), (tab, tab_out))
        )
    ]
    for copy in stores[:3] + stores[7:]:
        copy.start()
    for step in (1, 3, 2):
        there = 2 * ((x - step + 4) % 4) + yl
        for n, (_, ref) in enumerate(pairs_kv):
            ring_kv[n][step].wait_recv()
            relay(n, step, ref.at[there], ref.at[there])
    for copies in (*ring_kv, ring_q):
        copies[0].wait()
    for step in (1, 2, 3):
        ring_q[step].wait_recv()
    for copy in relays:
        copy.wait_recv()
    gather.forward(far[:1], 2)
    gather.ring(far[1], 2, 1)
    gather.ring(far[2], 2, 1)
    gather.forward(far[1:], 2)
    for copy in stores[3:6]:
        copy.start()
    for j in range(8):
        vt[j] = v_ref[j].T

    def one_block(n, _):
        queries = (q_ref[n, :, :HEAD_DIM], q_ref[n, :, HEAD_DIM:])

        def weigh(j, carry):
            after = []
            for q, (total, mixed) in zip(queries, carry):
                p = jnp.exp2(nt(k_ref[j], q) * (score_scale * log2e))
                total = total + jnp.sum(p, axis=0, keepdims=True)
                mixed = mixed + jnp.dot(
                    vt[j], p.astype(jnp.bfloat16), preferred_element_type=jnp.float32
                )
                after.append((total, mixed))
            return tuple(after)

        start = (jnp.zeros((1, BLOCK), jnp.float32), jnp.zeros((HEAD_DIM, BLOCK), jnp.float32))
        carry = lax.fori_loop(0, 2 * n + yl + 1, weigh, (start, start))
        for h, (total, mixed) in enumerate(carry):
            out = (mixed / total).T
            o32_ref[n, :, h * HEAD_DIM : (h + 1) * HEAD_DIM] = out
            o_low[n, :, h * HEAD_DIM : (h + 1) * HEAD_DIM] = out.astype(jnp.bfloat16)
            lse_ref[n, h] = jnp.log2(total)
        return 0

    leaving = moves_along_x(
        3, lambda t: o_low.at[t], lambda t: att.at[:, columns(t, 2)], head_send, head_recv, local
    )
    for step in (2, 1, 3, 0):
        one_block((x + step) % 4, 0)
        leaving[step].start()
    stores[6].start()
    g_low = g_ref[...].reshape(BLOCK, D)
    g_t = middle_refs[3]
    g_t[...] = g_low.T
    gather.arrive(far[1:2], 2)
    for copy in leaving:
        copy.wait()
    middle_layer(
        gather, far, att, x_ref, g_low, rows_ref, w_far, middle_refs, (output, grad_att_out, gmid_out, post_out, dw_out),
        pair_send, pair_recv, own, c, sib,
    )
    gather.drain()
    for copy in stores:
        copy.wait()
    keep_near.wait()
    for _, away in pairs:
        away.wait_send()
    for copies in (*ring_kv, ring_q):
        for copy in copies[1:]:
            copy.wait_send()
    for copy in relays:
        copy.wait_send()


def attend(gains, shards, tokens):
    blocks, pairs = (8, BLOCK, HEAD_DIM), (4, BLOCK, 2 * HEAD_DIM)
    low, wide = jnp.bfloat16, jnp.float32
    whole = [(2, 4, 4, 2, 2, 8, w) for w in WIDE]
    return pl.pallas_call(
        forward_kernel,
        out_shape=[
            jax.ShapeDtypeStruct(whole[NEAR], low),
            jax.ShapeDtypeStruct((2, 128, D), low),
            jax.ShapeDtypeStruct((2, 128, HEAD_DIM), wide),
        ]
        + [
            jax.ShapeDtypeStruct(pairs, low),
            jax.ShapeDtypeStruct(blocks, low),
            jax.ShapeDtypeStruct(blocks, low),
            jax.ShapeDtypeStruct(pairs, wide),
            jax.ShapeDtypeStruct((4, 2, 1, BLOCK), wide),
            jax.ShapeDtypeStruct((BLOCK, D), low),
            jax.ShapeDtypeStruct((BLOCK, 1024), wide),
            jax.ShapeDtypeStruct((BLOCK, 512), wide),
            jax.ShapeDtypeStruct((8, D), wide),
            jax.ShapeDtypeStruct((128, D), low),
            jax.ShapeDtypeStruct((BLOCK, 1024), low),
            jax.ShapeDtypeStruct((128, D), wide),
            jax.ShapeDtypeStruct((8, D), wide),
            jax.ShapeDtypeStruct((D, WIDE[FAR]), low),
        ],
        in_specs=[VMEM] * 15,
        out_specs=[HBM] * 7 + [VMEM] + [HBM] * 3 + [VMEM, VMEM, HBM, VMEM, VMEM, HBM],
        scratch_shapes=[
            pltpu.VMEM((2, 128, D), low),
            pltpu.VMEM((2, 128, D), low),
            pltpu.VMEM((2, 128, HEAD_DIM), wide),
            pltpu.VMEM(whole[NEAR], low),
            pltpu.VMEM(whole[FAR], low),
            pltpu.VMEM((BLOCK, D), low),
            pltpu.VMEM((BLOCK, 1024), wide),
            pltpu.VMEM((BLOCK, 512), wide),
            pltpu.VMEM((BLOCK, 1024), low),
            pltpu.VMEM((BLOCK, 512), low),
            pltpu.VMEM((BLOCK, 512), low),
        ]
        + [
            pltpu.VMEM(pairs, low),
            pltpu.VMEM(blocks, low),
            pltpu.VMEM(blocks, low),
            pltpu.VMEM(pairs, wide),
            pltpu.VMEM(pairs, low),
            pltpu.VMEM((BLOCK, 1024), low),
            pltpu.VMEM((8, HEAD_DIM, BLOCK), low),
            pltpu.VMEM((2, 8, WIDE[0]), low),
            pltpu.VMEM((2, 8, WIDE[1]), low),
            pltpu.VMEM((128, HEAD_DIM), wide),
        ]
        + middle_shapes()
        + [
            pltpu.SemaphoreType.DMA((6 * GATHER_SLOTS,)),
            pltpu.SemaphoreType.DMA((6 * GATHER_SLOTS,)),
            pltpu.SemaphoreType.DMA((6, 4)),
            pltpu.SemaphoreType.DMA((6, 4)),
            pltpu.SemaphoreType.DMA((4,)),
            pltpu.SemaphoreType.DMA((1,)),
            pltpu.SemaphoreType.DMA((9,)),
            pltpu.SemaphoreType.DMA((12,)),
            pltpu.SemaphoreType.DMA((12,)),
            pltpu.SemaphoreType.DMA((3,)),
            pltpu.SemaphoreType.DMA((11,)),
        ],
        compiler_params=pltpu.CompilerParams(
            collective_id=2, has_side_effects=True, vmem_limit_bytes=LIMIT
        ),
        name="attend",
    )(*gains, *shards, *tokens)


def backward_kernel(*refs):
    near, far = near_parts(), far_parts()
    n_scatter = len(scatter_shapes())
    ins, far_grad, do_in, refs = refs[:14], refs[14], refs[15], refs[16:]
    fin, input_grad, held, refs = refs[:2], refs[2], refs[3:17], refs[17:]
    q_ref, k_ref, v_ref, o32_ref, lse_ref, qpre, kpre, normed, tab, rows, x_ref = held[:11]
    w_near, gmid, post = held[11:]
    do_ref, dq_low, dk_low, dv_low, kt, dk_acc, dv_acc, k_in, v_in, k_sum, v_sum = refs[:11]
    gq, k_part_in, v_part_in, dqkv, normed_t, pair_out, pair_in, near_grad = refs[11:19]
    places, refs = refs[19 : 19 + n_scatter], refs[19 + n_scatter :]
    send, recv, pair_send, pair_recv, load, far_load, head_send, head_recv, head_local = refs
    yh, z, x, yl, c = place()
    sib = sibling()
    scatter = Scatter((near_grad, far_grad), fin, places, send, recv)
    loads = load_all(list(zip(ins, held)), load)
    for n, part in enumerate(far):
        scatter.load(part, far_load.at[n])
    greet(ring_devices() + [sib])
    await_greetings(ring_devices() + [sib])
    arriving = along_x(
        0, lambda t: do_in.at[:, columns(t, 2)], lambda t: do_ref.at[t], head_send, head_recv, head_local
    )
    scatter.begin(far[:1], 0)
    scatter.begin(far[1:], 0)
    for copy in loads[:5]:
        copy.wait()
    for j in range(8):
        kt[j] = k_ref[j].T
    dk_acc[...] = jnp.zeros_like(dk_acc)
    dv_acc[...] = jnp.zeros_like(dv_acc)
    for copy in arriving:
        copy.wait()

    def one_block(n, _):
        heads = []
        for h in range(2):
            at = slice(h * HEAD_DIM, (h + 1) * HEAD_DIM)
            q, do = q_ref[n, :, at], do_ref[n, :, at]
            delta = jnp.sum((do.astype(jnp.float32) * o32_ref[n, :, at]).T, axis=0, keepdims=True)
            heads.append((q, do, lse_ref[n, h], delta))

        def one_pair(j, dqts):
            after, dk_term, dv_term = [], 0.0, 0.0
            for (q, do, lse, delta), dqt in zip(heads, dqts):
                p = jnp.exp2(nt(k_ref[j], q) * (score_scale * log2e) - lse)
                ds = (p * (nt(v_ref[j], do) - delta)).astype(jnp.bfloat16)
                dv_term += jnp.dot(p.astype(jnp.bfloat16), do, preferred_element_type=jnp.float32)
                dk_term += jnp.dot(ds, q, preferred_element_type=jnp.float32)
                after.append(dqt + jnp.dot(kt[j], ds, preferred_element_type=jnp.float32))
            dv_acc[j // 2, j % 2] += dv_term
            dk_acc[j // 2, j % 2] += dk_term
            return tuple(after)

        start = jnp.zeros((HEAD_DIM, BLOCK), jnp.float32)
        dqts = lax.fori_loop(0, 2 * n + yl + 1, one_pair, (start, start))
        for h, dqt in enumerate(dqts):
            dq_low[n, :, h * HEAD_DIM : (h + 1) * HEAD_DIM] = (dqt * score_scale).T.astype(jnp.bfloat16)
        return 0

    ring_q = moves_along_x(
        1, lambda t: dq_low.at[t], lambda t: gq.at[:, columns(t, 2)], head_send, head_recv, head_local
    )
    for step in (2, 1, 3):
        one_block((x + step) % 4, 0)
        ring_q[step].start()
    scatter.middle(far[:1], 0)
    scatter.middle(far[1:], 0)
    one_block(x, 0)
    ring_q[0].start()
    sums = ((dk_acc, dk_low, k_in, k_sum, k_part_in, score_scale), (dv_acc, dv_low, v_in, v_sum, v_part_in, 1.0))
    across = {}
    for n, (acc, low, landing, _, _, scale) in enumerate(sums):
        low[...] = (acc[:, 1 - yl] * scale).astype(jnp.bfloat16)
        for step in (1, 2, 3, 0):
            there = (x + step) % 4
            copy = pltpu.make_async_remote_copy(
                low.at[there], landing.at[there], head_send.at[4 + n, step], head_recv.at[4 + n, step],
                device_id=y_partner(),
            )
            copy.start()
            across[n, step] = copy
    ring_kv = []
    for step in (1, 2, 3, 0):
        there = (x + step) % 4
        for n, (acc, _, landing, total, part_in, scale) in enumerate(sums):
            across[n, step].wait_recv()
            total[there] = (
                acc[there, yl] * scale + landing[there].astype(jnp.float32)
            ).astype(jnp.bfloat16)
            target = part_in.at[:, columns(x)]
            if step == 0:
                copy = pltpu.make_async_copy(total.at[there], target, head_local.at[2 + n])
            else:
                copy = pltpu.make_async_remote_copy(
                    total.at[there], target, head_send.at[2 + n, step], head_recv.at[2 + n, step],
                    device_id=ring_device("x", step, 0),
                )
            copy.start()
            ring_kv.append(copy)
    for copy in loads[5:]:
        copy.wait()
    normed_t[...] = normed[...].T
    cosine, sine = rope_pair(tab)
    gain_q, gain_k = rows[2:3, :HEAD_DIM], rows[3:4, :HEAD_DIM]

    def head_back(grad, values, gain):
        grad = grad * cosine - pltpu.roll(grad, HEAD_DIM // 2, 1) * sine
        grad_in, terms = norm_back(grad, values, rms_scale(values), gain)
        return grad_in.astype(jnp.bfloat16), jnp.sum(terms, axis=0, keepdims=True)

    def weight_grads(first):
        def one(n, _):
            lhs = normed_t[pl.ds(pl.multiple_of(n * 256, 256), 256), :]
            for at in (first, first + 512):
                block = jnp.dot(lhs, dqkv[:, at : at + 512], preferred_element_type=jnp.float32)
                near_grad[n // 2, pl.ds(n % 2 * 2, 2), :, :, :, at : at + 512] = block.astype(
                    jnp.bfloat16
                ).reshape(2, 4, 2, 16, 512)
            return 0

        lax.fori_loop(0, 4, one, 0)

    for copy in ring_q:
        copy.wait()
    q_part = jnp.zeros((1, HEAD_DIM), jnp.float32)
    k_part = jnp.zeros((1, HEAD_DIM), jnp.float32)
    for h in range(8):
        at = slice(h * HEAD_DIM, (h + 1) * HEAD_DIM)
        dqkv[:, at], part = head_back(gq[:, at].astype(jnp.float32), qpre[:, at], gain_q)
        q_part = q_part + part
    weight_grads(0)
    scatter.begin(near[:1], 0)
    scatter.end(far[:1], 0)
    scatter.begin(far[:1], 1)
    scatter.end(far[1:], 0)
    scatter.begin(far[1:], 1)
    for copy in ring_kv:
        copy.wait()
    for h in range(4):
        at = slice(h * HEAD_DIM, (h + 1) * HEAD_DIM)
        low_at = slice(1024 + h * HEAD_DIM, 1024 + (h + 1) * HEAD_DIM)
        dqkv[:, low_at], part = head_back(k_part_in[:, at].astype(jnp.float32), kpre[:, at], gain_k)
        k_part = k_part + part
    dqkv[:, 1536:] = v_part_in[...]
    weight_grads(1024)
    scatter.begin(near[1:2], 0)
    scatter.begin(near[2:], 0, (0,))

    def grad_normed(rows_at):
        return nt(dqkv[rows_at, :], w_near[:, :2048])

    away = pl.ds(pl.multiple_of((1 - c) * 128, 128), 128)
    own = pl.ds(pl.multiple_of(c * 128, 128), 128)
    pair_out[...] = grad_normed(away).astype(jnp.bfloat16)
    swap = pltpu.make_async_remote_copy(
        pair_out, pair_in, pair_send.at[0], pair_recv.at[0], device_id=sib
    )
    swap.start()
    grad = grad_normed(own)
    values = x_ref[c].astype(jnp.float32)
    swap.wait_recv()
    grad = grad + pair_in[...].astype(jnp.float32)
    grad_in, terms = norm_back(grad, values, rms_scale(values), rows[0:1, :])
    input_grad[...] = (gmid[...] + grad_in).astype(jnp.bfloat16)
    in_part = jnp.sum(terms, axis=0, keepdims=True)
    spread = (
        lax.broadcasted_iota(jnp.int32, (HEAD_DIM, D), 1)
        == 8 * lax.broadcasted_iota(jnp.int32, (HEAD_DIM, D), 0)
    ).astype(jnp.bfloat16)
    qk = jnp.concatenate([q_part, k_part, jnp.zeros((6, HEAD_DIM), jnp.float32)]).astype(jnp.bfloat16)
    qk = jnp.dot(qk, spread, preferred_element_type=jnp.float32)
    gain_rows = jnp.concatenate(
        [in_part, post[0:1, :], qk[0:2], jnp.zeros((TILE - 4, D), jnp.float32)]
    )
    near_grad[:, :, :, :, :, 2048:] = gain_rows.T.astype(jnp.bfloat16).reshape(2, 4, 4, 2, 16, TILE)
    scatter.begin(near[2:], 0, (1,))
    scatter.middle(near, 0)
    scatter.middle(far, 1)
    for part in near:
        scatter.end([part], 0)
        scatter.direct([part])
    for part in far:
        scatter.end([part], 1)
        scatter.deliver([part])
    for part in near:
        scatter.landed([part])
        scatter.deliver([part])
    scatter.finish(far)
    scatter.finish(near)
    scatter.drain()
    swap.wait_send()
    for copy in across.values():
        copy.wait_send()


def attend_back(arrays, far_grad, grad_att):
    blocks, pairs, split = (8, BLOCK, HEAD_DIM), (4, BLOCK, 2 * HEAD_DIM), (4, BLOCK, HEAD_DIM)
    low, wide = jnp.bfloat16, jnp.float32
    return pl.pallas_call(
        backward_kernel,
        out_shape=[jax.ShapeDtypeStruct((2, 8, w), wide) for w in WIDE]
        + [jax.ShapeDtypeStruct((128, D), low)],
        in_specs=[HBM] * (len(arrays) + 2),
        out_specs=[VMEM] * 3,
        scratch_shapes=[pltpu.VMEM(a.shape, a.dtype) for a in arrays]
        + [pltpu.VMEM(pairs, low)] * 2
        + [pltpu.VMEM(split, low)] * 2
        + [
            pltpu.VMEM((8, HEAD_DIM, BLOCK), low),
            pltpu.VMEM((4, 2, BLOCK, HEAD_DIM), wide),
            pltpu.VMEM((4, 2, BLOCK, HEAD_DIM), wide),
        ]
        + [pltpu.VMEM(split, low)] * 4
        + [
            pltpu.VMEM((BLOCK, 1024), low),
            pltpu.VMEM((BLOCK, 512), low),
            pltpu.VMEM((BLOCK, 512), low),
            pltpu.VMEM((BLOCK, 2048), low),
            pltpu.VMEM((D, BLOCK), low),
            pltpu.VMEM((128, D), low),
            pltpu.VMEM((128, D), low),
            pltpu.VMEM((2, 4, 4, 2, 16, WIDE[0]), low),
        ]
        + scatter_shapes()
        + [
            pltpu.SemaphoreType.DMA((6 * GATHER_SLOTS,)),
            pltpu.SemaphoreType.DMA((6 * GATHER_SLOTS,)),
            pltpu.SemaphoreType.DMA((1,)),
            pltpu.SemaphoreType.DMA((1,)),
            pltpu.SemaphoreType.DMA((len(arrays),)),
            pltpu.SemaphoreType.DMA((3, 4)),
            pltpu.SemaphoreType.DMA((6, 4)),
            pltpu.SemaphoreType.DMA((6, 4)),
            pltpu.SemaphoreType.DMA((4,)),
        ],
        compiler_params=pltpu.CompilerParams(
            collective_id=3, has_side_effects=True, vmem_limit_bytes=LIMIT
        ),
        name="attend_back",
    )(*arrays, far_grad, grad_att)


def results_kernel(near, far, grad_in, out_in, *refs):
    (q, k, v, in_gain, post_gain, q_gain, k_gain, w_out, gate, up, down, grad, out) = refs
    for source, group in ((near, ((q, 0), (k, 1024), (v, 1536))), (far, zip((w_out, gate, up, down), [s for s, _ in FAR_SPANS]))):
        for target, first in group:
            width = target.shape[1] // 2
            for half in range(2):
                target[:, half * width : (half + 1) * width] = source[half, :, first : first + width]
    gains = near[0, :, 2048:] + near[1, :, 2048:]
    gains = jnp.concatenate([gains, jnp.zeros((TILE - 8, TILE), jnp.float32)]).T
    in_gain[...] = gains[0:1, :8]
    post_gain[...] = gains[1:2, :8]
    q_gain[...] = gains[2:3, :1]
    k_gain[...] = gains[3:4, :1]
    grad[...] = grad_in[...]
    out[...] = out_in[...]


def results(arrays):
    shapes = [(8, 2048), (8, 1024), (8, 1024), (1, 8), (1, 8), (1, 1), (1, 1)]
    shapes += [(8, 2 * width) for _, width in FAR_SPANS]
    return pl.pallas_call(
        results_kernel,
        out_shape=[jax.ShapeDtypeStruct(s, jnp.float32) for s in shapes]
        + [jax.ShapeDtypeStruct((128, D), jnp.bfloat16)] * 2,
        in_specs=[VMEM] * 4,
        out_specs=[VMEM] * 13,
        name="results",
    )(*arrays)


def body(
    tokens,
    positions,
    in_gain,
    q_gain,
    k_gain,
    w_query,
    w_key,
    w_value,
    w_out,
    post_gain,
    w_gate,
    w_up,
    w_down,
    cotangent,
):
    half = HEAD_DIM // 2
    frequency = rope_base ** (-2.0 * jnp.arange(half, dtype=jnp.float32) / HEAD_DIM)
    angles = positions[0].astype(jnp.float32)[:, None] * frequency[None, :]
    gains = [g[None] for g in (in_gain, post_gain, q_gain, k_gain)]
    shards = [w_query, w_key, w_value, w_out.T, w_gate, w_up, w_down.T]
    (near, x_pair, tables, q_all, k_all, v_all, mixed, log_total, normed, q_pre, k_pre, rows, output,
     grad_att, grad_middle, post_part, far_grad) = attend(
        gains, shards, [tokens[0], cotangent[0], jnp.cos(angles), jnp.sin(angles)]
    )
    near_sum, far_sum, input_grad = attend_back(
        [q_all, k_all, v_all, mixed, log_total, q_pre, k_pre, normed, tables, rows, x_pair,
         near.reshape(D, WIDE[NEAR]), grad_middle, post_part],
        far_grad.reshape(2, 4, 4, 2, 16, WIDE[FAR]),
        grad_att,
    )
    (query, key, value, in_gain_grad, post_gain_grad, q_gain_grad, k_gain_grad, out_grad, gate, up, down,
     input_grad, output) = results([near_sum, far_sum, input_grad, output])
    return (
        output[None],
        input_grad[None],
        in_gain_grad[0],
        q_gain_grad[0],
        k_gain_grad[0],
        query,
        key,
        value,
        out_grad.T,
        post_gain_grad[0],
        gate,
        up,
        down.T,
    )


def solution(mesh):
    placed = (
        P("dp", "seq", None),
        P("dp", "seq"),
        P(("dp", "seq")),
        P(("dp", "seq")),
        P(("dp", "seq")),
        P(("dp", "seq"), None),
        P(("dp", "seq"), None),
        P(("dp", "seq"), None),
        P(None, ("dp", "seq")),
        P(("dp", "seq")),
        P(("dp", "seq"), None),
        P(("dp", "seq"), None),
        P(None, ("dp", "seq")),
        P("dp", "seq", None),
    )
    return jax.shard_map(
        body,
        mesh=mesh,
        in_specs=placed,
        out_specs=(
            P("dp", "seq", None),
            P("dp", "seq", None),
            P(("dp", "seq")),
            P(("dp", "seq")),
            P(("dp", "seq")),
            P(("dp", "seq"), None),
            P(("dp", "seq"), None),
            P(("dp", "seq"), None),
            P(None, ("dp", "seq")),
            P(("dp", "seq")),
            P(("dp", "seq"), None),
            P(("dp", "seq"), None),
            P(None, ("dp", "seq")),
        ),
        check_vma=False,
    )
```
